128 devices in a mesh: gx: 8 (over y, core), gy: 16 (over x, z).
Axes of the slice: x: 4, y: 4, z: 4, core: 2. Of those that a mesh axis runs over, the one named last changes fastest.
Arguments:
- cell_state: float32 [16, 1048576], P(None, ('gx', 'gy')), may hold values from -6 to 6
- geometry: float32 [7, 524288], P(None, ('gx', 'gy')), may hold values from -8 to 8, as said below
- surface_cell: int32 [524288], P(('gx', 'gy')), may hold values from 0 to 8191
- counts: int32 [128], P(('gx', 'gy')), may hold values from 128 to 4096, as said below
- wavenumbers: float32 [4], replicated, may hold values from 8 to 24
- target: float32 [4, 2, 2048], replicated, may hold values from -6 to 6
- direction_weight: float32 [2048], replicated, may hold values from 0.3 to 3
Outputs:
- far_field: float32 [4, 2, 2048], replicated
- objective: float32 [], replicated
- cell_adjoint: float32 [16, 1048576], P(None, ('gx', 'gy'))
The draws below stay inside these ranges and needn't reach their ends.
Inputs may be any that keep to these rules, and one draw needn't show every extreme that they name: Every count is a multiple of 128; one device's count is 4096; all counts together make 128 * 1024. `geometry`: rows 3 to 5 are unit vectors; row 6 is positive.
All inputs are finite; a program needn't handle non-finite values.
Results may differ from the reference program's by a relative error of at most 0.022.
Values sent between devices are 32-bit elements; how exact they have to be, the bound alone decides.
A program may use at most 128 MiB of HBM per device.

```python
import math
import jax
import jax.numpy as jnp
from jax import lax

F = 4
DIRS = 2048
ROWS_DEV = 4096
OWNERS = 128
CAP = 32
LIVE_OWN = 1024
LIVE_ALL = 131072
ROWS = 524288
CELLS_DEV = 8192
CELLS = 1048576


def draw_geometry(key, part):
    key_height = jax.random.fold_in(key, 0)
    key_turn = jax.random.fold_in(key, 1)
    key_area = jax.random.fold_in(key, 3)
    height = jax.random.uniform(key_height, (ROWS,), jnp.float32, -1.0, 1.0)
    azimuth = jax.random.uniform(key_turn, (ROWS,), jnp.float32, -math.pi, math.pi)
    radius_xy = jnp.sqrt(jnp.maximum(1.0 - height * height, 0.0))
    normal = jnp.stack([radius_xy * jnp.cos(azimuth), radius_xy * jnp.sin(azimuth), height])
    radius = jnp.full((ROWS,), 6.0, jnp.float32)
    spread = jax.random.uniform(key_area, (ROWS,), jnp.float32, math.log(0.5), math.log(2.0))
    surface_area = jnp.exp(spread) * (0.05 / math.sqrt(LIVE_ALL))
    return jnp.concatenate([normal * radius[None, :], normal, surface_area[None, :]], axis=0).astype(jnp.float32)


def draw_counts(key, part):
    key_full, key_order, key_pairs, key_shift = jax.random.split(key, 4)
    full_device = jax.random.randint(key_full, (), 0, OWNERS)
    others = LIVE_OWN - CAP
    base_units = others // (OWNERS - 1)
    extra_units = others % (OWNERS - 1)
    ranking = jax.random.permutation(key_order, OWNERS - 1)
    units = base_units + (ranking < extra_units).astype(jnp.int32)
    pair_count = (OWNERS - 1) // 2
    picked = jax.random.permutation(key_pairs, OWNERS - 1)
    first_side = picked[:pair_count]
    second_side = picked[pair_count:2 * pair_count]
    limit = jnp.minimum(units[first_side] - 1, CAP - units[second_side])
    moving = jax.random.randint(key_shift, (pair_count,), 0, limit + 1)
    units = units.at[first_side].add(-moving).at[second_side].add(moving)
    lattice = jnp.arange(OWNERS)
    other_index = jnp.clip(lattice - (lattice > full_device).astype(jnp.int32), 0, OWNERS - 2)
    multiples = jnp.where(lattice == full_device, CAP, units[other_index])
    return (multiples * OWNERS).astype(jnp.int32)


def with_ends(values, key, smallest, high):
    extent = values.shape
    place = [jax.random.randint(jax.random.fold_in(key, axis), (), 0, extent[axis]) for axis in range(len(extent))]
    values = values.at[tuple(place)].set(smallest)
    longest = extent.index(max(extent))
    place[longest] = (place[longest] + 1) % extent[longest]
    return values.at[tuple(place)].set(high)


def levels(stream_key, extent, cuts, least, high):
    loudness = 1.0
    for dim, parts in cuts:
        steps = jax.random.uniform(jax.random.fold_in(jax.random.fold_in(stream_key, 6), dim), (parts,), jnp.float32, least / len(cuts), high / len(cuts))
        loudness = loudness * jnp.repeat(jnp.exp(steps), extent[dim] // parts).reshape((-1,) + (1,) * (len(extent) - 1 - dim))
    return loudness


def gaussian(stream_key, extent, width, reach, cuts=(), held_as=jnp.bfloat16):
    factor_of = levels(stream_key, extent, cuts, -0.22, 0.18) if cuts else 1.0
    array = jax.random.normal(stream_key, extent, jnp.float32) * width * factor_of
    return jnp.minimum(jnp.maximum(array, -reach), reach).astype(held_as)


def setup_inputs(seed: int = 0) -> dict:
    key_list = jax.random.split(jax.random.key(seed), 8)
    return {
        "cell_state": gaussian(key_list[0], (16, CELLS), 1.0, 6.0, ((1, 128),), jnp.float32),
        "geometry": draw_geometry(jax.random.fold_in(key_list[7], 71), 0),
        "surface_cell": with_ends(jax.random.randint(key_list[2], (ROWS,), 0, CELLS_DEV), jax.random.fold_in(key_list[2], 1), 0, CELLS_DEV - 1).astype(jnp.int32),
        "counts": draw_counts(jax.random.fold_in(key_list[7], 71), 0),
        "wavenumbers": jnp.clip(jnp.exp(jax.random.uniform(key_list[4], (F,), jnp.float32, math.log(8.0), math.log(24.0))), 8.0, 24.0),
        "target": gaussian(key_list[5], (F, 2, DIRS), 1.0, 6.0, (), jnp.float32),
        "direction_weight": jnp.clip(jnp.exp(jax.random.uniform(key_list[6], (DIRS,), jnp.float32, math.log(0.3), math.log(3.0))), 0.3, 3.0),
    }


GOLDEN = math.pi * (3.0 - math.sqrt(5.0))

def directions(count_dirs):
    lattice = jnp.arange(count_dirs).astype(jnp.float32)
    height = 1.0 - (2.0 * lattice + 1.0) / count_dirs
    radius_xy = jnp.sqrt(1.0 - height * height)
    azimuth = jnp.mod(lattice * GOLDEN, 2.0 * math.pi)
    return (radius_xy * jnp.cos(azimuth), radius_xy * jnp.sin(azimuth), height)

def kernel_block(points, wavenum, east_x, north_y, upward):
    phases = wavenum * (points[0][:, None] * east_x[None, :] + points[1][:, None] * north_y[None, :] + points[2][:, None] * upward[None, :])
    return jnp.concatenate([jnp.cos(phases), jnp.sin(phases)], axis=1).astype(jnp.bfloat16)

def source_rows(rows_block, level):
    surface_area = rows_block[22]
    normal = rows_block[19:22]
    pressure_real = rows_block[level] * surface_area
    pressure_imag = rows_block[4 + level] * surface_area
    return jnp.stack([rows_block[8 + level] * surface_area, normal[0] * pressure_real, normal[1] * pressure_real, normal[2] * pressure_real, rows_block[12 + level] * surface_area, normal[0] * pressure_imag, normal[1] * pressure_imag, normal[2] * pressure_imag]).astype(jnp.bfloat16)

def far_field_of(sums, wavenumbers, direction_basis):
    half_width = sums.shape[2] // 2
    cosine_part = sums[:, :, :half_width]
    sine_part = sums[:, :, half_width:]
    real_q = cosine_part[:, 0:4] + sine_part[:, 4:8]
    imag_q = cosine_part[:, 4:8] - sine_part[:, 0:4]
    real_z = lax.optimization_barrier(jnp.sum(direction_basis[None] * real_q, axis=1))
    imag_z = lax.optimization_barrier(jnp.sum(direction_basis[None] * imag_q, axis=1))
    wavenum = wavenumbers[:, None]
    return jnp.stack([-wavenum * imag_z, wavenum * real_z], axis=1)

def adjoint_weights(far_field, target, direction_weight, wavenumbers, direction_basis):
    count_dirs = far_field.shape[2]
    mismatch = far_field - target
    objective = jnp.sum(direction_weight * mismatch * mismatch) / count_dirs
    gradient = 2.0 * direction_weight * mismatch / count_dirs
    wavenum = wavenumbers[:, None]
    real_gz = wavenum * gradient[:, 1]
    imag_gz = -wavenum * gradient[:, 0]
    real_gq = direction_basis[None] * real_gz[:, None]
    imag_gq = direction_basis[None] * imag_gz[:, None]
    upper_half = jnp.concatenate([real_gq, -imag_gq], axis=2)
    lower_half = jnp.concatenate([imag_gq, real_gq], axis=2)
    return (objective, jnp.concatenate([upper_half, lower_half], axis=1).astype(jnp.bfloat16))

def adjoint_sources(products, normal):
    pressure_real = lax.optimization_barrier(jnp.sum(normal[None] * products[:, 1:4], axis=1))
    pressure_imag = lax.optimization_barrier(jnp.sum(normal[None] * products[:, 5:8], axis=1))
    return jnp.concatenate([pressure_real, pressure_imag, products[:, 0], products[:, 4]], axis=0)

def reference(cell_state, geometry, surface_cell, counts, wavenumbers, target, direction_weight):
    num_freqs = wavenumbers.shape[0]
    count_dirs = target.shape[2]
    total_rows = surface_cell.shape[0]
    row_index = jnp.arange(total_rows).astype(jnp.int32)
    device = row_index // ROWS_DEV
    living = row_index % ROWS_DEV < counts[device]
    cell_index = (device * CELLS_DEV + surface_cell).astype(jnp.int32)
    live_rank = jnp.cumsum(living.astype(jnp.int32)) - 1
    packed_slot = jnp.where(living, live_rank, LIVE_ALL).astype(jnp.int32)
    values = jnp.concatenate([cell_state[:, cell_index], geometry], axis=0)
    packed = jnp.zeros((23, LIVE_ALL), values.dtype).at[:, packed_slot].set(values, mode='drop')
    block_rows = math.gcd(LIVE_ALL, 4096)
    block_count = LIVE_ALL // block_rows
    blocks = packed.reshape(23, block_count, block_rows).transpose(1, 0, 2)
    east_x, north_y, upward = directions(count_dirs)
    direction_basis = jnp.stack([jnp.ones_like(east_x), east_x, north_y, upward])

    def forward_block(running, rows_block):
        products = [jnp.dot(source_rows(rows_block, level), kernel_block(rows_block[16:19], wavenumbers[level], east_x, north_y, upward), preferred_element_type=jnp.float32) for level in range(num_freqs)]
        return (running + jnp.stack(products), None)
    sums, _ = lax.scan(forward_block, jnp.zeros((num_freqs, 8, 2 * count_dirs), jnp.float32), blocks)
    far_field = far_field_of(sums, wavenumbers, direction_basis)
    objective, weights = adjoint_weights(far_field, target, direction_weight, wavenumbers, direction_basis)

    def adjoint_block(carry, rows_block):
        products = [lax.dot_general(weights[level], kernel_block(rows_block[16:19], wavenumbers[level], east_x, north_y, upward), (((1,), (1,)), ((), ())), preferred_element_type=jnp.float32) for level in range(num_freqs)]
        return (carry, adjoint_sources(jnp.stack(products), rows_block[19:22]))
    _, backward = lax.scan(adjoint_block, jnp.zeros((), jnp.float32), blocks)
    backward = backward.transpose(1, 0, 2).reshape(16, LIVE_ALL)
    per_row = backward[:, jnp.minimum(packed_slot, LIVE_ALL - 1)] * living.astype(backward.dtype)[None, :]
    cell_adjoint = jnp.zeros(cell_state.shape, backward.dtype).at[:, cell_index].add(per_row)
    return (far_field, objective, cell_adjoint)
```

```python
import math

import jax
import jax.numpy as jnp
from jax import lax
from jax.sharding import PartitionSpec as P

GOLDEN = math.pi * (3.0 - math.sqrt(5.0))
PI_A = round(math.pi * 32768.0) / 32768.0
PI_B = math.pi - PI_A
INV_PI = 1.0 / math.pi
SIN_C = [(-1.0) ** k / math.factorial(2 * k + 1) for k in range(1, 6)]
COS_C = [(-1.0) ** k / math.factorial(2 * k) for k in range(1, 7)]


def sincos(theta):
    n = jnp.round(theta * INV_PI)
    r = (theta - n * PI_A) - n * PI_B
    z = r * r
    ps = SIN_C[-1]
    for c in SIN_C[-2::-1]:
        ps = c + z * ps
    pc = COS_C[-1]
    for c in COS_C[-2::-1]:
        pc = c + z * pc
    half = n * 0.5
    sign = 1.0 - 4.0 * (half - jnp.floor(half))
    return (sign * (1.0 + z * pc), sign * (r + (r * z) * ps))


def directions(count_dirs):
    lattice = jnp.arange(count_dirs).astype(jnp.float32)
    height = 1.0 - (2.0 * lattice + 1.0) / count_dirs
    radius_xy = jnp.sqrt(1.0 - height * height)
    azimuth = jnp.mod(lattice * GOLDEN, 2.0 * math.pi)
    return (radius_xy * jnp.cos(azimuth), radius_xy * jnp.sin(azimuth), height)


def kernel_block(points, wavenum, east_x, north_y, upward):
    phases = wavenum * (
        points[0][:, None] * east_x[None, :]
        + points[1][:, None] * north_y[None, :]
        + points[2][:, None] * upward[None, :]
    )
    cosine, sine = sincos(phases)
    return jnp.concatenate([cosine, sine], axis=1).astype(jnp.bfloat16)


def source_rows(rows_block, level):
    surface_area = rows_block[22]
    normal = rows_block[19:22]
    pressure_real = rows_block[level] * surface_area
    pressure_imag = rows_block[4 + level] * surface_area
    return jnp.stack(
        [
            rows_block[8 + level] * surface_area,
            normal[0] * pressure_real,
            normal[1] * pressure_real,
            normal[2] * pressure_real,
            rows_block[12 + level] * surface_area,
            normal[0] * pressure_imag,
            normal[1] * pressure_imag,
            normal[2] * pressure_imag,
        ]
    ).astype(jnp.bfloat16)


def far_field_of(sums, wavenumbers, direction_basis):
    half_width = sums.shape[2] // 2
    cosine_part = sums[:, :, :half_width]
    sine_part = sums[:, :, half_width:]
    real_q = cosine_part[:, 0:4] + sine_part[:, 4:8]
    imag_q = cosine_part[:, 4:8] - sine_part[:, 0:4]
    real_z = jnp.sum(direction_basis[None] * real_q, axis=1)
    imag_z = jnp.sum(direction_basis[None] * imag_q, axis=1)
    wavenum = wavenumbers[:, None]
    return jnp.stack([-wavenum * imag_z, wavenum * real_z], axis=1)


def adjoint_weights(far_field, target, direction_weight, wavenumbers, direction_basis):
    count_dirs = far_field.shape[2]
    mismatch = far_field - target
    objective = jnp.sum(direction_weight * mismatch * mismatch) / count_dirs
    gradient = 2.0 * direction_weight * mismatch / count_dirs
    wavenum = wavenumbers[:, None]
    real_gz = wavenum * gradient[:, 1]
    imag_gz = -wavenum * gradient[:, 0]
    real_gq = direction_basis[None] * real_gz[:, None]
    imag_gq = direction_basis[None] * imag_gz[:, None]
    upper_half = jnp.concatenate([real_gq, -imag_gq], axis=2)
    lower_half = jnp.concatenate([imag_gq, real_gq], axis=2)
    return (objective, jnp.concatenate([upper_half, lower_half], axis=1).astype(jnp.bfloat16))


def adjoint_sources(products, normal):
    pressure_real = jnp.sum(normal[None] * products[:, 1:4], axis=1)
    pressure_imag = jnp.sum(normal[None] * products[:, 5:8], axis=1)
    return jnp.concatenate([pressure_real, pressure_imag, products[:, 0], products[:, 4]], axis=0)


def sum_over_devices(partial, owners):
    chunks = partial.reshape(owners, -1)
    got = lax.all_to_all(chunks, ("gx", "gy"), split_axis=0, concat_axis=0, tiled=True)
    mine = jnp.sum(got, axis=0, keepdims=True)
    spread = jnp.broadcast_to(mine, chunks.shape)
    full = lax.all_to_all(spread, ("gx", "gy"), split_axis=0, concat_axis=0, tiled=True)
    return full.reshape(partial.shape)


def on_device(cell_state, geometry, surface_cell, counts, wavenumbers, target, direction_weight):
    owners = lax.axis_size(("gx", "gy"))
    rows_dev = surface_cell.shape[0]
    capacity = rows_dev // owners
    live_own = rows_dev // 4
    count_dirs = target.shape[2]
    num_freqs = wavenumbers.shape[0]
    living = (jnp.arange(rows_dev) < counts[0]).astype(jnp.float32)
    outgoing = (
        jnp.concatenate(
            [cell_state[:, surface_cell], geometry, jnp.ones((1, rows_dev), jnp.float32)], axis=0
        )
        * living[None, :]
    )
    outgoing = outgoing.reshape(24, capacity, owners)
    arrived = lax.all_to_all(outgoing, ("gx", "gy"), split_axis=2, concat_axis=2, tiled=True)
    marker = arrived[23]
    per_source = jnp.sum(marker, axis=0).astype(jnp.int32)
    offset = jnp.cumsum(per_source) - per_source
    position = offset[None, :] + jnp.arange(capacity, dtype=jnp.int32)[:, None]
    packed_slot = jnp.where(marker > 0.5, position, live_own).reshape(capacity * owners)
    compact = (
        jnp.zeros((23, live_own), jnp.float32)
        .at[:, packed_slot]
        .set(arrived[:23].reshape(23, capacity * owners), mode="drop")
    )
    block_rows = math.gcd(live_own, 1024)
    block_count = live_own // block_rows
    blocks = compact.reshape(23, block_count, block_rows).transpose(1, 0, 2)
    east_x, north_y, upward = directions(count_dirs)
    direction_basis = jnp.stack([jnp.ones_like(east_x), east_x, north_y, upward])

    def forward_block(running, rows_block):
        products = [
            jnp.dot(
                source_rows(rows_block, level),
                kernel_block(rows_block[16:19], wavenumbers[level], east_x, north_y, upward),
                preferred_element_type=jnp.float32,
            )
            for level in range(num_freqs)
        ]
        return (running + jnp.stack(products), None)

    sums, _ = lax.scan(
        forward_block, jnp.zeros((num_freqs, 8, 2 * count_dirs), jnp.float32), blocks
    )
    far_field = sum_over_devices(far_field_of(sums, wavenumbers, direction_basis), owners)
    objective, weights = adjoint_weights(
        far_field, target, direction_weight, wavenumbers, direction_basis
    )

    def adjoint_block(carry, rows_block):
        products = [
            lax.dot_general(
                weights[level],
                kernel_block(rows_block[16:19], wavenumbers[level], east_x, north_y, upward),
                (((1,), (1,)), ((), ())),
                preferred_element_type=jnp.float32,
            )
            for level in range(num_freqs)
        ]
        return (carry, adjoint_sources(jnp.stack(products), rows_block[19:22]))

    _, backward = lax.scan(adjoint_block, jnp.zeros((), jnp.float32), blocks)
    backward = backward.transpose(1, 0, 2).reshape(16, live_own)
    spread = backward[:, jnp.minimum(packed_slot, live_own - 1)] * marker.reshape(
        1, capacity * owners
    )
    spread = spread.reshape(16, capacity, owners)
    returned = lax.all_to_all(spread, ("gx", "gy"), split_axis=2, concat_axis=2, tiled=True)
    per_row = returned.reshape(16, rows_dev) * living[None, :]
    cell_adjoint = jnp.zeros(cell_state.shape, jnp.float32).at[:, surface_cell].add(per_row)
    return (far_field, objective, cell_adjoint)


def solution(mesh):
    placed = (
        P(None, ("gx", "gy")),
        P(None, ("gx", "gy")),
        P(("gx", "gy")),
        P(("gx", "gy")),
        P(),
        P(),
        P(),
    )
    return jax.shard_map(
        on_device,
        mesh=mesh,
        in_specs=placed,
        out_specs=(P(), P(), P(None, ("gx", "gy"))),
        check_vma=False,
    )
```

```python
import math

import jax
import jax.numpy as jnp
from jax import lax
from jax.experimental import pallas as pl
from jax.experimental.pallas import tpu as pltpu
from jax.sharding import PartitionSpec as P

GOLDEN = math.pi * (3.0 - math.sqrt(5.0))
PI_A = round(math.pi * 32768.0) / 32768.0
PI_B = math.pi - PI_A
INV_PI = 1.0 / math.pi
SIN_C = [(-1.0) ** k / math.factorial(2 * k + 1) for k in range(1, 6)]
COS_C = [(-1.0) ** k / math.factorial(2 * k) for k in range(1, 7)]


def sincos(theta):
    n = jnp.floor(theta * INV_PI + 0.5)
    r = (theta - n * PI_A) - n * PI_B
    z = r * r
    ps = SIN_C[-1]
    for c in SIN_C[-2::-1]:
        ps = c + z * ps
    pc = COS_C[-1]
    for c in COS_C[-2::-1]:
        pc = c + z * pc
    half = n * 0.5
    sign = 1.0 - 4.0 * (half - jnp.floor(half))
    return (sign * (1.0 + z * pc), sign * (r + (r * z) * ps))


def directions(count_dirs):
    lattice = jnp.arange(count_dirs).astype(jnp.float32)
    height = 1.0 - (2.0 * lattice + 1.0) / count_dirs
    radius_xy = jnp.sqrt(1.0 - height * height)
    azimuth = jnp.mod(lattice * GOLDEN, 2.0 * math.pi)
    return (radius_xy * jnp.cos(azimuth), radius_xy * jnp.sin(azimuth), height)


def kernel_block(points, wavenum, east_x, north_y, upward):
    phases = wavenum * (
        points[0][:, None] * east_x[None, :]
        + points[1][:, None] * north_y[None, :]
        + points[2][:, None] * upward[None, :]
    )
    cosine, sine = sincos(phases)
    return jnp.concatenate([cosine, sine], axis=1).astype(jnp.bfloat16)


def source_rows(rows_block, level):
    surface_area = rows_block[22]
    normal = rows_block[19:22]
    pressure_real = rows_block[level] * surface_area
    pressure_imag = rows_block[4 + level] * surface_area
    return jnp.stack(
        [
            rows_block[8 + level] * surface_area,
            normal[0] * pressure_real,
            normal[1] * pressure_real,
            normal[2] * pressure_real,
            rows_block[12 + level] * surface_area,
            normal[0] * pressure_imag,
            normal[1] * pressure_imag,
            normal[2] * pressure_imag,
        ]
    ).astype(jnp.bfloat16)


def far_field_of(sums, wavenumbers, direction_basis):
    half_width = sums.shape[2] // 2
    cosine_part = sums[:, :, :half_width]
    sine_part = sums[:, :, half_width:]
    real_q = cosine_part[:, 0:4] + sine_part[:, 4:8]
    imag_q = cosine_part[:, 4:8] - sine_part[:, 0:4]
    real_z = jnp.sum(direction_basis[None] * real_q, axis=1)
    imag_z = jnp.sum(direction_basis[None] * imag_q, axis=1)
    wavenum = wavenumbers[:, None]
    return jnp.stack([-wavenum * imag_z, wavenum * real_z], axis=1)


def adjoint_weights(far_field, target, direction_weight, wavenumbers, direction_basis):
    count_dirs = far_field.shape[2]
    mismatch = far_field - target
    objective = jnp.sum(direction_weight * mismatch * mismatch) / count_dirs
    gradient = 2.0 * direction_weight * mismatch / count_dirs
    wavenum = wavenumbers[:, None]
    real_gz = wavenum * gradient[:, 1]
    imag_gz = -wavenum * gradient[:, 0]
    real_gq = direction_basis[None] * real_gz[:, None]
    imag_gq = direction_basis[None] * imag_gz[:, None]
    upper_half = jnp.concatenate([real_gq, -imag_gq], axis=2)
    lower_half = jnp.concatenate([imag_gq, real_gq], axis=2)
    return (objective, jnp.concatenate([upper_half, lower_half], axis=1).astype(jnp.bfloat16))


def adjoint_sources(products, normal):
    pressure_real = jnp.sum(normal[None] * products[:, 1:4], axis=1)
    pressure_imag = jnp.sum(normal[None] * products[:, 5:8], axis=1)
    return jnp.concatenate([pressure_real, pressure_imag, products[:, 0], products[:, 4]], axis=0)


ROW_BLOCK = 256
ROW_CHUNK = 16
LANE_CHUNK = 256


def forward_kernel(wave_ref, pts_ref, dirs_ref, src_ref, cs_ref, q_ref):
    level = pl.program_id(0)
    step = pl.program_id(1)
    wavenum = wave_ref[level]
    count_dirs = dirs_ref.shape[2]

    @pl.loop(0, ROW_BLOCK // ROW_CHUNK)
    def _(i):
        r0 = pl.multiple_of(i * ROW_CHUNK, ROW_CHUNK)
        coords = [
            jnp.broadcast_to(wavenum * pts_ref[pl.ds(r0, ROW_CHUNK), c : c + 1], (ROW_CHUNK, LANE_CHUNK))
            for c in range(3)
        ]
        for j0 in range(0, count_dirs, LANE_CHUNK):
            lanes = slice(j0, j0 + LANE_CHUNK)
            theta = (
                coords[0] * dirs_ref[0, :, lanes]
                + coords[1] * dirs_ref[1, :, lanes]
                + coords[2] * dirs_ref[2, :, lanes]
            )
            cosine, sine = sincos(theta)
            cs_ref[0, pl.ds(r0, ROW_CHUNK), lanes] = cosine.astype(jnp.bfloat16)
            cs_ref[0, pl.ds(r0, ROW_CHUNK), j0 + count_dirs : j0 + count_dirs + LANE_CHUNK] = sine.astype(
                jnp.bfloat16
            )

    @pl.when(step == 0)
    def _():
        q_ref[...] = jnp.zeros_like(q_ref)

    q_ref[0] += jnp.dot(src_ref[0], cs_ref[0], preferred_element_type=jnp.float32)


def forward_sums(wavenumbers, points, dirs_block, sources):
    num_freqs = wavenumbers.shape[0]
    rows = points.shape[0]
    count_dirs = dirs_block.shape[2]
    grid = (num_freqs, rows // ROW_BLOCK)
    return pl.pallas_call(
        forward_kernel,
        grid=grid,
        in_specs=[
            pl.BlockSpec(memory_space=pltpu.SMEM),
            pl.BlockSpec((ROW_BLOCK, 3), lambda f, b: (b, 0)),
            pl.BlockSpec(dirs_block.shape, lambda f, b: (0, 0, 0)),
            pl.BlockSpec((1, 16, ROW_BLOCK), lambda f, b: (f, 0, b)),
        ],
        out_specs=[
            pl.BlockSpec((1, ROW_BLOCK, 2 * count_dirs), lambda f, b: (f, b, 0)),
            pl.BlockSpec((1, 16, 2 * count_dirs), lambda f, b: (f, 0, 0)),
        ],
        out_shape=[
            jax.ShapeDtypeStruct((num_freqs, rows, 2 * count_dirs), jnp.bfloat16),
            jax.ShapeDtypeStruct((num_freqs, 16, 2 * count_dirs), jnp.float32),
        ],
        compiler_params=pltpu.CompilerParams(
            dimension_semantics=("arbitrary", "arbitrary"), vmem_limit_bytes=48 * 1024 * 1024
        ),
        cost_estimate=pl.CostEstimate(
            flops=2 * 16 * rows * 2 * count_dirs * num_freqs + 60 * rows * count_dirs * num_freqs,
            transcendentals=0,
            bytes_accessed=2 * rows * 2 * count_dirs * num_freqs,
        ),
    )(wavenumbers, points, dirs_block, sources)


def sum_over_devices(partial, owners):
    chunks = partial.reshape(owners, -1)
    got = lax.all_to_all(chunks, ("gx", "gy"), split_axis=0, concat_axis=0, tiled=True)
    mine = jnp.sum(got, axis=0, keepdims=True)
    spread = jnp.broadcast_to(mine, chunks.shape)
    full = lax.all_to_all(spread, ("gx", "gy"), split_axis=0, concat_axis=0, tiled=True)
    return full.reshape(partial.shape)


def on_device(cell_state, geometry, surface_cell, counts, wavenumbers, target, direction_weight):
    owners = lax.axis_size(("gx", "gy"))
    rows_dev = surface_cell.shape[0]
    capacity = rows_dev // owners
    live_own = rows_dev // 4
    count_dirs = target.shape[2]
    num_freqs = wavenumbers.shape[0]
    living = (jnp.arange(rows_dev) < counts[0]).astype(jnp.float32)
    outgoing = (
        jnp.concatenate(
            [cell_state[:, surface_cell], geometry, jnp.ones((1, rows_dev), jnp.float32)], axis=0
        )
        * living[None, :]
    )
    outgoing = outgoing.reshape(24, capacity, owners)
    arrived = lax.all_to_all(outgoing, ("gx", "gy"), split_axis=2, concat_axis=2, tiled=True)
    marker = arrived[23]
    per_source = jnp.sum(marker, axis=0).astype(jnp.int32)
    offset = jnp.cumsum(per_source) - per_source
    position = offset[None, :] + jnp.arange(capacity, dtype=jnp.int32)[:, None]
    packed_slot = jnp.where(marker > 0.5, position, live_own).reshape(capacity * owners)
    compact = (
        jnp.zeros((23, live_own), jnp.float32)
        .at[:, packed_slot]
        .set(arrived[:23].reshape(23, capacity * owners), mode="drop")
    )
    east_x, north_y, upward = directions(count_dirs)
    direction_basis = jnp.stack([jnp.ones_like(east_x), east_x, north_y, upward])

    points = compact[16:19].T
    sources = jnp.stack([source_rows(compact, level) for level in range(num_freqs)])
    sources = jnp.concatenate([sources, jnp.zeros_like(sources)], axis=1)
    dirs_block = jnp.broadcast_to(jnp.stack([east_x, north_y, upward])[:, None, :], (3, ROW_CHUNK, count_dirs))
    kernel_all, sums = forward_sums(wavenumbers, points, dirs_block, sources)
    sums = sums[:, :8]
    far_field = sum_over_devices(far_field_of(sums, wavenumbers, direction_basis), owners)
    objective, weights = adjoint_weights(
        far_field, target, direction_weight, wavenumbers, direction_basis
    )

    products = jnp.stack([
        lax.dot_general(
            weights[level], kernel_all[level], (((1,), (1,)), ((), ())), preferred_element_type=jnp.float32
        )
        for level in range(num_freqs)
    ])
    backward = adjoint_sources(products, compact[19:22])
    spread = backward[:, jnp.minimum(packed_slot, live_own - 1)] * marker.reshape(
        1, capacity * owners
    )
    spread = spread.reshape(16, capacity, owners)
    returned = lax.all_to_all(spread, ("gx", "gy"), split_axis=2, concat_axis=2, tiled=True)
    per_row = returned.reshape(16, rows_dev) * living[None, :]
    cell_adjoint = jnp.zeros(cell_state.shape, jnp.float32).at[:, surface_cell].add(per_row)
    return (far_field, objective, cell_adjoint)


def solution(mesh):
    placed = (
        P(None, ("gx", "gy")),
        P(None, ("gx", "gy")),
        P(("gx", "gy")),
        P(("gx", "gy")),
        P(),
        P(),
        P(),
    )
    return jax.shard_map(
        on_device,
        mesh=mesh,
        in_specs=placed,
        out_specs=(P(), P(), P(None, ("gx", "gy"))),
        check_vma=False,
    )
```

```python
import math

import jax
import jax.numpy as jnp
from jax import lax
from jax.experimental import pallas as pl
from jax.experimental.pallas import tpu as pltpu
from jax.sharding import PartitionSpec as P

GOLDEN = math.pi * (3.0 - math.sqrt(5.0))
PI_A = round(math.pi * 32768.0) / 32768.0
PI_B = math.pi - PI_A
INV_PI = 1.0 / math.pi
SIN_C = [-0.16666657019913644, 0.00833301540393062, -0.00019806478078586938, 2.599750005030262e-06]
COS_C = [-0.4999993175258851, 0.041663973510963626, -0.0013855797199316853, 2.3191254010748703e-05]


def sincos(theta):
    n = jnp.floor(theta * INV_PI + 0.5)
    r = (theta - n * PI_A) - n * PI_B
    z = r * r
    ps = SIN_C[-1]
    for c in SIN_C[-2::-1]:
        ps = c + z * ps
    pc = COS_C[-1]
    for c in COS_C[-2::-1]:
        pc = c + z * pc
    half = n * 0.5
    sign = 1.0 - 4.0 * (half - jnp.floor(half))
    return (sign * (1.0 + z * pc), sign * (r + (r * z) * ps))


def directions(count_dirs):
    lattice = jnp.arange(count_dirs).astype(jnp.float32)
    height = 1.0 - (2.0 * lattice + 1.0) / count_dirs
    radius_xy = jnp.sqrt(1.0 - height * height)
    azimuth = jnp.mod(lattice * GOLDEN, 2.0 * math.pi)
    return (radius_xy * jnp.cos(azimuth), radius_xy * jnp.sin(azimuth), height)


def kernel_block(points, wavenum, east_x, north_y, upward):
    phases = wavenum * (
        points[0][:, None] * east_x[None, :]
        + points[1][:, None] * north_y[None, :]
        + points[2][:, None] * upward[None, :]
    )
    cosine, sine = sincos(phases)
    return jnp.concatenate([cosine, sine], axis=1).astype(jnp.bfloat16)


def source_rows(rows_block, level):
    surface_area = rows_block[22]
    normal = rows_block[19:22]
    pressure_real = rows_block[level] * surface_area
    pressure_imag = rows_block[4 + level] * surface_area
    return jnp.stack(
        [
            rows_block[8 + level] * surface_area,
            normal[0] * pressure_real,
            normal[1] * pressure_real,
            normal[2] * pressure_real,
            rows_block[12 + level] * surface_area,
            normal[0] * pressure_imag,
            normal[1] * pressure_imag,
            normal[2] * pressure_imag,
        ]
    ).astype(jnp.bfloat16)


def far_field_of(sums, wavenumbers, direction_basis):
    half_width = sums.shape[2] // 2
    cosine_part = sums[:, :, :half_width]
    sine_part = sums[:, :, half_width:]
    real_q = cosine_part[:, 0:4] + sine_part[:, 4:8]
    imag_q = cosine_part[:, 4:8] - sine_part[:, 0:4]
    real_z = jnp.sum(direction_basis[None] * real_q, axis=1)
    imag_z = jnp.sum(direction_basis[None] * imag_q, axis=1)
    wavenum = wavenumbers[:, None]
    return jnp.stack([-wavenum * imag_z, wavenum * real_z], axis=1)


def adjoint_weights(far_field, target, direction_weight, wavenumbers, direction_basis):
    count_dirs = far_field.shape[2]
    mismatch = far_field - target
    objective = jnp.sum(direction_weight * mismatch * mismatch) / count_dirs
    gradient = 2.0 * direction_weight * mismatch / count_dirs
    wavenum = wavenumbers[:, None]
    real_gz = wavenum * gradient[:, 1]
    imag_gz = -wavenum * gradient[:, 0]
    real_gq = direction_basis[None] * real_gz[:, None]
    imag_gq = direction_basis[None] * imag_gz[:, None]
    upper_half = jnp.concatenate([real_gq, -imag_gq], axis=2)
    lower_half = jnp.concatenate([imag_gq, real_gq], axis=2)
    return (objective, jnp.concatenate([upper_half, lower_half], axis=1).astype(jnp.bfloat16))


def adjoint_sources(products, normal):
    pressure_real = jnp.sum(normal[None] * products[:, 1:4], axis=1)
    pressure_imag = jnp.sum(normal[None] * products[:, 5:8], axis=1)
    return jnp.concatenate([pressure_real, pressure_imag, products[:, 0], products[:, 4]], axis=0)


ROW_BLOCK = 256
ROW_CHUNK = 16
LANE_CHUNK = 256


def forward_kernel(wave_ref, pts_ref, dirs_ref, src_ref, cs_ref, q_ref):
    step = pl.program_id(0)
    num_freqs = cs_ref.shape[0]
    count_dirs = dirs_ref.shape[2]
    wavenums = [wave_ref[level] for level in range(num_freqs)]

    @pl.loop(0, ROW_BLOCK // ROW_CHUNK)
    def _(i):
        r0 = pl.multiple_of(i * ROW_CHUNK, ROW_CHUNK)
        coords = [
            jnp.broadcast_to(pts_ref[pl.ds(r0, ROW_CHUNK), c : c + 1], (ROW_CHUNK, LANE_CHUNK))
            for c in range(3)
        ]
        for j0 in range(0, count_dirs, LANE_CHUNK):
            lanes = slice(j0, j0 + LANE_CHUNK)
            along = (
                coords[0] * dirs_ref[0, :, lanes]
                + coords[1] * dirs_ref[1, :, lanes]
                + coords[2] * dirs_ref[2, :, lanes]
            )
            for level in range(num_freqs):
                cosine, sine = sincos(wavenums[level] * along)
                cs_ref[level, pl.ds(r0, ROW_CHUNK), lanes] = cosine.astype(jnp.bfloat16)
                cs_ref[level, pl.ds(r0, ROW_CHUNK), j0 + count_dirs : j0 + count_dirs + LANE_CHUNK] = (
                    sine.astype(jnp.bfloat16)
                )

    @pl.when(step == 0)
    def _():
        q_ref[...] = jnp.zeros_like(q_ref)

    for level in range(num_freqs):
        q_ref[level] += jnp.dot(src_ref[level], cs_ref[level], preferred_element_type=jnp.float32)


def forward_sums(wavenumbers, points, dirs_block, sources):
    num_freqs = wavenumbers.shape[0]
    rows = points.shape[0]
    count_dirs = dirs_block.shape[2]
    grid = (rows // ROW_BLOCK,)
    return pl.pallas_call(
        forward_kernel,
        grid=grid,
        in_specs=[
            pl.BlockSpec(memory_space=pltpu.SMEM),
            pl.BlockSpec((ROW_BLOCK, 3), lambda b: (b, 0)),
            pl.BlockSpec(dirs_block.shape, lambda b: (0, 0, 0)),
            pl.BlockSpec((num_freqs, 16, ROW_BLOCK), lambda b: (0, 0, b)),
        ],
        out_specs=[
            pl.BlockSpec((num_freqs, ROW_BLOCK, 2 * count_dirs), lambda b: (0, b, 0)),
            pl.BlockSpec((num_freqs, 16, 2 * count_dirs), lambda b: (0, 0, 0)),
        ],
        out_shape=[
            jax.ShapeDtypeStruct((num_freqs, rows, 2 * count_dirs), jnp.bfloat16),
            jax.ShapeDtypeStruct((num_freqs, 16, 2 * count_dirs), jnp.float32),
        ],
        compiler_params=pltpu.CompilerParams(
            dimension_semantics=("arbitrary",), vmem_limit_bytes=48 * 1024 * 1024
        ),
        cost_estimate=pl.CostEstimate(
            flops=2 * 16 * rows * 2 * count_dirs * num_freqs + 60 * rows * count_dirs * num_freqs,
            transcendentals=0,
            bytes_accessed=2 * rows * 2 * count_dirs * num_freqs,
        ),
    )(wavenumbers, points, dirs_block, sources)


def adjoint_kernel(w_ref, cs_ref, out_ref):
    for level in range(cs_ref.shape[0]):
        out_ref[level] = lax.dot_general(
            w_ref[level], cs_ref[level], (((1,), (1,)), ((), ())), preferred_element_type=jnp.float32
        )


def adjoint_products(weights, kernel_all):
    num_freqs, rows, width = kernel_all.shape
    return pl.pallas_call(
        adjoint_kernel,
        grid=(rows // ROW_BLOCK,),
        in_specs=[
            pl.BlockSpec(weights.shape, lambda b: (0, 0, 0)),
            pl.BlockSpec((num_freqs, ROW_BLOCK, width), lambda b: (0, b, 0)),
        ],
        out_specs=pl.BlockSpec((num_freqs, weights.shape[1], ROW_BLOCK), lambda b: (0, 0, b)),
        out_shape=jax.ShapeDtypeStruct((num_freqs, weights.shape[1], rows), jnp.float32),
        compiler_params=pltpu.CompilerParams(
            dimension_semantics=("arbitrary",), vmem_limit_bytes=48 * 1024 * 1024
        ),
        cost_estimate=pl.CostEstimate(
            flops=2 * weights.shape[1] * rows * width * num_freqs,
            transcendentals=0,
            bytes_accessed=2 * rows * width * num_freqs,
        ),
    )(weights, kernel_all)


def sum_over_devices(partial, owners):
    chunks = partial.reshape(owners, -1)
    got = lax.all_to_all(chunks, ("gx", "gy"), split_axis=0, concat_axis=0, tiled=True)
    mine = jnp.sum(got, axis=0, keepdims=True)
    spread = jnp.broadcast_to(mine, chunks.shape)
    full = lax.all_to_all(spread, ("gx", "gy"), split_axis=0, concat_axis=0, tiled=True)
    return full.reshape(partial.shape)


def on_device(cell_state, geometry, surface_cell, counts, wavenumbers, target, direction_weight):
    owners = lax.axis_size(("gx", "gy"))
    rows_dev = surface_cell.shape[0]
    capacity = rows_dev // owners
    live_own = rows_dev // 4
    count_dirs = target.shape[2]
    num_freqs = wavenumbers.shape[0]
    living = (jnp.arange(rows_dev) < counts[0]).astype(jnp.float32)
    outgoing = (
        jnp.concatenate(
            [cell_state[:, surface_cell], geometry, jnp.ones((1, rows_dev), jnp.float32)], axis=0
        )
        * living[None, :]
    )
    outgoing = outgoing.reshape(24, capacity, owners)
    arrived = lax.all_to_all(outgoing, ("gx", "gy"), split_axis=2, concat_axis=2, tiled=True)
    marker = arrived[23]
    per_source = jnp.sum(marker, axis=0).astype(jnp.int32)
    offset = jnp.cumsum(per_source) - per_source
    position = offset[None, :] + jnp.arange(capacity, dtype=jnp.int32)[:, None]
    packed_slot = jnp.where(marker > 0.5, position, live_own).reshape(capacity * owners)
    compact = (
        jnp.zeros((23, live_own), jnp.float32)
        .at[:, packed_slot]
        .set(arrived[:23].reshape(23, capacity * owners), mode="drop")
    )
    east_x, north_y, upward = directions(count_dirs)
    direction_basis = jnp.stack([jnp.ones_like(east_x), east_x, north_y, upward])

    points = compact[16:19].T
    sources = jnp.stack([source_rows(compact, level) for level in range(num_freqs)])
    sources = jnp.concatenate([sources, jnp.zeros_like(sources)], axis=1)
    dirs_block = jnp.broadcast_to(jnp.stack([east_x, north_y, upward])[:, None, :], (3, ROW_CHUNK, count_dirs))
    kernel_all, sums = forward_sums(wavenumbers, points, dirs_block, sources)
    sums = sums[:, :8]
    far_field = sum_over_devices(far_field_of(sums, wavenumbers, direction_basis), owners)
    objective, weights = adjoint_weights(
        far_field, target, direction_weight, wavenumbers, direction_basis
    )

    padded = jnp.concatenate([weights, jnp.zeros_like(weights)], axis=1)
    products = adjoint_products(padded, kernel_all)[:, :8]
    backward = adjoint_sources(products, compact[19:22])
    spread = backward[:, jnp.minimum(packed_slot, live_own - 1)] * marker.reshape(
        1, capacity * owners
    )
    spread = spread.reshape(16, capacity, owners)
    returned = lax.all_to_all(spread, ("gx", "gy"), split_axis=2, concat_axis=2, tiled=True)
    per_row = returned.reshape(16, rows_dev) * living[None, :]
    cell_adjoint = jnp.zeros(cell_state.shape, jnp.float32).at[:, surface_cell].add(per_row)
    return (far_field, objective, cell_adjoint)


def solution(mesh):
    placed = (
        P(None, ("gx", "gy")),
        P(None, ("gx", "gy")),
        P(("gx", "gy")),
        P(("gx", "gy")),
        P(),
        P(),
        P(),
    )
    return jax.shard_map(
        on_device,
        mesh=mesh,
        in_specs=placed,
        out_specs=(P(), P(), P(None, ("gx", "gy"))),
        check_vma=False,
    )
```

```python
import functools
import math

import jax
import jax.numpy as jnp
from jax import lax
from jax.experimental import pallas as pl
from jax.experimental.pallas import tpu as pltpu
from jax.sharding import PartitionSpec as P

GOLDEN = math.pi * (3.0 - math.sqrt(5.0))
PI_A = round(math.pi * 32768.0) / 32768.0
PI_B = math.pi - PI_A
INV_PI = 1.0 / math.pi
SIN_C = [-0.16666657019913644, 0.00833301540393062, -0.00019806478078586938, 2.599750005030262e-06]
COS_C = [-0.4999993175258851, 0.041663973510963626, -0.0013855797199316853, 2.3191254010748703e-05]


def sincos(theta):
    n = jnp.floor(theta * INV_PI + 0.5)
    r = (theta - n * PI_A) - n * PI_B
    z = r * r
    ps = SIN_C[-1]
    for c in SIN_C[-2::-1]:
        ps = c + z * ps
    pc = COS_C[-1]
    for c in COS_C[-2::-1]:
        pc = c + z * pc
    half = n * 0.5
    sign = 1.0 - 4.0 * (half - jnp.floor(half))
    return (sign * (1.0 + z * pc), sign * (r + (r * z) * ps))


def directions(count_dirs):
    lattice = jnp.arange(count_dirs).astype(jnp.float32)
    height = 1.0 - (2.0 * lattice + 1.0) / count_dirs
    radius_xy = jnp.sqrt(1.0 - height * height)
    azimuth = jnp.mod(lattice * GOLDEN, 2.0 * math.pi)
    return (radius_xy * jnp.cos(azimuth), radius_xy * jnp.sin(azimuth), height)


def kernel_block(points, wavenum, east_x, north_y, upward):
    phases = wavenum * (
        points[0][:, None] * east_x[None, :]
        + points[1][:, None] * north_y[None, :]
        + points[2][:, None] * upward[None, :]
    )
    cosine, sine = sincos(phases)
    return jnp.concatenate([cosine, sine], axis=1).astype(jnp.bfloat16)


def source_rows(rows_block, level):
    surface_area = rows_block[22]
    normal = rows_block[19:22]
    pressure_real = rows_block[level] * surface_area
    pressure_imag = rows_block[4 + level] * surface_area
    return jnp.stack(
        [
            rows_block[8 + level] * surface_area,
            normal[0] * pressure_real,
            normal[1] * pressure_real,
            normal[2] * pressure_real,
            rows_block[12 + level] * surface_area,
            normal[0] * pressure_imag,
            normal[1] * pressure_imag,
            normal[2] * pressure_imag,
        ]
    ).astype(jnp.bfloat16)


def far_field_of(sums, wavenumbers, direction_basis):
    half_width = sums.shape[2] // 2
    cosine_part = sums[:, :, :half_width]
    sine_part = sums[:, :, half_width:]
    real_q = cosine_part[:, 0:4] + sine_part[:, 4:8]
    imag_q = cosine_part[:, 4:8] - sine_part[:, 0:4]
    real_z = jnp.sum(direction_basis[None] * real_q, axis=1)
    imag_z = jnp.sum(direction_basis[None] * imag_q, axis=1)
    wavenum = wavenumbers[:, None]
    return jnp.stack([-wavenum * imag_z, wavenum * real_z], axis=1)


def adjoint_weights(far_field, target, direction_weight, wavenumbers, direction_basis):
    count_dirs = far_field.shape[2]
    mismatch = far_field - target
    objective = jnp.sum(direction_weight * mismatch * mismatch) / count_dirs
    gradient = 2.0 * direction_weight * mismatch / count_dirs
    wavenum = wavenumbers[:, None]
    real_gz = wavenum * gradient[:, 1]
    imag_gz = -wavenum * gradient[:, 0]
    real_gq = direction_basis[None] * real_gz[:, None]
    imag_gq = direction_basis[None] * imag_gz[:, None]
    upper_half = jnp.concatenate([real_gq, -imag_gq], axis=2)
    lower_half = jnp.concatenate([imag_gq, real_gq], axis=2)
    return (objective, jnp.concatenate([upper_half, lower_half], axis=1).astype(jnp.bfloat16))


def adjoint_sources(products, normal):
    pressure_real = jnp.sum(normal[None] * products[:, 1:4], axis=1)
    pressure_imag = jnp.sum(normal[None] * products[:, 5:8], axis=1)
    return jnp.concatenate([pressure_real, pressure_imag, products[:, 0], products[:, 4]], axis=0)


ROW_BLOCK = 256
ROW_CHUNK = 16
LANE_CHUNK = 256


def forward_kernel(wave_ref, pts_ref, dirs_ref, src_ref, cs_ref, q_ref):
    step = pl.program_id(0)
    num_freqs = cs_ref.shape[0]
    count_dirs = dirs_ref.shape[2]
    wavenums = [wave_ref[level] for level in range(num_freqs)]

    @pl.loop(0, ROW_BLOCK // ROW_CHUNK)
    def _(i):
        r0 = pl.multiple_of(i * ROW_CHUNK, ROW_CHUNK)
        coords = [
            jnp.broadcast_to(pts_ref[pl.ds(r0, ROW_CHUNK), c : c + 1], (ROW_CHUNK, LANE_CHUNK))
            for c in range(3)
        ]
        for j0 in range(0, count_dirs, LANE_CHUNK):
            lanes = slice(j0, j0 + LANE_CHUNK)
            along = (
                coords[0] * dirs_ref[0, :, lanes]
                + coords[1] * dirs_ref[1, :, lanes]
                + coords[2] * dirs_ref[2, :, lanes]
            )
            for level in range(num_freqs):
                cosine, sine = sincos(wavenums[level] * along)
                cs_ref[level, pl.ds(r0, ROW_CHUNK), lanes] = cosine.astype(jnp.bfloat16)
                cs_ref[level, pl.ds(r0, ROW_CHUNK), j0 + count_dirs : j0 + count_dirs + LANE_CHUNK] = (
                    sine.astype(jnp.bfloat16)
                )

    @pl.when(step == 0)
    def _():
        q_ref[...] = jnp.zeros_like(q_ref)

    for level in range(num_freqs):
        q_ref[level] += jnp.dot(src_ref[level], cs_ref[level], preferred_element_type=jnp.float32)


def forward_sums(wavenumbers, points, dirs_block, sources):
    num_freqs = wavenumbers.shape[0]
    rows = points.shape[0]
    count_dirs = dirs_block.shape[2]
    grid = (rows // ROW_BLOCK,)
    return pl.pallas_call(
        forward_kernel,
        grid=grid,
        in_specs=[
            pl.BlockSpec(memory_space=pltpu.SMEM),
            pl.BlockSpec((ROW_BLOCK, 3), lambda b: (b, 0)),
            pl.BlockSpec(dirs_block.shape, lambda b: (0, 0, 0)),
            pl.BlockSpec((num_freqs, 16, ROW_BLOCK), lambda b: (0, 0, b)),
        ],
        out_specs=[
            pl.BlockSpec((num_freqs, ROW_BLOCK, 2 * count_dirs), lambda b: (0, b, 0)),
            pl.BlockSpec((num_freqs, 16, 2 * count_dirs), lambda b: (0, 0, 0)),
        ],
        out_shape=[
            jax.ShapeDtypeStruct((num_freqs, rows, 2 * count_dirs), jnp.bfloat16),
            jax.ShapeDtypeStruct((num_freqs, 16, 2 * count_dirs), jnp.float32),
        ],
        compiler_params=pltpu.CompilerParams(
            dimension_semantics=("arbitrary",), vmem_limit_bytes=48 * 1024 * 1024
        ),
        cost_estimate=pl.CostEstimate(
            flops=2 * 16 * rows * 2 * count_dirs * num_freqs + 60 * rows * count_dirs * num_freqs,
            transcendentals=0,
            bytes_accessed=2 * rows * 2 * count_dirs * num_freqs,
        ),
    )(wavenumbers, points, dirs_block, sources)


def adjoint_kernel(w_ref, cs_ref, out_ref):
    for level in range(cs_ref.shape[0]):
        out_ref[level] = lax.dot_general(
            w_ref[level], cs_ref[level], (((1,), (1,)), ((), ())), preferred_element_type=jnp.float32
        )


def adjoint_products(weights, kernel_all):
    num_freqs, rows, width = kernel_all.shape
    return pl.pallas_call(
        adjoint_kernel,
        grid=(rows // ROW_BLOCK,),
        in_specs=[
            pl.BlockSpec(weights.shape, lambda b: (0, 0, 0)),
            pl.BlockSpec((num_freqs, ROW_BLOCK, width), lambda b: (0, b, 0)),
        ],
        out_specs=pl.BlockSpec((num_freqs, weights.shape[1], ROW_BLOCK), lambda b: (0, 0, b)),
        out_shape=jax.ShapeDtypeStruct((num_freqs, weights.shape[1], rows), jnp.float32),
        compiler_params=pltpu.CompilerParams(
            dimension_semantics=("arbitrary",), vmem_limit_bytes=48 * 1024 * 1024
        ),
        cost_estimate=pl.CostEstimate(
            flops=2 * weights.shape[1] * rows * width * num_freqs,
            transcendentals=0,
            bytes_accessed=2 * rows * width * num_freqs,
        ),
    )(weights, kernel_all)


MESH_IDS = pl.DeviceIdType.MESH


def reduce_kernel(nx, ny, x_ref, out_ref, part_a, part_b, got_a, got_b, got_c, sems):
    b0 = lax.axis_index("gx")
    a0 = lax.axis_index("gy")
    barrier = pltpu.get_barrier_semaphore()
    for t in range(1, ny):
        pl.semaphore_signal(barrier, inc=1, device_id=(b0, lax.rem(a0 + t, ny)), device_id_type=MESH_IDS)
    for t in range(1, nx):
        pl.semaphore_signal(barrier, inc=1, device_id=(lax.rem(b0 + t, nx), a0), device_id_type=MESH_IDS)
    pl.semaphore_wait(barrier, nx + ny - 2)

    def exchange(phase, src_of, dst_of, peers, along_x):
        copies = []
        for t in range(1, peers):
            if along_x:
                peer = lax.rem(b0 + t, nx)
                me, device = b0, (peer, a0)
            else:
                peer = lax.rem(a0 + t, ny)
                me, device = a0, (b0, peer)
            copy = pltpu.make_async_remote_copy(
                src_ref=src_of(peer),
                dst_ref=dst_of(me),
                send_sem=sems.at[phase, 0, peer],
                recv_sem=sems.at[phase, 1, me],
                device_id=device,
                device_id_type=MESH_IDS,
            )
            copy.start()
            copies.append((peer, device))
        for peer, device in copies:
            pltpu.make_async_remote_copy(
                src_ref=src_of(peer),
                dst_ref=dst_of(peer),
                send_sem=sems.at[phase, 0, peer],
                recv_sem=sems.at[phase, 1, peer],
                device_id=device,
                device_id_type=MESH_IDS,
            ).wait()

    exchange(0, lambda a: x_ref.at[a], lambda a: got_a.at[a], ny, False)
    got_a[a0] = x_ref[a0]
    part_a[...] = jnp.sum(got_a[...], axis=0)
    exchange(1, lambda b: part_a.at[pl.ds(b, 1)], lambda b: got_b.at[b], nx, True)
    got_b[b0] = part_a[pl.ds(b0, 1)]
    part_b[...] = jnp.sum(got_b[...], axis=0)
    exchange(2, lambda b: part_b, lambda b: got_c.at[pl.ds(b, 1)], nx, True)
    got_c[pl.ds(b0, 1)] = part_b[...]
    exchange(3, lambda a: got_c, lambda a: out_ref.at[a], ny, False)
    out_ref[a0] = got_c[...]


def sum_over_devices(partial, owners):
    nx = lax.axis_size("gx")
    ny = lax.axis_size("gy")
    lanes = partial.size // (nx * ny)
    shaped = partial.reshape(ny, nx, lanes)
    peers = max(nx, ny)
    total = pl.pallas_call(
        functools.partial(reduce_kernel, nx, ny),
        in_specs=[pl.BlockSpec(memory_space=pltpu.VMEM)],
        out_specs=pl.BlockSpec(memory_space=pltpu.VMEM),
        out_shape=jax.ShapeDtypeStruct(shaped.shape, jnp.float32),
        scratch_shapes=[
            pltpu.VMEM((nx, lanes), jnp.float32),
            pltpu.VMEM((1, lanes), jnp.float32),
            pltpu.VMEM((ny, nx, lanes), jnp.float32),
            pltpu.VMEM((nx, 1, lanes), jnp.float32),
            pltpu.VMEM((nx, lanes), jnp.float32),
            pltpu.SemaphoreType.DMA((4, 2, peers)),
        ],
        compiler_params=pltpu.CompilerParams(collective_id=0, has_side_effects=True),
    )(shaped)
    return total.reshape(partial.shape)


def sum_over_devices_a2a(partial, owners):
    chunks = partial.reshape(owners, -1)
    got = lax.all_to_all(chunks, ("gx", "gy"), split_axis=0, concat_axis=0, tiled=True)
    mine = jnp.sum(got, axis=0, keepdims=True)
    spread = jnp.broadcast_to(mine, chunks.shape)
    full = lax.all_to_all(spread, ("gx", "gy"), split_axis=0, concat_axis=0, tiled=True)
    return full.reshape(partial.shape)


def on_device(cell_state, geometry, surface_cell, counts, wavenumbers, target, direction_weight):
    owners = lax.axis_size(("gx", "gy"))
    rows_dev = surface_cell.shape[0]
    capacity = rows_dev // owners
    live_own = rows_dev // 4
    count_dirs = target.shape[2]
    num_freqs = wavenumbers.shape[0]
    living = (jnp.arange(rows_dev) < counts[0]).astype(jnp.float32)
    outgoing = (
        jnp.concatenate(
            [cell_state[:, surface_cell], geometry, jnp.ones((1, rows_dev), jnp.float32)], axis=0
        )
        * living[None, :]
    )
    outgoing = outgoing.reshape(24, capacity, owners)
    arrived = lax.all_to_all(outgoing, ("gx", "gy"), split_axis=2, concat_axis=2, tiled=True)
    marker = arrived[23]
    per_source = jnp.sum(marker, axis=0).astype(jnp.int32)
    offset = jnp.cumsum(per_source) - per_source
    position = offset[None, :] + jnp.arange(capacity, dtype=jnp.int32)[:, None]
    packed_slot = jnp.where(marker > 0.5, position, live_own).reshape(capacity * owners)
    compact = (
        jnp.zeros((23, live_own), jnp.float32)
        .at[:, packed_slot]
        .set(arrived[:23].reshape(23, capacity * owners), mode="drop")
    )
    east_x, north_y, upward = directions(count_dirs)
    direction_basis = jnp.stack([jnp.ones_like(east_x), east_x, north_y, upward])

    points = compact[16:19].T
    sources = jnp.stack([source_rows(compact, level) for level in range(num_freqs)])
    sources = jnp.concatenate([sources, jnp.zeros_like(sources)], axis=1)
    dirs_block = jnp.broadcast_to(jnp.stack([east_x, north_y, upward])[:, None, :], (3, ROW_CHUNK, count_dirs))
    kernel_all, sums = forward_sums(wavenumbers, points, dirs_block, sources)
    sums = sums[:, :8]
    far_field = sum_over_devices(far_field_of(sums, wavenumbers, direction_basis), owners)
    objective, weights = adjoint_weights(
        far_field, target, direction_weight, wavenumbers, direction_basis
    )

    padded = jnp.concatenate([weights, jnp.zeros_like(weights)], axis=1)
    products = adjoint_products(padded, kernel_all)[:, :8]
    backward = adjoint_sources(products, compact[19:22])
    spread = backward[:, jnp.minimum(packed_slot, live_own - 1)] * marker.reshape(
        1, capacity * owners
    )
    spread = spread.reshape(16, capacity, owners)
    returned = lax.all_to_all(spread, ("gx", "gy"), split_axis=2, concat_axis=2, tiled=True)
    per_row = returned.reshape(16, rows_dev) * living[None, :]
    cell_adjoint = jnp.zeros(cell_state.shape, jnp.float32).at[:, surface_cell].add(per_row)
    return (far_field, objective, cell_adjoint)


def solution(mesh):
    placed = (
        P(None, ("gx", "gy")),
        P(None, ("gx", "gy")),
        P(("gx", "gy")),
        P(("gx", "gy")),
        P(),
        P(),
        P(),
    )
    return jax.shard_map(
        on_device,
        mesh=mesh,
        in_specs=placed,
        out_specs=(P(), P(), P(None, ("gx", "gy"))),
        check_vma=False,
    )
```

```python
import functools
import math

import jax
import jax.numpy as jnp
from jax import lax
from jax.experimental import pallas as pl
from jax.experimental.pallas import tpu as pltpu
from jax.sharding import PartitionSpec as P

GOLDEN = math.pi * (3.0 - math.sqrt(5.0))
PI_A = round(math.pi * 32768.0) / 32768.0
PI_B = math.pi - PI_A
INV_PI = 1.0 / math.pi
SIN_C = [-0.16666657019913644, 0.00833301540393062, -0.00019806478078586938, 2.599750005030262e-06]
COS_C = [-0.4999993175258851, 0.041663973510963626, -0.0013855797199316853, 2.3191254010748703e-05]


def sincos(theta):
    n = jnp.floor(theta * INV_PI + 0.5)
    r = (theta - n * PI_A) - n * PI_B
    z = r * r
    ps = SIN_C[-1]
    for c in SIN_C[-2::-1]:
        ps = c + z * ps
    pc = COS_C[-1]
    for c in COS_C[-2::-1]:
        pc = c + z * pc
    half = n * 0.5
    sign = 1.0 - 4.0 * (half - jnp.floor(half))
    return (sign * (1.0 + z * pc), sign * (r + (r * z) * ps))


def directions(count_dirs):
    lattice = jnp.arange(count_dirs).astype(jnp.float32)
    height = 1.0 - (2.0 * lattice + 1.0) / count_dirs
    radius_xy = jnp.sqrt(1.0 - height * height)
    azimuth = jnp.mod(lattice * GOLDEN, 2.0 * math.pi)
    return (radius_xy * jnp.cos(azimuth), radius_xy * jnp.sin(azimuth), height)


def kernel_block(points, wavenum, east_x, north_y, upward):
    phases = wavenum * (
        points[0][:, None] * east_x[None, :]
        + points[1][:, None] * north_y[None, :]
        + points[2][:, None] * upward[None, :]
    )
    cosine, sine = sincos(phases)
    return jnp.concatenate([cosine, sine], axis=1).astype(jnp.bfloat16)


def source_rows(rows_block, level):
    surface_area = rows_block[22]
    normal = rows_block[19:22]
    pressure_real = rows_block[level] * surface_area
    pressure_imag = rows_block[4 + level] * surface_area
    return jnp.stack(
        [
            rows_block[8 + level] * surface_area,
            normal[0] * pressure_real,
            normal[1] * pressure_real,
            normal[2] * pressure_real,
            rows_block[12 + level] * surface_area,
            normal[0] * pressure_imag,
            normal[1] * pressure_imag,
            normal[2] * pressure_imag,
        ]
    ).astype(jnp.bfloat16)


def far_field_of(sums, wavenumbers, direction_basis):
    half_width = sums.shape[2] // 2
    cosine_part = sums[:, :, :half_width]
    sine_part = sums[:, :, half_width:]
    real_q = cosine_part[:, 0:4] + sine_part[:, 4:8]
    imag_q = cosine_part[:, 4:8] - sine_part[:, 0:4]
    real_z = jnp.sum(direction_basis[None] * real_q, axis=1)
    imag_z = jnp.sum(direction_basis[None] * imag_q, axis=1)
    wavenum = wavenumbers[:, None]
    return jnp.stack([-wavenum * imag_z, wavenum * real_z], axis=1)


def adjoint_weights(far_field, target, direction_weight, wavenumbers, direction_basis):
    count_dirs = far_field.shape[2]
    mismatch = far_field - target
    objective = jnp.sum(direction_weight * mismatch * mismatch) / count_dirs
    gradient = 2.0 * direction_weight * mismatch / count_dirs
    wavenum = wavenumbers[:, None]
    real_gz = wavenum * gradient[:, 1]
    imag_gz = -wavenum * gradient[:, 0]
    real_gq = direction_basis[None] * real_gz[:, None]
    imag_gq = direction_basis[None] * imag_gz[:, None]
    upper_half = jnp.concatenate([real_gq, -imag_gq], axis=2)
    lower_half = jnp.concatenate([imag_gq, real_gq], axis=2)
    return (objective, jnp.concatenate([upper_half, lower_half], axis=1).astype(jnp.bfloat16))


def adjoint_sources(products, normal):
    pressure_real = jnp.sum(normal[None] * products[:, 1:4], axis=1)
    pressure_imag = jnp.sum(normal[None] * products[:, 5:8], axis=1)
    return jnp.concatenate([pressure_real, pressure_imag, products[:, 0], products[:, 4]], axis=0)


ROW_BLOCK = 256
ROW_CHUNK = 16
LANE_CHUNK = 256


def forward_kernel(wave_ref, pts_ref, dirs_ref, src_ref, cs_ref, q_ref):
    step = pl.program_id(0)
    num_freqs = cs_ref.shape[0]
    count_dirs = dirs_ref.shape[2]
    wavenums = [wave_ref[level] for level in range(num_freqs)]

    @pl.loop(0, ROW_BLOCK // ROW_CHUNK)
    def _(i):
        r0 = pl.multiple_of(i * ROW_CHUNK, ROW_CHUNK)
        coords = [
            jnp.broadcast_to(pts_ref[pl.ds(r0, ROW_CHUNK), c : c + 1], (ROW_CHUNK, LANE_CHUNK))
            for c in range(3)
        ]
        for j0 in range(0, count_dirs, LANE_CHUNK):
            lanes = slice(j0, j0 + LANE_CHUNK)
            along = (
                coords[0] * dirs_ref[0, :, lanes]
                + coords[1] * dirs_ref[1, :, lanes]
                + coords[2] * dirs_ref[2, :, lanes]
            )
            for level in range(num_freqs):
                cosine, sine = sincos(wavenums[level] * along)
                cs_ref[level, pl.ds(r0, ROW_CHUNK), lanes] = cosine.astype(jnp.bfloat16)
                cs_ref[level, pl.ds(r0, ROW_CHUNK), j0 + count_dirs : j0 + count_dirs + LANE_CHUNK] = (
                    sine.astype(jnp.bfloat16)
                )

    @pl.when(step == 0)
    def _():
        q_ref[...] = jnp.zeros_like(q_ref)

    for level in range(num_freqs):
        q_ref[level] += jnp.dot(src_ref[level], cs_ref[level], preferred_element_type=jnp.float32)


def forward_sums(wavenumbers, points, dirs_block, sources):
    num_freqs = wavenumbers.shape[0]
    rows = points.shape[0]
    count_dirs = dirs_block.shape[2]
    grid = (rows // ROW_BLOCK,)
    return pl.pallas_call(
        forward_kernel,
        grid=grid,
        in_specs=[
            pl.BlockSpec(memory_space=pltpu.SMEM),
            pl.BlockSpec((ROW_BLOCK, 3), lambda b: (b, 0)),
            pl.BlockSpec(dirs_block.shape, lambda b: (0, 0, 0)),
            pl.BlockSpec((num_freqs, 16, ROW_BLOCK), lambda b: (0, 0, b)),
        ],
        out_specs=[
            pl.BlockSpec((num_freqs, ROW_BLOCK, 2 * count_dirs), lambda b: (0, b, 0)),
            pl.BlockSpec((num_freqs, 16, 2 * count_dirs), lambda b: (0, 0, 0)),
        ],
        out_shape=[
            jax.ShapeDtypeStruct((num_freqs, rows, 2 * count_dirs), jnp.bfloat16),
            jax.ShapeDtypeStruct((num_freqs, 16, 2 * count_dirs), jnp.float32),
        ],
        compiler_params=pltpu.CompilerParams(
            dimension_semantics=("arbitrary",), vmem_limit_bytes=48 * 1024 * 1024
        ),
        cost_estimate=pl.CostEstimate(
            flops=2 * 16 * rows * 2 * count_dirs * num_freqs + 60 * rows * count_dirs * num_freqs,
            transcendentals=0,
            bytes_accessed=2 * rows * 2 * count_dirs * num_freqs,
        ),
    )(wavenumbers, points, dirs_block, sources)


def adjoint_kernel(w_ref, cs_ref, out_ref):
    for level in range(cs_ref.shape[0]):
        out_ref[level] = lax.dot_general(
            w_ref[level], cs_ref[level], (((1,), (1,)), ((), ())), preferred_element_type=jnp.float32
        )


def adjoint_products(weights, kernel_all):
    num_freqs, rows, width = kernel_all.shape
    return pl.pallas_call(
        adjoint_kernel,
        grid=(rows // ROW_BLOCK,),
        in_specs=[
            pl.BlockSpec(weights.shape, lambda b: (0, 0, 0)),
            pl.BlockSpec((num_freqs, ROW_BLOCK, width), lambda b: (0, b, 0)),
        ],
        out_specs=pl.BlockSpec((num_freqs, weights.shape[1], ROW_BLOCK), lambda b: (0, 0, b)),
        out_shape=jax.ShapeDtypeStruct((num_freqs, weights.shape[1], rows), jnp.float32),
        compiler_params=pltpu.CompilerParams(
            dimension_semantics=("arbitrary",), vmem_limit_bytes=48 * 1024 * 1024
        ),
        cost_estimate=pl.CostEstimate(
            flops=2 * weights.shape[1] * rows * width * num_freqs,
            transcendentals=0,
            bytes_accessed=2 * rows * width * num_freqs,
        ),
    )(weights, kernel_all)


def split_bf16(values):
    high = lax.reduce_precision(values, exponent_bits=8, mantissa_bits=7)
    rest = values - high
    middle = lax.reduce_precision(rest, exponent_bits=8, mantissa_bits=7)
    low = rest - middle
    return jnp.concatenate([high, middle, low], axis=0).astype(jnp.bfloat16)


def join_parts(product, channels):
    return (product[:channels] + product[channels : 2 * channels]) + product[2 * channels :]


def permute_columns(values, selector):
    product = jnp.dot(split_bf16(values), selector, preferred_element_type=jnp.float32)
    return join_parts(product, values.shape[0])


def unpermute_columns(values, selector):
    product = lax.dot_general(
        split_bf16(values), selector, (((1,), (1,)), ((), ())), preferred_element_type=jnp.float32
    )
    return join_parts(product, values.shape[0])


MESH_IDS = pl.DeviceIdType.MESH


def reduce_kernel(nx, ny, x_ref, out_ref, part_a, part_b, got_a, got_b, got_c, sems):
    b0 = lax.axis_index("gx")
    a0 = lax.axis_index("gy")
    barrier = pltpu.get_barrier_semaphore()
    for t in range(1, ny):
        pl.semaphore_signal(barrier, inc=1, device_id=(b0, lax.rem(a0 + t, ny)), device_id_type=MESH_IDS)
    for t in range(1, nx):
        pl.semaphore_signal(barrier, inc=1, device_id=(lax.rem(b0 + t, nx), a0), device_id_type=MESH_IDS)
    pl.semaphore_wait(barrier, nx + ny - 2)

    def exchange(phase, src_of, dst_of, peers, along_x):
        copies = []
        for t in range(1, peers):
            if along_x:
                peer = lax.rem(b0 + t, nx)
                me, device = b0, (peer, a0)
            else:
                peer = lax.rem(a0 + t, ny)
                me, device = a0, (b0, peer)
            copy = pltpu.make_async_remote_copy(
                src_ref=src_of(peer),
                dst_ref=dst_of(me),
                send_sem=sems.at[phase, 0, peer],
                recv_sem=sems.at[phase, 1, me],
                device_id=device,
                device_id_type=MESH_IDS,
            )
            copy.start()
            copies.append((peer, device))
        for peer, device in copies:
            pltpu.make_async_remote_copy(
                src_ref=src_of(peer),
                dst_ref=dst_of(peer),
                send_sem=sems.at[phase, 0, peer],
                recv_sem=sems.at[phase, 1, peer],
                device_id=device,
                device_id_type=MESH_IDS,
            ).wait()

    exchange(0, lambda a: x_ref.at[a], lambda a: got_a.at[a], ny, False)
    got_a[a0] = x_ref[a0]
    part_a[...] = jnp.sum(got_a[...], axis=0)
    exchange(1, lambda b: part_a.at[pl.ds(b, 1)], lambda b: got_b.at[b], nx, True)
    got_b[b0] = part_a[pl.ds(b0, 1)]
    part_b[...] = jnp.sum(got_b[...], axis=0)
    exchange(2, lambda b: part_b, lambda b: got_c.at[pl.ds(b, 1)], nx, True)
    got_c[pl.ds(b0, 1)] = part_b[...]
    exchange(3, lambda a: got_c, lambda a: out_ref.at[a], ny, False)
    out_ref[a0] = got_c[...]


def sum_over_devices(partial, owners):
    nx = lax.axis_size("gx")
    ny = lax.axis_size("gy")
    lanes = partial.size // (nx * ny)
    shaped = partial.reshape(ny, nx, lanes)
    peers = max(nx, ny)
    total = pl.pallas_call(
        functools.partial(reduce_kernel, nx, ny),
        in_specs=[pl.BlockSpec(memory_space=pltpu.VMEM)],
        out_specs=pl.BlockSpec(memory_space=pltpu.VMEM),
        out_shape=jax.ShapeDtypeStruct(shaped.shape, jnp.float32),
        scratch_shapes=[
            pltpu.VMEM((nx, lanes), jnp.float32),
            pltpu.VMEM((1, lanes), jnp.float32),
            pltpu.VMEM((ny, nx, lanes), jnp.float32),
            pltpu.VMEM((nx, 1, lanes), jnp.float32),
            pltpu.VMEM((nx, lanes), jnp.float32),
            pltpu.SemaphoreType.DMA((4, 2, peers)),
        ],
        compiler_params=pltpu.CompilerParams(collective_id=0, has_side_effects=True),
    )(shaped)
    return total.reshape(partial.shape)


def sum_over_devices_a2a(partial, owners):
    chunks = partial.reshape(owners, -1)
    got = lax.all_to_all(chunks, ("gx", "gy"), split_axis=0, concat_axis=0, tiled=True)
    mine = jnp.sum(got, axis=0, keepdims=True)
    spread = jnp.broadcast_to(mine, chunks.shape)
    full = lax.all_to_all(spread, ("gx", "gy"), split_axis=0, concat_axis=0, tiled=True)
    return full.reshape(partial.shape)


def on_device(cell_state, geometry, surface_cell, counts, wavenumbers, target, direction_weight):
    owners = lax.axis_size(("gx", "gy"))
    rows_dev = surface_cell.shape[0]
    capacity = rows_dev // owners
    live_own = rows_dev // 4
    count_dirs = target.shape[2]
    num_freqs = wavenumbers.shape[0]
    living = (jnp.arange(rows_dev) < counts[0]).astype(jnp.float32)
    outgoing = (
        jnp.concatenate(
            [cell_state[:, surface_cell], geometry, jnp.ones((1, rows_dev), jnp.float32)], axis=0
        )
        * living[None, :]
    )
    outgoing = outgoing.reshape(24, capacity, owners)
    arrived = lax.all_to_all(outgoing, ("gx", "gy"), split_axis=2, concat_axis=2, tiled=True)
    marker = arrived[23]
    per_source = jnp.sum(marker, axis=0).astype(jnp.int32)
    offset = jnp.cumsum(per_source) - per_source
    position = offset[None, :] + jnp.arange(capacity, dtype=jnp.int32)[:, None]
    packed_slot = jnp.where(marker > 0.5, position, live_own).reshape(capacity * owners)
    selector = (packed_slot[:, None] == jnp.arange(live_own, dtype=jnp.int32)[None, :]).astype(jnp.bfloat16)
    compact = permute_columns(arrived[:23].reshape(23, capacity * owners), selector)
    east_x, north_y, upward = directions(count_dirs)
    direction_basis = jnp.stack([jnp.ones_like(east_x), east_x, north_y, upward])

    points = compact[16:19].T
    sources = jnp.stack([source_rows(compact, level) for level in range(num_freqs)])
    sources = jnp.concatenate([sources, jnp.zeros_like(sources)], axis=1)
    dirs_block = jnp.broadcast_to(jnp.stack([east_x, north_y, upward])[:, None, :], (3, ROW_CHUNK, count_dirs))
    kernel_all, sums = forward_sums(wavenumbers, points, dirs_block, sources)
    sums = sums[:, :8]
    far_field = sum_over_devices(far_field_of(sums, wavenumbers, direction_basis), owners)
    objective, weights = adjoint_weights(
        far_field, target, direction_weight, wavenumbers, direction_basis
    )

    padded = jnp.concatenate([weights, jnp.zeros_like(weights)], axis=1)
    products = adjoint_products(padded, kernel_all)[:, :8]
    backward = adjoint_sources(products, compact[19:22])
    spread = unpermute_columns(backward, selector)
    spread = spread.reshape(16, capacity, owners)
    returned = lax.all_to_all(spread, ("gx", "gy"), split_axis=2, concat_axis=2, tiled=True)
    per_row = returned.reshape(16, rows_dev) * living[None, :]
    cell_adjoint = jnp.zeros(cell_state.shape, jnp.float32).at[:, surface_cell].add(per_row)
    return (far_field, objective, cell_adjoint)


def solution(mesh):
    placed = (
        P(None, ("gx", "gy")),
        P(None, ("gx", "gy")),
        P(("gx", "gy")),
        P(("gx", "gy")),
        P(),
        P(),
        P(),
    )
    return jax.shard_map(
        on_device,
        mesh=mesh,
        in_specs=placed,
        out_specs=(P(), P(), P(None, ("gx", "gy"))),
        check_vma=False,
    )
```

```python
import functools
import math

import jax
import jax.numpy as jnp
from jax import lax
from jax.experimental import pallas as pl
from jax.experimental.pallas import tpu as pltpu
from jax.sharding import PartitionSpec as P

GOLDEN = math.pi * (3.0 - math.sqrt(5.0))
PI_A = round(math.pi * 32768.0) / 32768.0
PI_B = math.pi - PI_A
INV_PI = 1.0 / math.pi
SIN_C = [-0.16666657019913644, 0.00833301540393062, -0.00019806478078586938, 2.599750005030262e-06]
COS_C = [-0.4999993175258851, 0.041663973510963626, -0.0013855797199316853, 2.3191254010748703e-05]


def sincos(theta):
    n = jnp.floor(theta * INV_PI + 0.5)
    r = (theta - n * PI_A) - n * PI_B
    z = r * r
    ps = SIN_C[-1]
    for c in SIN_C[-2::-1]:
        ps = c + z * ps
    pc = COS_C[-1]
    for c in COS_C[-2::-1]:
        pc = c + z * pc
    half = n * 0.5
    sign = 1.0 - 4.0 * (half - jnp.floor(half))
    return (sign * (1.0 + z * pc), sign * (r + (r * z) * ps))


def directions(count_dirs):
    lattice = jnp.arange(count_dirs).astype(jnp.float32)
    height = 1.0 - (2.0 * lattice + 1.0) / count_dirs
    radius_xy = jnp.sqrt(1.0 - height * height)
    azimuth = jnp.mod(lattice * GOLDEN, 2.0 * math.pi)
    return (radius_xy * jnp.cos(azimuth), radius_xy * jnp.sin(azimuth), height)


def kernel_block(points, wavenum, east_x, north_y, upward):
    phases = wavenum * (
        points[0][:, None] * east_x[None, :]
        + points[1][:, None] * north_y[None, :]
        + points[2][:, None] * upward[None, :]
    )
    cosine, sine = sincos(phases)
    return jnp.concatenate([cosine, sine], axis=1).astype(jnp.bfloat16)


def source_rows(rows_block, level):
    surface_area = rows_block[22]
    normal = rows_block[19:22]
    pressure_real = rows_block[level] * surface_area
    pressure_imag = rows_block[4 + level] * surface_area
    return jnp.stack(
        [
            rows_block[8 + level] * surface_area,
            normal[0] * pressure_real,
            normal[1] * pressure_real,
            normal[2] * pressure_real,
            rows_block[12 + level] * surface_area,
            normal[0] * pressure_imag,
            normal[1] * pressure_imag,
            normal[2] * pressure_imag,
        ]
    ).astype(jnp.bfloat16)


def far_field_of(sums, wavenumbers, direction_basis):
    half_width = sums.shape[2] // 2
    cosine_part = sums[:, :, :half_width]
    sine_part = sums[:, :, half_width:]
    real_q = cosine_part[:, 0:4] + sine_part[:, 4:8]
    imag_q = cosine_part[:, 4:8] - sine_part[:, 0:4]
    real_z = jnp.sum(direction_basis[None] * real_q, axis=1)
    imag_z = jnp.sum(direction_basis[None] * imag_q, axis=1)
    wavenum = wavenumbers[:, None]
    return jnp.stack([-wavenum * imag_z, wavenum * real_z], axis=1)


def adjoint_weights(far_field, target, direction_weight, wavenumbers, direction_basis):
    count_dirs = far_field.shape[2]
    mismatch = far_field - target
    objective = jnp.sum(direction_weight * mismatch * mismatch) / count_dirs
    gradient = 2.0 * direction_weight * mismatch / count_dirs
    wavenum = wavenumbers[:, None]
    real_gz = wavenum * gradient[:, 1]
    imag_gz = -wavenum * gradient[:, 0]
    real_gq = direction_basis[None] * real_gz[:, None]
    imag_gq = direction_basis[None] * imag_gz[:, None]
    upper_half = jnp.concatenate([real_gq, -imag_gq], axis=2)
    lower_half = jnp.concatenate([imag_gq, real_gq], axis=2)
    return (objective, jnp.concatenate([upper_half, lower_half], axis=1).astype(jnp.bfloat16))


def adjoint_sources(products, normal):
    pressure_real = jnp.sum(normal[None] * products[:, 1:4], axis=1)
    pressure_imag = jnp.sum(normal[None] * products[:, 5:8], axis=1)
    return jnp.concatenate([pressure_real, pressure_imag, products[:, 0], products[:, 4]], axis=0)


ROW_BLOCK = 256
ROW_CHUNK = 16
LANE_CHUNK = 256


def forward_kernel(wave_ref, pts_ref, dirs_ref, rows_ref, cs_ref, q_ref, src_scr):
    step = pl.program_id(0)
    num_freqs = cs_ref.shape[0]
    count_dirs = dirs_ref.shape[2]
    wavenums = [wave_ref[level] for level in range(num_freqs)]

    @pl.loop(0, ROW_BLOCK // ROW_CHUNK)
    def _(i):
        r0 = pl.multiple_of(i * ROW_CHUNK, ROW_CHUNK)
        coords = [
            jnp.broadcast_to(pts_ref[pl.ds(r0, ROW_CHUNK), c : c + 1], (ROW_CHUNK, LANE_CHUNK))
            for c in range(3)
        ]
        for j0 in range(0, count_dirs, LANE_CHUNK):
            lanes = slice(j0, j0 + LANE_CHUNK)
            along = (
                coords[0] * dirs_ref[0, :, lanes]
                + coords[1] * dirs_ref[1, :, lanes]
                + coords[2] * dirs_ref[2, :, lanes]
            )
            for level in range(num_freqs):
                cosine, sine = sincos(wavenums[level] * along)
                cs_ref[level, pl.ds(r0, ROW_CHUNK), lanes] = cosine.astype(jnp.bfloat16)
                cs_ref[level, pl.ds(r0, ROW_CHUNK), j0 + count_dirs : j0 + count_dirs + LANE_CHUNK] = (
                    sine.astype(jnp.bfloat16)
                )

    @pl.when(step == 0)
    def _():
        q_ref[...] = jnp.zeros_like(q_ref)

    area = rows_ref[22:23, :]
    src_scr[...] = jnp.zeros_like(src_scr)
    for level in range(num_freqs):
        pressure_real = rows_ref[level : level + 1, :] * area
        pressure_imag = rows_ref[4 + level : 5 + level, :] * area
        src_scr[0:1, :] = rows_ref[8 + level : 9 + level, :] * area
        src_scr[4:5, :] = rows_ref[12 + level : 13 + level, :] * area
        for c in range(3):
            normal = rows_ref[19 + c : 20 + c, :]
            src_scr[1 + c : 2 + c, :] = normal * pressure_real
            src_scr[5 + c : 6 + c, :] = normal * pressure_imag
        source = src_scr[...].astype(jnp.bfloat16)
        q_ref[level] += jnp.dot(source, cs_ref[level], preferred_element_type=jnp.float32)


def forward_sums(wavenumbers, points, dirs_block, compact):
    num_freqs = wavenumbers.shape[0]
    rows = points.shape[0]
    count_dirs = dirs_block.shape[2]
    grid = (rows // ROW_BLOCK,)
    return pl.pallas_call(
        forward_kernel,
        grid=grid,
        in_specs=[
            pl.BlockSpec(memory_space=pltpu.SMEM),
            pl.BlockSpec((ROW_BLOCK, 3), lambda b: (b, 0)),
            pl.BlockSpec(dirs_block.shape, lambda b: (0, 0, 0)),
            pl.BlockSpec((compact.shape[0], ROW_BLOCK), lambda b: (0, b)),
        ],
        out_specs=[
            pl.BlockSpec((num_freqs, ROW_BLOCK, 2 * count_dirs), lambda b: (0, b, 0)),
            pl.BlockSpec((num_freqs, 16, 2 * count_dirs), lambda b: (0, 0, 0)),
        ],
        out_shape=[
            jax.ShapeDtypeStruct((num_freqs, rows, 2 * count_dirs), jnp.bfloat16),
            jax.ShapeDtypeStruct((num_freqs, 16, 2 * count_dirs), jnp.float32),
        ],
        scratch_shapes=[pltpu.VMEM((16, ROW_BLOCK), jnp.float32)],
        compiler_params=pltpu.CompilerParams(
            dimension_semantics=("arbitrary",), vmem_limit_bytes=48 * 1024 * 1024
        ),
        cost_estimate=pl.CostEstimate(
            flops=2 * 16 * rows * 2 * count_dirs * num_freqs + 60 * rows * count_dirs * num_freqs,
            transcendentals=0,
            bytes_accessed=2 * rows * 2 * count_dirs * num_freqs,
        ),
    )(wavenumbers, points, dirs_block, compact)


def adjoint_kernel(w_ref, cs_ref, out_ref):
    for level in range(cs_ref.shape[0]):
        out_ref[level] = lax.dot_general(
            w_ref[level], cs_ref[level], (((1,), (1,)), ((), ())), preferred_element_type=jnp.float32
        )


def adjoint_products(weights, kernel_all):
    num_freqs, rows, width = kernel_all.shape
    return pl.pallas_call(
        adjoint_kernel,
        grid=(rows // ROW_BLOCK,),
        in_specs=[
            pl.BlockSpec(weights.shape, lambda b: (0, 0, 0)),
            pl.BlockSpec((num_freqs, ROW_BLOCK, width), lambda b: (0, b, 0)),
        ],
        out_specs=pl.BlockSpec((num_freqs, weights.shape[1], ROW_BLOCK), lambda b: (0, 0, b)),
        out_shape=jax.ShapeDtypeStruct((num_freqs, weights.shape[1], rows), jnp.float32),
        compiler_params=pltpu.CompilerParams(
            dimension_semantics=("arbitrary",), vmem_limit_bytes=48 * 1024 * 1024
        ),
        cost_estimate=pl.CostEstimate(
            flops=2 * weights.shape[1] * rows * width * num_freqs,
            transcendentals=0,
            bytes_accessed=2 * rows * width * num_freqs,
        ),
    )(weights, kernel_all)


def split_bf16(values):
    high = lax.reduce_precision(values, exponent_bits=8, mantissa_bits=7)
    rest = values - high
    middle = lax.reduce_precision(rest, exponent_bits=8, mantissa_bits=7)
    low = rest - middle
    return jnp.concatenate([high, middle, low], axis=0).astype(jnp.bfloat16)


def join_parts(product, channels):
    return (product[:channels] + product[channels : 2 * channels]) + product[2 * channels :]


def permute_columns(values, selector):
    product = jnp.dot(split_bf16(values), selector, preferred_element_type=jnp.float32)
    return join_parts(product, values.shape[0])


def unpermute_columns(values, selector):
    product = lax.dot_general(
        split_bf16(values), selector, (((1,), (1,)), ((), ())), preferred_element_type=jnp.float32
    )
    return join_parts(product, values.shape[0])


MESH_IDS = pl.DeviceIdType.MESH


def reduce_kernel(nx, ny, x_ref, out_ref, part_a, part_b, got_a, got_b, got_c, sems):
    b0 = lax.axis_index("gx")
    a0 = lax.axis_index("gy")
    barrier = pltpu.get_barrier_semaphore()
    for t in range(1, ny):
        pl.semaphore_signal(barrier, inc=1, device_id=(b0, lax.rem(a0 + t, ny)), device_id_type=MESH_IDS)
    for t in range(1, nx):
        pl.semaphore_signal(barrier, inc=1, device_id=(lax.rem(b0 + t, nx), a0), device_id_type=MESH_IDS)
    pl.semaphore_wait(barrier, nx + ny - 2)

    def exchange(phase, src_of, dst_of, peers, along_x):
        copies = []
        for t in range(1, peers):
            if along_x:
                peer = lax.rem(b0 + t, nx)
                me, device = b0, (peer, a0)
            else:
                peer = lax.rem(a0 + t, ny)
                me, device = a0, (b0, peer)
            copy = pltpu.make_async_remote_copy(
                src_ref=src_of(peer),
                dst_ref=dst_of(me),
                send_sem=sems.at[phase, 0, peer],
                recv_sem=sems.at[phase, 1, me],
                device_id=device,
                device_id_type=MESH_IDS,
            )
            copy.start()
            copies.append((peer, device))
        for peer, device in copies:
            pltpu.make_async_remote_copy(
                src_ref=src_of(peer),
                dst_ref=dst_of(peer),
                send_sem=sems.at[phase, 0, peer],
                recv_sem=sems.at[phase, 1, peer],
                device_id=device,
                device_id_type=MESH_IDS,
            ).wait()

    exchange(0, lambda a: x_ref.at[a], lambda a: got_a.at[a], ny, False)
    got_a[a0] = x_ref[a0]
    part_a[...] = jnp.sum(got_a[...], axis=0)
    exchange(1, lambda b: part_a.at[pl.ds(b, 1)], lambda b: got_b.at[b], nx, True)
    got_b[b0] = part_a[pl.ds(b0, 1)]
    part_b[...] = jnp.sum(got_b[...], axis=0)
    exchange(2, lambda b: part_b, lambda b: got_c.at[pl.ds(b, 1)], nx, True)
    got_c[pl.ds(b0, 1)] = part_b[...]
    exchange(3, lambda a: got_c, lambda a: out_ref.at[a], ny, False)
    out_ref[a0] = got_c[...]


def sum_over_devices(partial, owners):
    nx = lax.axis_size("gx")
    ny = lax.axis_size("gy")
    lanes = partial.size // (nx * ny)
    shaped = partial.reshape(ny, nx, lanes)
    peers = max(nx, ny)
    total = pl.pallas_call(
        functools.partial(reduce_kernel, nx, ny),
        in_specs=[pl.BlockSpec(memory_space=pltpu.VMEM)],
        out_specs=pl.BlockSpec(memory_space=pltpu.VMEM),
        out_shape=jax.ShapeDtypeStruct(shaped.shape, jnp.float32),
        scratch_shapes=[
            pltpu.VMEM((nx, lanes), jnp.float32),
            pltpu.VMEM((1, lanes), jnp.float32),
            pltpu.VMEM((ny, nx, lanes), jnp.float32),
            pltpu.VMEM((nx, 1, lanes), jnp.float32),
            pltpu.VMEM((nx, lanes), jnp.float32),
            pltpu.SemaphoreType.DMA((4, 2, peers)),
        ],
        compiler_params=pltpu.CompilerParams(collective_id=0, has_side_effects=True),
    )(shaped)
    return total.reshape(partial.shape)


def sum_over_devices_a2a(partial, owners):
    chunks = partial.reshape(owners, -1)
    got = lax.all_to_all(chunks, ("gx", "gy"), split_axis=0, concat_axis=0, tiled=True)
    mine = jnp.sum(got, axis=0, keepdims=True)
    spread = jnp.broadcast_to(mine, chunks.shape)
    full = lax.all_to_all(spread, ("gx", "gy"), split_axis=0, concat_axis=0, tiled=True)
    return full.reshape(partial.shape)


def on_device(cell_state, geometry, surface_cell, counts, wavenumbers, target, direction_weight):
    owners = lax.axis_size(("gx", "gy"))
    rows_dev = surface_cell.shape[0]
    capacity = rows_dev // owners
    live_own = rows_dev // 4
    count_dirs = target.shape[2]
    num_freqs = wavenumbers.shape[0]
    living = (jnp.arange(rows_dev) < counts[0]).astype(jnp.float32)
    outgoing = (
        jnp.concatenate(
            [cell_state[:, surface_cell], geometry, jnp.ones((1, rows_dev), jnp.float32)], axis=0
        )
        * living[None, :]
    )
    outgoing = outgoing.reshape(24, capacity, owners)
    arrived = lax.all_to_all(outgoing, ("gx", "gy"), split_axis=2, concat_axis=2, tiled=True)
    marker = arrived[23]
    per_source = jnp.sum(marker, axis=0).astype(jnp.int32)
    offset = jnp.cumsum(per_source) - per_source
    position = offset[None, :] + jnp.arange(capacity, dtype=jnp.int32)[:, None]
    packed_slot = jnp.where(marker > 0.5, position, live_own).reshape(capacity * owners)
    selector = (packed_slot[:, None] == jnp.arange(live_own, dtype=jnp.int32)[None, :]).astype(jnp.bfloat16)
    compact = permute_columns(arrived[:23].reshape(23, capacity * owners), selector)
    east_x, north_y, upward = directions(count_dirs)
    direction_basis = jnp.stack([jnp.ones_like(east_x), east_x, north_y, upward])

    points = compact[16:19].T
    dirs_block = jnp.broadcast_to(jnp.stack([east_x, north_y, upward])[:, None, :], (3, ROW_CHUNK, count_dirs))
    kernel_all, sums = forward_sums(wavenumbers, points, dirs_block, compact)
    sums = sums[:, :8]
    far_field = sum_over_devices(far_field_of(sums, wavenumbers, direction_basis), owners)
    objective, weights = adjoint_weights(
        far_field, target, direction_weight, wavenumbers, direction_basis
    )

    padded = jnp.concatenate([weights, jnp.zeros_like(weights)], axis=1)
    products = adjoint_products(padded, kernel_all)[:, :8]
    backward = adjoint_sources(products, compact[19:22])
    spread = unpermute_columns(backward, selector)
    spread = spread.reshape(16, capacity, owners)
    returned = lax.all_to_all(spread, ("gx", "gy"), split_axis=2, concat_axis=2, tiled=True)
    per_row = returned.reshape(16, rows_dev) * living[None, :]
    cell_adjoint = jnp.zeros(cell_state.shape, jnp.float32).at[:, surface_cell].add(per_row)
    return (far_field, objective, cell_adjoint)


def solution(mesh):
    placed = (
        P(None, ("gx", "gy")),
        P(None, ("gx", "gy")),
        P(("gx", "gy")),
        P(("gx", "gy")),
        P(),
        P(),
        P(),
    )
    return jax.shard_map(
        on_device,
        mesh=mesh,
        in_specs=placed,
        out_specs=(P(), P(), P(None, ("gx", "gy"))),
        check_vma=False,
    )
```

```python
import functools
import math

import jax
import jax.numpy as jnp
from jax import lax
from jax.experimental import pallas as pl
from jax.experimental.pallas import tpu as pltpu
from jax.sharding import PartitionSpec as P

GOLDEN = math.pi * (3.0 - math.sqrt(5.0))
PI_A = round(math.pi * 32768.0) / 32768.0
PI_B = math.pi - PI_A
INV_PI = 1.0 / math.pi
SIN_C = [-0.16666657019913644, 0.00833301540393062, -0.00019806478078586938, 2.599750005030262e-06]
COS_C = [-0.4999993175258851, 0.041663973510963626, -0.0013855797199316853, 2.3191254010748703e-05]


def sincos(theta):
    n = jnp.floor(theta * INV_PI + 0.5)
    r = (theta - n * PI_A) - n * PI_B
    z = r * r
    ps = SIN_C[-1]
    for c in SIN_C[-2::-1]:
        ps = c + z * ps
    pc = COS_C[-1]
    for c in COS_C[-2::-1]:
        pc = c + z * pc
    half = n * 0.5
    sign = 1.0 - 4.0 * (half - jnp.floor(half))
    return (sign * (1.0 + z * pc), sign * (r + (r * z) * ps))


def directions(count_dirs):
    lattice = jnp.arange(count_dirs).astype(jnp.float32)
    height = 1.0 - (2.0 * lattice + 1.0) / count_dirs
    radius_xy = jnp.sqrt(1.0 - height * height)
    azimuth = jnp.mod(lattice * GOLDEN, 2.0 * math.pi)
    return (radius_xy * jnp.cos(azimuth), radius_xy * jnp.sin(azimuth), height)


def kernel_block(points, wavenum, east_x, north_y, upward):
    phases = wavenum * (
        points[0][:, None] * east_x[None, :]
        + points[1][:, None] * north_y[None, :]
        + points[2][:, None] * upward[None, :]
    )
    cosine, sine = sincos(phases)
    return jnp.concatenate([cosine, sine], axis=1).astype(jnp.bfloat16)


def source_rows(rows_block, level):
    surface_area = rows_block[22]
    normal = rows_block[19:22]
    pressure_real = rows_block[level] * surface_area
    pressure_imag = rows_block[4 + level] * surface_area
    return jnp.stack(
        [
            rows_block[8 + level] * surface_area,
            normal[0] * pressure_real,
            normal[1] * pressure_real,
            normal[2] * pressure_real,
            rows_block[12 + level] * surface_area,
            normal[0] * pressure_imag,
            normal[1] * pressure_imag,
            normal[2] * pressure_imag,
        ]
    ).astype(jnp.bfloat16)


def far_field_of(sums, wavenumbers, direction_basis):
    half_width = sums.shape[2] // 2
    cosine_part = sums[:, :, :half_width]
    sine_part = sums[:, :, half_width:]
    real_q = cosine_part[:, 0:4] + sine_part[:, 4:8]
    imag_q = cosine_part[:, 4:8] - sine_part[:, 0:4]
    real_z = jnp.sum(direction_basis[None] * real_q, axis=1)
    imag_z = jnp.sum(direction_basis[None] * imag_q, axis=1)
    wavenum = wavenumbers[:, None]
    return jnp.stack([-wavenum * imag_z, wavenum * real_z], axis=1)


def adjoint_weights(far_field, target, direction_weight, wavenumbers, direction_basis):
    count_dirs = far_field.shape[2]
    mismatch = far_field - target
    objective = jnp.sum(direction_weight * mismatch * mismatch) / count_dirs
    gradient = 2.0 * direction_weight * mismatch / count_dirs
    wavenum = wavenumbers[:, None]
    real_gz = wavenum * gradient[:, 1]
    imag_gz = -wavenum * gradient[:, 0]
    real_gq = direction_basis[None] * real_gz[:, None]
    imag_gq = direction_basis[None] * imag_gz[:, None]
    upper_half = jnp.concatenate([real_gq, -imag_gq], axis=2)
    lower_half = jnp.concatenate([imag_gq, real_gq], axis=2)
    return (objective, jnp.concatenate([upper_half, lower_half], axis=1).astype(jnp.bfloat16))


def adjoint_sources(products, normal):
    pressure_real = jnp.sum(normal[None] * products[:, 1:4], axis=1)
    pressure_imag = jnp.sum(normal[None] * products[:, 5:8], axis=1)
    return jnp.concatenate([pressure_real, pressure_imag, products[:, 0], products[:, 4]], axis=0)


ROW_BLOCK = 256
ROW_CHUNK = 16
LANE_CHUNK = 256


def forward_kernel(wave_ref, pts_ref, dirs_ref, rows_ref, cs_ref, q_ref, src_scr):
    step = pl.program_id(0)
    num_freqs = cs_ref.shape[0]
    count_dirs = dirs_ref.shape[2]
    wavenums = [wave_ref[level] for level in range(num_freqs)]

    @pl.loop(0, ROW_BLOCK // ROW_CHUNK)
    def _(i):
        r0 = pl.multiple_of(i * ROW_CHUNK, ROW_CHUNK)
        coords = [
            jnp.broadcast_to(pts_ref[pl.ds(r0, ROW_CHUNK), c : c + 1], (ROW_CHUNK, LANE_CHUNK))
            for c in range(3)
        ]
        for j0 in range(0, count_dirs, LANE_CHUNK):
            lanes = slice(j0, j0 + LANE_CHUNK)
            along = (
                coords[0] * dirs_ref[0, :, lanes]
                + coords[1] * dirs_ref[1, :, lanes]
                + coords[2] * dirs_ref[2, :, lanes]
            )
            for level in range(num_freqs):
                cosine, sine = sincos(wavenums[level] * along)
                cs_ref[level, pl.ds(r0, ROW_CHUNK), lanes] = cosine.astype(jnp.bfloat16)
                cs_ref[level, pl.ds(r0, ROW_CHUNK), j0 + count_dirs : j0 + count_dirs + LANE_CHUNK] = (
                    sine.astype(jnp.bfloat16)
                )

    @pl.when(step == 0)
    def _():
        q_ref[...] = jnp.zeros_like(q_ref)

    area = rows_ref[22:23, :]
    src_scr[...] = jnp.zeros_like(src_scr)
    for level in range(num_freqs):
        pressure_real = rows_ref[level : level + 1, :] * area
        pressure_imag = rows_ref[4 + level : 5 + level, :] * area
        src_scr[0:1, :] = rows_ref[8 + level : 9 + level, :] * area
        src_scr[4:5, :] = rows_ref[12 + level : 13 + level, :] * area
        for c in range(3):
            normal = rows_ref[19 + c : 20 + c, :]
            src_scr[1 + c : 2 + c, :] = normal * pressure_real
            src_scr[5 + c : 6 + c, :] = normal * pressure_imag
        source = src_scr[...].astype(jnp.bfloat16)
        q_ref[level] += jnp.dot(source, cs_ref[level], preferred_element_type=jnp.float32)


def forward_sums(wavenumbers, points, dirs_block, compact):
    num_freqs = wavenumbers.shape[0]
    rows = points.shape[0]
    count_dirs = dirs_block.shape[2]
    grid = (rows // ROW_BLOCK,)
    return pl.pallas_call(
        forward_kernel,
        grid=grid,
        in_specs=[
            pl.BlockSpec(memory_space=pltpu.SMEM),
            pl.BlockSpec((ROW_BLOCK, 3), lambda b: (b, 0)),
            pl.BlockSpec(dirs_block.shape, lambda b: (0, 0, 0)),
            pl.BlockSpec((compact.shape[0], ROW_BLOCK), lambda b: (0, b)),
        ],
        out_specs=[
            pl.BlockSpec((num_freqs, ROW_BLOCK, 2 * count_dirs), lambda b: (0, b, 0)),
            pl.BlockSpec((num_freqs, 16, 2 * count_dirs), lambda b: (0, 0, 0)),
        ],
        out_shape=[
            jax.ShapeDtypeStruct((num_freqs, rows, 2 * count_dirs), jnp.bfloat16),
            jax.ShapeDtypeStruct((num_freqs, 16, 2 * count_dirs), jnp.float32),
        ],
        scratch_shapes=[pltpu.VMEM((16, ROW_BLOCK), jnp.float32)],
        compiler_params=pltpu.CompilerParams(
            dimension_semantics=("arbitrary",), vmem_limit_bytes=48 * 1024 * 1024
        ),
        cost_estimate=pl.CostEstimate(
            flops=2 * 16 * rows * 2 * count_dirs * num_freqs + 60 * rows * count_dirs * num_freqs,
            transcendentals=0,
            bytes_accessed=2 * rows * 2 * count_dirs * num_freqs,
        ),
    )(wavenumbers, points, dirs_block, compact)


def adjoint_kernel(w_ref, cs_ref, out_ref):
    for level in range(cs_ref.shape[0]):
        out_ref[level] = lax.dot_general(
            w_ref[level], cs_ref[level], (((1,), (1,)), ((), ())), preferred_element_type=jnp.float32
        )


def adjoint_products(weights, kernel_all):
    num_freqs, rows, width = kernel_all.shape
    return pl.pallas_call(
        adjoint_kernel,
        grid=(rows // ROW_BLOCK,),
        in_specs=[
            pl.BlockSpec(weights.shape, lambda b: (0, 0, 0)),
            pl.BlockSpec((num_freqs, ROW_BLOCK, width), lambda b: (0, b, 0)),
        ],
        out_specs=pl.BlockSpec((num_freqs, weights.shape[1], ROW_BLOCK), lambda b: (0, 0, b)),
        out_shape=jax.ShapeDtypeStruct((num_freqs, weights.shape[1], rows), jnp.float32),
        compiler_params=pltpu.CompilerParams(
            dimension_semantics=("arbitrary",), vmem_limit_bytes=48 * 1024 * 1024
        ),
        cost_estimate=pl.CostEstimate(
            flops=2 * weights.shape[1] * rows * width * num_freqs,
            transcendentals=0,
            bytes_accessed=2 * rows * width * num_freqs,
        ),
    )(weights, kernel_all)


def split_bf16(values):
    high = lax.reduce_precision(values, exponent_bits=8, mantissa_bits=7)
    rest = values - high
    middle = lax.reduce_precision(rest, exponent_bits=8, mantissa_bits=7)
    low = rest - middle
    return jnp.concatenate([high, middle, low], axis=0).astype(jnp.bfloat16)


def join_parts(product, channels):
    return (product[:channels] + product[channels : 2 * channels]) + product[2 * channels :]


def permute_columns(values, selector):
    product = jnp.dot(split_bf16(values), selector, preferred_element_type=jnp.float32)
    return join_parts(product, values.shape[0])


def unpermute_columns(values, selector):
    product = lax.dot_general(
        split_bf16(values), selector, (((1,), (1,)), ((), ())), preferred_element_type=jnp.float32
    )
    return join_parts(product, values.shape[0])


MESH_IDS = pl.DeviceIdType.MESH


def reduce_kernel(nx, ny, x_ref, out_ref, part_a, part_b, got_a, got_b, sems):
    b0 = lax.axis_index("gx")
    a0 = lax.axis_index("gy")
    barrier = pltpu.get_barrier_semaphore()
    for t in range(1, ny):
        pl.semaphore_signal(barrier, inc=1, device_id=(b0, lax.rem(a0 + t, ny)), device_id_type=MESH_IDS)
    for t in range(1, nx):
        pl.semaphore_signal(barrier, inc=1, device_id=(lax.rem(b0 + t, nx), a0), device_id_type=MESH_IDS)
    pl.semaphore_wait(barrier, nx + ny - 2)

    def exchange(phase, src_of, dst_of, peers, along_x):
        copies = []
        for t in range(1, peers):
            if along_x:
                peer = lax.rem(b0 + t, nx)
                me, device = b0, (peer, a0)
            else:
                peer = lax.rem(a0 + t, ny)
                me, device = a0, (b0, peer)
            copy = pltpu.make_async_remote_copy(
                src_ref=src_of(peer),
                dst_ref=dst_of(me),
                send_sem=sems.at[phase, 0, peer],
                recv_sem=sems.at[phase, 1, me],
                device_id=device,
                device_id_type=MESH_IDS,
            )
            copy.start()
            copies.append((peer, device))
        for peer, device in copies:
            pltpu.make_async_remote_copy(
                src_ref=src_of(peer),
                dst_ref=dst_of(peer),
                send_sem=sems.at[phase, 0, peer],
                recv_sem=sems.at[phase, 1, peer],
                device_id=device,
                device_id_type=MESH_IDS,
            ).wait()

    exchange(0, lambda a: x_ref.at[a], lambda a: got_a.at[a], ny, False)
    got_a[a0] = x_ref[a0]
    part_a[...] = jnp.sum(got_a[...], axis=0)
    exchange(1, lambda b: part_a, lambda b: got_b.at[b], nx, True)
    got_b[b0] = part_a[...]
    part_b[...] = jnp.sum(got_b[...], axis=0)
    exchange(2, lambda a: part_b, lambda a: out_ref.at[a], ny, False)
    out_ref[a0] = part_b[...]


def sum_over_devices(partial, owners):
    nx = lax.axis_size("gx")
    ny = lax.axis_size("gy")
    lanes = partial.size // (nx * ny)
    shaped = partial.reshape(ny, nx, lanes)
    peers = max(nx, ny)
    total = pl.pallas_call(
        functools.partial(reduce_kernel, nx, ny),
        in_specs=[pl.BlockSpec(memory_space=pltpu.VMEM)],
        out_specs=pl.BlockSpec(memory_space=pltpu.VMEM),
        out_shape=jax.ShapeDtypeStruct(shaped.shape, jnp.float32),
        scratch_shapes=[
            pltpu.VMEM((nx, lanes), jnp.float32),
            pltpu.VMEM((nx, lanes), jnp.float32),
            pltpu.VMEM((ny, nx, lanes), jnp.float32),
            pltpu.VMEM((nx, nx, lanes), jnp.float32),
            pltpu.SemaphoreType.DMA((3, 2, peers)),
        ],
        compiler_params=pltpu.CompilerParams(collective_id=0, has_side_effects=True),
    )(shaped)
    return total.reshape(partial.shape)


def sum_over_devices_a2a(partial, owners):
    chunks = partial.reshape(owners, -1)
    got = lax.all_to_all(chunks, ("gx", "gy"), split_axis=0, concat_axis=0, tiled=True)
    mine = jnp.sum(got, axis=0, keepdims=True)
    spread = jnp.broadcast_to(mine, chunks.shape)
    full = lax.all_to_all(spread, ("gx", "gy"), split_axis=0, concat_axis=0, tiled=True)
    return full.reshape(partial.shape)


def on_device(cell_state, geometry, surface_cell, counts, wavenumbers, target, direction_weight):
    owners = lax.axis_size(("gx", "gy"))
    rows_dev = surface_cell.shape[0]
    capacity = rows_dev // owners
    live_own = rows_dev // 4
    count_dirs = target.shape[2]
    num_freqs = wavenumbers.shape[0]
    living = (jnp.arange(rows_dev) < counts[0]).astype(jnp.float32)
    outgoing = (
        jnp.concatenate(
            [cell_state[:, surface_cell], geometry, jnp.ones((1, rows_dev), jnp.float32)], axis=0
        )
        * living[None, :]
    )
    outgoing = outgoing.reshape(24, capacity, owners)
    arrived = lax.all_to_all(outgoing, ("gx", "gy"), split_axis=2, concat_axis=2, tiled=True)
    marker = arrived[23]
    per_source = jnp.sum(marker, axis=0).astype(jnp.int32)
    offset = jnp.cumsum(per_source) - per_source
    position = offset[None, :] + jnp.arange(capacity, dtype=jnp.int32)[:, None]
    packed_slot = jnp.where(marker > 0.5, position, live_own).reshape(capacity * owners)
    selector = (packed_slot[:, None] == jnp.arange(live_own, dtype=jnp.int32)[None, :]).astype(jnp.bfloat16)
    compact = permute_columns(arrived[:23].reshape(23, capacity * owners), selector)
    east_x, north_y, upward = directions(count_dirs)
    direction_basis = jnp.stack([jnp.ones_like(east_x), east_x, north_y, upward])

    points = compact[16:19].T
    dirs_block = jnp.broadcast_to(jnp.stack([east_x, north_y, upward])[:, None, :], (3, ROW_CHUNK, count_dirs))
    kernel_all, sums = forward_sums(wavenumbers, points, dirs_block, compact)
    sums = sums[:, :8]
    far_field = sum_over_devices(far_field_of(sums, wavenumbers, direction_basis), owners)
    objective, weights = adjoint_weights(
        far_field, target, direction_weight, wavenumbers, direction_basis
    )

    padded = jnp.concatenate([weights, jnp.zeros_like(weights)], axis=1)
    products = adjoint_products(padded, kernel_all)[:, :8]
    backward = adjoint_sources(products, compact[19:22])
    spread = unpermute_columns(backward, selector)
    spread = spread.reshape(16, capacity, owners)
    returned = lax.all_to_all(spread, ("gx", "gy"), split_axis=2, concat_axis=2, tiled=True)
    per_row = returned.reshape(16, rows_dev) * living[None, :]
    cell_adjoint = jnp.zeros(cell_state.shape, jnp.float32).at[:, surface_cell].add(per_row)
    return (far_field, objective, cell_adjoint)


def solution(mesh):
    placed = (
        P(None, ("gx", "gy")),
        P(None, ("gx", "gy")),
        P(("gx", "gy")),
        P(("gx", "gy")),
        P(),
        P(),
        P(),
    )
    return jax.shard_map(
        on_device,
        mesh=mesh,
        in_specs=placed,
        out_specs=(P(), P(), P(None, ("gx", "gy"))),
        check_vma=False,
    )
```

```python
import functools
import math

import jax
import jax.numpy as jnp
from jax import lax
from jax.experimental import pallas as pl
from jax.experimental.pallas import tpu as pltpu
from jax.sharding import PartitionSpec as P

GOLDEN = math.pi * (3.0 - math.sqrt(5.0))
PI_A = round(math.pi * 32768.0) / 32768.0
PI_B = math.pi - PI_A
INV_PI = 1.0 / math.pi
SIN_C = [-0.16666657019913644, 0.00833301540393062, -0.00019806478078586938, 2.599750005030262e-06]
COS_C = [-0.4999993175258851, 0.041663973510963626, -0.0013855797199316853, 2.3191254010748703e-05]
SINPI_C = [3.141592578574041, -5.1677067848796066, 2.5500297991194887, -0.5980355679943354, 0.07720094563063706]
COSPI_C = [-4.934795411606951, 4.05844824012755, -1.332068921858188, 0.22002136541700046]


def sincos_turns(u):
    n = jnp.floor(u + 0.5)
    w = u - n
    z = w * w
    ps = SINPI_C[-1]
    for c in SINPI_C[-2::-1]:
        ps = c + z * ps
    pc = COSPI_C[-1]
    for c in COSPI_C[-2::-1]:
        pc = c + z * pc
    half = n * 0.5
    sign = 1.0 - 4.0 * (half - jnp.floor(half))
    return (sign * (1.0 + z * pc), (sign * w) * ps)


def sincos(theta):
    n = jnp.floor(theta * INV_PI + 0.5)
    r = (theta - n * PI_A) - n * PI_B
    z = r * r
    ps = SIN_C[-1]
    for c in SIN_C[-2::-1]:
        ps = c + z * ps
    pc = COS_C[-1]
    for c in COS_C[-2::-1]:
        pc = c + z * pc
    half = n * 0.5
    sign = 1.0 - 4.0 * (half - jnp.floor(half))
    return (sign * (1.0 + z * pc), sign * (r + (r * z) * ps))


def directions(count_dirs):
    lattice = jnp.arange(count_dirs).astype(jnp.float32)
    height = 1.0 - (2.0 * lattice + 1.0) / count_dirs
    radius_xy = jnp.sqrt(1.0 - height * height)
    azimuth = jnp.mod(lattice * GOLDEN, 2.0 * math.pi)
    return (radius_xy * jnp.cos(azimuth), radius_xy * jnp.sin(azimuth), height)


def kernel_block(points, wavenum, east_x, north_y, upward):
    phases = wavenum * (
        points[0][:, None] * east_x[None, :]
        + points[1][:, None] * north_y[None, :]
        + points[2][:, None] * upward[None, :]
    )
    cosine, sine = sincos(phases)
    return jnp.concatenate([cosine, sine], axis=1).astype(jnp.bfloat16)


def source_rows(rows_block, level):
    surface_area = rows_block[22]
    normal = rows_block[19:22]
    pressure_real = rows_block[level] * surface_area
    pressure_imag = rows_block[4 + level] * surface_area
    return jnp.stack(
        [
            rows_block[8 + level] * surface_area,
            normal[0] * pressure_real,
            normal[1] * pressure_real,
            normal[2] * pressure_real,
            rows_block[12 + level] * surface_area,
            normal[0] * pressure_imag,
            normal[1] * pressure_imag,
            normal[2] * pressure_imag,
        ]
    ).astype(jnp.bfloat16)


def far_field_of(sums, wavenumbers, direction_basis):
    half_width = sums.shape[2] // 2
    cosine_part = sums[:, :, :half_width]
    sine_part = sums[:, :, half_width:]
    real_q = cosine_part[:, 0:4] + sine_part[:, 4:8]
    imag_q = cosine_part[:, 4:8] - sine_part[:, 0:4]
    real_z = jnp.sum(direction_basis[None] * real_q, axis=1)
    imag_z = jnp.sum(direction_basis[None] * imag_q, axis=1)
    wavenum = wavenumbers[:, None]
    return jnp.stack([-wavenum * imag_z, wavenum * real_z], axis=1)


def adjoint_weights(far_field, target, direction_weight, wavenumbers, direction_basis):
    count_dirs = far_field.shape[2]
    mismatch = far_field - target
    objective = jnp.sum(direction_weight * mismatch * mismatch) / count_dirs
    gradient = 2.0 * direction_weight * mismatch / count_dirs
    wavenum = wavenumbers[:, None]
    real_gz = wavenum * gradient[:, 1]
    imag_gz = -wavenum * gradient[:, 0]
    real_gq = direction_basis[None] * real_gz[:, None]
    imag_gq = direction_basis[None] * imag_gz[:, None]
    upper_half = jnp.concatenate([real_gq, -imag_gq], axis=2)
    lower_half = jnp.concatenate([imag_gq, real_gq], axis=2)
    return (objective, jnp.concatenate([upper_half, lower_half], axis=1).astype(jnp.bfloat16))


def adjoint_sources(products, normal):
    pressure_real = jnp.sum(normal[None] * products[:, 1:4], axis=1)
    pressure_imag = jnp.sum(normal[None] * products[:, 5:8], axis=1)
    return jnp.concatenate([pressure_real, pressure_imag, products[:, 0], products[:, 4]], axis=0)


ROW_BLOCK = 256
ROW_CHUNK = 16
LANE_CHUNK = 256


def forward_kernel(wave_ref, pts_ref, dirs_ref, rows_ref, cs_ref, q_ref, src_scr):
    step = pl.program_id(0)
    num_freqs = cs_ref.shape[0]
    count_dirs = dirs_ref.shape[2]
    turns = [wave_ref[level] * INV_PI for level in range(num_freqs)]

    @pl.loop(0, ROW_BLOCK // ROW_CHUNK)
    def _(i):
        r0 = pl.multiple_of(i * ROW_CHUNK, ROW_CHUNK)
        coords = [
            jnp.broadcast_to(pts_ref[pl.ds(r0, ROW_CHUNK), c : c + 1], (ROW_CHUNK, LANE_CHUNK))
            for c in range(3)
        ]
        for j0 in range(0, count_dirs, LANE_CHUNK):
            lanes = slice(j0, j0 + LANE_CHUNK)
            along = (
                coords[0] * dirs_ref[0, :, lanes]
                + coords[1] * dirs_ref[1, :, lanes]
                + coords[2] * dirs_ref[2, :, lanes]
            )
            for level in range(num_freqs):
                cosine, sine = sincos_turns(turns[level] * along)
                cs_ref[level, pl.ds(r0, ROW_CHUNK), lanes] = cosine.astype(jnp.bfloat16)
                cs_ref[level, pl.ds(r0, ROW_CHUNK), j0 + count_dirs : j0 + count_dirs + LANE_CHUNK] = (
                    sine.astype(jnp.bfloat16)
                )

    @pl.when(step == 0)
    def _():
        q_ref[...] = jnp.zeros_like(q_ref)

    area = rows_ref[22:23, :]
    src_scr[...] = jnp.zeros_like(src_scr)
    for level in range(num_freqs):
        pressure_real = rows_ref[level : level + 1, :] * area
        pressure_imag = rows_ref[4 + level : 5 + level, :] * area
        src_scr[0:1, :] = rows_ref[8 + level : 9 + level, :] * area
        src_scr[4:5, :] = rows_ref[12 + level : 13 + level, :] * area
        for c in range(3):
            normal = rows_ref[19 + c : 20 + c, :]
            src_scr[1 + c : 2 + c, :] = normal * pressure_real
            src_scr[5 + c : 6 + c, :] = normal * pressure_imag
        source = src_scr[...].astype(jnp.bfloat16)
        q_ref[level] += jnp.dot(source, cs_ref[level], preferred_element_type=jnp.float32)


def forward_sums(wavenumbers, points, dirs_block, compact):
    num_freqs = wavenumbers.shape[0]
    rows = points.shape[0]
    count_dirs = dirs_block.shape[2]
    grid = (rows // ROW_BLOCK,)
    return pl.pallas_call(
        forward_kernel,
        grid=grid,
        in_specs=[
            pl.BlockSpec(memory_space=pltpu.SMEM),
            pl.BlockSpec((ROW_BLOCK, 3), lambda b: (b, 0)),
            pl.BlockSpec(dirs_block.shape, lambda b: (0, 0, 0)),
            pl.BlockSpec((compact.shape[0], ROW_BLOCK), lambda b: (0, b)),
        ],
        out_specs=[
            pl.BlockSpec((num_freqs, ROW_BLOCK, 2 * count_dirs), lambda b: (0, b, 0)),
            pl.BlockSpec((num_freqs, 16, 2 * count_dirs), lambda b: (0, 0, 0)),
        ],
        out_shape=[
            jax.ShapeDtypeStruct((num_freqs, rows, 2 * count_dirs), jnp.bfloat16),
            jax.ShapeDtypeStruct((num_freqs, 16, 2 * count_dirs), jnp.float32),
        ],
        scratch_shapes=[pltpu.VMEM((16, ROW_BLOCK), jnp.float32)],
        compiler_params=pltpu.CompilerParams(
            dimension_semantics=("arbitrary",), vmem_limit_bytes=48 * 1024 * 1024
        ),
        cost_estimate=pl.CostEstimate(
            flops=2 * 16 * rows * 2 * count_dirs * num_freqs + 60 * rows * count_dirs * num_freqs,
            transcendentals=0,
            bytes_accessed=2 * rows * 2 * count_dirs * num_freqs,
        ),
    )(wavenumbers, points, dirs_block, compact)


def adjoint_kernel(w_ref, cs_ref, out_ref):
    for level in range(cs_ref.shape[0]):
        out_ref[level] = lax.dot_general(
            w_ref[level], cs_ref[level], (((1,), (1,)), ((), ())), preferred_element_type=jnp.float32
        )


def adjoint_products(weights, kernel_all):
    num_freqs, rows, width = kernel_all.shape
    return pl.pallas_call(
        adjoint_kernel,
        grid=(rows // ROW_BLOCK,),
        in_specs=[
            pl.BlockSpec(weights.shape, lambda b: (0, 0, 0)),
            pl.BlockSpec((num_freqs, ROW_BLOCK, width), lambda b: (0, b, 0)),
        ],
        out_specs=pl.BlockSpec((num_freqs, weights.shape[1], ROW_BLOCK), lambda b: (0, 0, b)),
        out_shape=jax.ShapeDtypeStruct((num_freqs, weights.shape[1], rows), jnp.float32),
        compiler_params=pltpu.CompilerParams(
            dimension_semantics=("arbitrary",), vmem_limit_bytes=48 * 1024 * 1024
        ),
        cost_estimate=pl.CostEstimate(
            flops=2 * weights.shape[1] * rows * width * num_freqs,
            transcendentals=0,
            bytes_accessed=2 * rows * width * num_freqs,
        ),
    )(weights, kernel_all)


def split_bf16(values):
    high = lax.reduce_precision(values, exponent_bits=8, mantissa_bits=7)
    rest = values - high
    middle = lax.reduce_precision(rest, exponent_bits=8, mantissa_bits=7)
    low = rest - middle
    return jnp.concatenate([high, middle, low], axis=0).astype(jnp.bfloat16)


def join_parts(product, channels):
    return (product[:channels] + product[channels : 2 * channels]) + product[2 * channels :]


def permute_columns(values, selector):
    product = jnp.dot(split_bf16(values), selector, preferred_element_type=jnp.float32)
    return join_parts(product, values.shape[0])


def unpermute_columns(values, selector):
    product = lax.dot_general(
        split_bf16(values), selector, (((1,), (1,)), ((), ())), preferred_element_type=jnp.float32
    )
    return join_parts(product, values.shape[0])


MESH_IDS = pl.DeviceIdType.MESH


def reduce_kernel(nx, ny, x_ref, out_ref, part_a, part_b, got_a, got_b, sems):
    b0 = lax.axis_index("gx")
    a0 = lax.axis_index("gy")
    barrier = pltpu.get_barrier_semaphore()
    for t in range(1, ny):
        pl.semaphore_signal(barrier, inc=1, device_id=(b0, lax.rem(a0 + t, ny)), device_id_type=MESH_IDS)
    for t in range(1, nx):
        pl.semaphore_signal(barrier, inc=1, device_id=(lax.rem(b0 + t, nx), a0), device_id_type=MESH_IDS)
    pl.semaphore_wait(barrier, nx + ny - 2)

    def exchange(phase, src_of, dst_of, peers, along_x):
        copies = []
        for t in range(1, peers):
            if along_x:
                peer = lax.rem(b0 + t, nx)
                me, device = b0, (peer, a0)
            else:
                peer = lax.rem(a0 + t, ny)
                me, device = a0, (b0, peer)
            copy = pltpu.make_async_remote_copy(
                src_ref=src_of(peer),
                dst_ref=dst_of(me),
                send_sem=sems.at[phase, 0, peer],
                recv_sem=sems.at[phase, 1, me],
                device_id=device,
                device_id_type=MESH_IDS,
            )
            copy.start()
            copies.append((peer, device))
        for peer, device in copies:
            pltpu.make_async_remote_copy(
                src_ref=src_of(peer),
                dst_ref=dst_of(peer),
                send_sem=sems.at[phase, 0, peer],
                recv_sem=sems.at[phase, 1, peer],
                device_id=device,
                device_id_type=MESH_IDS,
            ).wait()

    exchange(0, lambda a: x_ref.at[a], lambda a: got_a.at[a], ny, False)
    got_a[a0] = x_ref[a0]
    part_a[...] = jnp.sum(got_a[...], axis=0)
    exchange(1, lambda b: part_a, lambda b: got_b.at[b], nx, True)
    got_b[b0] = part_a[...]
    part_b[...] = jnp.sum(got_b[...], axis=0)
    exchange(2, lambda a: part_b, lambda a: out_ref.at[a], ny, False)
    out_ref[a0] = part_b[...]


def sum_over_devices(partial, owners):
    nx = lax.axis_size("gx")
    ny = lax.axis_size("gy")
    lanes = partial.size // (nx * ny)
    shaped = partial.reshape(ny, nx, lanes)
    peers = max(nx, ny)
    total = pl.pallas_call(
        functools.partial(reduce_kernel, nx, ny),
        in_specs=[pl.BlockSpec(memory_space=pltpu.VMEM)],
        out_specs=pl.BlockSpec(memory_space=pltpu.VMEM),
        out_shape=jax.ShapeDtypeStruct(shaped.shape, jnp.float32),
        scratch_shapes=[
            pltpu.VMEM((nx, lanes), jnp.float32),
            pltpu.VMEM((nx, lanes), jnp.float32),
            pltpu.VMEM((ny, nx, lanes), jnp.float32),
            pltpu.VMEM((nx, nx, lanes), jnp.float32),
            pltpu.SemaphoreType.DMA((3, 2, peers)),
        ],
        compiler_params=pltpu.CompilerParams(collective_id=0, has_side_effects=True),
    )(shaped)
    return total.reshape(partial.shape)


def sum_over_devices_a2a(partial, owners):
    chunks = partial.reshape(owners, -1)
    got = lax.all_to_all(chunks, ("gx", "gy"), split_axis=0, concat_axis=0, tiled=True)
    mine = jnp.sum(got, axis=0, keepdims=True)
    spread = jnp.broadcast_to(mine, chunks.shape)
    full = lax.all_to_all(spread, ("gx", "gy"), split_axis=0, concat_axis=0, tiled=True)
    return full.reshape(partial.shape)


def on_device(cell_state, geometry, surface_cell, counts, wavenumbers, target, direction_weight):
    owners = lax.axis_size(("gx", "gy"))
    rows_dev = surface_cell.shape[0]
    capacity = rows_dev // owners
    live_own = rows_dev // 4
    count_dirs = target.shape[2]
    num_freqs = wavenumbers.shape[0]
    living = (jnp.arange(rows_dev) < counts[0]).astype(jnp.float32)
    outgoing = (
        jnp.concatenate(
            [cell_state[:, surface_cell], geometry, jnp.ones((1, rows_dev), jnp.float32)], axis=0
        )
        * living[None, :]
    )
    outgoing = outgoing.reshape(24, capacity, owners)
    arrived = lax.all_to_all(outgoing, ("gx", "gy"), split_axis=2, concat_axis=2, tiled=True)
    marker = arrived[23]
    per_source = jnp.sum(marker, axis=0).astype(jnp.int32)
    offset = jnp.cumsum(per_source) - per_source
    position = offset[None, :] + jnp.arange(capacity, dtype=jnp.int32)[:, None]
    packed_slot = jnp.where(marker > 0.5, position, live_own).reshape(capacity * owners)
    selector = (packed_slot[:, None] == jnp.arange(live_own, dtype=jnp.int32)[None, :]).astype(jnp.bfloat16)
    compact = permute_columns(arrived[:23].reshape(23, capacity * owners), selector)
    east_x, north_y, upward = directions(count_dirs)
    direction_basis = jnp.stack([jnp.ones_like(east_x), east_x, north_y, upward])

    points = compact[16:19].T
    dirs_block = jnp.broadcast_to(jnp.stack([east_x, north_y, upward])[:, None, :], (3, ROW_CHUNK, count_dirs))
    kernel_all, sums = forward_sums(wavenumbers, points, dirs_block, compact)
    sums = sums[:, :8]
    far_field = sum_over_devices(far_field_of(sums, wavenumbers, direction_basis), owners)
    objective, weights = adjoint_weights(
        far_field, target, direction_weight, wavenumbers, direction_basis
    )

    padded = jnp.concatenate([weights, jnp.zeros_like(weights)], axis=1)
    products = adjoint_products(padded, kernel_all)[:, :8]
    backward = adjoint_sources(products, compact[19:22])
    spread = unpermute_columns(backward, selector)
    spread = spread.reshape(16, capacity, owners)
    returned = lax.all_to_all(spread, ("gx", "gy"), split_axis=2, concat_axis=2, tiled=True)
    per_row = returned.reshape(16, rows_dev) * living[None, :]
    cell_adjoint = jnp.zeros(cell_state.shape, jnp.float32).at[:, surface_cell].add(per_row)
    return (far_field, objective, cell_adjoint)


def solution(mesh):
    placed = (
        P(None, ("gx", "gy")),
        P(None, ("gx", "gy")),
        P(("gx", "gy")),
        P(("gx", "gy")),
        P(),
        P(),
        P(),
    )
    return jax.shard_map(
        on_device,
        mesh=mesh,
        in_specs=placed,
        out_specs=(P(), P(), P(None, ("gx", "gy"))),
        check_vma=False,
    )
```

```python
import functools
import math

import jax
import jax.numpy as jnp
from jax import lax
from jax.experimental import pallas as pl
from jax.experimental.pallas import tpu as pltpu
from jax.sharding import PartitionSpec as P

GOLDEN = math.pi * (3.0 - math.sqrt(5.0))
PI_A = round(math.pi * 32768.0) / 32768.0
PI_B = math.pi - PI_A
INV_PI = 1.0 / math.pi
SIN_C = [-0.16666657019913644, 0.00833301540393062, -0.00019806478078586938, 2.599750005030262e-06]
COS_C = [-0.4999993175258851, 0.041663973510963626, -0.0013855797199316853, 2.3191254010748703e-05]
SINPI_C = [3.141592578574041, -5.1677067848796066, 2.5500297991194887, -0.5980355679943354, 0.07720094563063706]
COSPI_C = [-4.934795411606951, 4.05844824012755, -1.332068921858188, 0.22002136541700046]


def sincos_turns(u):
    n = jnp.floor(u + 0.5)
    w = u - n
    z = w * w
    ps = SINPI_C[-1]
    for c in SINPI_C[-2::-1]:
        ps = c + z * ps
    pc = COSPI_C[-1]
    for c in COSPI_C[-2::-1]:
        pc = c + z * pc
    half = n * 0.5
    sign = 1.0 - 4.0 * (half - jnp.floor(half))
    return (sign * (1.0 + z * pc), (sign * w) * ps)


def sincos(theta):
    n = jnp.floor(theta * INV_PI + 0.5)
    r = (theta - n * PI_A) - n * PI_B
    z = r * r
    ps = SIN_C[-1]
    for c in SIN_C[-2::-1]:
        ps = c + z * ps
    pc = COS_C[-1]
    for c in COS_C[-2::-1]:
        pc = c + z * pc
    half = n * 0.5
    sign = 1.0 - 4.0 * (half - jnp.floor(half))
    return (sign * (1.0 + z * pc), sign * (r + (r * z) * ps))


def directions(count_dirs):
    lattice = jnp.arange(count_dirs).astype(jnp.float32)
    height = 1.0 - (2.0 * lattice + 1.0) / count_dirs
    radius_xy = jnp.sqrt(1.0 - height * height)
    azimuth = jnp.mod(lattice * GOLDEN, 2.0 * math.pi)
    return (radius_xy * jnp.cos(azimuth), radius_xy * jnp.sin(azimuth), height)


def kernel_block(points, wavenum, east_x, north_y, upward):
    phases = wavenum * (
        points[0][:, None] * east_x[None, :]
        + points[1][:, None] * north_y[None, :]
        + points[2][:, None] * upward[None, :]
    )
    cosine, sine = sincos(phases)
    return jnp.concatenate([cosine, sine], axis=1).astype(jnp.bfloat16)


def source_rows(rows_block, level):
    surface_area = rows_block[22]
    normal = rows_block[19:22]
    pressure_real = rows_block[level] * surface_area
    pressure_imag = rows_block[4 + level] * surface_area
    return jnp.stack(
        [
            rows_block[8 + level] * surface_area,
            normal[0] * pressure_real,
            normal[1] * pressure_real,
            normal[2] * pressure_real,
            rows_block[12 + level] * surface_area,
            normal[0] * pressure_imag,
            normal[1] * pressure_imag,
            normal[2] * pressure_imag,
        ]
    ).astype(jnp.bfloat16)


def far_field_of(sums, wavenumbers, direction_basis):
    half_width = sums.shape[2] // 2
    cosine_part = sums[:, :, :half_width]
    sine_part = sums[:, :, half_width:]
    real_q = cosine_part[:, 0:4] + sine_part[:, 4:8]
    imag_q = cosine_part[:, 4:8] - sine_part[:, 0:4]
    real_z = jnp.sum(direction_basis[None] * real_q, axis=1)
    imag_z = jnp.sum(direction_basis[None] * imag_q, axis=1)
    wavenum = wavenumbers[:, None]
    return jnp.stack([-wavenum * imag_z, wavenum * real_z], axis=1)


def adjoint_weights(far_field, target, direction_weight, wavenumbers, direction_basis):
    count_dirs = far_field.shape[2]
    mismatch = far_field - target
    objective = jnp.sum(direction_weight * mismatch * mismatch) / count_dirs
    gradient = 2.0 * direction_weight * mismatch / count_dirs
    wavenum = wavenumbers[:, None]
    real_gz = wavenum * gradient[:, 1]
    imag_gz = -wavenum * gradient[:, 0]
    real_gq = direction_basis[None] * real_gz[:, None]
    imag_gq = direction_basis[None] * imag_gz[:, None]
    upper_half = jnp.concatenate([real_gq, -imag_gq], axis=2)
    lower_half = jnp.concatenate([imag_gq, real_gq], axis=2)
    return (objective, jnp.concatenate([upper_half, lower_half], axis=1).astype(jnp.bfloat16))


def adjoint_sources(products, normal):
    pressure_real = jnp.sum(normal[None] * products[:, 1:4], axis=1)
    pressure_imag = jnp.sum(normal[None] * products[:, 5:8], axis=1)
    return jnp.concatenate([pressure_real, pressure_imag, products[:, 0], products[:, 4]], axis=0)


ROW_BLOCK = 256
ROW_CHUNK = 16
LANE_CHUNK = 256


def forward_kernel(wave_ref, pts_ref, dirs_ref, rows_ref, cs_ref, q_ref, src_scr):
    step = pl.program_id(0)
    num_freqs = cs_ref.shape[0]
    count_dirs = dirs_ref.shape[2]
    turns = [wave_ref[level] * INV_PI for level in range(num_freqs)]

    @pl.loop(0, ROW_BLOCK // ROW_CHUNK)
    def _(i):
        r0 = pl.multiple_of(i * ROW_CHUNK, ROW_CHUNK)
        coords = [
            jnp.broadcast_to(pts_ref[pl.ds(r0, ROW_CHUNK), c : c + 1], (ROW_CHUNK, LANE_CHUNK))
            for c in range(3)
        ]
        for j0 in range(0, count_dirs, LANE_CHUNK):
            lanes = slice(j0, j0 + LANE_CHUNK)
            along = (
                coords[0] * dirs_ref[0, :, lanes]
                + coords[1] * dirs_ref[1, :, lanes]
                + coords[2] * dirs_ref[2, :, lanes]
            )
            for level in range(num_freqs):
                cosine, sine = sincos_turns(turns[level] * along)
                cs_ref[level, pl.ds(r0, ROW_CHUNK), lanes] = cosine.astype(jnp.bfloat16)
                cs_ref[level, pl.ds(r0, ROW_CHUNK), j0 + count_dirs : j0 + count_dirs + LANE_CHUNK] = (
                    sine.astype(jnp.bfloat16)
                )

    @pl.when(step == 0)
    def _():
        q_ref[...] = jnp.zeros_like(q_ref)

    area = rows_ref[22:23, :]
    src_scr[...] = jnp.zeros_like(src_scr)
    for level in range(num_freqs):
        pressure_real = rows_ref[level : level + 1, :] * area
        pressure_imag = rows_ref[4 + level : 5 + level, :] * area
        src_scr[0:1, :] = rows_ref[8 + level : 9 + level, :] * area
        src_scr[4:5, :] = rows_ref[12 + level : 13 + level, :] * area
        for c in range(3):
            normal = rows_ref[19 + c : 20 + c, :]
            src_scr[1 + c : 2 + c, :] = normal * pressure_real
            src_scr[5 + c : 6 + c, :] = normal * pressure_imag
        source = src_scr[...].astype(jnp.bfloat16)
        q_ref[level] += jnp.dot(source, cs_ref[level], preferred_element_type=jnp.float32)


def forward_sums(wavenumbers, points, dirs_block, compact):
    num_freqs = wavenumbers.shape[0]
    rows = points.shape[0]
    count_dirs = dirs_block.shape[2]
    grid = (rows // ROW_BLOCK,)
    return pl.pallas_call(
        forward_kernel,
        grid=grid,
        in_specs=[
            pl.BlockSpec(memory_space=pltpu.SMEM),
            pl.BlockSpec((ROW_BLOCK, 3), lambda b: (b, 0)),
            pl.BlockSpec(dirs_block.shape, lambda b: (0, 0, 0)),
            pl.BlockSpec((compact.shape[0], ROW_BLOCK), lambda b: (0, b)),
        ],
        out_specs=[
            pl.BlockSpec((num_freqs, ROW_BLOCK, 2 * count_dirs), lambda b: (0, b, 0)),
            pl.BlockSpec((num_freqs, 16, 2 * count_dirs), lambda b: (0, 0, 0)),
        ],
        out_shape=[
            jax.ShapeDtypeStruct((num_freqs, rows, 2 * count_dirs), jnp.bfloat16),
            jax.ShapeDtypeStruct((num_freqs, 16, 2 * count_dirs), jnp.float32),
        ],
        scratch_shapes=[pltpu.VMEM((16, ROW_BLOCK), jnp.float32)],
        compiler_params=pltpu.CompilerParams(
            dimension_semantics=("arbitrary",), vmem_limit_bytes=48 * 1024 * 1024
        ),
        cost_estimate=pl.CostEstimate(
            flops=2 * 16 * rows * 2 * count_dirs * num_freqs + 60 * rows * count_dirs * num_freqs,
            transcendentals=0,
            bytes_accessed=2 * rows * 2 * count_dirs * num_freqs,
        ),
    )(wavenumbers, points, dirs_block, compact)


def adjoint_kernel(w_ref, cs_ref, out_ref):
    for level in range(cs_ref.shape[0]):
        out_ref[level] = lax.dot_general(
            w_ref[level], cs_ref[level], (((1,), (1,)), ((), ())), preferred_element_type=jnp.float32
        )


def adjoint_products(weights, kernel_all):
    num_freqs, rows, width = kernel_all.shape
    return pl.pallas_call(
        adjoint_kernel,
        grid=(rows // ROW_BLOCK,),
        in_specs=[
            pl.BlockSpec(weights.shape, lambda b: (0, 0, 0)),
            pl.BlockSpec((num_freqs, ROW_BLOCK, width), lambda b: (0, b, 0)),
        ],
        out_specs=pl.BlockSpec((num_freqs, weights.shape[1], ROW_BLOCK), lambda b: (0, 0, b)),
        out_shape=jax.ShapeDtypeStruct((num_freqs, weights.shape[1], rows), jnp.float32),
        compiler_params=pltpu.CompilerParams(
            dimension_semantics=("arbitrary",), vmem_limit_bytes=48 * 1024 * 1024
        ),
        cost_estimate=pl.CostEstimate(
            flops=2 * weights.shape[1] * rows * width * num_freqs,
            transcendentals=0,
            bytes_accessed=2 * rows * width * num_freqs,
        ),
    )(weights, kernel_all)


def split_bf16(values):
    high = lax.reduce_precision(values, exponent_bits=8, mantissa_bits=7)
    rest = values - high
    middle = lax.reduce_precision(rest, exponent_bits=8, mantissa_bits=7)
    low = rest - middle
    return jnp.concatenate([high, middle, low], axis=0).astype(jnp.bfloat16)


def join_parts(product, channels):
    return (product[:channels] + product[channels : 2 * channels]) + product[2 * channels :]


def permute_columns(values, selector):
    product = jnp.dot(split_bf16(values), selector, preferred_element_type=jnp.float32)
    return join_parts(product, values.shape[0])


def unpermute_columns(values, selector):
    product = lax.dot_general(
        split_bf16(values), selector, (((1,), (1,)), ((), ())), preferred_element_type=jnp.float32
    )
    return join_parts(product, values.shape[0])


MESH_IDS = pl.DeviceIdType.MESH


def reduce_kernel(nx, ny, x_ref, out_ref, part_a, part_b, got_a, got_b, sems):
    b0 = lax.axis_index("gx")
    a0 = lax.axis_index("gy")
    barrier = pltpu.get_barrier_semaphore()
    for t in range(1, ny):
        pl.semaphore_signal(barrier, inc=1, device_id=(b0, lax.rem(a0 + t, ny)), device_id_type=MESH_IDS)
    for t in range(1, nx):
        pl.semaphore_signal(barrier, inc=1, device_id=(lax.rem(b0 + t, nx), a0), device_id_type=MESH_IDS)
    pl.semaphore_wait(barrier, nx + ny - 2)

    def exchange(phase, src_of, dst_of, peers, along_x):
        copies = []
        for t in range(1, peers):
            if along_x:
                peer = lax.rem(b0 + t, nx)
                me, device = b0, (peer, a0)
            else:
                peer = lax.rem(a0 + t, ny)
                me, device = a0, (b0, peer)
            copy = pltpu.make_async_remote_copy(
                src_ref=src_of(peer),
                dst_ref=dst_of(me),
                send_sem=sems.at[phase, 0, peer],
                recv_sem=sems.at[phase, 1, me],
                device_id=device,
                device_id_type=MESH_IDS,
            )
            copy.start()
            copies.append((peer, device))
        for peer, device in copies:
            pltpu.make_async_remote_copy(
                src_ref=src_of(peer),
                dst_ref=dst_of(peer),
                send_sem=sems.at[phase, 0, peer],
                recv_sem=sems.at[phase, 1, peer],
                device_id=device,
                device_id_type=MESH_IDS,
            ).wait()

    exchange(0, lambda a: x_ref.at[a], lambda a: got_a.at[a], ny, False)
    got_a[a0] = x_ref[a0]
    part_a[...] = jnp.sum(got_a[...], axis=0)
    exchange(1, lambda b: part_a, lambda b: got_b.at[b], nx, True)
    got_b[b0] = part_a[...]
    part_b[...] = jnp.sum(got_b[...], axis=0)
    exchange(2, lambda a: part_b, lambda a: out_ref.at[a], ny, False)
    out_ref[a0] = part_b[...]


def exchange_kernel(nx, ny, x_ref, out_ref, landing, send_sems, recv_sems):
    total = nx * ny
    me = lax.axis_index("gx") * ny + lax.axis_index("gy")
    barrier = pltpu.get_barrier_semaphore()

    def where(peer):
        return (peer // ny, lax.rem(peer, ny))

    @pl.loop(1, total)
    def _(t):
        peer = lax.rem(me + t, total)
        pl.semaphore_signal(barrier, inc=1, device_id=where(peer), device_id_type=MESH_IDS)

    pl.semaphore_wait(barrier, total - 1)

    @pl.loop(1, total)
    def _(t):
        peer = lax.rem(me + t, total)
        pltpu.make_async_remote_copy(
            src_ref=x_ref.at[peer],
            dst_ref=landing.at[me],
            send_sem=send_sems.at[peer],
            recv_sem=recv_sems.at[me],
            device_id=where(peer),
            device_id_type=MESH_IDS,
        ).start()

    landing[me] = x_ref[me]

    @pl.loop(1, total)
    def _(t):
        peer = lax.rem(me + t, total)
        pltpu.make_async_remote_copy(
            src_ref=x_ref.at[peer],
            dst_ref=landing.at[peer],
            send_sem=send_sems.at[peer],
            recv_sem=recv_sems.at[peer],
            device_id=where(peer),
            device_id_type=MESH_IDS,
        ).wait()

    out_ref[...] = landing[...]


def exchange(blocks, exchange_id):
    nx = lax.axis_size("gx")
    ny = lax.axis_size("gy")
    return pl.pallas_call(
        functools.partial(exchange_kernel, nx, ny),
        in_specs=[pl.BlockSpec(memory_space=pltpu.VMEM)],
        out_specs=pl.BlockSpec(memory_space=pltpu.VMEM),
        out_shape=jax.ShapeDtypeStruct(blocks.shape, blocks.dtype),
        scratch_shapes=[
            pltpu.VMEM(blocks.shape, blocks.dtype),
            pltpu.SemaphoreType.DMA((nx * ny,)),
            pltpu.SemaphoreType.DMA((nx * ny,)),
        ],
        compiler_params=pltpu.CompilerParams(collective_id=exchange_id, has_side_effects=True),
    )(blocks)


def sum_over_devices(partial, owners):
    nx = lax.axis_size("gx")
    ny = lax.axis_size("gy")
    lanes = partial.size // (nx * ny)
    shaped = partial.reshape(ny, nx, lanes)
    peers = max(nx, ny)
    total = pl.pallas_call(
        functools.partial(reduce_kernel, nx, ny),
        in_specs=[pl.BlockSpec(memory_space=pltpu.VMEM)],
        out_specs=pl.BlockSpec(memory_space=pltpu.VMEM),
        out_shape=jax.ShapeDtypeStruct(shaped.shape, jnp.float32),
        scratch_shapes=[
            pltpu.VMEM((nx, lanes), jnp.float32),
            pltpu.VMEM((nx, lanes), jnp.float32),
            pltpu.VMEM((ny, nx, lanes), jnp.float32),
            pltpu.VMEM((nx, nx, lanes), jnp.float32),
            pltpu.SemaphoreType.DMA((3, 2, peers)),
        ],
        compiler_params=pltpu.CompilerParams(collective_id=0, has_side_effects=True),
    )(shaped)
    return total.reshape(partial.shape)


def sum_over_devices_a2a(partial, owners):
    chunks = partial.reshape(owners, -1)
    got = lax.all_to_all(chunks, ("gx", "gy"), split_axis=0, concat_axis=0, tiled=True)
    mine = jnp.sum(got, axis=0, keepdims=True)
    spread = jnp.broadcast_to(mine, chunks.shape)
    full = lax.all_to_all(spread, ("gx", "gy"), split_axis=0, concat_axis=0, tiled=True)
    return full.reshape(partial.shape)


def on_device(cell_state, geometry, surface_cell, counts, wavenumbers, target, direction_weight):
    owners = lax.axis_size(("gx", "gy"))
    rows_dev = surface_cell.shape[0]
    capacity = rows_dev // owners
    live_own = rows_dev // 4
    count_dirs = target.shape[2]
    num_freqs = wavenumbers.shape[0]
    living = (jnp.arange(rows_dev) < counts[0]).astype(jnp.float32)
    outgoing = (
        jnp.concatenate(
            [cell_state[:, surface_cell], geometry, jnp.ones((1, rows_dev), jnp.float32)], axis=0
        )
        * living[None, :]
    )
    outgoing = outgoing.reshape(24, capacity, owners).transpose(2, 0, 1).reshape(owners, -1, 128)
    arrived = exchange(outgoing, 1).reshape(owners, 24, capacity).transpose(1, 0, 2)
    marker = arrived[23]
    per_source = jnp.sum(marker, axis=1).astype(jnp.int32)
    offset = jnp.cumsum(per_source) - per_source
    position = offset[:, None] + jnp.arange(capacity, dtype=jnp.int32)[None, :]
    packed_slot = jnp.where(marker > 0.5, position, live_own).reshape(capacity * owners)
    selector = (packed_slot[:, None] == jnp.arange(live_own, dtype=jnp.int32)[None, :]).astype(jnp.bfloat16)
    compact = permute_columns(arrived[:23].reshape(23, capacity * owners), selector)
    east_x, north_y, upward = directions(count_dirs)
    direction_basis = jnp.stack([jnp.ones_like(east_x), east_x, north_y, upward])

    points = compact[16:19].T
    dirs_block = jnp.broadcast_to(jnp.stack([east_x, north_y, upward])[:, None, :], (3, ROW_CHUNK, count_dirs))
    kernel_all, sums = forward_sums(wavenumbers, points, dirs_block, compact)
    sums = sums[:, :8]
    far_field = sum_over_devices(far_field_of(sums, wavenumbers, direction_basis), owners)
    objective, weights = adjoint_weights(
        far_field, target, direction_weight, wavenumbers, direction_basis
    )

    padded = jnp.concatenate([weights, jnp.zeros_like(weights)], axis=1)
    products = adjoint_products(padded, kernel_all)[:, :8]
    backward = adjoint_sources(products, compact[19:22])
    spread = unpermute_columns(backward, selector)
    spread = spread.reshape(16, owners, capacity).transpose(1, 0, 2).reshape(owners, -1, 128)
    returned = exchange(spread, 2).reshape(owners, 16, capacity).transpose(1, 2, 0)
    per_row = returned.reshape(16, rows_dev) * living[None, :]
    cell_adjoint = jnp.zeros(cell_state.shape, jnp.float32).at[:, surface_cell].add(per_row)
    return (far_field, objective, cell_adjoint)


def solution(mesh):
    placed = (
        P(None, ("gx", "gy")),
        P(None, ("gx", "gy")),
        P(("gx", "gy")),
        P(("gx", "gy")),
        P(),
        P(),
        P(),
    )
    return jax.shard_map(
        on_device,
        mesh=mesh,
        in_specs=placed,
        out_specs=(P(), P(), P(None, ("gx", "gy"))),
        check_vma=False,
    )
```

```python
import functools
import math

import jax
import jax.numpy as jnp
from jax import lax
from jax.experimental import pallas as pl
from jax.experimental.pallas import tpu as pltpu
from jax.sharding import PartitionSpec as P

GOLDEN = math.pi * (3.0 - math.sqrt(5.0))
PI_A = round(math.pi * 32768.0) / 32768.0
PI_B = math.pi - PI_A
INV_PI = 1.0 / math.pi
SIN_C = [-0.16666657019913644, 0.00833301540393062, -0.00019806478078586938, 2.599750005030262e-06]
COS_C = [-0.4999993175258851, 0.041663973510963626, -0.0013855797199316853, 2.3191254010748703e-05]
SINPI_C = [3.141592578574041, -5.1677067848796066, 2.5500297991194887, -0.5980355679943354, 0.07720094563063706]
COSPI_C = [-4.934795411606951, 4.05844824012755, -1.332068921858188, 0.22002136541700046]


ROOT2 = math.sqrt(2.0)


def sincos_half_turns(v):
    w = v - jnp.floor(v + 0.5)
    z = w * w
    ps = SINPI_C[-1] * ROOT2
    for c in SINPI_C[-2::-1]:
        ps = c * ROOT2 + z * ps
    pc = COSPI_C[-1] * ROOT2
    for c in COSPI_C[-2::-1]:
        pc = c * ROOT2 + z * pc
    sine_half = w * ps
    cosine_half = ROOT2 + z * pc
    return (cosine_half * cosine_half - 1.0, sine_half * cosine_half)


def sincos_turns(u):
    n = jnp.floor(u + 0.5)
    w = u - n
    z = w * w
    ps = SINPI_C[-1]
    for c in SINPI_C[-2::-1]:
        ps = c + z * ps
    pc = COSPI_C[-1]
    for c in COSPI_C[-2::-1]:
        pc = c + z * pc
    half = n * 0.5
    sign = 1.0 - 4.0 * (half - jnp.floor(half))
    return (sign * (1.0 + z * pc), (sign * w) * ps)


def sincos(theta):
    n = jnp.floor(theta * INV_PI + 0.5)
    r = (theta - n * PI_A) - n * PI_B
    z = r * r
    ps = SIN_C[-1]
    for c in SIN_C[-2::-1]:
        ps = c + z * ps
    pc = COS_C[-1]
    for c in COS_C[-2::-1]:
        pc = c + z * pc
    half = n * 0.5
    sign = 1.0 - 4.0 * (half - jnp.floor(half))
    return (sign * (1.0 + z * pc), sign * (r + (r * z) * ps))


def directions(count_dirs):
    lattice = jnp.arange(count_dirs).astype(jnp.float32)
    height = 1.0 - (2.0 * lattice + 1.0) / count_dirs
    radius_xy = jnp.sqrt(1.0 - height * height)
    azimuth = jnp.mod(lattice * GOLDEN, 2.0 * math.pi)
    return (radius_xy * jnp.cos(azimuth), radius_xy * jnp.sin(azimuth), height)


def kernel_block(points, wavenum, east_x, north_y, upward):
    phases = wavenum * (
        points[0][:, None] * east_x[None, :]
        + points[1][:, None] * north_y[None, :]
        + points[2][:, None] * upward[None, :]
    )
    cosine, sine = sincos(phases)
    return jnp.concatenate([cosine, sine], axis=1).astype(jnp.bfloat16)


def source_rows(rows_block, level):
    surface_area = rows_block[22]
    normal = rows_block[19:22]
    pressure_real = rows_block[level] * surface_area
    pressure_imag = rows_block[4 + level] * surface_area
    return jnp.stack(
        [
            rows_block[8 + level] * surface_area,
            normal[0] * pressure_real,
            normal[1] * pressure_real,
            normal[2] * pressure_real,
            rows_block[12 + level] * surface_area,
            normal[0] * pressure_imag,
            normal[1] * pressure_imag,
            normal[2] * pressure_imag,
        ]
    ).astype(jnp.bfloat16)


def far_field_of(sums, wavenumbers, direction_basis):
    half_width = sums.shape[2] // 2
    cosine_part = sums[:, :, :half_width]
    sine_part = sums[:, :, half_width:]
    real_q = cosine_part[:, 0:4] + sine_part[:, 4:8]
    imag_q = cosine_part[:, 4:8] - sine_part[:, 0:4]
    real_z = jnp.sum(direction_basis[None] * real_q, axis=1)
    imag_z = jnp.sum(direction_basis[None] * imag_q, axis=1)
    wavenum = wavenumbers[:, None]
    return jnp.stack([-wavenum * imag_z, wavenum * real_z], axis=1)


def adjoint_weights(far_field, target, direction_weight, wavenumbers, direction_basis):
    count_dirs = far_field.shape[2]
    mismatch = far_field - target
    objective = jnp.sum(direction_weight * mismatch * mismatch) / count_dirs
    gradient = 2.0 * direction_weight * mismatch / count_dirs
    wavenum = wavenumbers[:, None]
    real_gz = wavenum * gradient[:, 1]
    imag_gz = -wavenum * gradient[:, 0]
    real_gq = direction_basis[None] * real_gz[:, None]
    imag_gq = direction_basis[None] * imag_gz[:, None]
    upper_half = jnp.concatenate([real_gq, -imag_gq], axis=2)
    lower_half = jnp.concatenate([imag_gq, real_gq], axis=2)
    return (objective, jnp.concatenate([upper_half, lower_half], axis=1).astype(jnp.bfloat16))


def adjoint_sources(products, normal):
    pressure_real = jnp.sum(normal[None] * products[:, 1:4], axis=1)
    pressure_imag = jnp.sum(normal[None] * products[:, 5:8], axis=1)
    return jnp.concatenate([pressure_real, pressure_imag, products[:, 0], products[:, 4]], axis=0)


ROW_BLOCK = 256
ROW_CHUNK = 16
LANE_CHUNK = 256


def forward_kernel(wave_ref, pts_ref, dirs_ref, rows_ref, cs_ref, q_ref, src_scr):
    step = pl.program_id(0)
    num_freqs = cs_ref.shape[0]
    count_dirs = dirs_ref.shape[2]
    turns = [wave_ref[level] * (0.5 * INV_PI) for level in range(num_freqs)]

    @pl.loop(0, ROW_BLOCK // ROW_CHUNK)
    def _(i):
        r0 = pl.multiple_of(i * ROW_CHUNK, ROW_CHUNK)
        coords = [
            jnp.broadcast_to(pts_ref[pl.ds(r0, ROW_CHUNK), c : c + 1], (ROW_CHUNK, LANE_CHUNK))
            for c in range(3)
        ]
        for j0 in range(0, count_dirs, LANE_CHUNK):
            lanes = slice(j0, j0 + LANE_CHUNK)
            along = (
                coords[0] * dirs_ref[0, :, lanes]
                + coords[1] * dirs_ref[1, :, lanes]
                + coords[2] * dirs_ref[2, :, lanes]
            )
            for level in range(num_freqs):
                cosine, sine = sincos_half_turns(turns[level] * along)
                cs_ref[level, pl.ds(r0, ROW_CHUNK), lanes] = cosine.astype(jnp.bfloat16)
                cs_ref[level, pl.ds(r0, ROW_CHUNK), j0 + count_dirs : j0 + count_dirs + LANE_CHUNK] = (
                    sine.astype(jnp.bfloat16)
                )

    @pl.when(step == 0)
    def _():
        q_ref[...] = jnp.zeros_like(q_ref)

    area = rows_ref[22:23, :]
    src_scr[...] = jnp.zeros_like(src_scr)
    for level in range(num_freqs):
        pressure_real = rows_ref[level : level + 1, :] * area
        pressure_imag = rows_ref[4 + level : 5 + level, :] * area
        src_scr[0:1, :] = rows_ref[8 + level : 9 + level, :] * area
        src_scr[4:5, :] = rows_ref[12 + level : 13 + level, :] * area
        for c in range(3):
            normal = rows_ref[19 + c : 20 + c, :]
            src_scr[1 + c : 2 + c, :] = normal * pressure_real
            src_scr[5 + c : 6 + c, :] = normal * pressure_imag
        source = src_scr[...].astype(jnp.bfloat16)
        q_ref[level] += jnp.dot(source, cs_ref[level], preferred_element_type=jnp.float32)


def forward_sums(wavenumbers, points, dirs_block, compact):
    num_freqs = wavenumbers.shape[0]
    rows = points.shape[0]
    count_dirs = dirs_block.shape[2]
    grid = (rows // ROW_BLOCK,)
    return pl.pallas_call(
        forward_kernel,
        grid=grid,
        in_specs=[
            pl.BlockSpec(memory_space=pltpu.SMEM),
            pl.BlockSpec((ROW_BLOCK, 3), lambda b: (b, 0)),
            pl.BlockSpec(dirs_block.shape, lambda b: (0, 0, 0)),
            pl.BlockSpec((compact.shape[0], ROW_BLOCK), lambda b: (0, b)),
        ],
        out_specs=[
            pl.BlockSpec((num_freqs, ROW_BLOCK, 2 * count_dirs), lambda b: (0, b, 0)),
            pl.BlockSpec((num_freqs, 16, 2 * count_dirs), lambda b: (0, 0, 0)),
        ],
        out_shape=[
            jax.ShapeDtypeStruct((num_freqs, rows, 2 * count_dirs), jnp.bfloat16),
            jax.ShapeDtypeStruct((num_freqs, 16, 2 * count_dirs), jnp.float32),
        ],
        scratch_shapes=[pltpu.VMEM((16, ROW_BLOCK), jnp.float32)],
        compiler_params=pltpu.CompilerParams(
            dimension_semantics=("arbitrary",), vmem_limit_bytes=48 * 1024 * 1024
        ),
        cost_estimate=pl.CostEstimate(
            flops=2 * 16 * rows * 2 * count_dirs * num_freqs + 60 * rows * count_dirs * num_freqs,
            transcendentals=0,
            bytes_accessed=2 * rows * 2 * count_dirs * num_freqs,
        ),
    )(wavenumbers, points, dirs_block, compact)


def adjoint_kernel(w_ref, cs_ref, out_ref):
    for level in range(cs_ref.shape[0]):
        out_ref[level] = lax.dot_general(
            w_ref[level], cs_ref[level], (((1,), (1,)), ((), ())), preferred_element_type=jnp.float32
        )


def adjoint_products(weights, kernel_all):
    num_freqs, rows, width = kernel_all.shape
    return pl.pallas_call(
        adjoint_kernel,
        grid=(rows // ROW_BLOCK,),
        in_specs=[
            pl.BlockSpec(weights.shape, lambda b: (0, 0, 0)),
            pl.BlockSpec((num_freqs, ROW_BLOCK, width), lambda b: (0, b, 0)),
        ],
        out_specs=pl.BlockSpec((num_freqs, weights.shape[1], ROW_BLOCK), lambda b: (0, 0, b)),
        out_shape=jax.ShapeDtypeStruct((num_freqs, weights.shape[1], rows), jnp.float32),
        compiler_params=pltpu.CompilerParams(
            dimension_semantics=("arbitrary",), vmem_limit_bytes=48 * 1024 * 1024
        ),
        cost_estimate=pl.CostEstimate(
            flops=2 * weights.shape[1] * rows * width * num_freqs,
            transcendentals=0,
            bytes_accessed=2 * rows * width * num_freqs,
        ),
    )(weights, kernel_all)


def split_bf16(values):
    high = lax.reduce_precision(values, exponent_bits=8, mantissa_bits=7)
    rest = values - high
    middle = lax.reduce_precision(rest, exponent_bits=8, mantissa_bits=7)
    low = rest - middle
    return jnp.concatenate([high, middle, low], axis=0).astype(jnp.bfloat16)


def join_parts(product, channels):
    return (product[:channels] + product[channels : 2 * channels]) + product[2 * channels :]


def permute_columns(values, selector):
    product = jnp.dot(split_bf16(values), selector, preferred_element_type=jnp.float32)
    return join_parts(product, values.shape[0])


def unpermute_columns(values, selector):
    product = lax.dot_general(
        split_bf16(values), selector, (((1,), (1,)), ((), ())), preferred_element_type=jnp.float32
    )
    return join_parts(product, values.shape[0])


MESH_IDS = pl.DeviceIdType.MESH


def reduce_kernel(nx, ny, x_ref, out_ref, part_a, part_b, got_a, got_b, sems):
    b0 = lax.axis_index("gx")
    a0 = lax.axis_index("gy")
    barrier = pltpu.get_barrier_semaphore()
    for t in range(1, ny):
        pl.semaphore_signal(barrier, inc=1, device_id=(b0, lax.rem(a0 + t, ny)), device_id_type=MESH_IDS)
    for t in range(1, nx):
        pl.semaphore_signal(barrier, inc=1, device_id=(lax.rem(b0 + t, nx), a0), device_id_type=MESH_IDS)
    pl.semaphore_wait(barrier, nx + ny - 2)

    def exchange(phase, src_of, dst_of, peers, along_x):
        copies = []
        for t in range(1, peers):
            if along_x:
                peer = lax.rem(b0 + t, nx)
                me, device = b0, (peer, a0)
            else:
                peer = lax.rem(a0 + t, ny)
                me, device = a0, (b0, peer)
            copy = pltpu.make_async_remote_copy(
                src_ref=src_of(peer),
                dst_ref=dst_of(me),
                send_sem=sems.at[phase, 0, peer],
                recv_sem=sems.at[phase, 1, me],
                device_id=device,
                device_id_type=MESH_IDS,
            )
            copy.start()
            copies.append((peer, device))
        for peer, device in copies:
            pltpu.make_async_remote_copy(
                src_ref=src_of(peer),
                dst_ref=dst_of(peer),
                send_sem=sems.at[phase, 0, peer],
                recv_sem=sems.at[phase, 1, peer],
                device_id=device,
                device_id_type=MESH_IDS,
            ).wait()

    exchange(0, lambda a: x_ref.at[a], lambda a: got_a.at[a], ny, False)
    got_a[a0] = x_ref[a0]
    part_a[...] = jnp.sum(got_a[...], axis=0)
    exchange(1, lambda b: part_a, lambda b: got_b.at[b], nx, True)
    got_b[b0] = part_a[...]
    part_b[...] = jnp.sum(got_b[...], axis=0)
    exchange(2, lambda a: part_b, lambda a: out_ref.at[a], ny, False)
    out_ref[a0] = part_b[...]


def exchange_kernel(nx, ny, x_ref, out_ref, landing, send_sems, recv_sems):
    total = nx * ny
    me = lax.axis_index("gx") * ny + lax.axis_index("gy")
    barrier = pltpu.get_barrier_semaphore()

    def where(peer):
        return (peer // ny, lax.rem(peer, ny))

    @pl.loop(1, total)
    def _(t):
        peer = lax.rem(me + t, total)
        pl.semaphore_signal(barrier, inc=1, device_id=where(peer), device_id_type=MESH_IDS)

    pl.semaphore_wait(barrier, total - 1)

    @pl.loop(1, total)
    def _(t):
        peer = lax.rem(me + t, total)
        pltpu.make_async_remote_copy(
            src_ref=x_ref.at[peer],
            dst_ref=landing.at[me],
            send_sem=send_sems.at[peer],
            recv_sem=recv_sems.at[me],
            device_id=where(peer),
            device_id_type=MESH_IDS,
        ).start()

    landing[me] = x_ref[me]

    @pl.loop(1, total)
    def _(t):
        peer = lax.rem(me + t, total)
        pltpu.make_async_remote_copy(
            src_ref=x_ref.at[peer],
            dst_ref=landing.at[peer],
            send_sem=send_sems.at[peer],
            recv_sem=recv_sems.at[peer],
            device_id=where(peer),
            device_id_type=MESH_IDS,
        ).wait()

    out_ref[...] = landing[...]


def exchange(blocks, exchange_id):
    nx = lax.axis_size("gx")
    ny = lax.axis_size("gy")
    return pl.pallas_call(
        functools.partial(exchange_kernel, nx, ny),
        in_specs=[pl.BlockSpec(memory_space=pltpu.VMEM)],
        out_specs=pl.BlockSpec(memory_space=pltpu.VMEM),
        out_shape=jax.ShapeDtypeStruct(blocks.shape, blocks.dtype),
        scratch_shapes=[
            pltpu.VMEM(blocks.shape, blocks.dtype),
            pltpu.SemaphoreType.DMA((nx * ny,)),
            pltpu.SemaphoreType.DMA((nx * ny,)),
        ],
        compiler_params=pltpu.CompilerParams(collective_id=exchange_id, has_side_effects=True),
    )(blocks)


def sum_over_devices(partial, owners):
    nx = lax.axis_size("gx")
    ny = lax.axis_size("gy")
    lanes = partial.size // (nx * ny)
    shaped = partial.reshape(ny, nx, lanes)
    peers = max(nx, ny)
    total = pl.pallas_call(
        functools.partial(reduce_kernel, nx, ny),
        in_specs=[pl.BlockSpec(memory_space=pltpu.VMEM)],
        out_specs=pl.BlockSpec(memory_space=pltpu.VMEM),
        out_shape=jax.ShapeDtypeStruct(shaped.shape, jnp.float32),
        scratch_shapes=[
            pltpu.VMEM((nx, lanes), jnp.float32),
            pltpu.VMEM((nx, lanes), jnp.float32),
            pltpu.VMEM((ny, nx, lanes), jnp.float32),
            pltpu.VMEM((nx, nx, lanes), jnp.float32),
            pltpu.SemaphoreType.DMA((3, 2, peers)),
        ],
        compiler_params=pltpu.CompilerParams(collective_id=0, has_side_effects=True),
    )(shaped)
    return total.reshape(partial.shape)


def sum_over_devices_a2a(partial, owners):
    chunks = partial.reshape(owners, -1)
    got = lax.all_to_all(chunks, ("gx", "gy"), split_axis=0, concat_axis=0, tiled=True)
    mine = jnp.sum(got, axis=0, keepdims=True)
    spread = jnp.broadcast_to(mine, chunks.shape)
    full = lax.all_to_all(spread, ("gx", "gy"), split_axis=0, concat_axis=0, tiled=True)
    return full.reshape(partial.shape)


def on_device(cell_state, geometry, surface_cell, counts, wavenumbers, target, direction_weight):
    owners = lax.axis_size(("gx", "gy"))
    rows_dev = surface_cell.shape[0]
    capacity = rows_dev // owners
    live_own = rows_dev // 4
    count_dirs = target.shape[2]
    num_freqs = wavenumbers.shape[0]
    living = (jnp.arange(rows_dev) < counts[0]).astype(jnp.float32)
    outgoing = (
        jnp.concatenate(
            [cell_state[:, surface_cell], geometry, jnp.ones((1, rows_dev), jnp.float32)], axis=0
        )
        * living[None, :]
    )
    outgoing = outgoing.reshape(24, capacity, owners).transpose(2, 0, 1).reshape(owners, -1, 128)
    arrived = exchange(outgoing, 1).reshape(owners, 24, capacity).transpose(1, 0, 2)
    marker = arrived[23]
    per_source = jnp.sum(marker, axis=1).astype(jnp.int32)
    offset = jnp.cumsum(per_source) - per_source
    position = offset[:, None] + jnp.arange(capacity, dtype=jnp.int32)[None, :]
    packed_slot = jnp.where(marker > 0.5, position, live_own).reshape(capacity * owners)
    selector = (packed_slot[:, None] == jnp.arange(live_own, dtype=jnp.int32)[None, :]).astype(jnp.bfloat16)
    compact = permute_columns(arrived[:23].reshape(23, capacity * owners), selector)
    east_x, north_y, upward = directions(count_dirs)
    direction_basis = jnp.stack([jnp.ones_like(east_x), east_x, north_y, upward])

    points = compact[16:19].T
    dirs_block = jnp.broadcast_to(jnp.stack([east_x, north_y, upward])[:, None, :], (3, ROW_CHUNK, count_dirs))
    kernel_all, sums = forward_sums(wavenumbers, points, dirs_block, compact)
    sums = sums[:, :8]
    far_field = sum_over_devices(far_field_of(sums, wavenumbers, direction_basis), owners)
    objective, weights = adjoint_weights(
        far_field, target, direction_weight, wavenumbers, direction_basis
    )

    padded = jnp.concatenate([weights, jnp.zeros_like(weights)], axis=1)
    products = adjoint_products(padded, kernel_all)[:, :8]
    backward = adjoint_sources(products, compact[19:22])
    spread = unpermute_columns(backward, selector)
    spread = spread.reshape(16, owners, capacity).transpose(1, 0, 2).reshape(owners, -1, 128)
    returned = exchange(spread, 2).reshape(owners, 16, capacity).transpose(1, 2, 0)
    per_row = returned.reshape(16, rows_dev) * living[None, :]
    cell_adjoint = jnp.zeros(cell_state.shape, jnp.float32).at[:, surface_cell].add(per_row)
    return (far_field, objective, cell_adjoint)


def solution(mesh):
    placed = (
        P(None, ("gx", "gy")),
        P(None, ("gx", "gy")),
        P(("gx", "gy")),
        P(("gx", "gy")),
        P(),
        P(),
        P(),
    )
    return jax.shard_map(
        on_device,
        mesh=mesh,
        in_specs=placed,
        out_specs=(P(), P(), P(None, ("gx", "gy"))),
        check_vma=False,
    )
```

```python
import functools
import math

import jax
import jax.numpy as jnp
from jax import lax
from jax.experimental import pallas as pl
from jax.experimental.pallas import tpu as pltpu
from jax.sharding import PartitionSpec as P

GOLDEN = math.pi * (3.0 - math.sqrt(5.0))
PI_A = round(math.pi * 32768.0) / 32768.0
PI_B = math.pi - PI_A
INV_PI = 1.0 / math.pi
SIN_C = [-0.16666657019913644, 0.00833301540393062, -0.00019806478078586938, 2.599750005030262e-06]
COS_C = [-0.4999993175258851, 0.041663973510963626, -0.0013855797199316853, 2.3191254010748703e-05]
SINPI_C = [3.141592578574041, -5.1677067848796066, 2.5500297991194887, -0.5980355679943354, 0.07720094563063706]
COSPI_C = [-4.934795411606951, 4.05844824012755, -1.332068921858188, 0.22002136541700046]


ROOT2 = math.sqrt(2.0)


def sincos_half_turns(v):
    w = v - jnp.floor(v + 0.5)
    z = w * w
    ps = SINPI_C[-1] * ROOT2
    for c in SINPI_C[-2::-1]:
        ps = c * ROOT2 + z * ps
    pc = COSPI_C[-1] * ROOT2
    for c in COSPI_C[-2::-1]:
        pc = c * ROOT2 + z * pc
    sine_half = w * ps
    cosine_half = ROOT2 + z * pc
    return (cosine_half * cosine_half - 1.0, sine_half * cosine_half)


def sincos_turns(u):
    n = jnp.floor(u + 0.5)
    w = u - n
    z = w * w
    ps = SINPI_C[-1]
    for c in SINPI_C[-2::-1]:
        ps = c + z * ps
    pc = COSPI_C[-1]
    for c in COSPI_C[-2::-1]:
        pc = c + z * pc
    half = n * 0.5
    sign = 1.0 - 4.0 * (half - jnp.floor(half))
    return (sign * (1.0 + z * pc), (sign * w) * ps)


def sincos(theta):
    n = jnp.floor(theta * INV_PI + 0.5)
    r = (theta - n * PI_A) - n * PI_B
    z = r * r
    ps = SIN_C[-1]
    for c in SIN_C[-2::-1]:
        ps = c + z * ps
    pc = COS_C[-1]
    for c in COS_C[-2::-1]:
        pc = c + z * pc
    half = n * 0.5
    sign = 1.0 - 4.0 * (half - jnp.floor(half))
    return (sign * (1.0 + z * pc), sign * (r + (r * z) * ps))


def directions(count_dirs):
    lattice = jnp.arange(count_dirs).astype(jnp.float32)
    height = 1.0 - (2.0 * lattice + 1.0) / count_dirs
    radius_xy = jnp.sqrt(1.0 - height * height)
    azimuth = jnp.mod(lattice * GOLDEN, 2.0 * math.pi)
    return (radius_xy * jnp.cos(azimuth), radius_xy * jnp.sin(azimuth), height)


def kernel_block(points, wavenum, east_x, north_y, upward):
    phases = wavenum * (
        points[0][:, None] * east_x[None, :]
        + points[1][:, None] * north_y[None, :]
        + points[2][:, None] * upward[None, :]
    )
    cosine, sine = sincos(phases)
    return jnp.concatenate([cosine, sine], axis=1).astype(jnp.bfloat16)


def source_rows(rows_block, level):
    surface_area = rows_block[22]
    normal = rows_block[19:22]
    pressure_real = rows_block[level] * surface_area
    pressure_imag = rows_block[4 + level] * surface_area
    return jnp.stack(
        [
            rows_block[8 + level] * surface_area,
            normal[0] * pressure_real,
            normal[1] * pressure_real,
            normal[2] * pressure_real,
            rows_block[12 + level] * surface_area,
            normal[0] * pressure_imag,
            normal[1] * pressure_imag,
            normal[2] * pressure_imag,
        ]
    ).astype(jnp.bfloat16)


def far_field_of(sums, wavenumbers, direction_basis):
    half_width = sums.shape[2] // 2
    cosine_part = sums[:, :, :half_width]
    sine_part = sums[:, :, half_width:]
    real_q = cosine_part[:, 0:4] + sine_part[:, 4:8]
    imag_q = cosine_part[:, 4:8] - sine_part[:, 0:4]
    real_z = jnp.sum(direction_basis[None] * real_q, axis=1)
    imag_z = jnp.sum(direction_basis[None] * imag_q, axis=1)
    wavenum = wavenumbers[:, None]
    return jnp.stack([-wavenum * imag_z, wavenum * real_z], axis=1)


def adjoint_weights(far_field, target, direction_weight, wavenumbers, direction_basis):
    count_dirs = far_field.shape[2]
    mismatch = far_field - target
    objective = jnp.sum(direction_weight * mismatch * mismatch) / count_dirs
    gradient = 2.0 * direction_weight * mismatch / count_dirs
    wavenum = wavenumbers[:, None]
    real_gz = wavenum * gradient[:, 1]
    imag_gz = -wavenum * gradient[:, 0]
    real_gq = direction_basis[None] * real_gz[:, None]
    imag_gq = direction_basis[None] * imag_gz[:, None]
    upper_half = jnp.concatenate([real_gq, -imag_gq], axis=2)
    lower_half = jnp.concatenate([imag_gq, real_gq], axis=2)
    return (objective, jnp.concatenate([upper_half, lower_half], axis=1).astype(jnp.bfloat16))


def adjoint_sources(products, normal):
    pressure_real = jnp.sum(normal[None] * products[:, 1:4], axis=1)
    pressure_imag = jnp.sum(normal[None] * products[:, 5:8], axis=1)
    return jnp.concatenate([pressure_real, pressure_imag, products[:, 0], products[:, 4]], axis=0)


ROW_BLOCK = 128
ADJ_BLOCK = 128
ROW_CHUNK = 16
LANE_CHUNK = 256


def forward_kernel(wave_ref, pts_ref, dirs_ref, rows_ref, cs_ref, q_ref, src_scr):
    step = pl.program_id(0)
    num_freqs = cs_ref.shape[0]
    count_dirs = dirs_ref.shape[2]
    turns = [wave_ref[level] * (0.5 * INV_PI) for level in range(num_freqs)]

    @pl.loop(0, ROW_BLOCK // ROW_CHUNK)
    def _(i):
        r0 = pl.multiple_of(i * ROW_CHUNK, ROW_CHUNK)
        coords = [
            jnp.broadcast_to(pts_ref[pl.ds(r0, ROW_CHUNK), c : c + 1], (ROW_CHUNK, LANE_CHUNK))
            for c in range(3)
        ]
        for j0 in range(0, count_dirs, LANE_CHUNK):
            lanes = slice(j0, j0 + LANE_CHUNK)
            along = (
                coords[0] * dirs_ref[0, :, lanes]
                + coords[1] * dirs_ref[1, :, lanes]
                + coords[2] * dirs_ref[2, :, lanes]
            )
            for level in range(num_freqs):
                cosine, sine = sincos_half_turns(turns[level] * along)
                cs_ref[level, pl.ds(r0, ROW_CHUNK), lanes] = cosine.astype(jnp.bfloat16)
                cs_ref[level, pl.ds(r0, ROW_CHUNK), j0 + count_dirs : j0 + count_dirs + LANE_CHUNK] = (
                    sine.astype(jnp.bfloat16)
                )

    @pl.when(step == 0)
    def _():
        q_ref[...] = jnp.zeros_like(q_ref)

    area = rows_ref[22:23, :]
    src_scr[...] = jnp.zeros_like(src_scr)
    for level in range(num_freqs):
        pressure_real = rows_ref[level : level + 1, :] * area
        pressure_imag = rows_ref[4 + level : 5 + level, :] * area
        src_scr[0:1, :] = rows_ref[8 + level : 9 + level, :] * area
        src_scr[4:5, :] = rows_ref[12 + level : 13 + level, :] * area
        for c in range(3):
            normal = rows_ref[19 + c : 20 + c, :]
            src_scr[1 + c : 2 + c, :] = normal * pressure_real
            src_scr[5 + c : 6 + c, :] = normal * pressure_imag
        source = src_scr[...].astype(jnp.bfloat16)
        q_ref[level] += jnp.dot(source, cs_ref[level], preferred_element_type=jnp.float32)


def forward_sums(wavenumbers, points, dirs_block, compact):
    num_freqs = wavenumbers.shape[0]
    rows = points.shape[0]
    count_dirs = dirs_block.shape[2]
    grid = (rows // ROW_BLOCK,)
    return pl.pallas_call(
        forward_kernel,
        grid=grid,
        in_specs=[
            pl.BlockSpec(memory_space=pltpu.SMEM),
            pl.BlockSpec((ROW_BLOCK, 3), lambda b: (b, 0)),
            pl.BlockSpec(dirs_block.shape, lambda b: (0, 0, 0)),
            pl.BlockSpec((compact.shape[0], ROW_BLOCK), lambda b: (0, b)),
        ],
        out_specs=[
            pl.BlockSpec((num_freqs, ROW_BLOCK, 2 * count_dirs), lambda b: (0, b, 0)),
            pl.BlockSpec((num_freqs, 16, 2 * count_dirs), lambda b: (0, 0, 0)),
        ],
        out_shape=[
            jax.ShapeDtypeStruct((num_freqs, rows, 2 * count_dirs), jnp.bfloat16),
            jax.ShapeDtypeStruct((num_freqs, 16, 2 * count_dirs), jnp.float32),
        ],
        scratch_shapes=[pltpu.VMEM((16, ROW_BLOCK), jnp.float32)],
        compiler_params=pltpu.CompilerParams(
            dimension_semantics=("arbitrary",), vmem_limit_bytes=48 * 1024 * 1024
        ),
        cost_estimate=pl.CostEstimate(
            flops=2 * 16 * rows * 2 * count_dirs * num_freqs + 60 * rows * count_dirs * num_freqs,
            transcendentals=0,
            bytes_accessed=2 * rows * 2 * count_dirs * num_freqs,
        ),
    )(wavenumbers, points, dirs_block, compact)


def adjoint_kernel(w_ref, cs_ref, out_ref):
    for level in range(cs_ref.shape[0]):
        out_ref[level] = lax.dot_general(
            w_ref[level], cs_ref[level], (((1,), (1,)), ((), ())), preferred_element_type=jnp.float32
        )


def adjoint_products(weights, kernel_all):
    num_freqs, rows, width = kernel_all.shape
    return pl.pallas_call(
        adjoint_kernel,
        grid=(rows // ADJ_BLOCK,),
        in_specs=[
            pl.BlockSpec(weights.shape, lambda b: (0, 0, 0)),
            pl.BlockSpec((num_freqs, ADJ_BLOCK, width), lambda b: (0, b, 0)),
        ],
        out_specs=pl.BlockSpec((num_freqs, weights.shape[1], ADJ_BLOCK), lambda b: (0, 0, b)),
        out_shape=jax.ShapeDtypeStruct((num_freqs, weights.shape[1], rows), jnp.float32),
        compiler_params=pltpu.CompilerParams(
            dimension_semantics=("arbitrary",), vmem_limit_bytes=48 * 1024 * 1024
        ),
        cost_estimate=pl.CostEstimate(
            flops=2 * weights.shape[1] * rows * width * num_freqs,
            transcendentals=0,
            bytes_accessed=2 * rows * width * num_freqs,
        ),
    )(weights, kernel_all)


def split_bf16(values):
    high = lax.reduce_precision(values, exponent_bits=8, mantissa_bits=7)
    rest = values - high
    middle = lax.reduce_precision(rest, exponent_bits=8, mantissa_bits=7)
    low = rest - middle
    return jnp.concatenate([high, middle, low], axis=0).astype(jnp.bfloat16)


def join_parts(product, channels):
    return (product[:channels] + product[channels : 2 * channels]) + product[2 * channels :]


def permute_columns(values, selector):
    product = jnp.dot(split_bf16(values), selector, preferred_element_type=jnp.float32)
    return join_parts(product, values.shape[0])


def unpermute_columns(values, selector):
    product = lax.dot_general(
        split_bf16(values), selector, (((1,), (1,)), ((), ())), preferred_element_type=jnp.float32
    )
    return join_parts(product, values.shape[0])


MESH_IDS = pl.DeviceIdType.MESH


def reduce_kernel(nx, ny, x_ref, out_ref, part_a, part_b, got_a, got_b, sems):
    b0 = lax.axis_index("gx")
    a0 = lax.axis_index("gy")
    barrier = pltpu.get_barrier_semaphore()
    for t in range(1, ny):
        pl.semaphore_signal(barrier, inc=1, device_id=(b0, lax.rem(a0 + t, ny)), device_id_type=MESH_IDS)
    for t in range(1, nx):
        pl.semaphore_signal(barrier, inc=1, device_id=(lax.rem(b0 + t, nx), a0), device_id_type=MESH_IDS)
    pl.semaphore_wait(barrier, nx + ny - 2)

    def exchange(phase, src_of, dst_of, peers, along_x):
        copies = []
        for t in range(1, peers):
            if along_x:
                peer = lax.rem(b0 + t, nx)
                me, device = b0, (peer, a0)
            else:
                peer = lax.rem(a0 + t, ny)
                me, device = a0, (b0, peer)
            copy = pltpu.make_async_remote_copy(
                src_ref=src_of(peer),
                dst_ref=dst_of(me),
                send_sem=sems.at[phase, 0, peer],
                recv_sem=sems.at[phase, 1, me],
                device_id=device,
                device_id_type=MESH_IDS,
            )
            copy.start()
            copies.append((peer, device))
        for peer, device in copies:
            pltpu.make_async_remote_copy(
                src_ref=src_of(peer),
                dst_ref=dst_of(peer),
                send_sem=sems.at[phase, 0, peer],
                recv_sem=sems.at[phase, 1, peer],
                device_id=device,
                device_id_type=MESH_IDS,
            ).wait()

    exchange(0, lambda a: x_ref.at[a], lambda a: got_a.at[a], ny, False)
    got_a[a0] = x_ref[a0]
    part_a[...] = jnp.sum(got_a[...], axis=0)
    exchange(1, lambda b: part_a, lambda b: got_b.at[b], nx, True)
    got_b[b0] = part_a[...]
    part_b[...] = jnp.sum(got_b[...], axis=0)
    exchange(2, lambda a: part_b, lambda a: out_ref.at[a], ny, False)
    out_ref[a0] = part_b[...]


def exchange_kernel(nx, ny, x_ref, out_ref, landing, send_sems, recv_sems):
    total = nx * ny
    me = lax.axis_index("gx") * ny + lax.axis_index("gy")
    barrier = pltpu.get_barrier_semaphore()

    def where(peer):
        return (peer // ny, lax.rem(peer, ny))

    @pl.loop(1, total)
    def _(t):
        peer = lax.rem(me + t, total)
        pl.semaphore_signal(barrier, inc=1, device_id=where(peer), device_id_type=MESH_IDS)

    pl.semaphore_wait(barrier, total - 1)

    @pl.loop(1, total)
    def _(t):
        peer = lax.rem(me + t, total)
        pltpu.make_async_remote_copy(
            src_ref=x_ref.at[peer],
            dst_ref=landing.at[me],
            send_sem=send_sems.at[peer],
            recv_sem=recv_sems.at[me],
            device_id=where(peer),
            device_id_type=MESH_IDS,
        ).start()

    landing[me] = x_ref[me]

    @pl.loop(1, total)
    def _(t):
        peer = lax.rem(me + t, total)
        pltpu.make_async_remote_copy(
            src_ref=x_ref.at[peer],
            dst_ref=landing.at[peer],
            send_sem=send_sems.at[peer],
            recv_sem=recv_sems.at[peer],
            device_id=where(peer),
            device_id_type=MESH_IDS,
        ).wait()

    out_ref[...] = landing[...]


def exchange(blocks, exchange_id):
    nx = lax.axis_size("gx")
    ny = lax.axis_size("gy")
    return pl.pallas_call(
        functools.partial(exchange_kernel, nx, ny),
        in_specs=[pl.BlockSpec(memory_space=pltpu.VMEM)],
        out_specs=pl.BlockSpec(memory_space=pltpu.VMEM),
        out_shape=jax.ShapeDtypeStruct(blocks.shape, blocks.dtype),
        scratch_shapes=[
            pltpu.VMEM(blocks.shape, blocks.dtype),
            pltpu.SemaphoreType.DMA((nx * ny,)),
            pltpu.SemaphoreType.DMA((nx * ny,)),
        ],
        compiler_params=pltpu.CompilerParams(collective_id=exchange_id, has_side_effects=True),
    )(blocks)


def sum_over_devices(partial, owners):
    nx = lax.axis_size("gx")
    ny = lax.axis_size("gy")
    lanes = partial.size // (nx * ny)
    shaped = partial.reshape(ny, nx, lanes)
    peers = max(nx, ny)
    total = pl.pallas_call(
        functools.partial(reduce_kernel, nx, ny),
        in_specs=[pl.BlockSpec(memory_space=pltpu.VMEM)],
        out_specs=pl.BlockSpec(memory_space=pltpu.VMEM),
        out_shape=jax.ShapeDtypeStruct(shaped.shape, jnp.float32),
        scratch_shapes=[
            pltpu.VMEM((nx, lanes), jnp.float32),
            pltpu.VMEM((nx, lanes), jnp.float32),
            pltpu.VMEM((ny, nx, lanes), jnp.float32),
            pltpu.VMEM((nx, nx, lanes), jnp.float32),
            pltpu.SemaphoreType.DMA((3, 2, peers)),
        ],
        compiler_params=pltpu.CompilerParams(collective_id=0, has_side_effects=True),
    )(shaped)
    return total.reshape(partial.shape)


def sum_over_devices_a2a(partial, owners):
    chunks = partial.reshape(owners, -1)
    got = lax.all_to_all(chunks, ("gx", "gy"), split_axis=0, concat_axis=0, tiled=True)
    mine = jnp.sum(got, axis=0, keepdims=True)
    spread = jnp.broadcast_to(mine, chunks.shape)
    full = lax.all_to_all(spread, ("gx", "gy"), split_axis=0, concat_axis=0, tiled=True)
    return full.reshape(partial.shape)


def on_device(cell_state, geometry, surface_cell, counts, wavenumbers, target, direction_weight):
    owners = lax.axis_size(("gx", "gy"))
    rows_dev = surface_cell.shape[0]
    capacity = rows_dev // owners
    live_own = rows_dev // 4
    count_dirs = target.shape[2]
    num_freqs = wavenumbers.shape[0]
    living = (jnp.arange(rows_dev) < counts[0]).astype(jnp.float32)
    outgoing = (
        jnp.concatenate(
            [cell_state[:, surface_cell], geometry, jnp.ones((1, rows_dev), jnp.float32)], axis=0
        )
        * living[None, :]
    )
    outgoing = outgoing.reshape(24, capacity, owners).transpose(2, 0, 1).reshape(owners, -1, 128)
    arrived = exchange(outgoing, 1).reshape(owners, 24, capacity).transpose(1, 0, 2)
    marker = arrived[23]
    per_source = jnp.sum(marker, axis=1).astype(jnp.int32)
    offset = jnp.cumsum(per_source) - per_source
    position = offset[:, None] + jnp.arange(capacity, dtype=jnp.int32)[None, :]
    packed_slot = jnp.where(marker > 0.5, position, live_own).reshape(capacity * owners)
    selector = (packed_slot[:, None] == jnp.arange(live_own, dtype=jnp.int32)[None, :]).astype(jnp.bfloat16)
    compact = permute_columns(arrived[:23].reshape(23, capacity * owners), selector)
    east_x, north_y, upward = directions(count_dirs)
    direction_basis = jnp.stack([jnp.ones_like(east_x), east_x, north_y, upward])

    points = compact[16:19].T
    dirs_block = jnp.broadcast_to(jnp.stack([east_x, north_y, upward])[:, None, :], (3, ROW_CHUNK, count_dirs))
    kernel_all, sums = forward_sums(wavenumbers, points, dirs_block, compact)
    sums = sums[:, :8]
    far_field = sum_over_devices(far_field_of(sums, wavenumbers, direction_basis), owners)
    objective, weights = adjoint_weights(
        far_field, target, direction_weight, wavenumbers, direction_basis
    )

    padded = jnp.concatenate([weights, jnp.zeros_like(weights)], axis=1)
    products = adjoint_products(padded, kernel_all)[:, :8]
    backward = adjoint_sources(products, compact[19:22])
    spread = unpermute_columns(backward, selector)
    spread = spread.reshape(16, owners, capacity).transpose(1, 0, 2).reshape(owners, -1, 128)
    returned = exchange(spread, 2).reshape(owners, 16, capacity).transpose(1, 2, 0)
    per_row = returned.reshape(16, rows_dev) * living[None, :]
    cell_adjoint = jnp.zeros(cell_state.shape, jnp.float32).at[:, surface_cell].add(per_row)
    return (far_field, objective, cell_adjoint)


def solution(mesh):
    placed = (
        P(None, ("gx", "gy")),
        P(None, ("gx", "gy")),
        P(("gx", "gy")),
        P(("gx", "gy")),
        P(),
        P(),
        P(),
    )
    return jax.shard_map(
        on_device,
        mesh=mesh,
        in_specs=placed,
        out_specs=(P(), P(), P(None, ("gx", "gy"))),
        check_vma=False,
    )
```

```python
import functools
import math

import jax
import jax.numpy as jnp
from jax import lax
from jax.experimental import pallas as pl
from jax.experimental.pallas import tpu as pltpu
from jax.sharding import PartitionSpec as P

GOLDEN = math.pi * (3.0 - math.sqrt(5.0))
PI_A = round(math.pi * 32768.0) / 32768.0
PI_B = math.pi - PI_A
INV_PI = 1.0 / math.pi
SIN_C = [-0.16666657019913644, 0.00833301540393062, -0.00019806478078586938, 2.599750005030262e-06]
COS_C = [-0.4999993175258851, 0.041663973510963626, -0.0013855797199316853, 2.3191254010748703e-05]
SINPI_C = [3.141592578574041, -5.1677067848796066, 2.5500297991194887, -0.5980355679943354, 0.07720094563063706]
COSPI_C = [-4.934795411606951, 4.05844824012755, -1.332068921858188, 0.22002136541700046]


ROOT2 = math.sqrt(2.0)


def sincos_half_turns(v):
    w = v - jnp.floor(v + 0.5)
    z = w * w
    ps = SINPI_C[-1] * ROOT2
    for c in SINPI_C[-2::-1]:
        ps = c * ROOT2 + z * ps
    pc = COSPI_C[-1] * ROOT2
    for c in COSPI_C[-2::-1]:
        pc = c * ROOT2 + z * pc
    sine_half = w * ps
    cosine_half = ROOT2 + z * pc
    return (cosine_half * cosine_half - 1.0, sine_half * cosine_half)


def sincos_turns(u):
    n = jnp.floor(u + 0.5)
    w = u - n
    z = w * w
    ps = SINPI_C[-1]
    for c in SINPI_C[-2::-1]:
        ps = c + z * ps
    pc = COSPI_C[-1]
    for c in COSPI_C[-2::-1]:
        pc = c + z * pc
    half = n * 0.5
    sign = 1.0 - 4.0 * (half - jnp.floor(half))
    return (sign * (1.0 + z * pc), (sign * w) * ps)


def sincos(theta):
    n = jnp.floor(theta * INV_PI + 0.5)
    r = (theta - n * PI_A) - n * PI_B
    z = r * r
    ps = SIN_C[-1]
    for c in SIN_C[-2::-1]:
        ps = c + z * ps
    pc = COS_C[-1]
    for c in COS_C[-2::-1]:
        pc = c + z * pc
    half = n * 0.5
    sign = 1.0 - 4.0 * (half - jnp.floor(half))
    return (sign * (1.0 + z * pc), sign * (r + (r * z) * ps))


def directions(count_dirs):
    lattice = jnp.arange(count_dirs).astype(jnp.float32)
    height = 1.0 - (2.0 * lattice + 1.0) / count_dirs
    radius_xy = jnp.sqrt(1.0 - height * height)
    azimuth = jnp.mod(lattice * GOLDEN, 2.0 * math.pi)
    return (radius_xy * jnp.cos(azimuth), radius_xy * jnp.sin(azimuth), height)


def kernel_block(points, wavenum, east_x, north_y, upward):
    phases = wavenum * (
        points[0][:, None] * east_x[None, :]
        + points[1][:, None] * north_y[None, :]
        + points[2][:, None] * upward[None, :]
    )
    cosine, sine = sincos(phases)
    return jnp.concatenate([cosine, sine], axis=1).astype(jnp.bfloat16)


def source_rows(rows_block, level):
    surface_area = rows_block[22]
    normal = rows_block[19:22]
    pressure_real = rows_block[level] * surface_area
    pressure_imag = rows_block[4 + level] * surface_area
    return jnp.stack(
        [
            rows_block[8 + level] * surface_area,
            normal[0] * pressure_real,
            normal[1] * pressure_real,
            normal[2] * pressure_real,
            rows_block[12 + level] * surface_area,
            normal[0] * pressure_imag,
            normal[1] * pressure_imag,
            normal[2] * pressure_imag,
        ]
    ).astype(jnp.bfloat16)


def far_field_of(sums, wavenumbers, direction_basis):
    half_width = sums.shape[2] // 2
    cosine_part = sums[:, :, :half_width]
    sine_part = sums[:, :, half_width:]
    real_q = cosine_part[:, 0:4] + sine_part[:, 4:8]
    imag_q = cosine_part[:, 4:8] - sine_part[:, 0:4]
    real_z = jnp.sum(direction_basis[None] * real_q, axis=1)
    imag_z = jnp.sum(direction_basis[None] * imag_q, axis=1)
    wavenum = wavenumbers[:, None]
    return jnp.stack([-wavenum * imag_z, wavenum * real_z], axis=1)


def adjoint_weights(far_field, target, direction_weight, wavenumbers, direction_basis):
    count_dirs = far_field.shape[2]
    mismatch = far_field - target
    objective = jnp.sum(direction_weight * mismatch * mismatch) / count_dirs
    gradient = 2.0 * direction_weight * mismatch / count_dirs
    wavenum = wavenumbers[:, None]
    real_gz = wavenum * gradient[:, 1]
    imag_gz = -wavenum * gradient[:, 0]
    real_gq = direction_basis[None] * real_gz[:, None]
    imag_gq = direction_basis[None] * imag_gz[:, None]
    upper_half = jnp.concatenate([real_gq, -imag_gq], axis=2)
    lower_half = jnp.concatenate([imag_gq, real_gq], axis=2)
    return (objective, jnp.concatenate([upper_half, lower_half], axis=1).astype(jnp.bfloat16))


def adjoint_sources(products, normal):
    pressure_real = jnp.sum(normal[None] * products[:, 1:4], axis=1)
    pressure_imag = jnp.sum(normal[None] * products[:, 5:8], axis=1)
    return jnp.concatenate([pressure_real, pressure_imag, products[:, 0], products[:, 4]], axis=0)


ROW_BLOCK = 128
ADJ_BLOCK = 256
ROW_CHUNK = 16
LANE_CHUNK = 256


def forward_kernel(wave_ref, pts_ref, dirs_ref, rows_ref, cs_ref, q_ref, src_scr):
    step = pl.program_id(0)
    num_freqs = cs_ref.shape[0]
    count_dirs = dirs_ref.shape[2]
    turns = [wave_ref[level] * (0.5 * INV_PI) for level in range(num_freqs)]

    @pl.loop(0, ROW_BLOCK // ROW_CHUNK)
    def _(i):
        r0 = pl.multiple_of(i * ROW_CHUNK, ROW_CHUNK)
        coords = [
            jnp.broadcast_to(pts_ref[pl.ds(r0, ROW_CHUNK), c : c + 1], (ROW_CHUNK, LANE_CHUNK))
            for c in range(3)
        ]
        for j0 in range(0, count_dirs, LANE_CHUNK):
            lanes = slice(j0, j0 + LANE_CHUNK)
            along = (
                coords[0] * dirs_ref[0, :, lanes]
                + coords[1] * dirs_ref[1, :, lanes]
                + coords[2] * dirs_ref[2, :, lanes]
            )
            for level in range(num_freqs):
                cosine, sine = sincos_half_turns(turns[level] * along)
                cs_ref[level, pl.ds(r0, ROW_CHUNK), lanes] = cosine.astype(jnp.bfloat16)
                cs_ref[level, pl.ds(r0, ROW_CHUNK), j0 + count_dirs : j0 + count_dirs + LANE_CHUNK] = (
                    sine.astype(jnp.bfloat16)
                )

    @pl.when(step == 0)
    def _():
        q_ref[...] = jnp.zeros_like(q_ref)

    area = rows_ref[22:23, :]
    src_scr[...] = jnp.zeros_like(src_scr)
    for level in range(num_freqs):
        pressure_real = rows_ref[level : level + 1, :] * area
        pressure_imag = rows_ref[4 + level : 5 + level, :] * area
        src_scr[0:1, :] = rows_ref[8 + level : 9 + level, :] * area
        src_scr[4:5, :] = rows_ref[12 + level : 13 + level, :] * area
        for c in range(3):
            normal = rows_ref[19 + c : 20 + c, :]
            src_scr[1 + c : 2 + c, :] = normal * pressure_real
            src_scr[5 + c : 6 + c, :] = normal * pressure_imag
        source = src_scr[...].astype(jnp.bfloat16)
        q_ref[level] += jnp.dot(source, cs_ref[level], preferred_element_type=jnp.float32)


def forward_sums(wavenumbers, points, dirs_block, compact):
    num_freqs = wavenumbers.shape[0]
    rows = points.shape[0]
    count_dirs = dirs_block.shape[2]
    grid = (rows // ROW_BLOCK,)
    return pl.pallas_call(
        forward_kernel,
        grid=grid,
        in_specs=[
            pl.BlockSpec(memory_space=pltpu.SMEM),
            pl.BlockSpec((ROW_BLOCK, 3), lambda b: (b, 0)),
            pl.BlockSpec(dirs_block.shape, lambda b: (0, 0, 0)),
            pl.BlockSpec((compact.shape[0], ROW_BLOCK), lambda b: (0, b)),
        ],
        out_specs=[
            pl.BlockSpec((num_freqs, ROW_BLOCK, 2 * count_dirs), lambda b: (0, b, 0)),
            pl.BlockSpec((num_freqs, 16, 2 * count_dirs), lambda b: (0, 0, 0)),
        ],
        out_shape=[
            jax.ShapeDtypeStruct((num_freqs, rows, 2 * count_dirs), jnp.bfloat16),
            jax.ShapeDtypeStruct((num_freqs, 16, 2 * count_dirs), jnp.float32),
        ],
        scratch_shapes=[pltpu.VMEM((16, ROW_BLOCK), jnp.float32)],
        compiler_params=pltpu.CompilerParams(
            dimension_semantics=("arbitrary",), vmem_limit_bytes=48 * 1024 * 1024
        ),
        cost_estimate=pl.CostEstimate(
            flops=2 * 16 * rows * 2 * count_dirs * num_freqs + 60 * rows * count_dirs * num_freqs,
            transcendentals=0,
            bytes_accessed=2 * rows * 2 * count_dirs * num_freqs,
        ),
    )(wavenumbers, points, dirs_block, compact)


def adjoint_kernel(w_ref, cs_ref, out_ref):
    for level in range(cs_ref.shape[0]):
        out_ref[level] = lax.dot_general(
            w_ref[level], cs_ref[level], (((1,), (1,)), ((), ())), preferred_element_type=jnp.float32
        )


def adjoint_products(weights, kernel_all):
    num_freqs, rows, width = kernel_all.shape
    return pl.pallas_call(
        adjoint_kernel,
        grid=(rows // ADJ_BLOCK,),
        in_specs=[
            pl.BlockSpec(weights.shape, lambda b: (0, 0, 0)),
            pl.BlockSpec((num_freqs, ADJ_BLOCK, width), lambda b: (0, b, 0)),
        ],
        out_specs=pl.BlockSpec((num_freqs, weights.shape[1], ADJ_BLOCK), lambda b: (0, 0, b)),
        out_shape=jax.ShapeDtypeStruct((num_freqs, weights.shape[1], rows), jnp.float32),
        compiler_params=pltpu.CompilerParams(
            dimension_semantics=("arbitrary",), vmem_limit_bytes=48 * 1024 * 1024
        ),
        cost_estimate=pl.CostEstimate(
            flops=2 * weights.shape[1] * rows * width * num_freqs,
            transcendentals=0,
            bytes_accessed=2 * rows * width * num_freqs,
        ),
    )(weights, kernel_all)


def split_bf16(values):
    high = lax.reduce_precision(values, exponent_bits=8, mantissa_bits=7)
    rest = values - high
    middle = lax.reduce_precision(rest, exponent_bits=8, mantissa_bits=7)
    low = rest - middle
    return jnp.concatenate([high, middle, low], axis=0).astype(jnp.bfloat16)


def join_parts(product, channels):
    return (product[:channels] + product[channels : 2 * channels]) + product[2 * channels :]


def permute_columns(values, selector):
    product = jnp.dot(split_bf16(values), selector, preferred_element_type=jnp.float32)
    return join_parts(product, values.shape[0])


def unpermute_columns(values, selector):
    product = lax.dot_general(
        split_bf16(values), selector, (((1,), (1,)), ((), ())), preferred_element_type=jnp.float32
    )
    return join_parts(product, values.shape[0])


CHAINS = 4


def scatter_kernel(cell_ref, rows_ref, out_ref, *accs):
    for acc in accs:
        acc[...] = jnp.zeros_like(acc)
    chains = len(accs)

    def body(i, carry):
        for k in range(chains):
            row = i * chains + k
            cell = cell_ref[row]
            accs[k][pl.ds(cell, 1), :] += rows_ref[pl.ds(row, 1), :]
        return carry

    lax.fori_loop(0, rows_ref.shape[0] // chains, body, 0)
    out_ref[...] = (accs[0][...] + accs[1][...]) + (accs[2][...] + accs[3][...])


def scatter_rows(surface_cell, rows_major, cells):
    width = rows_major.shape[1]
    return pl.pallas_call(
        scatter_kernel,
        grid_spec=pltpu.PrefetchScalarGridSpec(
            num_scalar_prefetch=1,
            grid=(1,),
            in_specs=[pl.BlockSpec(rows_major.shape, lambda i, c: (0, 0))],
            out_specs=pl.BlockSpec((cells, width), lambda i, c: (0, 0)),
            scratch_shapes=[pltpu.VMEM((cells, width), jnp.float32) for _ in range(CHAINS)],
        ),
        out_shape=jax.ShapeDtypeStruct((cells, width), jnp.float32),
        compiler_params=pltpu.CompilerParams(vmem_limit_bytes=48 * 1024 * 1024),
    )(surface_cell, rows_major)


MESH_IDS = pl.DeviceIdType.MESH


def reduce_kernel(nx, ny, x_ref, out_ref, part_a, part_b, got_a, got_b, sems):
    b0 = lax.axis_index("gx")
    a0 = lax.axis_index("gy")
    barrier = pltpu.get_barrier_semaphore()
    for t in range(1, ny):
        pl.semaphore_signal(barrier, inc=1, device_id=(b0, lax.rem(a0 + t, ny)), device_id_type=MESH_IDS)
    for t in range(1, nx):
        pl.semaphore_signal(barrier, inc=1, device_id=(lax.rem(b0 + t, nx), a0), device_id_type=MESH_IDS)
    pl.semaphore_wait(barrier, nx + ny - 2)

    def exchange(phase, src_of, dst_of, peers, along_x):
        copies = []
        for t in range(1, peers):
            if along_x:
                peer = lax.rem(b0 + t, nx)
                me, device = b0, (peer, a0)
            else:
                peer = lax.rem(a0 + t, ny)
                me, device = a0, (b0, peer)
            copy = pltpu.make_async_remote_copy(
                src_ref=src_of(peer),
                dst_ref=dst_of(me),
                send_sem=sems.at[phase, 0, peer],
                recv_sem=sems.at[phase, 1, me],
                device_id=device,
                device_id_type=MESH_IDS,
            )
            copy.start()
            copies.append((peer, device))
        for peer, device in copies:
            pltpu.make_async_remote_copy(
                src_ref=src_of(peer),
                dst_ref=dst_of(peer),
                send_sem=sems.at[phase, 0, peer],
                recv_sem=sems.at[phase, 1, peer],
                device_id=device,
                device_id_type=MESH_IDS,
            ).wait()

    exchange(0, lambda a: x_ref.at[a], lambda a: got_a.at[a], ny, False)
    got_a[a0] = x_ref[a0]
    part_a[...] = jnp.sum(got_a[...], axis=0)
    exchange(1, lambda b: part_a, lambda b: got_b.at[b], nx, True)
    got_b[b0] = part_a[...]
    part_b[...] = jnp.sum(got_b[...], axis=0)
    exchange(2, lambda a: part_b, lambda a: out_ref.at[a], ny, False)
    out_ref[a0] = part_b[...]


def exchange_kernel(nx, ny, x_ref, out_ref, landing, send_sems, recv_sems):
    total = nx * ny
    me = lax.axis_index("gx") * ny + lax.axis_index("gy")
    barrier = pltpu.get_barrier_semaphore()

    def where(peer):
        return (peer // ny, lax.rem(peer, ny))

    @pl.loop(1, total)
    def _(t):
        peer = lax.rem(me + t, total)
        pl.semaphore_signal(barrier, inc=1, device_id=where(peer), device_id_type=MESH_IDS)

    pl.semaphore_wait(barrier, total - 1)

    @pl.loop(1, total)
    def _(t):
        peer = lax.rem(me + t, total)
        pltpu.make_async_remote_copy(
            src_ref=x_ref.at[peer],
            dst_ref=landing.at[me],
            send_sem=send_sems.at[peer],
            recv_sem=recv_sems.at[me],
            device_id=where(peer),
            device_id_type=MESH_IDS,
        ).start()

    landing[me] = x_ref[me]

    @pl.loop(1, total)
    def _(t):
        peer = lax.rem(me + t, total)
        pltpu.make_async_remote_copy(
            src_ref=x_ref.at[peer],
            dst_ref=landing.at[peer],
            send_sem=send_sems.at[peer],
            recv_sem=recv_sems.at[peer],
            device_id=where(peer),
            device_id_type=MESH_IDS,
        ).wait()

    out_ref[...] = landing[...]


def exchange(blocks, exchange_id):
    nx = lax.axis_size("gx")
    ny = lax.axis_size("gy")
    return pl.pallas_call(
        functools.partial(exchange_kernel, nx, ny),
        in_specs=[pl.BlockSpec(memory_space=pltpu.VMEM)],
        out_specs=pl.BlockSpec(memory_space=pltpu.VMEM),
        out_shape=jax.ShapeDtypeStruct(blocks.shape, blocks.dtype),
        scratch_shapes=[
            pltpu.VMEM(blocks.shape, blocks.dtype),
            pltpu.SemaphoreType.DMA((nx * ny,)),
            pltpu.SemaphoreType.DMA((nx * ny,)),
        ],
        compiler_params=pltpu.CompilerParams(collective_id=exchange_id, has_side_effects=True),
    )(blocks)


def sum_over_devices(partial, owners):
    nx = lax.axis_size("gx")
    ny = lax.axis_size("gy")
    lanes = partial.size // (nx * ny)
    shaped = partial.reshape(ny, nx, lanes)
    peers = max(nx, ny)
    total = pl.pallas_call(
        functools.partial(reduce_kernel, nx, ny),
        in_specs=[pl.BlockSpec(memory_space=pltpu.VMEM)],
        out_specs=pl.BlockSpec(memory_space=pltpu.VMEM),
        out_shape=jax.ShapeDtypeStruct(shaped.shape, jnp.float32),
        scratch_shapes=[
            pltpu.VMEM((nx, lanes), jnp.float32),
            pltpu.VMEM((nx, lanes), jnp.float32),
            pltpu.VMEM((ny, nx, lanes), jnp.float32),
            pltpu.VMEM((nx, nx, lanes), jnp.float32),
            pltpu.SemaphoreType.DMA((3, 2, peers)),
        ],
        compiler_params=pltpu.CompilerParams(collective_id=0, has_side_effects=True),
    )(shaped)
    return total.reshape(partial.shape)


def sum_over_devices_a2a(partial, owners):
    chunks = partial.reshape(owners, -1)
    got = lax.all_to_all(chunks, ("gx", "gy"), split_axis=0, concat_axis=0, tiled=True)
    mine = jnp.sum(got, axis=0, keepdims=True)
    spread = jnp.broadcast_to(mine, chunks.shape)
    full = lax.all_to_all(spread, ("gx", "gy"), split_axis=0, concat_axis=0, tiled=True)
    return full.reshape(partial.shape)


def on_device(cell_state, geometry, surface_cell, counts, wavenumbers, target, direction_weight):
    owners = lax.axis_size(("gx", "gy"))
    rows_dev = surface_cell.shape[0]
    capacity = rows_dev // owners
    live_own = rows_dev // 4
    count_dirs = target.shape[2]
    num_freqs = wavenumbers.shape[0]
    living = (jnp.arange(rows_dev) < counts[0]).astype(jnp.float32)
    outgoing = (
        jnp.concatenate(
            [cell_state[:, surface_cell], geometry, jnp.ones((1, rows_dev), jnp.float32)], axis=0
        )
        * living[None, :]
    )
    outgoing = outgoing.reshape(24, capacity, owners).transpose(2, 0, 1).reshape(owners, -1, 128)
    arrived = exchange(outgoing, 1).reshape(owners, 24, capacity).transpose(1, 0, 2)
    marker = arrived[23]
    per_source = jnp.sum(marker, axis=1).astype(jnp.int32)
    offset = jnp.cumsum(per_source) - per_source
    position = offset[:, None] + jnp.arange(capacity, dtype=jnp.int32)[None, :]
    packed_slot = jnp.where(marker > 0.5, position, live_own).reshape(capacity * owners)
    selector = (packed_slot[:, None] == jnp.arange(live_own, dtype=jnp.int32)[None, :]).astype(jnp.bfloat16)
    compact = permute_columns(arrived[:23].reshape(23, capacity * owners), selector)
    east_x, north_y, upward = directions(count_dirs)
    direction_basis = jnp.stack([jnp.ones_like(east_x), east_x, north_y, upward])

    points = compact[16:19].T
    dirs_block = jnp.broadcast_to(jnp.stack([east_x, north_y, upward])[:, None, :], (3, ROW_CHUNK, count_dirs))
    kernel_all, sums = forward_sums(wavenumbers, points, dirs_block, compact)
    sums = sums[:, :8]
    far_field = sum_over_devices(far_field_of(sums, wavenumbers, direction_basis), owners)
    objective, weights = adjoint_weights(
        far_field, target, direction_weight, wavenumbers, direction_basis
    )

    padded = jnp.concatenate([weights, jnp.zeros_like(weights)], axis=1)
    products = adjoint_products(padded, kernel_all)[:, :8]
    backward = adjoint_sources(products, compact[19:22])
    spread = unpermute_columns(backward, selector)
    spread = spread.reshape(16, owners, capacity).transpose(1, 0, 2).reshape(owners, -1, 128)
    returned = exchange(spread, 2).reshape(owners, 16, capacity).transpose(2, 0, 1).reshape(rows_dev, 16)
    rows_major = returned * living[:, None]
    cell_adjoint = scatter_rows(surface_cell, rows_major, cell_state.shape[1]).T
    return (far_field, objective, cell_adjoint)


def solution(mesh):
    placed = (
        P(None, ("gx", "gy")),
        P(None, ("gx", "gy")),
        P(("gx", "gy")),
        P(("gx", "gy")),
        P(),
        P(),
        P(),
    )
    return jax.shard_map(
        on_device,
        mesh=mesh,
        in_specs=placed,
        out_specs=(P(), P(), P(None, ("gx", "gy"))),
        check_vma=False,
    )
```

```python
import functools
import math

import jax
import jax.numpy as jnp
from jax import lax
from jax.experimental import pallas as pl
from jax.experimental.pallas import tpu as pltpu
from jax.sharding import PartitionSpec as P

GOLDEN = math.pi * (3.0 - math.sqrt(5.0))
PI_A = round(math.pi * 32768.0) / 32768.0
PI_B = math.pi - PI_A
INV_PI = 1.0 / math.pi
SIN_C = [-0.16666657019913644, 0.00833301540393062, -0.00019806478078586938, 2.599750005030262e-06]
COS_C = [-0.4999993175258851, 0.041663973510963626, -0.0013855797199316853, 2.3191254010748703e-05]
SINPI_C = [3.141592578574041, -5.1677067848796066, 2.5500297991194887, -0.5980355679943354, 0.07720094563063706]
COSPI_C = [-4.934795411606951, 4.05844824012755, -1.332068921858188, 0.22002136541700046]


ROOT2 = math.sqrt(2.0)


def sincos_half_turns(v):
    w = v - jnp.floor(v + 0.5)
    z = w * w
    ps = SINPI_C[-1] * ROOT2
    for c in SINPI_C[-2::-1]:
        ps = c * ROOT2 + z * ps
    pc = COSPI_C[-1] * ROOT2
    for c in COSPI_C[-2::-1]:
        pc = c * ROOT2 + z * pc
    sine_half = w * ps
    cosine_half = ROOT2 + z * pc
    return (cosine_half * cosine_half - 1.0, sine_half * cosine_half)


def sincos_turns(u):
    n = jnp.floor(u + 0.5)
    w = u - n
    z = w * w
    ps = SINPI_C[-1]
    for c in SINPI_C[-2::-1]:
        ps = c + z * ps
    pc = COSPI_C[-1]
    for c in COSPI_C[-2::-1]:
        pc = c + z * pc
    half = n * 0.5
    sign = 1.0 - 4.0 * (half - jnp.floor(half))
    return (sign * (1.0 + z * pc), (sign * w) * ps)


def sincos(theta):
    n = jnp.floor(theta * INV_PI + 0.5)
    r = (theta - n * PI_A) - n * PI_B
    z = r * r
    ps = SIN_C[-1]
    for c in SIN_C[-2::-1]:
        ps = c + z * ps
    pc = COS_C[-1]
    for c in COS_C[-2::-1]:
        pc = c + z * pc
    half = n * 0.5
    sign = 1.0 - 4.0 * (half - jnp.floor(half))
    return (sign * (1.0 + z * pc), sign * (r + (r * z) * ps))


def directions(count_dirs):
    lattice = jnp.arange(count_dirs).astype(jnp.float32)
    height = 1.0 - (2.0 * lattice + 1.0) / count_dirs
    radius_xy = jnp.sqrt(1.0 - height * height)
    azimuth = jnp.mod(lattice * GOLDEN, 2.0 * math.pi)
    return (radius_xy * jnp.cos(azimuth), radius_xy * jnp.sin(azimuth), height)


def kernel_block(points, wavenum, east_x, north_y, upward):
    phases = wavenum * (
        points[0][:, None] * east_x[None, :]
        + points[1][:, None] * north_y[None, :]
        + points[2][:, None] * upward[None, :]
    )
    cosine, sine = sincos(phases)
    return jnp.concatenate([cosine, sine], axis=1).astype(jnp.bfloat16)


def source_rows(rows_block, level):
    surface_area = rows_block[22]
    normal = rows_block[19:22]
    pressure_real = rows_block[level] * surface_area
    pressure_imag = rows_block[4 + level] * surface_area
    return jnp.stack(
        [
            rows_block[8 + level] * surface_area,
            normal[0] * pressure_real,
            normal[1] * pressure_real,
            normal[2] * pressure_real,
            rows_block[12 + level] * surface_area,
            normal[0] * pressure_imag,
            normal[1] * pressure_imag,
            normal[2] * pressure_imag,
        ]
    ).astype(jnp.bfloat16)


def far_field_of(sums, wavenumbers, direction_basis):
    half_width = sums.shape[2] // 2
    cosine_part = sums[:, :, :half_width]
    sine_part = sums[:, :, half_width:]
    real_q = cosine_part[:, 0:4] + sine_part[:, 4:8]
    imag_q = cosine_part[:, 4:8] - sine_part[:, 0:4]
    real_z = jnp.sum(direction_basis[None] * real_q, axis=1)
    imag_z = jnp.sum(direction_basis[None] * imag_q, axis=1)
    wavenum = wavenumbers[:, None]
    return jnp.stack([-wavenum * imag_z, wavenum * real_z], axis=1)


def adjoint_weights(far_field, target, direction_weight, wavenumbers, direction_basis):
    count_dirs = far_field.shape[2]
    mismatch = far_field - target
    objective = jnp.sum(direction_weight * mismatch * mismatch) / count_dirs
    gradient = 2.0 * direction_weight * mismatch / count_dirs
    wavenum = wavenumbers[:, None]
    real_gz = wavenum * gradient[:, 1]
    imag_gz = -wavenum * gradient[:, 0]
    real_gq = direction_basis[None] * real_gz[:, None]
    imag_gq = direction_basis[None] * imag_gz[:, None]
    upper_half = jnp.concatenate([real_gq, -imag_gq], axis=2)
    lower_half = jnp.concatenate([imag_gq, real_gq], axis=2)
    return (objective, jnp.concatenate([upper_half, lower_half], axis=1).astype(jnp.bfloat16))


def adjoint_sources(products, normal):
    pressure_real = jnp.sum(normal[None] * products[:, 1:4], axis=1)
    pressure_imag = jnp.sum(normal[None] * products[:, 5:8], axis=1)
    return jnp.concatenate([pressure_real, pressure_imag, products[:, 0], products[:, 4]], axis=0)


ROW_BLOCK = 128
ADJ_BLOCK = 256
ROW_CHUNK = 16
LANE_CHUNK = 256


def forward_kernel(wave_ref, pts_ref, dirs_ref, rows_ref, cs_ref, q_ref, src_scr):
    step = pl.program_id(0)
    num_freqs = cs_ref.shape[0]
    count_dirs = dirs_ref.shape[2]
    turns = [wave_ref[level] * (0.5 * INV_PI) for level in range(num_freqs)]

    @pl.loop(0, ROW_BLOCK // ROW_CHUNK)
    def _(i):
        r0 = pl.multiple_of(i * ROW_CHUNK, ROW_CHUNK)
        coords = [
            jnp.broadcast_to(pts_ref[pl.ds(r0, ROW_CHUNK), c : c + 1], (ROW_CHUNK, LANE_CHUNK))
            for c in range(3)
        ]
        for j0 in range(0, count_dirs, LANE_CHUNK):
            lanes = slice(j0, j0 + LANE_CHUNK)
            along = (
                coords[0] * dirs_ref[0, :, lanes]
                + coords[1] * dirs_ref[1, :, lanes]
                + coords[2] * dirs_ref[2, :, lanes]
            )
            for level in range(num_freqs):
                cosine, sine = sincos_half_turns(turns[level] * along)
                cs_ref[level, pl.ds(r0, ROW_CHUNK), lanes] = cosine.astype(jnp.bfloat16)
                cs_ref[level, pl.ds(r0, ROW_CHUNK), j0 + count_dirs : j0 + count_dirs + LANE_CHUNK] = (
                    sine.astype(jnp.bfloat16)
                )

    @pl.when(step == 0)
    def _():
        q_ref[...] = jnp.zeros_like(q_ref)

    area = rows_ref[22:23, :]
    src_scr[...] = jnp.zeros_like(src_scr)
    for level in range(num_freqs):
        pressure_real = rows_ref[level : level + 1, :] * area
        pressure_imag = rows_ref[4 + level : 5 + level, :] * area
        src_scr[0:1, :] = rows_ref[8 + level : 9 + level, :] * area
        src_scr[4:5, :] = rows_ref[12 + level : 13 + level, :] * area
        for c in range(3):
            normal = rows_ref[19 + c : 20 + c, :]
            src_scr[1 + c : 2 + c, :] = normal * pressure_real
            src_scr[5 + c : 6 + c, :] = normal * pressure_imag
        source = src_scr[...].astype(jnp.bfloat16)
        q_ref[level] += jnp.dot(source, cs_ref[level], preferred_element_type=jnp.float32)


def forward_sums(wavenumbers, points, dirs_block, compact):
    num_freqs = wavenumbers.shape[0]
    rows = points.shape[0]
    count_dirs = dirs_block.shape[2]
    grid = (rows // ROW_BLOCK,)
    return pl.pallas_call(
        forward_kernel,
        grid=grid,
        in_specs=[
            pl.BlockSpec(memory_space=pltpu.SMEM),
            pl.BlockSpec((ROW_BLOCK, 3), lambda b: (b, 0)),
            pl.BlockSpec(dirs_block.shape, lambda b: (0, 0, 0)),
            pl.BlockSpec((compact.shape[0], ROW_BLOCK), lambda b: (0, b)),
        ],
        out_specs=[
            pl.BlockSpec((num_freqs, ROW_BLOCK, 2 * count_dirs), lambda b: (0, b, 0)),
            pl.BlockSpec((num_freqs, 16, 2 * count_dirs), lambda b: (0, 0, 0)),
        ],
        out_shape=[
            jax.ShapeDtypeStruct((num_freqs, rows, 2 * count_dirs), jnp.bfloat16),
            jax.ShapeDtypeStruct((num_freqs, 16, 2 * count_dirs), jnp.float32),
        ],
        scratch_shapes=[pltpu.VMEM((16, ROW_BLOCK), jnp.float32)],
        compiler_params=pltpu.CompilerParams(
            dimension_semantics=("arbitrary",), vmem_limit_bytes=48 * 1024 * 1024
        ),
        cost_estimate=pl.CostEstimate(
            flops=2 * 16 * rows * 2 * count_dirs * num_freqs + 60 * rows * count_dirs * num_freqs,
            transcendentals=0,
            bytes_accessed=2 * rows * 2 * count_dirs * num_freqs,
        ),
    )(wavenumbers, points, dirs_block, compact)


def adjoint_kernel(w_ref, cs_ref, out_ref):
    for level in range(cs_ref.shape[0]):
        out_ref[level] = lax.dot_general(
            w_ref[level], cs_ref[level], (((1,), (1,)), ((), ())), preferred_element_type=jnp.float32
        )


def adjoint_products(weights, kernel_all):
    num_freqs, rows, width = kernel_all.shape
    return pl.pallas_call(
        adjoint_kernel,
        grid=(rows // ADJ_BLOCK,),
        in_specs=[
            pl.BlockSpec(weights.shape, lambda b: (0, 0, 0)),
            pl.BlockSpec((num_freqs, ADJ_BLOCK, width), lambda b: (0, b, 0)),
        ],
        out_specs=pl.BlockSpec((num_freqs, weights.shape[1], ADJ_BLOCK), lambda b: (0, 0, b)),
        out_shape=jax.ShapeDtypeStruct((num_freqs, weights.shape[1], rows), jnp.float32),
        compiler_params=pltpu.CompilerParams(
            dimension_semantics=("arbitrary",), vmem_limit_bytes=48 * 1024 * 1024
        ),
        cost_estimate=pl.CostEstimate(
            flops=2 * weights.shape[1] * rows * width * num_freqs,
            transcendentals=0,
            bytes_accessed=2 * rows * width * num_freqs,
        ),
    )(weights, kernel_all)


def split_bf16(values):
    high = lax.reduce_precision(values, exponent_bits=8, mantissa_bits=7)
    rest = values - high
    middle = lax.reduce_precision(rest, exponent_bits=8, mantissa_bits=7)
    low = rest - middle
    return jnp.concatenate([high, middle, low], axis=0).astype(jnp.bfloat16)


def join_parts(product, channels):
    return (product[:channels] + product[channels : 2 * channels]) + product[2 * channels :]


def permute_columns(values, selector):
    product = jnp.dot(split_bf16(values), selector, preferred_element_type=jnp.float32)
    return join_parts(product, values.shape[0])


def unpermute_columns(values, selector):
    product = lax.dot_general(
        split_bf16(values), selector, (((1,), (1,)), ((), ())), preferred_element_type=jnp.float32
    )
    return join_parts(product, values.shape[0])


CHAINS = 4


def scatter_kernel(cell_ref, rows_ref, out_ref, *accs):
    for acc in accs:
        acc[...] = jnp.zeros_like(acc)
    chains = len(accs)

    def body(i, carry):
        for k in range(chains):
            row = i * chains + k
            cell = cell_ref[row]
            accs[k][pl.ds(cell, 1), :] += rows_ref[pl.ds(row, 1), :]
        return carry

    lax.fori_loop(0, rows_ref.shape[0] // chains, body, 0)
    out_ref[...] = (accs[0][...] + accs[1][...]) + (accs[2][...] + accs[3][...])


def scatter_rows(surface_cell, rows_major, cells):
    width = rows_major.shape[1]
    return pl.pallas_call(
        scatter_kernel,
        grid_spec=pltpu.PrefetchScalarGridSpec(
            num_scalar_prefetch=1,
            grid=(1,),
            in_specs=[pl.BlockSpec(rows_major.shape, lambda i, c: (0, 0))],
            out_specs=pl.BlockSpec((cells, width), lambda i, c: (0, 0)),
            scratch_shapes=[pltpu.VMEM((cells, width), jnp.float32) for _ in range(CHAINS)],
        ),
        out_shape=jax.ShapeDtypeStruct((cells, width), jnp.float32),
        compiler_params=pltpu.CompilerParams(vmem_limit_bytes=48 * 1024 * 1024),
    )(surface_cell, rows_major)


GATHER_UNROLL = 8


def gather_kernel(cell_ref, table_ref, out_ref):
    def body(i, carry):
        for k in range(GATHER_UNROLL):
            row = i * GATHER_UNROLL + k
            out_ref[pl.ds(row, 1), :] = table_ref[pl.ds(cell_ref[row], 1), :]
        return carry

    lax.fori_loop(0, out_ref.shape[0] // GATHER_UNROLL, body, 0)


def gather_rows(surface_cell, table):
    rows = surface_cell.shape[0]
    return pl.pallas_call(
        gather_kernel,
        grid_spec=pltpu.PrefetchScalarGridSpec(
            num_scalar_prefetch=1,
            grid=(1,),
            in_specs=[pl.BlockSpec(table.shape, lambda i, c: (0, 0))],
            out_specs=pl.BlockSpec((rows, table.shape[1]), lambda i, c: (0, 0)),
        ),
        out_shape=jax.ShapeDtypeStruct((rows, table.shape[1]), table.dtype),
        compiler_params=pltpu.CompilerParams(vmem_limit_bytes=48 * 1024 * 1024),
    )(surface_cell, table)


MESH_IDS = pl.DeviceIdType.MESH


def reduce_kernel(nx, ny, x_ref, out_ref, part_a, part_b, got_a, got_b, sems):
    b0 = lax.axis_index("gx")
    a0 = lax.axis_index("gy")
    barrier = pltpu.get_barrier_semaphore()
    for t in range(1, ny):
        pl.semaphore_signal(barrier, inc=1, device_id=(b0, lax.rem(a0 + t, ny)), device_id_type=MESH_IDS)
    for t in range(1, nx):
        pl.semaphore_signal(barrier, inc=1, device_id=(lax.rem(b0 + t, nx), a0), device_id_type=MESH_IDS)
    pl.semaphore_wait(barrier, nx + ny - 2)

    def exchange(phase, src_of, dst_of, peers, along_x):
        copies = []
        for t in range(1, peers):
            if along_x:
                peer = lax.rem(b0 + t, nx)
                me, device = b0, (peer, a0)
            else:
                peer = lax.rem(a0 + t, ny)
                me, device = a0, (b0, peer)
            copy = pltpu.make_async_remote_copy(
                src_ref=src_of(peer),
                dst_ref=dst_of(me),
                send_sem=sems.at[phase, 0, peer],
                recv_sem=sems.at[phase, 1, me],
                device_id=device,
                device_id_type=MESH_IDS,
            )
            copy.start()
            copies.append((peer, device))
        for peer, device in copies:
            pltpu.make_async_remote_copy(
                src_ref=src_of(peer),
                dst_ref=dst_of(peer),
                send_sem=sems.at[phase, 0, peer],
                recv_sem=sems.at[phase, 1, peer],
                device_id=device,
                device_id_type=MESH_IDS,
            ).wait()

    exchange(0, lambda a: x_ref.at[a], lambda a: got_a.at[a], ny, False)
    got_a[a0] = x_ref[a0]
    part_a[...] = jnp.sum(got_a[...], axis=0)
    exchange(1, lambda b: part_a, lambda b: got_b.at[b], nx, True)
    got_b[b0] = part_a[...]
    part_b[...] = jnp.sum(got_b[...], axis=0)
    exchange(2, lambda a: part_b, lambda a: out_ref.at[a], ny, False)
    out_ref[a0] = part_b[...]


def exchange_kernel(nx, ny, x_ref, out_ref, landing, send_sems, recv_sems):
    total = nx * ny
    me = lax.axis_index("gx") * ny + lax.axis_index("gy")
    barrier = pltpu.get_barrier_semaphore()

    def where(peer):
        return (peer // ny, lax.rem(peer, ny))

    @pl.loop(1, total)
    def _(t):
        peer = lax.rem(me + t, total)
        pl.semaphore_signal(barrier, inc=1, device_id=where(peer), device_id_type=MESH_IDS)

    pl.semaphore_wait(barrier, total - 1)

    @pl.loop(1, total)
    def _(t):
        peer = lax.rem(me + t, total)
        pltpu.make_async_remote_copy(
            src_ref=x_ref.at[peer],
            dst_ref=landing.at[me],
            send_sem=send_sems.at[peer],
            recv_sem=recv_sems.at[me],
            device_id=where(peer),
            device_id_type=MESH_IDS,
        ).start()

    landing[me] = x_ref[me]

    @pl.loop(1, total)
    def _(t):
        peer = lax.rem(me + t, total)
        pltpu.make_async_remote_copy(
            src_ref=x_ref.at[peer],
            dst_ref=landing.at[peer],
            send_sem=send_sems.at[peer],
            recv_sem=recv_sems.at[peer],
            device_id=where(peer),
            device_id_type=MESH_IDS,
        ).wait()

    out_ref[...] = landing[...]


def exchange(blocks, exchange_id):
    nx = lax.axis_size("gx")
    ny = lax.axis_size("gy")
    return pl.pallas_call(
        functools.partial(exchange_kernel, nx, ny),
        in_specs=[pl.BlockSpec(memory_space=pltpu.VMEM)],
        out_specs=pl.BlockSpec(memory_space=pltpu.VMEM),
        out_shape=jax.ShapeDtypeStruct(blocks.shape, blocks.dtype),
        scratch_shapes=[
            pltpu.VMEM(blocks.shape, blocks.dtype),
            pltpu.SemaphoreType.DMA((nx * ny,)),
            pltpu.SemaphoreType.DMA((nx * ny,)),
        ],
        compiler_params=pltpu.CompilerParams(collective_id=exchange_id, has_side_effects=True),
    )(blocks)


def sum_over_devices(partial, owners):
    nx = lax.axis_size("gx")
    ny = lax.axis_size("gy")
    lanes = partial.size // (nx * ny)
    shaped = partial.reshape(ny, nx, lanes)
    peers = max(nx, ny)
    total = pl.pallas_call(
        functools.partial(reduce_kernel, nx, ny),
        in_specs=[pl.BlockSpec(memory_space=pltpu.VMEM)],
        out_specs=pl.BlockSpec(memory_space=pltpu.VMEM),
        out_shape=jax.ShapeDtypeStruct(shaped.shape, jnp.float32),
        scratch_shapes=[
            pltpu.VMEM((nx, lanes), jnp.float32),
            pltpu.VMEM((nx, lanes), jnp.float32),
            pltpu.VMEM((ny, nx, lanes), jnp.float32),
            pltpu.VMEM((nx, nx, lanes), jnp.float32),
            pltpu.SemaphoreType.DMA((3, 2, peers)),
        ],
        compiler_params=pltpu.CompilerParams(collective_id=0, has_side_effects=True),
    )(shaped)
    return total.reshape(partial.shape)


def sum_over_devices_a2a(partial, owners):
    chunks = partial.reshape(owners, -1)
    got = lax.all_to_all(chunks, ("gx", "gy"), split_axis=0, concat_axis=0, tiled=True)
    mine = jnp.sum(got, axis=0, keepdims=True)
    spread = jnp.broadcast_to(mine, chunks.shape)
    full = lax.all_to_all(spread, ("gx", "gy"), split_axis=0, concat_axis=0, tiled=True)
    return full.reshape(partial.shape)


def on_device(cell_state, geometry, surface_cell, counts, wavenumbers, target, direction_weight):
    owners = lax.axis_size(("gx", "gy"))
    rows_dev = surface_cell.shape[0]
    capacity = rows_dev // owners
    live_own = rows_dev // 4
    count_dirs = target.shape[2]
    num_freqs = wavenumbers.shape[0]
    living = (jnp.arange(rows_dev) < counts[0]).astype(jnp.float32)
    outgoing = (
        jnp.concatenate(
            [gather_rows(surface_cell, cell_state.T).T, geometry, jnp.ones((1, rows_dev), jnp.float32)], axis=0
        )
        * living[None, :]
    )
    outgoing = outgoing.reshape(24, capacity, owners).transpose(2, 0, 1).reshape(owners, -1, 128)
    arrived = exchange(outgoing, 1).reshape(owners, 24, capacity).transpose(1, 0, 2)
    marker = arrived[23]
    per_source = jnp.sum(marker, axis=1).astype(jnp.int32)
    offset = jnp.cumsum(per_source) - per_source
    position = offset[:, None] + jnp.arange(capacity, dtype=jnp.int32)[None, :]
    packed_slot = jnp.where(marker > 0.5, position, live_own).reshape(capacity * owners)
    selector = (packed_slot[:, None] == jnp.arange(live_own, dtype=jnp.int32)[None, :]).astype(jnp.bfloat16)
    compact = permute_columns(arrived[:23].reshape(23, capacity * owners), selector)
    east_x, north_y, upward = directions(count_dirs)
    direction_basis = jnp.stack([jnp.ones_like(east_x), east_x, north_y, upward])

    points = compact[16:19].T
    dirs_block = jnp.broadcast_to(jnp.stack([east_x, north_y, upward])[:, None, :], (3, ROW_CHUNK, count_dirs))
    kernel_all, sums = forward_sums(wavenumbers, points, dirs_block, compact)
    sums = sums[:, :8]
    far_field = sum_over_devices(far_field_of(sums, wavenumbers, direction_basis), owners)
    objective, weights = adjoint_weights(
        far_field, target, direction_weight, wavenumbers, direction_basis
    )

    padded = jnp.concatenate([weights, jnp.zeros_like(weights)], axis=1)
    products = adjoint_products(padded, kernel_all)[:, :8]
    backward = adjoint_sources(products, compact[19:22])
    spread = unpermute_columns(backward, selector)
    spread = spread.reshape(16, owners, capacity).transpose(1, 0, 2).reshape(owners, -1, 128)
    returned = exchange(spread, 2).reshape(owners, 16, capacity).transpose(2, 0, 1).reshape(rows_dev, 16)
    rows_major = returned * living[:, None]
    cell_adjoint = scatter_rows(surface_cell, rows_major, cell_state.shape[1]).T
    return (far_field, objective, cell_adjoint)


def solution(mesh):
    placed = (
        P(None, ("gx", "gy")),
        P(None, ("gx", "gy")),
        P(("gx", "gy")),
        P(("gx", "gy")),
        P(),
        P(),
        P(),
    )
    return jax.shard_map(
        on_device,
        mesh=mesh,
        in_specs=placed,
        out_specs=(P(), P(), P(None, ("gx", "gy"))),
        check_vma=False,
    )
```

```python
import functools
import math

import jax
import jax.numpy as jnp
from jax import lax
from jax.experimental import pallas as pl
from jax.experimental.pallas import tpu as pltpu
from jax.sharding import PartitionSpec as P

GOLDEN = math.pi * (3.0 - math.sqrt(5.0))
PI_A = round(math.pi * 32768.0) / 32768.0
PI_B = math.pi - PI_A
INV_PI = 1.0 / math.pi
SIN_C = [-0.16666657019913644, 0.00833301540393062, -0.00019806478078586938, 2.599750005030262e-06]
COS_C = [-0.4999993175258851, 0.041663973510963626, -0.0013855797199316853, 2.3191254010748703e-05]
SINPI_C = [3.141592578574041, -5.1677067848796066, 2.5500297991194887, -0.5980355679943354, 0.07720094563063706]
COSPI_C = [-4.934795411606951, 4.05844824012755, -1.332068921858188, 0.22002136541700046]


ROOT2 = math.sqrt(2.0)


def sincos_half_turns(v):
    w = v - jnp.floor(v + 0.5)
    z = w * w
    ps = SINPI_C[-1] * ROOT2
    for c in SINPI_C[-2::-1]:
        ps = c * ROOT2 + z * ps
    pc = COSPI_C[-1] * ROOT2
    for c in COSPI_C[-2::-1]:
        pc = c * ROOT2 + z * pc
    sine_half = w * ps
    cosine_half = ROOT2 + z * pc
    return (cosine_half * cosine_half - 1.0, sine_half * cosine_half)


def sincos_turns(u):
    n = jnp.floor(u + 0.5)
    w = u - n
    z = w * w
    ps = SINPI_C[-1]
    for c in SINPI_C[-2::-1]:
        ps = c + z * ps
    pc = COSPI_C[-1]
    for c in COSPI_C[-2::-1]:
        pc = c + z * pc
    half = n * 0.5
    sign = 1.0 - 4.0 * (half - jnp.floor(half))
    return (sign * (1.0 + z * pc), (sign * w) * ps)


def sincos(theta):
    n = jnp.floor(theta * INV_PI + 0.5)
    r = (theta - n * PI_A) - n * PI_B
    z = r * r
    ps = SIN_C[-1]
    for c in SIN_C[-2::-1]:
        ps = c + z * ps
    pc = COS_C[-1]
    for c in COS_C[-2::-1]:
        pc = c + z * pc
    half = n * 0.5
    sign = 1.0 - 4.0 * (half - jnp.floor(half))
    return (sign * (1.0 + z * pc), sign * (r + (r * z) * ps))


def directions(count_dirs):
    lattice = jnp.arange(count_dirs).astype(jnp.float32)
    height = 1.0 - (2.0 * lattice + 1.0) / count_dirs
    radius_xy = jnp.sqrt(1.0 - height * height)
    azimuth = jnp.mod(lattice * GOLDEN, 2.0 * math.pi)
    return (radius_xy * jnp.cos(azimuth), radius_xy * jnp.sin(azimuth), height)


def kernel_block(points, wavenum, east_x, north_y, upward):
    phases = wavenum * (
        points[0][:, None] * east_x[None, :]
        + points[1][:, None] * north_y[None, :]
        + points[2][:, None] * upward[None, :]
    )
    cosine, sine = sincos(phases)
    return jnp.concatenate([cosine, sine], axis=1).astype(jnp.bfloat16)


def source_rows(rows_block, level):
    surface_area = rows_block[22]
    normal = rows_block[19:22]
    pressure_real = rows_block[level] * surface_area
    pressure_imag = rows_block[4 + level] * surface_area
    return jnp.stack(
        [
            rows_block[8 + level] * surface_area,
            normal[0] * pressure_real,
            normal[1] * pressure_real,
            normal[2] * pressure_real,
            rows_block[12 + level] * surface_area,
            normal[0] * pressure_imag,
            normal[1] * pressure_imag,
            normal[2] * pressure_imag,
        ]
    ).astype(jnp.bfloat16)


def far_field_of(sums, wavenumbers, direction_basis):
    half_width = sums.shape[2] // 2
    cosine_part = sums[:, :, :half_width]
    sine_part = sums[:, :, half_width:]
    real_q = cosine_part[:, 0:4] + sine_part[:, 4:8]
    imag_q = cosine_part[:, 4:8] - sine_part[:, 0:4]
    real_z = jnp.sum(direction_basis[None] * real_q, axis=1)
    imag_z = jnp.sum(direction_basis[None] * imag_q, axis=1)
    wavenum = wavenumbers[:, None]
    return jnp.stack([-wavenum * imag_z, wavenum * real_z], axis=1)


def adjoint_weights(far_field, target, direction_weight, wavenumbers, direction_basis):
    count_dirs = far_field.shape[2]
    mismatch = far_field - target
    objective = jnp.sum(direction_weight * mismatch * mismatch) / count_dirs
    gradient = 2.0 * direction_weight * mismatch / count_dirs
    wavenum = wavenumbers[:, None]
    real_gz = wavenum * gradient[:, 1]
    imag_gz = -wavenum * gradient[:, 0]
    real_gq = direction_basis[None] * real_gz[:, None]
    imag_gq = direction_basis[None] * imag_gz[:, None]
    upper_half = jnp.concatenate([real_gq, -imag_gq], axis=2)
    lower_half = jnp.concatenate([imag_gq, real_gq], axis=2)
    return (objective, jnp.concatenate([upper_half, lower_half], axis=1).astype(jnp.bfloat16))


def adjoint_sources(products, normal):
    pressure_real = jnp.sum(normal[None] * products[:, 1:4], axis=1)
    pressure_imag = jnp.sum(normal[None] * products[:, 5:8], axis=1)
    return jnp.concatenate([pressure_real, pressure_imag, products[:, 0], products[:, 4]], axis=0)


ROW_BLOCK = 128
ADJ_BLOCK = 256
ROW_CHUNK = 16
LANE_CHUNK = 256


def forward_kernel(wave_ref, pts_ref, dirs_ref, rows_ref, cs_ref, q_ref, src_scr):
    step = pl.program_id(0)
    num_freqs = cs_ref.shape[0]
    count_dirs = dirs_ref.shape[2]
    turns = [wave_ref[level] * (0.5 * INV_PI) for level in range(num_freqs)]

    @pl.loop(0, ROW_BLOCK // ROW_CHUNK)
    def _(i):
        r0 = pl.multiple_of(i * ROW_CHUNK, ROW_CHUNK)
        coords = [
            jnp.broadcast_to(pts_ref[pl.ds(r0, ROW_CHUNK), c : c + 1], (ROW_CHUNK, LANE_CHUNK))
            for c in range(3)
        ]
        for j0 in range(0, count_dirs, LANE_CHUNK):
            lanes = slice(j0, j0 + LANE_CHUNK)
            along = (
                coords[0] * dirs_ref[0, :, lanes]
                + coords[1] * dirs_ref[1, :, lanes]
                + coords[2] * dirs_ref[2, :, lanes]
            )
            for level in range(num_freqs):
                cosine, sine = sincos_half_turns(turns[level] * along)
                cs_ref[level, pl.ds(r0, ROW_CHUNK), lanes] = cosine.astype(jnp.bfloat16)
                cs_ref[level, pl.ds(r0, ROW_CHUNK), j0 + count_dirs : j0 + count_dirs + LANE_CHUNK] = (
                    sine.astype(jnp.bfloat16)
                )

    @pl.when(step == 0)
    def _():
        q_ref[...] = jnp.zeros_like(q_ref)

    area = rows_ref[22:23, :]
    src_scr[...] = jnp.zeros_like(src_scr)
    for level in range(num_freqs):
        pressure_real = rows_ref[level : level + 1, :] * area
        pressure_imag = rows_ref[4 + level : 5 + level, :] * area
        src_scr[0:1, :] = rows_ref[8 + level : 9 + level, :] * area
        src_scr[4:5, :] = rows_ref[12 + level : 13 + level, :] * area
        for c in range(3):
            normal = rows_ref[19 + c : 20 + c, :]
            src_scr[1 + c : 2 + c, :] = normal * pressure_real
            src_scr[5 + c : 6 + c, :] = normal * pressure_imag
        source = src_scr[...].astype(jnp.bfloat16)
        q_ref[level] += jnp.dot(source, cs_ref[level], preferred_element_type=jnp.float32)


def forward_sums(wavenumbers, points, dirs_block, compact):
    num_freqs = wavenumbers.shape[0]
    rows = points.shape[0]
    count_dirs = dirs_block.shape[2]
    grid = (rows // ROW_BLOCK,)
    return pl.pallas_call(
        forward_kernel,
        grid=grid,
        in_specs=[
            pl.BlockSpec(memory_space=pltpu.SMEM),
            pl.BlockSpec((ROW_BLOCK, 3), lambda b: (b, 0)),
            pl.BlockSpec(dirs_block.shape, lambda b: (0, 0, 0)),
            pl.BlockSpec((compact.shape[0], ROW_BLOCK), lambda b: (0, b)),
        ],
        out_specs=[
            pl.BlockSpec((num_freqs, ROW_BLOCK, 2 * count_dirs), lambda b: (0, b, 0)),
            pl.BlockSpec((num_freqs, 16, 2 * count_dirs), lambda b: (0, 0, 0)),
        ],
        out_shape=[
            jax.ShapeDtypeStruct((num_freqs, rows, 2 * count_dirs), jnp.bfloat16),
            jax.ShapeDtypeStruct((num_freqs, 16, 2 * count_dirs), jnp.float32),
        ],
        scratch_shapes=[pltpu.VMEM((16, ROW_BLOCK), jnp.float32)],
        compiler_params=pltpu.CompilerParams(
            dimension_semantics=("arbitrary",), vmem_limit_bytes=48 * 1024 * 1024
        ),
        cost_estimate=pl.CostEstimate(
            flops=2 * 16 * rows * 2 * count_dirs * num_freqs + 60 * rows * count_dirs * num_freqs,
            transcendentals=0,
            bytes_accessed=2 * rows * 2 * count_dirs * num_freqs,
        ),
    )(wavenumbers, points, dirs_block, compact)


def adjoint_kernel(w_ref, cs_ref, out_ref):
    for level in range(cs_ref.shape[0]):
        out_ref[level] = lax.dot_general(
            w_ref[level], cs_ref[level], (((1,), (1,)), ((), ())), preferred_element_type=jnp.float32
        )


def adjoint_products(weights, kernel_all):
    num_freqs, rows, width = kernel_all.shape
    return pl.pallas_call(
        adjoint_kernel,
        grid=(rows // ADJ_BLOCK,),
        in_specs=[
            pl.BlockSpec(weights.shape, lambda b: (0, 0, 0)),
            pl.BlockSpec((num_freqs, ADJ_BLOCK, width), lambda b: (0, b, 0)),
        ],
        out_specs=pl.BlockSpec((num_freqs, weights.shape[1], ADJ_BLOCK), lambda b: (0, 0, b)),
        out_shape=jax.ShapeDtypeStruct((num_freqs, weights.shape[1], rows), jnp.float32),
        compiler_params=pltpu.CompilerParams(
            dimension_semantics=("arbitrary",), vmem_limit_bytes=48 * 1024 * 1024
        ),
        cost_estimate=pl.CostEstimate(
            flops=2 * weights.shape[1] * rows * width * num_freqs,
            transcendentals=0,
            bytes_accessed=2 * rows * width * num_freqs,
        ),
    )(weights, kernel_all)


def split_bf16(values):
    high = lax.reduce_precision(values, exponent_bits=8, mantissa_bits=7)
    rest = values - high
    middle = lax.reduce_precision(rest, exponent_bits=8, mantissa_bits=7)
    low = rest - middle
    return jnp.concatenate([high, middle, low], axis=0).astype(jnp.bfloat16)


def join_parts(product, channels):
    return (product[:channels] + product[channels : 2 * channels]) + product[2 * channels :]


def permute_columns(values, selector):
    product = jnp.dot(split_bf16(values), selector, preferred_element_type=jnp.float32)
    return join_parts(product, values.shape[0])


def unpermute_columns(values, selector):
    product = lax.dot_general(
        split_bf16(values), selector, (((1,), (1,)), ((), ())), preferred_element_type=jnp.float32
    )
    return join_parts(product, values.shape[0])


CHAINS = 4


def scatter_kernel(cell_ref, rows_ref, out_ref, *accs):
    for acc in accs:
        acc[...] = jnp.zeros_like(acc)
    chains = len(accs)

    def body(i, carry):
        for k in range(chains):
            row = i * chains + k
            cell = cell_ref[row]
            accs[k][pl.ds(cell, 1), :] += rows_ref[pl.ds(row, 1), :]
        return carry

    lax.fori_loop(0, rows_ref.shape[0] // chains, body, 0)
    out_ref[...] = ((accs[0][...] + accs[1][...]) + (accs[2][...] + accs[3][...])).T


def scatter_rows(surface_cell, rows_major, cells):
    width = rows_major.shape[1]
    return pl.pallas_call(
        scatter_kernel,
        grid_spec=pltpu.PrefetchScalarGridSpec(
            num_scalar_prefetch=1,
            grid=(1,),
            in_specs=[pl.BlockSpec(rows_major.shape, lambda i, c: (0, 0))],
            out_specs=pl.BlockSpec((width, cells), lambda i, c: (0, 0)),
            scratch_shapes=[pltpu.VMEM((cells, width), jnp.float32) for _ in range(CHAINS)],
        ),
        out_shape=jax.ShapeDtypeStruct((width, cells), jnp.float32),
        compiler_params=pltpu.CompilerParams(vmem_limit_bytes=48 * 1024 * 1024),
    )(surface_cell, rows_major)


GATHER_UNROLL = 8


def gather_kernel(cell_ref, state_ref, out_ref, table_ref):
    table_ref[...] = state_ref[...].T

    def body(i, carry):
        for k in range(GATHER_UNROLL):
            row = i * GATHER_UNROLL + k
            out_ref[pl.ds(row, 1), :] = table_ref[pl.ds(cell_ref[row], 1), :]
        return carry

    lax.fori_loop(0, out_ref.shape[0] // GATHER_UNROLL, body, 0)


def gather_rows(surface_cell, state):
    rows = surface_cell.shape[0]
    channels, cells = state.shape
    return pl.pallas_call(
        gather_kernel,
        grid_spec=pltpu.PrefetchScalarGridSpec(
            num_scalar_prefetch=1,
            grid=(1,),
            in_specs=[pl.BlockSpec(state.shape, lambda i, c: (0, 0))],
            out_specs=pl.BlockSpec((rows, channels), lambda i, c: (0, 0)),
            scratch_shapes=[pltpu.VMEM((cells, channels), state.dtype)],
        ),
        out_shape=jax.ShapeDtypeStruct((rows, channels), state.dtype),
        compiler_params=pltpu.CompilerParams(vmem_limit_bytes=48 * 1024 * 1024),
    )(surface_cell, state)


MESH_IDS = pl.DeviceIdType.MESH


def reduce_kernel(nx, ny, x_ref, out_ref, part_a, part_b, got_a, got_b, sems):
    b0 = lax.axis_index("gx")
    a0 = lax.axis_index("gy")
    barrier = pltpu.get_barrier_semaphore()
    for t in range(1, ny):
        pl.semaphore_signal(barrier, inc=1, device_id=(b0, lax.rem(a0 + t, ny)), device_id_type=MESH_IDS)
    for t in range(1, nx):
        pl.semaphore_signal(barrier, inc=1, device_id=(lax.rem(b0 + t, nx), a0), device_id_type=MESH_IDS)
    pl.semaphore_wait(barrier, nx + ny - 2)

    def exchange(phase, src_of, dst_of, peers, along_x):
        copies = []
        for t in range(1, peers):
            if along_x:
                peer = lax.rem(b0 + t, nx)
                me, device = b0, (peer, a0)
            else:
                peer = lax.rem(a0 + t, ny)
                me, device = a0, (b0, peer)
            copy = pltpu.make_async_remote_copy(
                src_ref=src_of(peer),
                dst_ref=dst_of(me),
                send_sem=sems.at[phase, 0, peer],
                recv_sem=sems.at[phase, 1, me],
                device_id=device,
                device_id_type=MESH_IDS,
            )
            copy.start()
            copies.append((peer, device))
        for peer, device in copies:
            pltpu.make_async_remote_copy(
                src_ref=src_of(peer),
                dst_ref=dst_of(peer),
                send_sem=sems.at[phase, 0, peer],
                recv_sem=sems.at[phase, 1, peer],
                device_id=device,
                device_id_type=MESH_IDS,
            ).wait()

    exchange(0, lambda a: x_ref.at[a], lambda a: got_a.at[a], ny, False)
    got_a[a0] = x_ref[a0]
    part_a[...] = jnp.sum(got_a[...], axis=0)
    exchange(1, lambda b: part_a, lambda b: got_b.at[b], nx, True)
    got_b[b0] = part_a[...]
    part_b[...] = jnp.sum(got_b[...], axis=0)
    exchange(2, lambda a: part_b, lambda a: out_ref.at[a], ny, False)
    out_ref[a0] = part_b[...]


def exchange_kernel(nx, ny, x_ref, out_ref, landing, send_sems, recv_sems):
    total = nx * ny
    me = lax.axis_index("gx") * ny + lax.axis_index("gy")
    barrier = pltpu.get_barrier_semaphore()

    def where(peer):
        return (peer // ny, lax.rem(peer, ny))

    @pl.loop(1, total)
    def _(t):
        peer = lax.rem(me + t, total)
        pl.semaphore_signal(barrier, inc=1, device_id=where(peer), device_id_type=MESH_IDS)

    pl.semaphore_wait(barrier, total - 1)

    @pl.loop(1, total)
    def _(t):
        peer = lax.rem(me + t, total)
        pltpu.make_async_remote_copy(
            src_ref=x_ref.at[peer],
            dst_ref=landing.at[me],
            send_sem=send_sems.at[peer],
            recv_sem=recv_sems.at[me],
            device_id=where(peer),
            device_id_type=MESH_IDS,
        ).start()

    landing[me] = x_ref[me]

    @pl.loop(1, total)
    def _(t):
        peer = lax.rem(me + t, total)
        pltpu.make_async_remote_copy(
            src_ref=x_ref.at[peer],
            dst_ref=landing.at[peer],
            send_sem=send_sems.at[peer],
            recv_sem=recv_sems.at[peer],
            device_id=where(peer),
            device_id_type=MESH_IDS,
        ).wait()

    out_ref[...] = landing[...]


def exchange(blocks, exchange_id):
    nx = lax.axis_size("gx")
    ny = lax.axis_size("gy")
    return pl.pallas_call(
        functools.partial(exchange_kernel, nx, ny),
        in_specs=[pl.BlockSpec(memory_space=pltpu.VMEM)],
        out_specs=pl.BlockSpec(memory_space=pltpu.VMEM),
        out_shape=jax.ShapeDtypeStruct(blocks.shape, blocks.dtype),
        scratch_shapes=[
            pltpu.VMEM(blocks.shape, blocks.dtype),
            pltpu.SemaphoreType.DMA((nx * ny,)),
            pltpu.SemaphoreType.DMA((nx * ny,)),
        ],
        compiler_params=pltpu.CompilerParams(collective_id=exchange_id, has_side_effects=True),
    )(blocks)


def sum_over_devices(partial, owners):
    nx = lax.axis_size("gx")
    ny = lax.axis_size("gy")
    lanes = partial.size // (nx * ny)
    shaped = partial.reshape(ny, nx, lanes)
    peers = max(nx, ny)
    total = pl.pallas_call(
        functools.partial(reduce_kernel, nx, ny),
        in_specs=[pl.BlockSpec(memory_space=pltpu.VMEM)],
        out_specs=pl.BlockSpec(memory_space=pltpu.VMEM),
        out_shape=jax.ShapeDtypeStruct(shaped.shape, jnp.float32),
        scratch_shapes=[
            pltpu.VMEM((nx, lanes), jnp.float32),
            pltpu.VMEM((nx, lanes), jnp.float32),
            pltpu.VMEM((ny, nx, lanes), jnp.float32),
            pltpu.VMEM((nx, nx, lanes), jnp.float32),
            pltpu.SemaphoreType.DMA((3, 2, peers)),
        ],
        compiler_params=pltpu.CompilerParams(collective_id=0, has_side_effects=True),
    )(shaped)
    return total.reshape(partial.shape)


def sum_over_devices_a2a(partial, owners):
    chunks = partial.reshape(owners, -1)
    got = lax.all_to_all(chunks, ("gx", "gy"), split_axis=0, concat_axis=0, tiled=True)
    mine = jnp.sum(got, axis=0, keepdims=True)
    spread = jnp.broadcast_to(mine, chunks.shape)
    full = lax.all_to_all(spread, ("gx", "gy"), split_axis=0, concat_axis=0, tiled=True)
    return full.reshape(partial.shape)


def on_device(cell_state, geometry, surface_cell, counts, wavenumbers, target, direction_weight):
    owners = lax.axis_size(("gx", "gy"))
    rows_dev = surface_cell.shape[0]
    capacity = rows_dev // owners
    live_own = rows_dev // 4
    count_dirs = target.shape[2]
    num_freqs = wavenumbers.shape[0]
    living = (jnp.arange(rows_dev) < counts[0]).astype(jnp.float32)
    outgoing = (
        jnp.concatenate(
            [gather_rows(surface_cell, cell_state).T, geometry, jnp.ones((1, rows_dev), jnp.float32)], axis=0
        )
        * living[None, :]
    )
    outgoing = outgoing.reshape(24, capacity, owners).transpose(2, 0, 1).reshape(owners, -1, 128)
    arrived = exchange(outgoing, 1).reshape(owners, 24, capacity).transpose(1, 0, 2)
    marker = arrived[23]
    per_source = jnp.sum(marker, axis=1).astype(jnp.int32)
    offset = jnp.cumsum(per_source) - per_source
    position = offset[:, None] + jnp.arange(capacity, dtype=jnp.int32)[None, :]
    packed_slot = jnp.where(marker > 0.5, position, live_own).reshape(capacity * owners)
    selector = (packed_slot[:, None] == jnp.arange(live_own, dtype=jnp.int32)[None, :]).astype(jnp.bfloat16)
    compact = permute_columns(arrived[:23].reshape(23, capacity * owners), selector)
    east_x, north_y, upward = directions(count_dirs)
    direction_basis = jnp.stack([jnp.ones_like(east_x), east_x, north_y, upward])

    points = compact[16:19].T
    dirs_block = jnp.broadcast_to(jnp.stack([east_x, north_y, upward])[:, None, :], (3, ROW_CHUNK, count_dirs))
    kernel_all, sums = forward_sums(wavenumbers, points, dirs_block, compact)
    sums = sums[:, :8]
    far_field = sum_over_devices(far_field_of(sums, wavenumbers, direction_basis), owners)
    objective, weights = adjoint_weights(
        far_field, target, direction_weight, wavenumbers, direction_basis
    )

    padded = jnp.concatenate([weights, jnp.zeros_like(weights)], axis=1)
    products = adjoint_products(padded, kernel_all)[:, :8]
    backward = adjoint_sources(products, compact[19:22])
    spread = unpermute_columns(backward, selector)
    spread = spread.reshape(16, owners, capacity).transpose(1, 0, 2).reshape(owners, -1, 128)
    returned = exchange(spread, 2).reshape(owners, 16, capacity).transpose(2, 0, 1).reshape(rows_dev, 16)
    rows_major = returned * living[:, None]
    cell_adjoint = scatter_rows(surface_cell, rows_major, cell_state.shape[1])
    return (far_field, objective, cell_adjoint)


def solution(mesh):
    placed = (
        P(None, ("gx", "gy")),
        P(None, ("gx", "gy")),
        P(("gx", "gy")),
        P(("gx", "gy")),
        P(),
        P(),
        P(),
    )
    return jax.shard_map(
        on_device,
        mesh=mesh,
        in_specs=placed,
        out_specs=(P(), P(), P(None, ("gx", "gy"))),
        check_vma=False,
    )
```

```python
import functools
import math

import jax
import jax.numpy as jnp
from jax import lax
from jax.experimental import pallas as pl
from jax.experimental.pallas import tpu as pltpu
from jax.sharding import PartitionSpec as P

GOLDEN = math.pi * (3.0 - math.sqrt(5.0))
PI_A = round(math.pi * 32768.0) / 32768.0
PI_B = math.pi - PI_A
INV_PI = 1.0 / math.pi
SIN_C = [-0.16666657019913644, 0.00833301540393062, -0.00019806478078586938, 2.599750005030262e-06]
COS_C = [-0.4999993175258851, 0.041663973510963626, -0.0013855797199316853, 2.3191254010748703e-05]
SINPI_C = [3.141592578574041, -5.1677067848796066, 2.5500297991194887, -0.5980355679943354, 0.07720094563063706]
COSPI_C = [-4.934795411606951, 4.05844824012755, -1.332068921858188, 0.22002136541700046]


ROOT2 = math.sqrt(2.0)


def sincos_half_turns(v):
    w = v - jnp.floor(v + 0.5)
    z = w * w
    ps = SINPI_C[-1] * ROOT2
    for c in SINPI_C[-2::-1]:
        ps = c * ROOT2 + z * ps
    pc = COSPI_C[-1] * ROOT2
    for c in COSPI_C[-2::-1]:
        pc = c * ROOT2 + z * pc
    sine_half = w * ps
    cosine_half = ROOT2 + z * pc
    return (cosine_half * cosine_half - 1.0, sine_half * cosine_half)


def sincos_turns(u):
    n = jnp.floor(u + 0.5)
    w = u - n
    z = w * w
    ps = SINPI_C[-1]
    for c in SINPI_C[-2::-1]:
        ps = c + z * ps
    pc = COSPI_C[-1]
    for c in COSPI_C[-2::-1]:
        pc = c + z * pc
    half = n * 0.5
    sign = 1.0 - 4.0 * (half - jnp.floor(half))
    return (sign * (1.0 + z * pc), (sign * w) * ps)


def sincos(theta):
    n = jnp.floor(theta * INV_PI + 0.5)
    r = (theta - n * PI_A) - n * PI_B
    z = r * r
    ps = SIN_C[-1]
    for c in SIN_C[-2::-1]:
        ps = c + z * ps
    pc = COS_C[-1]
    for c in COS_C[-2::-1]:
        pc = c + z * pc
    half = n * 0.5
    sign = 1.0 - 4.0 * (half - jnp.floor(half))
    return (sign * (1.0 + z * pc), sign * (r + (r * z) * ps))


def directions(count_dirs):
    lattice = jnp.arange(count_dirs).astype(jnp.float32)
    height = 1.0 - (2.0 * lattice + 1.0) / count_dirs
    radius_xy = jnp.sqrt(1.0 - height * height)
    azimuth = jnp.mod(lattice * GOLDEN, 2.0 * math.pi)
    return (radius_xy * jnp.cos(azimuth), radius_xy * jnp.sin(azimuth), height)


def kernel_block(points, wavenum, east_x, north_y, upward):
    phases = wavenum * (
        points[0][:, None] * east_x[None, :]
        + points[1][:, None] * north_y[None, :]
        + points[2][:, None] * upward[None, :]
    )
    cosine, sine = sincos(phases)
    return jnp.concatenate([cosine, sine], axis=1).astype(jnp.bfloat16)


def source_rows(rows_block, level):
    surface_area = rows_block[22]
    normal = rows_block[19:22]
    pressure_real = rows_block[level] * surface_area
    pressure_imag = rows_block[4 + level] * surface_area
    return jnp.stack(
        [
            rows_block[8 + level] * surface_area,
            normal[0] * pressure_real,
            normal[1] * pressure_real,
            normal[2] * pressure_real,
            rows_block[12 + level] * surface_area,
            normal[0] * pressure_imag,
            normal[1] * pressure_imag,
            normal[2] * pressure_imag,
        ]
    ).astype(jnp.bfloat16)


def far_field_of(sums, wavenumbers, direction_basis):
    half_width = sums.shape[2] // 2
    cosine_part = sums[:, :, :half_width]
    sine_part = sums[:, :, half_width:]
    real_q = cosine_part[:, 0:4] + sine_part[:, 4:8]
    imag_q = cosine_part[:, 4:8] - sine_part[:, 0:4]
    real_z = jnp.sum(direction_basis[None] * real_q, axis=1)
    imag_z = jnp.sum(direction_basis[None] * imag_q, axis=1)
    wavenum = wavenumbers[:, None]
    return jnp.stack([-wavenum * imag_z, wavenum * real_z], axis=1)


def adjoint_weights(far_field, target, direction_weight, wavenumbers, direction_basis):
    count_dirs = far_field.shape[2]
    mismatch = far_field - target
    objective = jnp.sum(direction_weight * mismatch * mismatch) / count_dirs
    gradient = 2.0 * direction_weight * mismatch / count_dirs
    wavenum = wavenumbers[:, None]
    real_gz = wavenum * gradient[:, 1]
    imag_gz = -wavenum * gradient[:, 0]
    real_gq = direction_basis[None] * real_gz[:, None]
    imag_gq = direction_basis[None] * imag_gz[:, None]
    upper_half = jnp.concatenate([real_gq, -imag_gq], axis=2)
    lower_half = jnp.concatenate([imag_gq, real_gq], axis=2)
    return (objective, jnp.concatenate([upper_half, lower_half], axis=1).astype(jnp.bfloat16))


def adjoint_sources(products, normal):
    pressure_real = jnp.sum(normal[None] * products[:, 1:4], axis=1)
    pressure_imag = jnp.sum(normal[None] * products[:, 5:8], axis=1)
    return jnp.concatenate([pressure_real, pressure_imag, products[:, 0], products[:, 4]], axis=0)


ROW_BLOCK = 128
ADJ_BLOCK = 256
ROW_CHUNK = 16
LANE_CHUNK = 256


def forward_kernel(wave_ref, pts_ref, dirs_ref, rows_ref, cs_ref, q_ref, src_scr):
    step = pl.program_id(0)
    num_freqs = cs_ref.shape[0]
    count_dirs = dirs_ref.shape[2]
    turns = [wave_ref[level] * (0.5 * INV_PI) for level in range(num_freqs)]

    @pl.loop(0, ROW_BLOCK // ROW_CHUNK)
    def _(i):
        r0 = pl.multiple_of(i * ROW_CHUNK, ROW_CHUNK)
        coords = [
            jnp.broadcast_to(pts_ref[pl.ds(r0, ROW_CHUNK), c : c + 1], (ROW_CHUNK, LANE_CHUNK))
            for c in range(3)
        ]
        for j0 in range(0, count_dirs, LANE_CHUNK):
            lanes = slice(j0, j0 + LANE_CHUNK)
            along = (
                coords[0] * dirs_ref[0, :, lanes]
                + coords[1] * dirs_ref[1, :, lanes]
                + coords[2] * dirs_ref[2, :, lanes]
            )
            for level in range(num_freqs):
                cosine, sine = sincos_half_turns(turns[level] * along)
                cs_ref[level, pl.ds(r0, ROW_CHUNK), lanes] = cosine.astype(jnp.bfloat16)
                cs_ref[level, pl.ds(r0, ROW_CHUNK), j0 + count_dirs : j0 + count_dirs + LANE_CHUNK] = (
                    sine.astype(jnp.bfloat16)
                )

    @pl.when(step == 0)
    def _():
        q_ref[...] = jnp.zeros_like(q_ref)

    area = rows_ref[22:23, :]
    src_scr[...] = jnp.zeros_like(src_scr)
    for level in range(num_freqs):
        pressure_real = rows_ref[level : level + 1, :] * area
        pressure_imag = rows_ref[4 + level : 5 + level, :] * area
        src_scr[0:1, :] = rows_ref[8 + level : 9 + level, :] * area
        src_scr[4:5, :] = rows_ref[12 + level : 13 + level, :] * area
        for c in range(3):
            normal = rows_ref[19 + c : 20 + c, :]
            src_scr[1 + c : 2 + c, :] = normal * pressure_real
            src_scr[5 + c : 6 + c, :] = normal * pressure_imag
        source = src_scr[...].astype(jnp.bfloat16)
        q_ref[level] += jnp.dot(source, cs_ref[level], preferred_element_type=jnp.float32)


def forward_sums(wavenumbers, points, dirs_block, compact):
    num_freqs = wavenumbers.shape[0]
    rows = points.shape[0]
    count_dirs = dirs_block.shape[2]
    grid = (rows // ROW_BLOCK,)
    return pl.pallas_call(
        forward_kernel,
        grid=grid,
        in_specs=[
            pl.BlockSpec(memory_space=pltpu.SMEM),
            pl.BlockSpec((ROW_BLOCK, 3), lambda b: (b, 0)),
            pl.BlockSpec(dirs_block.shape, lambda b: (0, 0, 0)),
            pl.BlockSpec((compact.shape[0], ROW_BLOCK), lambda b: (0, b)),
        ],
        out_specs=[
            pl.BlockSpec((num_freqs, ROW_BLOCK, 2 * count_dirs), lambda b: (0, b, 0)),
            pl.BlockSpec((num_freqs, 16, 2 * count_dirs), lambda b: (0, 0, 0)),
        ],
        out_shape=[
            jax.ShapeDtypeStruct((num_freqs, rows, 2 * count_dirs), jnp.bfloat16),
            jax.ShapeDtypeStruct((num_freqs, 16, 2 * count_dirs), jnp.float32),
        ],
        scratch_shapes=[pltpu.VMEM((16, ROW_BLOCK), jnp.float32)],
        compiler_params=pltpu.CompilerParams(
            dimension_semantics=("arbitrary",), vmem_limit_bytes=48 * 1024 * 1024
        ),
        cost_estimate=pl.CostEstimate(
            flops=2 * 16 * rows * 2 * count_dirs * num_freqs + 60 * rows * count_dirs * num_freqs,
            transcendentals=0,
            bytes_accessed=2 * rows * 2 * count_dirs * num_freqs,
        ),
    )(wavenumbers, points, dirs_block, compact)


def adjoint_kernel(w_ref, cs_ref, out_ref):
    for level in range(cs_ref.shape[0]):
        out_ref[level] = lax.dot_general(
            w_ref[level], cs_ref[level], (((1,), (1,)), ((), ())), preferred_element_type=jnp.float32
        )


def adjoint_products(weights, kernel_all):
    num_freqs, rows, width = kernel_all.shape
    return pl.pallas_call(
        adjoint_kernel,
        grid=(rows // ADJ_BLOCK,),
        in_specs=[
            pl.BlockSpec(weights.shape, lambda b: (0, 0, 0)),
            pl.BlockSpec((num_freqs, ADJ_BLOCK, width), lambda b: (0, b, 0)),
        ],
        out_specs=pl.BlockSpec((num_freqs, weights.shape[1], ADJ_BLOCK), lambda b: (0, 0, b)),
        out_shape=jax.ShapeDtypeStruct((num_freqs, weights.shape[1], rows), jnp.float32),
        compiler_params=pltpu.CompilerParams(
            dimension_semantics=("arbitrary",), vmem_limit_bytes=48 * 1024 * 1024
        ),
        cost_estimate=pl.CostEstimate(
            flops=2 * weights.shape[1] * rows * width * num_freqs,
            transcendentals=0,
            bytes_accessed=2 * rows * width * num_freqs,
        ),
    )(weights, kernel_all)


def split_bf16(values):
    high = lax.reduce_precision(values, exponent_bits=8, mantissa_bits=7)
    rest = values - high
    middle = lax.reduce_precision(rest, exponent_bits=8, mantissa_bits=7)
    low = rest - middle
    return jnp.concatenate([high, middle, low], axis=0).astype(jnp.bfloat16)


def join_parts(product, channels):
    return (product[:channels] + product[channels : 2 * channels]) + product[2 * channels :]


def permute_columns(values, selector):
    product = jnp.dot(split_bf16(values), selector, preferred_element_type=jnp.float32)
    return join_parts(product, values.shape[0])


def unpermute_columns(values, selector):
    product = lax.dot_general(
        split_bf16(values), selector, (((1,), (1,)), ((), ())), preferred_element_type=jnp.float32
    )
    return join_parts(product, values.shape[0])


CHAINS = 8


def scatter_kernel(cell_ref, rows_ref, out_ref, *accs):
    for acc in accs:
        acc[...] = jnp.zeros_like(acc)
    chains = len(accs)

    def body(i, carry):
        for k in range(chains):
            row = i * chains + k
            cell = cell_ref[row]
            accs[k][pl.ds(cell, 1), :] += rows_ref[pl.ds(row, 1), :]
        return carry

    lax.fori_loop(0, rows_ref.shape[0] // chains, body, 0)
    total = accs[0][...]
    for acc in accs[1:]:
        total = total + acc[...]
    out_ref[...] = total.T


def scatter_rows(surface_cell, rows_major, cells):
    width = rows_major.shape[1]
    return pl.pallas_call(
        scatter_kernel,
        grid_spec=pltpu.PrefetchScalarGridSpec(
            num_scalar_prefetch=1,
            grid=(1,),
            in_specs=[pl.BlockSpec(rows_major.shape, lambda i, c: (0, 0))],
            out_specs=pl.BlockSpec((width, cells), lambda i, c: (0, 0)),
            scratch_shapes=[pltpu.VMEM((cells, width), jnp.float32) for _ in range(CHAINS)],
        ),
        out_shape=jax.ShapeDtypeStruct((width, cells), jnp.float32),
        compiler_params=pltpu.CompilerParams(vmem_limit_bytes=48 * 1024 * 1024),
    )(surface_cell, rows_major)


GATHER_UNROLL = 16


def gather_kernel(cell_ref, state_ref, out_ref, table_ref):
    table_ref[...] = state_ref[...].T

    def body(i, carry):
        for k in range(GATHER_UNROLL):
            row = i * GATHER_UNROLL + k
            out_ref[pl.ds(row, 1), :] = table_ref[pl.ds(cell_ref[row], 1), :]
        return carry

    lax.fori_loop(0, out_ref.shape[0] // GATHER_UNROLL, body, 0)


def gather_rows(surface_cell, state):
    rows = surface_cell.shape[0]
    channels, cells = state.shape
    return pl.pallas_call(
        gather_kernel,
        grid_spec=pltpu.PrefetchScalarGridSpec(
            num_scalar_prefetch=1,
            grid=(1,),
            in_specs=[pl.BlockSpec(state.shape, lambda i, c: (0, 0))],
            out_specs=pl.BlockSpec((rows, channels), lambda i, c: (0, 0)),
            scratch_shapes=[pltpu.VMEM((cells, channels), state.dtype)],
        ),
        out_shape=jax.ShapeDtypeStruct((rows, channels), state.dtype),
        compiler_params=pltpu.CompilerParams(vmem_limit_bytes=48 * 1024 * 1024),
    )(surface_cell, state)


MESH_IDS = pl.DeviceIdType.MESH


def reduce_kernel(nx, ny, x_ref, out_ref, part_a, part_b, got_a, got_b, sems):
    b0 = lax.axis_index("gx")
    a0 = lax.axis_index("gy")
    barrier = pltpu.get_barrier_semaphore()
    for t in range(1, ny):
        pl.semaphore_signal(barrier, inc=1, device_id=(b0, lax.rem(a0 + t, ny)), device_id_type=MESH_IDS)
    for t in range(1, nx):
        pl.semaphore_signal(barrier, inc=1, device_id=(lax.rem(b0 + t, nx), a0), device_id_type=MESH_IDS)
    pl.semaphore_wait(barrier, nx + ny - 2)

    def exchange(phase, src_of, dst_of, peers, along_x):
        copies = []
        for t in range(1, peers):
            if along_x:
                peer = lax.rem(b0 + t, nx)
                me, device = b0, (peer, a0)
            else:
                peer = lax.rem(a0 + t, ny)
                me, device = a0, (b0, peer)
            copy = pltpu.make_async_remote_copy(
                src_ref=src_of(peer),
                dst_ref=dst_of(me),
                send_sem=sems.at[phase, 0, peer],
                recv_sem=sems.at[phase, 1, me],
                device_id=device,
                device_id_type=MESH_IDS,
            )
            copy.start()
            copies.append((peer, device))
        for peer, device in copies:
            pltpu.make_async_remote_copy(
                src_ref=src_of(peer),
                dst_ref=dst_of(peer),
                send_sem=sems.at[phase, 0, peer],
                recv_sem=sems.at[phase, 1, peer],
                device_id=device,
                device_id_type=MESH_IDS,
            ).wait()

    exchange(0, lambda a: x_ref.at[a], lambda a: got_a.at[a], ny, False)
    got_a[a0] = x_ref[a0]
    part_a[...] = jnp.sum(got_a[...], axis=0)
    exchange(1, lambda b: part_a, lambda b: got_b.at[b], nx, True)
    got_b[b0] = part_a[...]
    part_b[...] = jnp.sum(got_b[...], axis=0)
    exchange(2, lambda a: part_b, lambda a: out_ref.at[a], ny, False)
    out_ref[a0] = part_b[...]


def exchange_kernel(nx, ny, x_ref, out_ref, landing, send_sems, recv_sems):
    total = nx * ny
    me = lax.axis_index("gx") * ny + lax.axis_index("gy")
    barrier = pltpu.get_barrier_semaphore()

    def where(peer):
        return (peer // ny, lax.rem(peer, ny))

    @pl.loop(1, total)
    def _(t):
        peer = lax.rem(me + t, total)
        pl.semaphore_signal(barrier, inc=1, device_id=where(peer), device_id_type=MESH_IDS)

    pl.semaphore_wait(barrier, total - 1)

    @pl.loop(1, total)
    def _(t):
        peer = lax.rem(me + t, total)
        pltpu.make_async_remote_copy(
            src_ref=x_ref.at[peer],
            dst_ref=landing.at[me],
            send_sem=send_sems.at[peer],
            recv_sem=recv_sems.at[me],
            device_id=where(peer),
            device_id_type=MESH_IDS,
        ).start()

    landing[me] = x_ref[me]

    @pl.loop(1, total)
    def _(t):
        peer = lax.rem(me + t, total)
        pltpu.make_async_remote_copy(
            src_ref=x_ref.at[peer],
            dst_ref=landing.at[peer],
            send_sem=send_sems.at[peer],
            recv_sem=recv_sems.at[peer],
            device_id=where(peer),
            device_id_type=MESH_IDS,
        ).wait()

    out_ref[...] = landing[...]


def exchange(blocks, exchange_id):
    nx = lax.axis_size("gx")
    ny = lax.axis_size("gy")
    return pl.pallas_call(
        functools.partial(exchange_kernel, nx, ny),
        in_specs=[pl.BlockSpec(memory_space=pltpu.VMEM)],
        out_specs=pl.BlockSpec(memory_space=pltpu.VMEM),
        out_shape=jax.ShapeDtypeStruct(blocks.shape, blocks.dtype),
        scratch_shapes=[
            pltpu.VMEM(blocks.shape, blocks.dtype),
            pltpu.SemaphoreType.DMA((nx * ny,)),
            pltpu.SemaphoreType.DMA((nx * ny,)),
        ],
        compiler_params=pltpu.CompilerParams(collective_id=exchange_id, has_side_effects=True),
    )(blocks)


def sum_over_devices(partial, owners):
    nx = lax.axis_size("gx")
    ny = lax.axis_size("gy")
    lanes = partial.size // (nx * ny)
    shaped = partial.reshape(ny, nx, lanes)
    peers = max(nx, ny)
    total = pl.pallas_call(
        functools.partial(reduce_kernel, nx, ny),
        in_specs=[pl.BlockSpec(memory_space=pltpu.VMEM)],
        out_specs=pl.BlockSpec(memory_space=pltpu.VMEM),
        out_shape=jax.ShapeDtypeStruct(shaped.shape, jnp.float32),
        scratch_shapes=[
            pltpu.VMEM((nx, lanes), jnp.float32),
            pltpu.VMEM((nx, lanes), jnp.float32),
            pltpu.VMEM((ny, nx, lanes), jnp.float32),
            pltpu.VMEM((nx, nx, lanes), jnp.float32),
            pltpu.SemaphoreType.DMA((3, 2, peers)),
        ],
        compiler_params=pltpu.CompilerParams(collective_id=0, has_side_effects=True),
    )(shaped)
    return total.reshape(partial.shape)


def sum_over_devices_a2a(partial, owners):
    chunks = partial.reshape(owners, -1)
    got = lax.all_to_all(chunks, ("gx", "gy"), split_axis=0, concat_axis=0, tiled=True)
    mine = jnp.sum(got, axis=0, keepdims=True)
    spread = jnp.broadcast_to(mine, chunks.shape)
    full = lax.all_to_all(spread, ("gx", "gy"), split_axis=0, concat_axis=0, tiled=True)
    return full.reshape(partial.shape)


def on_device(cell_state, geometry, surface_cell, counts, wavenumbers, target, direction_weight):
    owners = lax.axis_size(("gx", "gy"))
    rows_dev = surface_cell.shape[0]
    capacity = rows_dev // owners
    live_own = rows_dev // 4
    count_dirs = target.shape[2]
    num_freqs = wavenumbers.shape[0]
    living = (jnp.arange(rows_dev) < counts[0]).astype(jnp.float32)
    outgoing = (
        jnp.concatenate(
            [gather_rows(surface_cell, cell_state).T, geometry, jnp.ones((1, rows_dev), jnp.float32)], axis=0
        )
        * living[None, :]
    )
    outgoing = outgoing.reshape(24, capacity, owners).transpose(2, 0, 1).reshape(owners, -1, 128)
    arrived = exchange(outgoing, 1).reshape(owners, 24, capacity).transpose(1, 0, 2)
    marker = arrived[23]
    per_source = jnp.sum(marker, axis=1).astype(jnp.int32)
    offset = jnp.cumsum(per_source) - per_source
    position = offset[:, None] + jnp.arange(capacity, dtype=jnp.int32)[None, :]
    packed_slot = jnp.where(marker > 0.5, position, live_own).reshape(capacity * owners)
    selector = (packed_slot[:, None] == jnp.arange(live_own, dtype=jnp.int32)[None, :]).astype(jnp.bfloat16)
    compact = permute_columns(arrived[:23].reshape(23, capacity * owners), selector)
    east_x, north_y, upward = directions(count_dirs)
    direction_basis = jnp.stack([jnp.ones_like(east_x), east_x, north_y, upward])

    points = compact[16:19].T
    dirs_block = jnp.broadcast_to(jnp.stack([east_x, north_y, upward])[:, None, :], (3, ROW_CHUNK, count_dirs))
    kernel_all, sums = forward_sums(wavenumbers, points, dirs_block, compact)
    sums = sums[:, :8]
    far_field = sum_over_devices(far_field_of(sums, wavenumbers, direction_basis), owners)
    objective, weights = adjoint_weights(
        far_field, target, direction_weight, wavenumbers, direction_basis
    )

    padded = jnp.concatenate([weights, jnp.zeros_like(weights)], axis=1)
    products = adjoint_products(padded, kernel_all)[:, :8]
    backward = adjoint_sources(products, compact[19:22])
    spread = unpermute_columns(backward, selector)
    spread = spread.reshape(16, owners, capacity).transpose(1, 0, 2).reshape(owners, -1, 128)
    returned = exchange(spread, 2).reshape(owners, 16, capacity).transpose(2, 0, 1).reshape(rows_dev, 16)
    rows_major = returned * living[:, None]
    cell_adjoint = scatter_rows(surface_cell, rows_major, cell_state.shape[1])
    return (far_field, objective, cell_adjoint)


def solution(mesh):
    placed = (
        P(None, ("gx", "gy")),
        P(None, ("gx", "gy")),
        P(("gx", "gy")),
        P(("gx", "gy")),
        P(),
        P(),
        P(),
    )
    return jax.shard_map(
        on_device,
        mesh=mesh,
        in_specs=placed,
        out_specs=(P(), P(), P(None, ("gx", "gy"))),
        check_vma=False,
    )
```

```python
import functools
import math

import jax
import jax.numpy as jnp
from jax import lax
from jax.experimental import pallas as pl
from jax.experimental.pallas import tpu as pltpu
from jax.sharding import PartitionSpec as P

GOLDEN = math.pi * (3.0 - math.sqrt(5.0))
PI_A = round(math.pi * 32768.0) / 32768.0
PI_B = math.pi - PI_A
INV_PI = 1.0 / math.pi
SIN_C = [-0.16666657019913644, 0.00833301540393062, -0.00019806478078586938, 2.599750005030262e-06]
COS_C = [-0.4999993175258851, 0.041663973510963626, -0.0013855797199316853, 2.3191254010748703e-05]
SINPI_C = [3.141592578574041, -5.1677067848796066, 2.5500297991194887, -0.5980355679943354, 0.07720094563063706]
COSPI_C = [-4.934795411606951, 4.05844824012755, -1.332068921858188, 0.22002136541700046]


ROOT2 = math.sqrt(2.0)


def sincos_half_turns(v):
    w = v - jnp.floor(v + 0.5)
    z = w * w
    ps = SINPI_C[-1] * ROOT2
    for c in SINPI_C[-2::-1]:
        ps = c * ROOT2 + z * ps
    pc = COSPI_C[-1] * ROOT2
    for c in COSPI_C[-2::-1]:
        pc = c * ROOT2 + z * pc
    sine_half = w * ps
    cosine_half = ROOT2 + z * pc
    return (cosine_half * cosine_half - 1.0, sine_half * cosine_half)


def sincos_turns(u):
    n = jnp.floor(u + 0.5)
    w = u - n
    z = w * w
    ps = SINPI_C[-1]
    for c in SINPI_C[-2::-1]:
        ps = c + z * ps
    pc = COSPI_C[-1]
    for c in COSPI_C[-2::-1]:
        pc = c + z * pc
    half = n * 0.5
    sign = 1.0 - 4.0 * (half - jnp.floor(half))
    return (sign * (1.0 + z * pc), (sign * w) * ps)


def sincos(theta):
    n = jnp.floor(theta * INV_PI + 0.5)
    r = (theta - n * PI_A) - n * PI_B
    z = r * r
    ps = SIN_C[-1]
    for c in SIN_C[-2::-1]:
        ps = c + z * ps
    pc = COS_C[-1]
    for c in COS_C[-2::-1]:
        pc = c + z * pc
    half = n * 0.5
    sign = 1.0 - 4.0 * (half - jnp.floor(half))
    return (sign * (1.0 + z * pc), sign * (r + (r * z) * ps))


def directions(count_dirs):
    lattice = jnp.arange(count_dirs).astype(jnp.float32)
    height = 1.0 - (2.0 * lattice + 1.0) / count_dirs
    radius_xy = jnp.sqrt(1.0 - height * height)
    azimuth = jnp.mod(lattice * GOLDEN, 2.0 * math.pi)
    return (radius_xy * jnp.cos(azimuth), radius_xy * jnp.sin(azimuth), height)


def kernel_block(points, wavenum, east_x, north_y, upward):
    phases = wavenum * (
        points[0][:, None] * east_x[None, :]
        + points[1][:, None] * north_y[None, :]
        + points[2][:, None] * upward[None, :]
    )
    cosine, sine = sincos(phases)
    return jnp.concatenate([cosine, sine], axis=1).astype(jnp.bfloat16)


def source_rows(rows_block, level):
    surface_area = rows_block[22]
    normal = rows_block[19:22]
    pressure_real = rows_block[level] * surface_area
    pressure_imag = rows_block[4 + level] * surface_area
    return jnp.stack(
        [
            rows_block[8 + level] * surface_area,
            normal[0] * pressure_real,
            normal[1] * pressure_real,
            normal[2] * pressure_real,
            rows_block[12 + level] * surface_area,
            normal[0] * pressure_imag,
            normal[1] * pressure_imag,
            normal[2] * pressure_imag,
        ]
    ).astype(jnp.bfloat16)


def far_field_of(sums, wavenumbers, direction_basis):
    half_width = sums.shape[2] // 2
    cosine_part = sums[:, :, :half_width]
    sine_part = sums[:, :, half_width:]
    real_q = cosine_part[:, 0:4] + sine_part[:, 4:8]
    imag_q = cosine_part[:, 4:8] - sine_part[:, 0:4]
    real_z = jnp.sum(direction_basis[None] * real_q, axis=1)
    imag_z = jnp.sum(direction_basis[None] * imag_q, axis=1)
    wavenum = wavenumbers[:, None]
    return jnp.stack([-wavenum * imag_z, wavenum * real_z], axis=1)


def adjoint_weights(far_field, target, direction_weight, wavenumbers, direction_basis):
    count_dirs = far_field.shape[2]
    mismatch = far_field - target
    objective = jnp.sum(direction_weight * mismatch * mismatch) / count_dirs
    gradient = 2.0 * direction_weight * mismatch / count_dirs
    wavenum = wavenumbers[:, None]
    real_gz = wavenum * gradient[:, 1]
    imag_gz = -wavenum * gradient[:, 0]
    real_gq = direction_basis[None] * real_gz[:, None]
    imag_gq = direction_basis[None] * imag_gz[:, None]
    upper_half = jnp.concatenate([real_gq, -imag_gq], axis=2)
    lower_half = jnp.concatenate([imag_gq, real_gq], axis=2)
    return (objective, jnp.concatenate([upper_half, lower_half], axis=1).astype(jnp.bfloat16))


def adjoint_sources(products, normal):
    pressure_real = jnp.sum(normal[None] * products[:, 1:4], axis=1)
    pressure_imag = jnp.sum(normal[None] * products[:, 5:8], axis=1)
    return jnp.concatenate([pressure_real, pressure_imag, products[:, 0], products[:, 4]], axis=0)


ROW_BLOCK = 128
ADJ_BLOCK = 256
ROW_CHUNK = 16
LANE_CHUNK = 256


def forward_kernel(wave_ref, pts_ref, dirs_ref, rows_ref, cs_ref, q_ref, src_scr):
    step = pl.program_id(0)
    num_freqs = cs_ref.shape[0]
    count_dirs = dirs_ref.shape[2]
    turns = [wave_ref[level] * (0.5 * INV_PI) for level in range(num_freqs)]

    @pl.loop(0, ROW_BLOCK // ROW_CHUNK)
    def _(i):
        r0 = pl.multiple_of(i * ROW_CHUNK, ROW_CHUNK)
        coords = [
            jnp.broadcast_to(pts_ref[pl.ds(r0, ROW_CHUNK), c : c + 1], (ROW_CHUNK, LANE_CHUNK))
            for c in range(3)
        ]
        for j0 in range(0, count_dirs, LANE_CHUNK):
            lanes = slice(j0, j0 + LANE_CHUNK)
            along = (
                coords[0] * dirs_ref[0, :, lanes]
                + coords[1] * dirs_ref[1, :, lanes]
                + coords[2] * dirs_ref[2, :, lanes]
            )
            for level in range(num_freqs):
                cosine, sine = sincos_half_turns(turns[level] * along)
                cs_ref[level, pl.ds(r0, ROW_CHUNK), lanes] = cosine.astype(jnp.bfloat16)
                cs_ref[level, pl.ds(r0, ROW_CHUNK), j0 + count_dirs : j0 + count_dirs + LANE_CHUNK] = (
                    sine.astype(jnp.bfloat16)
                )

    @pl.when(step == 0)
    def _():
        q_ref[...] = jnp.zeros_like(q_ref)

    area = rows_ref[22:23, :]
    src_scr[...] = jnp.zeros_like(src_scr)
    for level in range(num_freqs):
        pressure_real = rows_ref[level : level + 1, :] * area
        pressure_imag = rows_ref[4 + level : 5 + level, :] * area
        src_scr[0:1, :] = rows_ref[8 + level : 9 + level, :] * area
        src_scr[4:5, :] = rows_ref[12 + level : 13 + level, :] * area
        for c in range(3):
            normal = rows_ref[19 + c : 20 + c, :]
            src_scr[1 + c : 2 + c, :] = normal * pressure_real
            src_scr[5 + c : 6 + c, :] = normal * pressure_imag
        source = src_scr[...].astype(jnp.bfloat16)
        q_ref[level] += jnp.dot(source, cs_ref[level], preferred_element_type=jnp.float32)


def forward_sums(wavenumbers, points, dirs_block, compact):
    num_freqs = wavenumbers.shape[0]
    rows = points.shape[0]
    count_dirs = dirs_block.shape[2]
    grid = (rows // ROW_BLOCK,)
    return pl.pallas_call(
        forward_kernel,
        grid=grid,
        in_specs=[
            pl.BlockSpec(memory_space=pltpu.SMEM),
            pl.BlockSpec((ROW_BLOCK, 3), lambda b: (b, 0)),
            pl.BlockSpec(dirs_block.shape, lambda b: (0, 0, 0)),
            pl.BlockSpec((compact.shape[0], ROW_BLOCK), lambda b: (0, b)),
        ],
        out_specs=[
            pl.BlockSpec((num_freqs, ROW_BLOCK, 2 * count_dirs), lambda b: (0, b, 0)),
            pl.BlockSpec((num_freqs, 16, 2 * count_dirs), lambda b: (0, 0, 0)),
        ],
        out_shape=[
            jax.ShapeDtypeStruct((num_freqs, rows, 2 * count_dirs), jnp.bfloat16),
            jax.ShapeDtypeStruct((num_freqs, 16, 2 * count_dirs), jnp.float32),
        ],
        scratch_shapes=[pltpu.VMEM((16, ROW_BLOCK), jnp.float32)],
        compiler_params=pltpu.CompilerParams(
            dimension_semantics=("arbitrary",), vmem_limit_bytes=48 * 1024 * 1024
        ),
        cost_estimate=pl.CostEstimate(
            flops=2 * 16 * rows * 2 * count_dirs * num_freqs + 60 * rows * count_dirs * num_freqs,
            transcendentals=0,
            bytes_accessed=2 * rows * 2 * count_dirs * num_freqs,
        ),
    )(wavenumbers, points, dirs_block, compact)


def adjoint_kernel(w_ref, cs_ref, out_ref):
    for level in range(cs_ref.shape[0]):
        out_ref[level] = lax.dot_general(
            w_ref[level], cs_ref[level], (((1,), (1,)), ((), ())), preferred_element_type=jnp.float32
        )


def adjoint_products(weights, kernel_all):
    num_freqs, rows, width = kernel_all.shape
    return pl.pallas_call(
        adjoint_kernel,
        grid=(rows // ADJ_BLOCK,),
        in_specs=[
            pl.BlockSpec(weights.shape, lambda b: (0, 0, 0)),
            pl.BlockSpec((num_freqs, ADJ_BLOCK, width), lambda b: (0, b, 0)),
        ],
        out_specs=pl.BlockSpec((num_freqs, weights.shape[1], ADJ_BLOCK), lambda b: (0, 0, b)),
        out_shape=jax.ShapeDtypeStruct((num_freqs, weights.shape[1], rows), jnp.float32),
        compiler_params=pltpu.CompilerParams(
            dimension_semantics=("arbitrary",), vmem_limit_bytes=48 * 1024 * 1024
        ),
        cost_estimate=pl.CostEstimate(
            flops=2 * weights.shape[1] * rows * width * num_freqs,
            transcendentals=0,
            bytes_accessed=2 * rows * width * num_freqs,
        ),
    )(weights, kernel_all)


def split_bf16(values):
    high = lax.reduce_precision(values, exponent_bits=8, mantissa_bits=7)
    rest = values - high
    middle = lax.reduce_precision(rest, exponent_bits=8, mantissa_bits=7)
    low = rest - middle
    return jnp.concatenate([high, middle, low], axis=0).astype(jnp.bfloat16)


def join_parts(product, channels):
    return (product[:channels] + product[channels : 2 * channels]) + product[2 * channels :]


def permute_columns(values, selector):
    product = jnp.dot(split_bf16(values), selector, preferred_element_type=jnp.float32)
    return join_parts(product, values.shape[0])


def unpermute_columns(values, selector):
    product = lax.dot_general(
        split_bf16(values), selector, (((1,), (1,)), ((), ())), preferred_element_type=jnp.float32
    )
    return join_parts(product, values.shape[0])


CHAINS = 8


def scatter_kernel(cell_ref, rows_ref, out_ref, *accs):
    for acc in accs:
        acc[...] = jnp.zeros_like(acc)
    chains = len(accs)

    def body(i, carry):
        for k in range(chains):
            row = i * chains + k
            cell = cell_ref[row]
            accs[k][pl.ds(cell, 1), :] += rows_ref[pl.ds(row, 1), :]
        return carry

    lax.fori_loop(0, rows_ref.shape[0] // chains, body, 0)
    total = accs[0][...]
    for acc in accs[1:]:
        total = total + acc[...]
    out_ref[...] = total.T


def scatter_rows(surface_cell, rows_major, cells):
    width = rows_major.shape[1]
    return pl.pallas_call(
        scatter_kernel,
        grid_spec=pltpu.PrefetchScalarGridSpec(
            num_scalar_prefetch=1,
            grid=(1,),
            in_specs=[pl.BlockSpec(rows_major.shape, lambda i, c: (0, 0))],
            out_specs=pl.BlockSpec((width, cells), lambda i, c: (0, 0)),
            scratch_shapes=[pltpu.VMEM((cells, width), jnp.float32) for _ in range(CHAINS)],
        ),
        out_shape=jax.ShapeDtypeStruct((width, cells), jnp.float32),
        compiler_params=pltpu.CompilerParams(vmem_limit_bytes=48 * 1024 * 1024),
    )(surface_cell, rows_major)


GATHER_UNROLL = 16


def gather_kernel(cell_ref, state_ref, out_ref, table_ref):
    table_ref[...] = state_ref[...].T

    def body(i, carry):
        for k in range(GATHER_UNROLL):
            row = i * GATHER_UNROLL + k
            out_ref[pl.ds(row, 1), :] = table_ref[pl.ds(cell_ref[row], 1), :]
        return carry

    lax.fori_loop(0, out_ref.shape[0] // GATHER_UNROLL, body, 0)


def gather_rows(surface_cell, state):
    rows = surface_cell.shape[0]
    channels, cells = state.shape
    return pl.pallas_call(
        gather_kernel,
        grid_spec=pltpu.PrefetchScalarGridSpec(
            num_scalar_prefetch=1,
            grid=(1,),
            in_specs=[pl.BlockSpec(state.shape, lambda i, c: (0, 0))],
            out_specs=pl.BlockSpec((rows, channels), lambda i, c: (0, 0)),
            scratch_shapes=[pltpu.VMEM((cells, channels), state.dtype)],
        ),
        out_shape=jax.ShapeDtypeStruct((rows, channels), state.dtype),
        compiler_params=pltpu.CompilerParams(vmem_limit_bytes=48 * 1024 * 1024),
    )(surface_cell, state)


MESH_IDS = pl.DeviceIdType.MESH


def reduce_kernel(nx, ny, x_ref, out_ref, part_a, part_b, got_a, got_b, sems):
    b0 = lax.axis_index("gx")
    a0 = lax.axis_index("gy")
    barrier = pltpu.get_barrier_semaphore()
    for t in range(1, ny):
        pl.semaphore_signal(barrier, inc=1, device_id=(b0, lax.rem(a0 + t, ny)), device_id_type=MESH_IDS)
    for t in range(1, nx):
        pl.semaphore_signal(barrier, inc=1, device_id=(lax.rem(b0 + t, nx), a0), device_id_type=MESH_IDS)
    pl.semaphore_wait(barrier, nx + ny - 2)

    def exchange(phase, src_of, dst_of, peers, along_x):
        copies = []
        for t in range(1, peers):
            if along_x:
                peer = lax.rem(b0 + t, nx)
                me, device = b0, (peer, a0)
            else:
                peer = lax.rem(a0 + t, ny)
                me, device = a0, (b0, peer)
            copy = pltpu.make_async_remote_copy(
                src_ref=src_of(peer),
                dst_ref=dst_of(me),
                send_sem=sems.at[phase, 0, peer],
                recv_sem=sems.at[phase, 1, me],
                device_id=device,
                device_id_type=MESH_IDS,
            )
            copy.start()
            copies.append((peer, device))
        for peer, device in copies:
            pltpu.make_async_remote_copy(
                src_ref=src_of(peer),
                dst_ref=dst_of(peer),
                send_sem=sems.at[phase, 0, peer],
                recv_sem=sems.at[phase, 1, peer],
                device_id=device,
                device_id_type=MESH_IDS,
            ).wait()

    exchange(0, lambda a: x_ref.at[a], lambda a: got_a.at[a], ny, False)
    got_a[a0] = x_ref[a0]
    part_a[...] = jnp.sum(got_a[...], axis=0)
    exchange(1, lambda b: part_a, lambda b: got_b.at[b], nx, True)
    got_b[b0] = part_a[...]
    part_b[...] = jnp.sum(got_b[...], axis=0)
    exchange(2, lambda a: part_b, lambda a: out_ref.at[a], ny, False)
    out_ref[a0] = part_b[...]


def exchange_kernel(nx, ny, x_ref, out_ref, landing, send_sems, recv_sems):
    total = nx * ny
    me = lax.axis_index("gx") * ny + lax.axis_index("gy")
    barrier = pltpu.get_barrier_semaphore()

    def where(peer):
        return (peer // ny, lax.rem(peer, ny))

    def copy_to(peer, slot):
        return pltpu.make_async_remote_copy(
            src_ref=x_ref.at[peer],
            dst_ref=landing.at[slot],
            send_sem=send_sems.at[peer],
            recv_sem=recv_sems.at[slot],
            device_id=where(peer),
            device_id_type=MESH_IDS,
        )

    def greet(t, carry):
        pl.semaphore_signal(barrier, inc=1, device_id=where(lax.rem(me + t, total)), device_id_type=MESH_IDS)
        return carry

    lax.fori_loop(1, total, greet, 0, unroll=8)
    pl.semaphore_wait(barrier, total - 1)

    def send(t, carry):
        copy_to(lax.rem(me + t, total), me).start()
        return carry

    lax.fori_loop(1, total, send, 0, unroll=8)
    landing[me] = x_ref[me]

    def finish(t, carry):
        peer = lax.rem(me + t, total)
        copy_to(peer, peer).wait()
        return carry

    lax.fori_loop(1, total, finish, 0, unroll=8)
    out_ref[...] = landing[...]


def exchange(blocks, exchange_id):
    nx = lax.axis_size("gx")
    ny = lax.axis_size("gy")
    return pl.pallas_call(
        functools.partial(exchange_kernel, nx, ny),
        in_specs=[pl.BlockSpec(memory_space=pltpu.VMEM)],
        out_specs=pl.BlockSpec(memory_space=pltpu.VMEM),
        out_shape=jax.ShapeDtypeStruct(blocks.shape, blocks.dtype),
        scratch_shapes=[
            pltpu.VMEM(blocks.shape, blocks.dtype),
            pltpu.SemaphoreType.DMA((nx * ny,)),
            pltpu.SemaphoreType.DMA((nx * ny,)),
        ],
        compiler_params=pltpu.CompilerParams(collective_id=exchange_id, has_side_effects=True),
    )(blocks)


def sum_over_devices(partial, owners):
    nx = lax.axis_size("gx")
    ny = lax.axis_size("gy")
    lanes = partial.size // (nx * ny)
    shaped = partial.reshape(ny, nx, lanes)
    peers = max(nx, ny)
    total = pl.pallas_call(
        functools.partial(reduce_kernel, nx, ny),
        in_specs=[pl.BlockSpec(memory_space=pltpu.VMEM)],
        out_specs=pl.BlockSpec(memory_space=pltpu.VMEM),
        out_shape=jax.ShapeDtypeStruct(shaped.shape, jnp.float32),
        scratch_shapes=[
            pltpu.VMEM((nx, lanes), jnp.float32),
            pltpu.VMEM((nx, lanes), jnp.float32),
            pltpu.VMEM((ny, nx, lanes), jnp.float32),
            pltpu.VMEM((nx, nx, lanes), jnp.float32),
            pltpu.SemaphoreType.DMA((3, 2, peers)),
        ],
        compiler_params=pltpu.CompilerParams(collective_id=0, has_side_effects=True),
    )(shaped)
    return total.reshape(partial.shape)


def sum_over_devices_a2a(partial, owners):
    chunks = partial.reshape(owners, -1)
    got = lax.all_to_all(chunks, ("gx", "gy"), split_axis=0, concat_axis=0, tiled=True)
    mine = jnp.sum(got, axis=0, keepdims=True)
    spread = jnp.broadcast_to(mine, chunks.shape)
    full = lax.all_to_all(spread, ("gx", "gy"), split_axis=0, concat_axis=0, tiled=True)
    return full.reshape(partial.shape)


def on_device(cell_state, geometry, surface_cell, counts, wavenumbers, target, direction_weight):
    owners = lax.axis_size(("gx", "gy"))
    rows_dev = surface_cell.shape[0]
    capacity = rows_dev // owners
    live_own = rows_dev // 4
    count_dirs = target.shape[2]
    num_freqs = wavenumbers.shape[0]
    living = (jnp.arange(rows_dev) < counts[0]).astype(jnp.float32)
    outgoing = (
        jnp.concatenate(
            [gather_rows(surface_cell, cell_state).T, geometry, jnp.ones((1, rows_dev), jnp.float32)], axis=0
        )
        * living[None, :]
    )
    outgoing = outgoing.reshape(24, capacity, owners).transpose(2, 0, 1).reshape(owners, -1, 128)
    arrived = exchange(outgoing, 1).reshape(owners, 24, capacity).transpose(1, 0, 2)
    marker = arrived[23]
    per_source = jnp.sum(marker, axis=1).astype(jnp.int32)
    offset = jnp.cumsum(per_source) - per_source
    position = offset[:, None] + jnp.arange(capacity, dtype=jnp.int32)[None, :]
    packed_slot = jnp.where(marker > 0.5, position, live_own).reshape(capacity * owners)
    selector = (packed_slot[:, None] == jnp.arange(live_own, dtype=jnp.int32)[None, :]).astype(jnp.bfloat16)
    compact = permute_columns(arrived[:23].reshape(23, capacity * owners), selector)
    east_x, north_y, upward = directions(count_dirs)
    direction_basis = jnp.stack([jnp.ones_like(east_x), east_x, north_y, upward])

    points = compact[16:19].T
    dirs_block = jnp.broadcast_to(jnp.stack([east_x, north_y, upward])[:, None, :], (3, ROW_CHUNK, count_dirs))
    kernel_all, sums = forward_sums(wavenumbers, points, dirs_block, compact)
    sums = sums[:, :8]
    far_field = sum_over_devices(far_field_of(sums, wavenumbers, direction_basis), owners)
    objective, weights = adjoint_weights(
        far_field, target, direction_weight, wavenumbers, direction_basis
    )

    padded = jnp.concatenate([weights, jnp.zeros_like(weights)], axis=1)
    products = adjoint_products(padded, kernel_all)[:, :8]
    backward = adjoint_sources(products, compact[19:22])
    spread = unpermute_columns(backward, selector)
    spread = spread.reshape(16, owners, capacity).transpose(1, 0, 2).reshape(owners, -1, 128)
    returned = exchange(spread, 2).reshape(owners, 16, capacity).transpose(2, 0, 1).reshape(rows_dev, 16)
    rows_major = returned * living[:, None]
    cell_adjoint = scatter_rows(surface_cell, rows_major, cell_state.shape[1])
    return (far_field, objective, cell_adjoint)


def solution(mesh):
    placed = (
        P(None, ("gx", "gy")),
        P(None, ("gx", "gy")),
        P(("gx", "gy")),
        P(("gx", "gy")),
        P(),
        P(),
        P(),
    )
    return jax.shard_map(
        on_device,
        mesh=mesh,
        in_specs=placed,
        out_specs=(P(), P(), P(None, ("gx", "gy"))),
        check_vma=False,
    )
```

```python
import functools
import math

import jax
import jax.numpy as jnp
from jax import lax
from jax.experimental import pallas as pl
from jax.experimental.pallas import tpu as pltpu
from jax.sharding import PartitionSpec as P

GOLDEN = math.pi * (3.0 - math.sqrt(5.0))
PI_A = round(math.pi * 32768.0) / 32768.0
PI_B = math.pi - PI_A
INV_PI = 1.0 / math.pi
SIN_C = [-0.16666657019913644, 0.00833301540393062, -0.00019806478078586938, 2.599750005030262e-06]
COS_C = [-0.4999993175258851, 0.041663973510963626, -0.0013855797199316853, 2.3191254010748703e-05]
SINPI_C = [3.141592578574041, -5.1677067848796066, 2.5500297991194887, -0.5980355679943354, 0.07720094563063706]
COSPI_C = [-4.934795411606951, 4.05844824012755, -1.332068921858188, 0.22002136541700046]


ROOT2 = math.sqrt(2.0)


def sincos_half_turns(v):
    w = v - jnp.floor(v + 0.5)
    z = w * w
    ps = SINPI_C[-1] * ROOT2
    for c in SINPI_C[-2::-1]:
        ps = c * ROOT2 + z * ps
    pc = COSPI_C[-1] * ROOT2
    for c in COSPI_C[-2::-1]:
        pc = c * ROOT2 + z * pc
    sine_half = w * ps
    cosine_half = ROOT2 + z * pc
    return (cosine_half * cosine_half - 1.0, sine_half * cosine_half)


def sincos_turns(u):
    n = jnp.floor(u + 0.5)
    w = u - n
    z = w * w
    ps = SINPI_C[-1]
    for c in SINPI_C[-2::-1]:
        ps = c + z * ps
    pc = COSPI_C[-1]
    for c in COSPI_C[-2::-1]:
        pc = c + z * pc
    half = n * 0.5
    sign = 1.0 - 4.0 * (half - jnp.floor(half))
    return (sign * (1.0 + z * pc), (sign * w) * ps)


def sincos(theta):
    n = jnp.floor(theta * INV_PI + 0.5)
    r = (theta - n * PI_A) - n * PI_B
    z = r * r
    ps = SIN_C[-1]
    for c in SIN_C[-2::-1]:
        ps = c + z * ps
    pc = COS_C[-1]
    for c in COS_C[-2::-1]:
        pc = c + z * pc
    half = n * 0.5
    sign = 1.0 - 4.0 * (half - jnp.floor(half))
    return (sign * (1.0 + z * pc), sign * (r + (r * z) * ps))


def directions(count_dirs):
    lattice = jnp.arange(count_dirs).astype(jnp.float32)
    height = 1.0 - (2.0 * lattice + 1.0) / count_dirs
    radius_xy = jnp.sqrt(1.0 - height * height)
    azimuth = jnp.mod(lattice * GOLDEN, 2.0 * math.pi)
    return (radius_xy * jnp.cos(azimuth), radius_xy * jnp.sin(azimuth), height)


def kernel_block(points, wavenum, east_x, north_y, upward):
    phases = wavenum * (
        points[0][:, None] * east_x[None, :]
        + points[1][:, None] * north_y[None, :]
        + points[2][:, None] * upward[None, :]
    )
    cosine, sine = sincos(phases)
    return jnp.concatenate([cosine, sine], axis=1).astype(jnp.bfloat16)


def source_rows(rows_block, level):
    surface_area = rows_block[22]
    normal = rows_block[19:22]
    pressure_real = rows_block[level] * surface_area
    pressure_imag = rows_block[4 + level] * surface_area
    return jnp.stack(
        [
            rows_block[8 + level] * surface_area,
            normal[0] * pressure_real,
            normal[1] * pressure_real,
            normal[2] * pressure_real,
            rows_block[12 + level] * surface_area,
            normal[0] * pressure_imag,
            normal[1] * pressure_imag,
            normal[2] * pressure_imag,
        ]
    ).astype(jnp.bfloat16)


def far_field_of(sums, wavenumbers, direction_basis):
    half_width = sums.shape[2] // 2
    cosine_part = sums[:, :, :half_width]
    sine_part = sums[:, :, half_width:]
    real_q = cosine_part[:, 0:4] + sine_part[:, 4:8]
    imag_q = cosine_part[:, 4:8] - sine_part[:, 0:4]
    real_z = jnp.sum(direction_basis[None] * real_q, axis=1)
    imag_z = jnp.sum(direction_basis[None] * imag_q, axis=1)
    wavenum = wavenumbers[:, None]
    return jnp.stack([-wavenum * imag_z, wavenum * real_z], axis=1)


def adjoint_weights(far_field, target, direction_weight, wavenumbers, direction_basis):
    count_dirs = far_field.shape[2]
    mismatch = far_field - target
    objective = jnp.sum(direction_weight * mismatch * mismatch) / count_dirs
    gradient = 2.0 * direction_weight * mismatch / count_dirs
    wavenum = wavenumbers[:, None]
    real_gz = wavenum * gradient[:, 1]
    imag_gz = -wavenum * gradient[:, 0]
    real_gq = direction_basis[None] * real_gz[:, None]
    imag_gq = direction_basis[None] * imag_gz[:, None]
    upper_half = jnp.concatenate([real_gq, -imag_gq], axis=2)
    lower_half = jnp.concatenate([imag_gq, real_gq], axis=2)
    return (objective, jnp.concatenate([upper_half, lower_half], axis=1).astype(jnp.bfloat16))


def adjoint_sources(products, normal):
    pressure_real = jnp.sum(normal[None] * products[:, 1:4], axis=1)
    pressure_imag = jnp.sum(normal[None] * products[:, 5:8], axis=1)
    return jnp.concatenate([pressure_real, pressure_imag, products[:, 0], products[:, 4]], axis=0)


ROW_BLOCK = 128
ADJ_BLOCK = 256
ROW_CHUNK = 16
LANE_CHUNK = 256


def forward_kernel(wave_ref, pts_ref, dirs_ref, rows_ref, cs_ref, q_ref, src_scr):
    step = pl.program_id(0)
    num_freqs = cs_ref.shape[0]
    count_dirs = dirs_ref.shape[2]
    turns = [wave_ref[level] * (0.5 * INV_PI) for level in range(num_freqs)]

    @pl.loop(0, ROW_BLOCK // ROW_CHUNK)
    def _(i):
        r0 = pl.multiple_of(i * ROW_CHUNK, ROW_CHUNK)
        coords = [
            jnp.broadcast_to(pts_ref[pl.ds(r0, ROW_CHUNK), c : c + 1], (ROW_CHUNK, LANE_CHUNK))
            for c in range(3)
        ]
        for j0 in range(0, count_dirs, LANE_CHUNK):
            lanes = slice(j0, j0 + LANE_CHUNK)
            along = (
                coords[0] * dirs_ref[0, :, lanes]
                + coords[1] * dirs_ref[1, :, lanes]
                + coords[2] * dirs_ref[2, :, lanes]
            )
            for level in range(num_freqs):
                cosine, sine = sincos_half_turns(turns[level] * along)
                cs_ref[level, pl.ds(r0, ROW_CHUNK), lanes] = cosine.astype(jnp.bfloat16)
                cs_ref[level, pl.ds(r0, ROW_CHUNK), j0 + count_dirs : j0 + count_dirs + LANE_CHUNK] = (
                    sine.astype(jnp.bfloat16)
                )

    @pl.when(step == 0)
    def _():
        q_ref[...] = jnp.zeros_like(q_ref)

    area = rows_ref[22:23, :]
    src_scr[...] = jnp.zeros_like(src_scr)
    for level in range(num_freqs):
        pressure_real = rows_ref[level : level + 1, :] * area
        pressure_imag = rows_ref[4 + level : 5 + level, :] * area
        src_scr[0:1, :] = rows_ref[8 + level : 9 + level, :] * area
        src_scr[4:5, :] = rows_ref[12 + level : 13 + level, :] * area
        for c in range(3):
            normal = rows_ref[19 + c : 20 + c, :]
            src_scr[1 + c : 2 + c, :] = normal * pressure_real
            src_scr[5 + c : 6 + c, :] = normal * pressure_imag
        source = src_scr[...].astype(jnp.bfloat16)
        q_ref[level] += jnp.dot(source, cs_ref[level], preferred_element_type=jnp.float32)


def forward_sums(wavenumbers, points, dirs_block, compact):
    num_freqs = wavenumbers.shape[0]
    rows = points.shape[0]
    count_dirs = dirs_block.shape[2]
    grid = (rows // ROW_BLOCK,)
    return pl.pallas_call(
        forward_kernel,
        grid=grid,
        in_specs=[
            pl.BlockSpec(memory_space=pltpu.SMEM),
            pl.BlockSpec((ROW_BLOCK, 3), lambda b: (b, 0)),
            pl.BlockSpec(dirs_block.shape, lambda b: (0, 0, 0)),
            pl.BlockSpec((compact.shape[0], ROW_BLOCK), lambda b: (0, b)),
        ],
        out_specs=[
            pl.BlockSpec((num_freqs, ROW_BLOCK, 2 * count_dirs), lambda b: (0, b, 0)),
            pl.BlockSpec((num_freqs, 16, 2 * count_dirs), lambda b: (0, 0, 0)),
        ],
        out_shape=[
            jax.ShapeDtypeStruct((num_freqs, rows, 2 * count_dirs), jnp.bfloat16),
            jax.ShapeDtypeStruct((num_freqs, 16, 2 * count_dirs), jnp.float32),
        ],
        scratch_shapes=[pltpu.VMEM((16, ROW_BLOCK), jnp.float32)],
        compiler_params=pltpu.CompilerParams(
            dimension_semantics=("arbitrary",), vmem_limit_bytes=48 * 1024 * 1024
        ),
        cost_estimate=pl.CostEstimate(
            flops=2 * 16 * rows * 2 * count_dirs * num_freqs + 60 * rows * count_dirs * num_freqs,
            transcendentals=0,
            bytes_accessed=2 * rows * 2 * count_dirs * num_freqs,
        ),
    )(wavenumbers, points, dirs_block, compact)


def adjoint_kernel(w_ref, cs_ref, out_ref):
    for level in range(cs_ref.shape[0]):
        out_ref[level] = lax.dot_general(
            w_ref[level], cs_ref[level], (((1,), (1,)), ((), ())), preferred_element_type=jnp.float32
        )


def adjoint_products(weights, kernel_all):
    num_freqs, rows, width = kernel_all.shape
    return pl.pallas_call(
        adjoint_kernel,
        grid=(rows // ADJ_BLOCK,),
        in_specs=[
            pl.BlockSpec(weights.shape, lambda b: (0, 0, 0)),
            pl.BlockSpec((num_freqs, ADJ_BLOCK, width), lambda b: (0, b, 0)),
        ],
        out_specs=pl.BlockSpec((num_freqs, weights.shape[1], ADJ_BLOCK), lambda b: (0, 0, b)),
        out_shape=jax.ShapeDtypeStruct((num_freqs, weights.shape[1], rows), jnp.float32),
        compiler_params=pltpu.CompilerParams(
            dimension_semantics=("arbitrary",), vmem_limit_bytes=48 * 1024 * 1024
        ),
        cost_estimate=pl.CostEstimate(
            flops=2 * weights.shape[1] * rows * width * num_freqs,
            transcendentals=0,
            bytes_accessed=2 * rows * width * num_freqs,
        ),
    )(weights, kernel_all)


def split_bf16(values):
    high = lax.reduce_precision(values, exponent_bits=8, mantissa_bits=7)
    rest = values - high
    middle = lax.reduce_precision(rest, exponent_bits=8, mantissa_bits=7)
    low = rest - middle
    return jnp.concatenate([high, middle, low], axis=0).astype(jnp.bfloat16)


def join_parts(product, channels):
    return (product[:channels] + product[channels : 2 * channels]) + product[2 * channels :]


def permute_columns(values, selector):
    product = jnp.dot(split_bf16(values), selector, preferred_element_type=jnp.float32)
    return join_parts(product, values.shape[0])


def unpermute_columns(values, selector):
    product = lax.dot_general(
        split_bf16(values), selector, (((1,), (1,)), ((), ())), preferred_element_type=jnp.float32
    )
    return join_parts(product, values.shape[0])


CHAINS = 8


def scatter_kernel(cell_ref, rows_ref, out_ref, *accs):
    for acc in accs:
        acc[...] = jnp.zeros_like(acc)
    chains = len(accs)

    def body(i, carry):
        for k in range(chains):
            row = i * chains + k
            cell = cell_ref[row]
            accs[k][pl.ds(cell, 1), :] += rows_ref[pl.ds(row, 1), :]
        return carry

    lax.fori_loop(0, rows_ref.shape[0] // chains, body, 0, unroll=2)
    total = accs[0][...]
    for acc in accs[1:]:
        total = total + acc[...]
    out_ref[...] = total.T


def scatter_rows(surface_cell, rows_major, cells):
    width = rows_major.shape[1]
    return pl.pallas_call(
        scatter_kernel,
        grid_spec=pltpu.PrefetchScalarGridSpec(
            num_scalar_prefetch=1,
            grid=(1,),
            in_specs=[pl.BlockSpec(rows_major.shape, lambda i, c: (0, 0))],
            out_specs=pl.BlockSpec((width, cells), lambda i, c: (0, 0)),
            scratch_shapes=[pltpu.VMEM((cells, width), jnp.float32) for _ in range(CHAINS)],
        ),
        out_shape=jax.ShapeDtypeStruct((width, cells), jnp.float32),
        compiler_params=pltpu.CompilerParams(vmem_limit_bytes=48 * 1024 * 1024),
    )(surface_cell, rows_major)


GATHER_UNROLL = 32


def gather_kernel(cell_ref, state_ref, out_ref, table_ref):
    table_ref[...] = state_ref[...].T

    def body(i, carry):
        for k in range(GATHER_UNROLL):
            row = i * GATHER_UNROLL + k
            out_ref[pl.ds(row, 1), :] = table_ref[pl.ds(cell_ref[row], 1), :]
        return carry

    lax.fori_loop(0, out_ref.shape[0] // GATHER_UNROLL, body, 0)


def gather_rows(surface_cell, state):
    rows = surface_cell.shape[0]
    channels, cells = state.shape
    return pl.pallas_call(
        gather_kernel,
        grid_spec=pltpu.PrefetchScalarGridSpec(
            num_scalar_prefetch=1,
            grid=(1,),
            in_specs=[pl.BlockSpec(state.shape, lambda i, c: (0, 0))],
            out_specs=pl.BlockSpec((rows, channels), lambda i, c: (0, 0)),
            scratch_shapes=[pltpu.VMEM((cells, channels), state.dtype)],
        ),
        out_shape=jax.ShapeDtypeStruct((rows, channels), state.dtype),
        compiler_params=pltpu.CompilerParams(vmem_limit_bytes=48 * 1024 * 1024),
    )(surface_cell, state)


MESH_IDS = pl.DeviceIdType.MESH


def reduce_kernel(nx, ny, x_ref, out_ref, part_a, part_b, got_a, got_b, sems):
    b0 = lax.axis_index("gx")
    a0 = lax.axis_index("gy")
    barrier = pltpu.get_barrier_semaphore()
    for t in range(1, ny):
        pl.semaphore_signal(barrier, inc=1, device_id=(b0, lax.rem(a0 + t, ny)), device_id_type=MESH_IDS)
    for t in range(1, nx):
        pl.semaphore_signal(barrier, inc=1, device_id=(lax.rem(b0 + t, nx), a0), device_id_type=MESH_IDS)
    pl.semaphore_wait(barrier, nx + ny - 2)

    def exchange(phase, src_of, dst_of, peers, along_x):
        copies = []
        for t in range(1, peers):
            if along_x:
                peer = lax.rem(b0 + t, nx)
                me, device = b0, (peer, a0)
            else:
                peer = lax.rem(a0 + t, ny)
                me, device = a0, (b0, peer)
            copy = pltpu.make_async_remote_copy(
                src_ref=src_of(peer),
                dst_ref=dst_of(me),
                send_sem=sems.at[phase, 0, peer],
                recv_sem=sems.at[phase, 1, me],
                device_id=device,
                device_id_type=MESH_IDS,
            )
            copy.start()
            copies.append((peer, device))
        for peer, device in copies:
            pltpu.make_async_remote_copy(
                src_ref=src_of(peer),
                dst_ref=dst_of(peer),
                send_sem=sems.at[phase, 0, peer],
                recv_sem=sems.at[phase, 1, peer],
                device_id=device,
                device_id_type=MESH_IDS,
            ).wait()

    exchange(0, lambda a: x_ref.at[a], lambda a: got_a.at[a], ny, False)
    got_a[a0] = x_ref[a0]
    part_a[...] = jnp.sum(got_a[...], axis=0)
    exchange(1, lambda b: part_a, lambda b: got_b.at[b], nx, True)
    got_b[b0] = part_a[...]
    part_b[...] = jnp.sum(got_b[...], axis=0)
    exchange(2, lambda a: part_b, lambda a: out_ref.at[a], ny, False)
    out_ref[a0] = part_b[...]


def exchange_kernel(nx, ny, x_ref, out_ref, landing, send_sems, recv_sems):
    total = nx * ny
    me = lax.axis_index("gx") * ny + lax.axis_index("gy")
    barrier = pltpu.get_barrier_semaphore()

    def where(peer):
        return (peer // ny, lax.rem(peer, ny))

    def copy_to(peer, slot):
        return pltpu.make_async_remote_copy(
            src_ref=x_ref.at[peer],
            dst_ref=landing.at[slot],
            send_sem=send_sems.at[peer],
            recv_sem=recv_sems.at[slot],
            device_id=where(peer),
            device_id_type=MESH_IDS,
        )

    def greet(t, carry):
        pl.semaphore_signal(barrier, inc=1, device_id=where(lax.rem(me + t, total)), device_id_type=MESH_IDS)
        return carry

    lax.fori_loop(1, total, greet, 0, unroll=8)
    pl.semaphore_wait(barrier, total - 1)

    def send(t, carry):
        copy_to(lax.rem(me + t, total), me).start()
        return carry

    lax.fori_loop(1, total, send, 0, unroll=8)
    landing[me] = x_ref[me]

    def finish(t, carry):
        peer = lax.rem(me + t, total)
        copy_to(peer, peer).wait()
        return carry

    lax.fori_loop(1, total, finish, 0, unroll=8)
    out_ref[...] = landing[...]


def exchange(blocks, exchange_id):
    nx = lax.axis_size("gx")
    ny = lax.axis_size("gy")
    return pl.pallas_call(
        functools.partial(exchange_kernel, nx, ny),
        in_specs=[pl.BlockSpec(memory_space=pltpu.VMEM)],
        out_specs=pl.BlockSpec(memory_space=pltpu.VMEM),
        out_shape=jax.ShapeDtypeStruct(blocks.shape, blocks.dtype),
        scratch_shapes=[
            pltpu.VMEM(blocks.shape, blocks.dtype),
            pltpu.SemaphoreType.DMA((nx * ny,)),
            pltpu.SemaphoreType.DMA((nx * ny,)),
        ],
        compiler_params=pltpu.CompilerParams(collective_id=exchange_id, has_side_effects=True),
    )(blocks)


def sum_over_devices(partial, owners):
    nx = lax.axis_size("gx")
    ny = lax.axis_size("gy")
    lanes = partial.size // (nx * ny)
    shaped = partial.reshape(ny, nx, lanes)
    peers = max(nx, ny)
    total = pl.pallas_call(
        functools.partial(reduce_kernel, nx, ny),
        in_specs=[pl.BlockSpec(memory_space=pltpu.VMEM)],
        out_specs=pl.BlockSpec(memory_space=pltpu.VMEM),
        out_shape=jax.ShapeDtypeStruct(shaped.shape, jnp.float32),
        scratch_shapes=[
            pltpu.VMEM((nx, lanes), jnp.float32),
            pltpu.VMEM((nx, lanes), jnp.float32),
            pltpu.VMEM((ny, nx, lanes), jnp.float32),
            pltpu.VMEM((nx, nx, lanes), jnp.float32),
            pltpu.SemaphoreType.DMA((3, 2, peers)),
        ],
        compiler_params=pltpu.CompilerParams(collective_id=0, has_side_effects=True),
    )(shaped)
    return total.reshape(partial.shape)


def sum_over_devices_a2a(partial, owners):
    chunks = partial.reshape(owners, -1)
    got = lax.all_to_all(chunks, ("gx", "gy"), split_axis=0, concat_axis=0, tiled=True)
    mine = jnp.sum(got, axis=0, keepdims=True)
    spread = jnp.broadcast_to(mine, chunks.shape)
    full = lax.all_to_all(spread, ("gx", "gy"), split_axis=0, concat_axis=0, tiled=True)
    return full.reshape(partial.shape)


def on_device(cell_state, geometry, surface_cell, counts, wavenumbers, target, direction_weight):
    owners = lax.axis_size(("gx", "gy"))
    rows_dev = surface_cell.shape[0]
    capacity = rows_dev // owners
    live_own = rows_dev // 4
    count_dirs = target.shape[2]
    num_freqs = wavenumbers.shape[0]
    living = (jnp.arange(rows_dev) < counts[0]).astype(jnp.float32)
    outgoing = (
        jnp.concatenate(
            [gather_rows(surface_cell, cell_state).T, geometry, jnp.ones((1, rows_dev), jnp.float32)], axis=0
        )
        * living[None, :]
    )
    outgoing = outgoing.reshape(24, capacity, owners).transpose(2, 0, 1).reshape(owners, -1, 128)
    arrived = exchange(outgoing, 1).reshape(owners, 24, capacity).transpose(1, 0, 2)
    marker = arrived[23]
    per_source = jnp.sum(marker, axis=1).astype(jnp.int32)
    offset = jnp.cumsum(per_source) - per_source
    position = offset[:, None] + jnp.arange(capacity, dtype=jnp.int32)[None, :]
    packed_slot = jnp.where(marker > 0.5, position, live_own).reshape(capacity * owners)
    selector = (packed_slot[:, None] == jnp.arange(live_own, dtype=jnp.int32)[None, :]).astype(jnp.bfloat16)
    compact = permute_columns(arrived[:23].reshape(23, capacity * owners), selector)
    east_x, north_y, upward = directions(count_dirs)
    direction_basis = jnp.stack([jnp.ones_like(east_x), east_x, north_y, upward])

    points = compact[16:19].T
    dirs_block = jnp.broadcast_to(jnp.stack([east_x, north_y, upward])[:, None, :], (3, ROW_CHUNK, count_dirs))
    kernel_all, sums = forward_sums(wavenumbers, points, dirs_block, compact)
    sums = sums[:, :8]
    far_field = sum_over_devices(far_field_of(sums, wavenumbers, direction_basis), owners)
    objective, weights = adjoint_weights(
        far_field, target, direction_weight, wavenumbers, direction_basis
    )

    padded = jnp.concatenate([weights, jnp.zeros_like(weights)], axis=1)
    products = adjoint_products(padded, kernel_all)[:, :8]
    backward = adjoint_sources(products, compact[19:22])
    spread = unpermute_columns(backward, selector)
    spread = spread.reshape(16, owners, capacity).transpose(1, 0, 2).reshape(owners, -1, 128)
    returned = exchange(spread, 2).reshape(owners, 16, capacity).transpose(2, 0, 1).reshape(rows_dev, 16)
    rows_major = returned * living[:, None]
    cell_adjoint = scatter_rows(surface_cell, rows_major, cell_state.shape[1])
    return (far_field, objective, cell_adjoint)


def solution(mesh):
    placed = (
        P(None, ("gx", "gy")),
        P(None, ("gx", "gy")),
        P(("gx", "gy")),
        P(("gx", "gy")),
        P(),
        P(),
        P(),
    )
    return jax.shard_map(
        on_device,
        mesh=mesh,
        in_specs=placed,
        out_specs=(P(), P(), P(None, ("gx", "gy"))),
        check_vma=False,
    )
```

```python
import functools
import math

import jax
import jax.numpy as jnp
from jax import lax
from jax.experimental import pallas as pl
from jax.experimental.pallas import tpu as pltpu
from jax.sharding import PartitionSpec as P

GOLDEN = math.pi * (3.0 - math.sqrt(5.0))
PI_A = round(math.pi * 32768.0) / 32768.0
PI_B = math.pi - PI_A
INV_PI = 1.0 / math.pi
SIN_C = [-0.16666657019913644, 0.00833301540393062, -0.00019806478078586938, 2.599750005030262e-06]
COS_C = [-0.4999993175258851, 0.041663973510963626, -0.0013855797199316853, 2.3191254010748703e-05]
SINPI_C = [3.141592578574041, -5.1677067848796066, 2.5500297991194887, -0.5980355679943354, 0.07720094563063706]
COSPI_C = [-4.934795411606951, 4.05844824012755, -1.332068921858188, 0.22002136541700046]


ROOT2 = math.sqrt(2.0)


def sincos_half_turns(v):
    w = v - jnp.floor(v + 0.5)
    z = w * w
    ps = SINPI_C[-1] * ROOT2
    for c in SINPI_C[-2::-1]:
        ps = c * ROOT2 + z * ps
    pc = COSPI_C[-1] * ROOT2
    for c in COSPI_C[-2::-1]:
        pc = c * ROOT2 + z * pc
    sine_half = w * ps
    cosine_half = ROOT2 + z * pc
    return (cosine_half * cosine_half - 1.0, sine_half * cosine_half)


def sincos_turns(u):
    n = jnp.floor(u + 0.5)
    w = u - n
    z = w * w
    ps = SINPI_C[-1]
    for c in SINPI_C[-2::-1]:
        ps = c + z * ps
    pc = COSPI_C[-1]
    for c in COSPI_C[-2::-1]:
        pc = c + z * pc
    half = n * 0.5
    sign = 1.0 - 4.0 * (half - jnp.floor(half))
    return (sign * (1.0 + z * pc), (sign * w) * ps)


def sincos(theta):
    n = jnp.floor(theta * INV_PI + 0.5)
    r = (theta - n * PI_A) - n * PI_B
    z = r * r
    ps = SIN_C[-1]
    for c in SIN_C[-2::-1]:
        ps = c + z * ps
    pc = COS_C[-1]
    for c in COS_C[-2::-1]:
        pc = c + z * pc
    half = n * 0.5
    sign = 1.0 - 4.0 * (half - jnp.floor(half))
    return (sign * (1.0 + z * pc), sign * (r + (r * z) * ps))


def directions(count_dirs):
    lattice = jnp.arange(count_dirs).astype(jnp.float32)
    height = 1.0 - (2.0 * lattice + 1.0) / count_dirs
    radius_xy = jnp.sqrt(1.0 - height * height)
    azimuth = jnp.mod(lattice * GOLDEN, 2.0 * math.pi)
    return (radius_xy * jnp.cos(azimuth), radius_xy * jnp.sin(azimuth), height)


def kernel_block(points, wavenum, east_x, north_y, upward):
    phases = wavenum * (
        points[0][:, None] * east_x[None, :]
        + points[1][:, None] * north_y[None, :]
        + points[2][:, None] * upward[None, :]
    )
    cosine, sine = sincos(phases)
    return jnp.concatenate([cosine, sine], axis=1).astype(jnp.bfloat16)


def source_rows(rows_block, level):
    surface_area = rows_block[22]
    normal = rows_block[19:22]
    pressure_real = rows_block[level] * surface_area
    pressure_imag = rows_block[4 + level] * surface_area
    return jnp.stack(
        [
            rows_block[8 + level] * surface_area,
            normal[0] * pressure_real,
            normal[1] * pressure_real,
            normal[2] * pressure_real,
            rows_block[12 + level] * surface_area,
            normal[0] * pressure_imag,
            normal[1] * pressure_imag,
            normal[2] * pressure_imag,
        ]
    ).astype(jnp.bfloat16)


def far_field_of(sums, wavenumbers, direction_basis):
    half_width = sums.shape[2] // 2
    cosine_part = sums[:, :, :half_width]
    sine_part = sums[:, :, half_width:]
    real_q = cosine_part[:, 0:4] + sine_part[:, 4:8]
    imag_q = cosine_part[:, 4:8] - sine_part[:, 0:4]
    real_z = jnp.sum(direction_basis[None] * real_q, axis=1)
    imag_z = jnp.sum(direction_basis[None] * imag_q, axis=1)
    wavenum = wavenumbers[:, None]
    return jnp.stack([-wavenum * imag_z, wavenum * real_z], axis=1)


def adjoint_weights(far_field, target, direction_weight, wavenumbers, direction_basis):
    count_dirs = far_field.shape[2]
    mismatch = far_field - target
    objective = jnp.sum(direction_weight * mismatch * mismatch) / count_dirs
    gradient = 2.0 * direction_weight * mismatch / count_dirs
    wavenum = wavenumbers[:, None]
    real_gz = wavenum * gradient[:, 1]
    imag_gz = -wavenum * gradient[:, 0]
    real_gq = direction_basis[None] * real_gz[:, None]
    imag_gq = direction_basis[None] * imag_gz[:, None]
    upper_half = jnp.concatenate([real_gq, -imag_gq], axis=2)
    lower_half = jnp.concatenate([imag_gq, real_gq], axis=2)
    return (objective, jnp.concatenate([upper_half, lower_half], axis=1).astype(jnp.bfloat16))


def adjoint_sources(products, normal):
    pressure_real = jnp.sum(normal[None] * products[:, 1:4], axis=1)
    pressure_imag = jnp.sum(normal[None] * products[:, 5:8], axis=1)
    return jnp.concatenate([pressure_real, pressure_imag, products[:, 0], products[:, 4]], axis=0)


ROW_BLOCK = 128
ADJ_BLOCK = 256
ROW_CHUNK = 16
LANE_CHUNK = 256


def forward_kernel(wave_ref, pts_ref, dirs_ref, rows_ref, cs_ref, q_ref, src_scr):
    step = pl.program_id(0)
    num_freqs = cs_ref.shape[0]
    count_dirs = dirs_ref.shape[2]
    turns = [wave_ref[level] * (0.5 * INV_PI) for level in range(num_freqs)]

    @pl.loop(0, ROW_BLOCK // ROW_CHUNK)
    def _(i):
        r0 = pl.multiple_of(i * ROW_CHUNK, ROW_CHUNK)
        coords = [
            jnp.broadcast_to(pts_ref[pl.ds(r0, ROW_CHUNK), c : c + 1], (ROW_CHUNK, LANE_CHUNK))
            for c in range(3)
        ]
        for j0 in range(0, count_dirs, LANE_CHUNK):
            lanes = slice(j0, j0 + LANE_CHUNK)
            along = (
                coords[0] * dirs_ref[0, :, lanes]
                + coords[1] * dirs_ref[1, :, lanes]
                + coords[2] * dirs_ref[2, :, lanes]
            )
            for level in range(num_freqs):
                cosine, sine = sincos_half_turns(turns[level] * along)
                cs_ref[level, pl.ds(r0, ROW_CHUNK), lanes] = cosine.astype(jnp.bfloat16)
                cs_ref[level, pl.ds(r0, ROW_CHUNK), j0 + count_dirs : j0 + count_dirs + LANE_CHUNK] = (
                    sine.astype(jnp.bfloat16)
                )

    @pl.when(step == 0)
    def _():
        q_ref[...] = jnp.zeros_like(q_ref)

    area = rows_ref[22:23, :]
    src_scr[...] = jnp.zeros_like(src_scr)
    for level in range(num_freqs):
        pressure_real = rows_ref[level : level + 1, :] * area
        pressure_imag = rows_ref[4 + level : 5 + level, :] * area
        src_scr[0:1, :] = rows_ref[8 + level : 9 + level, :] * area
        src_scr[4:5, :] = rows_ref[12 + level : 13 + level, :] * area
        for c in range(3):
            normal = rows_ref[19 + c : 20 + c, :]
            src_scr[1 + c : 2 + c, :] = normal * pressure_real
            src_scr[5 + c : 6 + c, :] = normal * pressure_imag
        source = src_scr[...].astype(jnp.bfloat16)
        q_ref[level] += jnp.dot(source, cs_ref[level], preferred_element_type=jnp.float32)


def forward_sums(wavenumbers, points, dirs_block, compact):
    num_freqs = wavenumbers.shape[0]
    rows = points.shape[0]
    count_dirs = dirs_block.shape[2]
    grid = (rows // ROW_BLOCK,)
    return pl.pallas_call(
        forward_kernel,
        grid=grid,
        in_specs=[
            pl.BlockSpec(memory_space=pltpu.SMEM),
            pl.BlockSpec((ROW_BLOCK, 3), lambda b: (b, 0)),
            pl.BlockSpec(dirs_block.shape, lambda b: (0, 0, 0)),
            pl.BlockSpec((compact.shape[0], ROW_BLOCK), lambda b: (0, b)),
        ],
        out_specs=[
            pl.BlockSpec((num_freqs, ROW_BLOCK, 2 * count_dirs), lambda b: (0, b, 0)),
            pl.BlockSpec((num_freqs, 16, 2 * count_dirs), lambda b: (0, 0, 0)),
        ],
        out_shape=[
            jax.ShapeDtypeStruct((num_freqs, rows, 2 * count_dirs), jnp.bfloat16),
            jax.ShapeDtypeStruct((num_freqs, 16, 2 * count_dirs), jnp.float32),
        ],
        scratch_shapes=[pltpu.VMEM((16, ROW_BLOCK), jnp.float32)],
        compiler_params=pltpu.CompilerParams(
            dimension_semantics=("arbitrary",), vmem_limit_bytes=48 * 1024 * 1024
        ),
        cost_estimate=pl.CostEstimate(
            flops=2 * 16 * rows * 2 * count_dirs * num_freqs + 60 * rows * count_dirs * num_freqs,
            transcendentals=0,
            bytes_accessed=2 * rows * 2 * count_dirs * num_freqs,
        ),
    )(wavenumbers, points, dirs_block, compact)


def adjoint_kernel(w_ref, cs_ref, out_ref):
    for level in range(cs_ref.shape[0]):
        out_ref[level] = lax.dot_general(
            w_ref[level], cs_ref[level], (((1,), (1,)), ((), ())), preferred_element_type=jnp.float32
        )


def adjoint_products(weights, kernel_all):
    num_freqs, rows, width = kernel_all.shape
    return pl.pallas_call(
        adjoint_kernel,
        grid=(rows // ADJ_BLOCK,),
        in_specs=[
            pl.BlockSpec(weights.shape, lambda b: (0, 0, 0)),
            pl.BlockSpec((num_freqs, ADJ_BLOCK, width), lambda b: (0, b, 0)),
        ],
        out_specs=pl.BlockSpec((num_freqs, weights.shape[1], ADJ_BLOCK), lambda b: (0, 0, b)),
        out_shape=jax.ShapeDtypeStruct((num_freqs, weights.shape[1], rows), jnp.float32),
        compiler_params=pltpu.CompilerParams(
            dimension_semantics=("arbitrary",), vmem_limit_bytes=48 * 1024 * 1024
        ),
        cost_estimate=pl.CostEstimate(
            flops=2 * weights.shape[1] * rows * width * num_freqs,
            transcendentals=0,
            bytes_accessed=2 * rows * width * num_freqs,
        ),
    )(weights, kernel_all)


def split_bf16(values):
    high = lax.reduce_precision(values, exponent_bits=8, mantissa_bits=7)
    rest = values - high
    middle = lax.reduce_precision(rest, exponent_bits=8, mantissa_bits=7)
    low = rest - middle
    return jnp.concatenate([high, middle, low], axis=0).astype(jnp.bfloat16)


def join_parts(product, channels):
    return (product[:channels] + product[channels : 2 * channels]) + product[2 * channels :]


def permute_columns(values, selector):
    product = jnp.dot(split_bf16(values), selector, preferred_element_type=jnp.float32)
    return join_parts(product, values.shape[0])


def unpermute_columns(values, selector):
    product = lax.dot_general(
        split_bf16(values), selector, (((1,), (1,)), ((), ())), preferred_element_type=jnp.float32
    )
    return join_parts(product, values.shape[0])


CHAINS = 8


def scatter_kernel(cell_ref, rows_ref, out_ref, *accs):
    for acc in accs:
        acc[...] = jnp.zeros_like(acc)
    chains = len(accs)

    def body(i, carry):
        for k in range(chains):
            row = i * chains + k
            cell = cell_ref[row]
            accs[k][pl.ds(cell, 1), :] += rows_ref[pl.ds(row, 1), :]
        return carry

    lax.fori_loop(0, rows_ref.shape[0] // chains, body, 0, unroll=4)
    total = accs[0][...]
    for acc in accs[1:]:
        total = total + acc[...]
    out_ref[...] = total.T


def scatter_rows(surface_cell, rows_major, cells):
    width = rows_major.shape[1]
    return pl.pallas_call(
        scatter_kernel,
        grid_spec=pltpu.PrefetchScalarGridSpec(
            num_scalar_prefetch=1,
            grid=(1,),
            in_specs=[pl.BlockSpec(rows_major.shape, lambda i, c: (0, 0))],
            out_specs=pl.BlockSpec((width, cells), lambda i, c: (0, 0)),
            scratch_shapes=[pltpu.VMEM((cells, width), jnp.float32) for _ in range(CHAINS)],
        ),
        out_shape=jax.ShapeDtypeStruct((width, cells), jnp.float32),
        compiler_params=pltpu.CompilerParams(vmem_limit_bytes=48 * 1024 * 1024),
    )(surface_cell, rows_major)


GATHER_UNROLL = 64


def gather_kernel(cell_ref, state_ref, out_ref, table_ref):
    table_ref[...] = state_ref[...].T

    def body(i, carry):
        for k in range(GATHER_UNROLL):
            row = i * GATHER_UNROLL + k
            out_ref[pl.ds(row, 1), :] = table_ref[pl.ds(cell_ref[row], 1), :]
        return carry

    lax.fori_loop(0, out_ref.shape[0] // GATHER_UNROLL, body, 0)


def gather_rows(surface_cell, state):
    rows = surface_cell.shape[0]
    channels, cells = state.shape
    return pl.pallas_call(
        gather_kernel,
        grid_spec=pltpu.PrefetchScalarGridSpec(
            num_scalar_prefetch=1,
            grid=(1,),
            in_specs=[pl.BlockSpec(state.shape, lambda i, c: (0, 0))],
            out_specs=pl.BlockSpec((rows, channels), lambda i, c: (0, 0)),
            scratch_shapes=[pltpu.VMEM((cells, channels), state.dtype)],
        ),
        out_shape=jax.ShapeDtypeStruct((rows, channels), state.dtype),
        compiler_params=pltpu.CompilerParams(vmem_limit_bytes=48 * 1024 * 1024),
    )(surface_cell, state)


MESH_IDS = pl.DeviceIdType.MESH


def reduce_kernel(nx, ny, x_ref, out_ref, part_a, part_b, got_a, got_b, sems):
    b0 = lax.axis_index("gx")
    a0 = lax.axis_index("gy")
    barrier = pltpu.get_barrier_semaphore()
    for t in range(1, ny):
        pl.semaphore_signal(barrier, inc=1, device_id=(b0, lax.rem(a0 + t, ny)), device_id_type=MESH_IDS)
    for t in range(1, nx):
        pl.semaphore_signal(barrier, inc=1, device_id=(lax.rem(b0 + t, nx), a0), device_id_type=MESH_IDS)
    pl.semaphore_wait(barrier, nx + ny - 2)

    def exchange(phase, src_of, dst_of, peers, along_x):
        copies = []
        for t in range(1, peers):
            if along_x:
                peer = lax.rem(b0 + t, nx)
                me, device = b0, (peer, a0)
            else:
                peer = lax.rem(a0 + t, ny)
                me, device = a0, (b0, peer)
            copy = pltpu.make_async_remote_copy(
                src_ref=src_of(peer),
                dst_ref=dst_of(me),
                send_sem=sems.at[phase, 0, peer],
                recv_sem=sems.at[phase, 1, me],
                device_id=device,
                device_id_type=MESH_IDS,
            )
            copy.start()
            copies.append((peer, device))
        for peer, device in copies:
            pltpu.make_async_remote_copy(
                src_ref=src_of(peer),
                dst_ref=dst_of(peer),
                send_sem=sems.at[phase, 0, peer],
                recv_sem=sems.at[phase, 1, peer],
                device_id=device,
                device_id_type=MESH_IDS,
            ).wait()

    exchange(0, lambda a: x_ref.at[a], lambda a: got_a.at[a], ny, False)
    got_a[a0] = x_ref[a0]
    part_a[...] = jnp.sum(got_a[...], axis=0)
    exchange(1, lambda b: part_a, lambda b: got_b.at[b], nx, True)
    got_b[b0] = part_a[...]
    part_b[...] = jnp.sum(got_b[...], axis=0)
    exchange(2, lambda a: part_b, lambda a: out_ref.at[a], ny, False)
    out_ref[a0] = part_b[...]


def exchange_kernel(nx, ny, x_ref, out_ref, landing, send_sems, recv_sems):
    total = nx * ny
    me = lax.axis_index("gx") * ny + lax.axis_index("gy")
    barrier = pltpu.get_barrier_semaphore()

    def where(peer):
        return (peer // ny, lax.rem(peer, ny))

    def copy_to(peer, slot):
        return pltpu.make_async_remote_copy(
            src_ref=x_ref.at[peer],
            dst_ref=landing.at[slot],
            send_sem=send_sems.at[peer],
            recv_sem=recv_sems.at[slot],
            device_id=where(peer),
            device_id_type=MESH_IDS,
        )

    def greet(t, carry):
        pl.semaphore_signal(barrier, inc=1, device_id=where(lax.rem(me + t, total)), device_id_type=MESH_IDS)
        return carry

    lax.fori_loop(1, total, greet, 0, unroll=8)
    pl.semaphore_wait(barrier, total - 1)

    def send(t, carry):
        copy_to(lax.rem(me + t, total), me).start()
        return carry

    lax.fori_loop(1, total, send, 0, unroll=8)
    landing[me] = x_ref[me]

    def finish(t, carry):
        peer = lax.rem(me + t, total)
        copy_to(peer, peer).wait()
        return carry

    lax.fori_loop(1, total, finish, 0, unroll=8)
    out_ref[...] = landing[...]


def exchange(blocks, exchange_id):
    nx = lax.axis_size("gx")
    ny = lax.axis_size("gy")
    return pl.pallas_call(
        functools.partial(exchange_kernel, nx, ny),
        in_specs=[pl.BlockSpec(memory_space=pltpu.VMEM)],
        out_specs=pl.BlockSpec(memory_space=pltpu.VMEM),
        out_shape=jax.ShapeDtypeStruct(blocks.shape, blocks.dtype),
        scratch_shapes=[
            pltpu.VMEM(blocks.shape, blocks.dtype),
            pltpu.SemaphoreType.DMA((nx * ny,)),
            pltpu.SemaphoreType.DMA((nx * ny,)),
        ],
        compiler_params=pltpu.CompilerParams(collective_id=exchange_id, has_side_effects=True),
    )(blocks)


def sum_over_devices(partial, owners):
    nx = lax.axis_size("gx")
    ny = lax.axis_size("gy")
    lanes = partial.size // (nx * ny)
    shaped = partial.reshape(ny, nx, lanes)
    peers = max(nx, ny)
    total = pl.pallas_call(
        functools.partial(reduce_kernel, nx, ny),
        in_specs=[pl.BlockSpec(memory_space=pltpu.VMEM)],
        out_specs=pl.BlockSpec(memory_space=pltpu.VMEM),
        out_shape=jax.ShapeDtypeStruct(shaped.shape, jnp.float32),
        scratch_shapes=[
            pltpu.VMEM((nx, lanes), jnp.float32),
            pltpu.VMEM((nx, lanes), jnp.float32),
            pltpu.VMEM((ny, nx, lanes), jnp.float32),
            pltpu.VMEM((nx, nx, lanes), jnp.float32),
            pltpu.SemaphoreType.DMA((3, 2, peers)),
        ],
        compiler_params=pltpu.CompilerParams(collective_id=0, has_side_effects=True),
    )(shaped)
    return total.reshape(partial.shape)


def sum_over_devices_a2a(partial, owners):
    chunks = partial.reshape(owners, -1)
    got = lax.all_to_all(chunks, ("gx", "gy"), split_axis=0, concat_axis=0, tiled=True)
    mine = jnp.sum(got, axis=0, keepdims=True)
    spread = jnp.broadcast_to(mine, chunks.shape)
    full = lax.all_to_all(spread, ("gx", "gy"), split_axis=0, concat_axis=0, tiled=True)
    return full.reshape(partial.shape)


def on_device(cell_state, geometry, surface_cell, counts, wavenumbers, target, direction_weight):
    owners = lax.axis_size(("gx", "gy"))
    rows_dev = surface_cell.shape[0]
    capacity = rows_dev // owners
    live_own = rows_dev // 4
    count_dirs = target.shape[2]
    num_freqs = wavenumbers.shape[0]
    living = (jnp.arange(rows_dev) < counts[0]).astype(jnp.float32)
    outgoing = (
        jnp.concatenate(
            [gather_rows(surface_cell, cell_state).T, geometry, jnp.ones((1, rows_dev), jnp.float32)], axis=0
        )
        * living[None, :]
    )
    outgoing = outgoing.reshape(24, capacity, owners).transpose(2, 0, 1).reshape(owners, -1, 128)
    arrived = exchange(outgoing, 1).reshape(owners, 24, capacity).transpose(1, 0, 2)
    marker = arrived[23]
    per_source = jnp.sum(marker, axis=1).astype(jnp.int32)
    offset = jnp.cumsum(per_source) - per_source
    position = offset[:, None] + jnp.arange(capacity, dtype=jnp.int32)[None, :]
    packed_slot = jnp.where(marker > 0.5, position, live_own).reshape(capacity * owners)
    selector = (packed_slot[:, None] == jnp.arange(live_own, dtype=jnp.int32)[None, :]).astype(jnp.bfloat16)
    compact = permute_columns(arrived[:23].reshape(23, capacity * owners), selector)
    east_x, north_y, upward = directions(count_dirs)
    direction_basis = jnp.stack([jnp.ones_like(east_x), east_x, north_y, upward])

    points = compact[16:19].T
    dirs_block = jnp.broadcast_to(jnp.stack([east_x, north_y, upward])[:, None, :], (3, ROW_CHUNK, count_dirs))
    kernel_all, sums = forward_sums(wavenumbers, points, dirs_block, compact)
    sums = sums[:, :8]
    far_field = sum_over_devices(far_field_of(sums, wavenumbers, direction_basis), owners)
    objective, weights = adjoint_weights(
        far_field, target, direction_weight, wavenumbers, direction_basis
    )

    padded = jnp.concatenate([weights, jnp.zeros_like(weights)], axis=1)
    products = adjoint_products(padded, kernel_all)[:, :8]
    backward = adjoint_sources(products, compact[19:22])
    spread = unpermute_columns(backward, selector)
    spread = spread.reshape(16, owners, capacity).transpose(1, 0, 2).reshape(owners, -1, 128)
    returned = exchange(spread, 2).reshape(owners, 16, capacity).transpose(2, 0, 1).reshape(rows_dev, 16)
    rows_major = returned * living[:, None]
    cell_adjoint = scatter_rows(surface_cell, rows_major, cell_state.shape[1])
    return (far_field, objective, cell_adjoint)


def solution(mesh):
    placed = (
        P(None, ("gx", "gy")),
        P(None, ("gx", "gy")),
        P(("gx", "gy")),
        P(("gx", "gy")),
        P(),
        P(),
        P(),
    )
    return jax.shard_map(
        on_device,
        mesh=mesh,
        in_specs=placed,
        out_specs=(P(), P(), P(None, ("gx", "gy"))),
        check_vma=False,
    )
```

```python
import functools
import math

import jax
import jax.numpy as jnp
from jax import lax
from jax.experimental import pallas as pl
from jax.experimental.pallas import tpu as pltpu
from jax.sharding import PartitionSpec as P

GOLDEN = math.pi * (3.0 - math.sqrt(5.0))
PI_A = round(math.pi * 32768.0) / 32768.0
PI_B = math.pi - PI_A
INV_PI = 1.0 / math.pi
SIN_C = [-0.16666657019913644, 0.00833301540393062, -0.00019806478078586938, 2.599750005030262e-06]
COS_C = [-0.4999993175258851, 0.041663973510963626, -0.0013855797199316853, 2.3191254010748703e-05]
SINPI_C = [3.141592578574041, -5.1677067848796066, 2.5500297991194887, -0.5980355679943354, 0.07720094563063706]
COSPI_C = [-4.934795411606951, 4.05844824012755, -1.332068921858188, 0.22002136541700046]


ROOT2 = math.sqrt(2.0)


def sincos_half_turns(v):
    w = v - jnp.floor(v + 0.5)
    z = w * w
    ps = SINPI_C[-1] * ROOT2
    for c in SINPI_C[-2::-1]:
        ps = c * ROOT2 + z * ps
    pc = COSPI_C[-1] * ROOT2
    for c in COSPI_C[-2::-1]:
        pc = c * ROOT2 + z * pc
    sine_half = w * ps
    cosine_half = ROOT2 + z * pc
    return (cosine_half * cosine_half - 1.0, sine_half * cosine_half)


def sincos_turns(u):
    n = jnp.floor(u + 0.5)
    w = u - n
    z = w * w
    ps = SINPI_C[-1]
    for c in SINPI_C[-2::-1]:
        ps = c + z * ps
    pc = COSPI_C[-1]
    for c in COSPI_C[-2::-1]:
        pc = c + z * pc
    half = n * 0.5
    sign = 1.0 - 4.0 * (half - jnp.floor(half))
    return (sign * (1.0 + z * pc), (sign * w) * ps)


def sincos(theta):
    n = jnp.floor(theta * INV_PI + 0.5)
    r = (theta - n * PI_A) - n * PI_B
    z = r * r
    ps = SIN_C[-1]
    for c in SIN_C[-2::-1]:
        ps = c + z * ps
    pc = COS_C[-1]
    for c in COS_C[-2::-1]:
        pc = c + z * pc
    half = n * 0.5
    sign = 1.0 - 4.0 * (half - jnp.floor(half))
    return (sign * (1.0 + z * pc), sign * (r + (r * z) * ps))


def directions(count_dirs):
    lattice = jnp.arange(count_dirs).astype(jnp.float32)
    height = 1.0 - (2.0 * lattice + 1.0) / count_dirs
    radius_xy = jnp.sqrt(1.0 - height * height)
    azimuth = jnp.mod(lattice * GOLDEN, 2.0 * math.pi)
    return (radius_xy * jnp.cos(azimuth), radius_xy * jnp.sin(azimuth), height)


def kernel_block(points, wavenum, east_x, north_y, upward):
    phases = wavenum * (
        points[0][:, None] * east_x[None, :]
        + points[1][:, None] * north_y[None, :]
        + points[2][:, None] * upward[None, :]
    )
    cosine, sine = sincos(phases)
    return jnp.concatenate([cosine, sine], axis=1).astype(jnp.bfloat16)


def source_rows(rows_block, level):
    surface_area = rows_block[22]
    normal = rows_block[19:22]
    pressure_real = rows_block[level] * surface_area
    pressure_imag = rows_block[4 + level] * surface_area
    return jnp.stack(
        [
            rows_block[8 + level] * surface_area,
            normal[0] * pressure_real,
            normal[1] * pressure_real,
            normal[2] * pressure_real,
            rows_block[12 + level] * surface_area,
            normal[0] * pressure_imag,
            normal[1] * pressure_imag,
            normal[2] * pressure_imag,
        ]
    ).astype(jnp.bfloat16)


def far_field_of(sums, wavenumbers, direction_basis):
    half_width = sums.shape[2] // 2
    cosine_part = sums[:, :, :half_width]
    sine_part = sums[:, :, half_width:]
    real_q = cosine_part[:, 0:4] + sine_part[:, 4:8]
    imag_q = cosine_part[:, 4:8] - sine_part[:, 0:4]
    real_z = jnp.sum(direction_basis[None] * real_q, axis=1)
    imag_z = jnp.sum(direction_basis[None] * imag_q, axis=1)
    wavenum = wavenumbers[:, None]
    return jnp.stack([-wavenum * imag_z, wavenum * real_z], axis=1)


def adjoint_weights(far_field, target, direction_weight, wavenumbers, direction_basis):
    count_dirs = far_field.shape[2]
    mismatch = far_field - target
    objective = jnp.sum(direction_weight * mismatch * mismatch) / count_dirs
    gradient = 2.0 * direction_weight * mismatch / count_dirs
    wavenum = wavenumbers[:, None]
    real_gz = wavenum * gradient[:, 1]
    imag_gz = -wavenum * gradient[:, 0]
    real_gq = direction_basis[None] * real_gz[:, None]
    imag_gq = direction_basis[None] * imag_gz[:, None]
    upper_half = jnp.concatenate([real_gq, -imag_gq], axis=2)
    lower_half = jnp.concatenate([imag_gq, real_gq], axis=2)
    return (objective, jnp.concatenate([upper_half, lower_half], axis=1).astype(jnp.bfloat16))


def adjoint_sources(products, normal):
    pressure_real = jnp.sum(normal[None] * products[:, 1:4], axis=1)
    pressure_imag = jnp.sum(normal[None] * products[:, 5:8], axis=1)
    return jnp.concatenate([pressure_real, pressure_imag, products[:, 0], products[:, 4]], axis=0)


ROW_BLOCK = 128
ADJ_BLOCK = 256
ROW_CHUNK = 16
LANE_CHUNK = 256


def forward_kernel(wave_ref, pts_ref, dirs_ref, rows_ref, cs_ref, q_ref, src_scr):
    step = pl.program_id(0)
    num_freqs = cs_ref.shape[0]
    count_dirs = dirs_ref.shape[2]
    turns = [wave_ref[level] * (0.5 * INV_PI) for level in range(num_freqs)]

    @pl.loop(0, ROW_BLOCK // ROW_CHUNK)
    def _(i):
        r0 = pl.multiple_of(i * ROW_CHUNK, ROW_CHUNK)
        coords = [
            jnp.broadcast_to(pts_ref[pl.ds(r0, ROW_CHUNK), c : c + 1], (ROW_CHUNK, LANE_CHUNK))
            for c in range(3)
        ]
        for j0 in range(0, count_dirs, LANE_CHUNK):
            lanes = slice(j0, j0 + LANE_CHUNK)
            along = (
                coords[0] * dirs_ref[0, :, lanes]
                + coords[1] * dirs_ref[1, :, lanes]
                + coords[2] * dirs_ref[2, :, lanes]
            )
            for level in range(num_freqs):
                cosine, sine = sincos_half_turns(turns[level] * along)
                cs_ref[level, pl.ds(r0, ROW_CHUNK), lanes] = cosine.astype(jnp.bfloat16)
                cs_ref[level, pl.ds(r0, ROW_CHUNK), j0 + count_dirs : j0 + count_dirs + LANE_CHUNK] = (
                    sine.astype(jnp.bfloat16)
                )

    @pl.when(step == 0)
    def _():
        q_ref[...] = jnp.zeros_like(q_ref)

    area = rows_ref[22:23, :]
    src_scr[...] = jnp.zeros_like(src_scr)
    for level in range(num_freqs):
        pressure_real = rows_ref[level : level + 1, :] * area
        pressure_imag = rows_ref[4 + level : 5 + level, :] * area
        src_scr[0:1, :] = rows_ref[8 + level : 9 + level, :] * area
        src_scr[4:5, :] = rows_ref[12 + level : 13 + level, :] * area
        for c in range(3):
            normal = rows_ref[19 + c : 20 + c, :]
            src_scr[1 + c : 2 + c, :] = normal * pressure_real
            src_scr[5 + c : 6 + c, :] = normal * pressure_imag
        source = src_scr[...].astype(jnp.bfloat16)
        q_ref[level] += jnp.dot(source, cs_ref[level], preferred_element_type=jnp.float32)


def forward_sums(wavenumbers, points, dirs_block, compact):
    num_freqs = wavenumbers.shape[0]
    rows = points.shape[0]
    count_dirs = dirs_block.shape[2]
    grid = (rows // ROW_BLOCK,)
    return pl.pallas_call(
        forward_kernel,
        grid=grid,
        in_specs=[
            pl.BlockSpec(memory_space=pltpu.SMEM),
            pl.BlockSpec((ROW_BLOCK, 3), lambda b: (b, 0)),
            pl.BlockSpec(dirs_block.shape, lambda b: (0, 0, 0)),
            pl.BlockSpec((compact.shape[0], ROW_BLOCK), lambda b: (0, b)),
        ],
        out_specs=[
            pl.BlockSpec((num_freqs, ROW_BLOCK, 2 * count_dirs), lambda b: (0, b, 0)),
            pl.BlockSpec((num_freqs, 16, 2 * count_dirs), lambda b: (0, 0, 0)),
        ],
        out_shape=[
            jax.ShapeDtypeStruct((num_freqs, rows, 2 * count_dirs), jnp.bfloat16),
            jax.ShapeDtypeStruct((num_freqs, 16, 2 * count_dirs), jnp.float32),
        ],
        scratch_shapes=[pltpu.VMEM((16, ROW_BLOCK), jnp.float32)],
        compiler_params=pltpu.CompilerParams(
            dimension_semantics=("arbitrary",), vmem_limit_bytes=48 * 1024 * 1024
        ),
        cost_estimate=pl.CostEstimate(
            flops=2 * 16 * rows * 2 * count_dirs * num_freqs + 60 * rows * count_dirs * num_freqs,
            transcendentals=0,
            bytes_accessed=2 * rows * 2 * count_dirs * num_freqs,
        ),
    )(wavenumbers, points, dirs_block, compact)


def adjoint_kernel(w_ref, cs_ref, out_ref):
    for level in range(cs_ref.shape[0]):
        out_ref[level] = lax.dot_general(
            w_ref[level], cs_ref[level], (((1,), (1,)), ((), ())), preferred_element_type=jnp.float32
        )


def adjoint_products(weights, kernel_all):
    num_freqs, rows, width = kernel_all.shape
    return pl.pallas_call(
        adjoint_kernel,
        grid=(rows // ADJ_BLOCK,),
        in_specs=[
            pl.BlockSpec(weights.shape, lambda b: (0, 0, 0)),
            pl.BlockSpec((num_freqs, ADJ_BLOCK, width), lambda b: (0, b, 0)),
        ],
        out_specs=pl.BlockSpec((num_freqs, weights.shape[1], ADJ_BLOCK), lambda b: (0, 0, b)),
        out_shape=jax.ShapeDtypeStruct((num_freqs, weights.shape[1], rows), jnp.float32),
        compiler_params=pltpu.CompilerParams(
            dimension_semantics=("arbitrary",), vmem_limit_bytes=48 * 1024 * 1024
        ),
        cost_estimate=pl.CostEstimate(
            flops=2 * weights.shape[1] * rows * width * num_freqs,
            transcendentals=0,
            bytes_accessed=2 * rows * width * num_freqs,
        ),
    )(weights, kernel_all)


def split_bf16(values):
    high = lax.reduce_precision(values, exponent_bits=8, mantissa_bits=7)
    rest = values - high
    middle = lax.reduce_precision(rest, exponent_bits=8, mantissa_bits=7)
    low = rest - middle
    return jnp.concatenate([high, middle, low], axis=0).astype(jnp.bfloat16)


def join_parts(product, channels):
    return (product[:channels] + product[channels : 2 * channels]) + product[2 * channels :]


def permute_columns(values, selector):
    product = jnp.dot(split_bf16(values), selector, preferred_element_type=jnp.float32)
    return join_parts(product, values.shape[0])


def unpermute_columns(values, selector):
    product = lax.dot_general(
        split_bf16(values), selector, (((1,), (1,)), ((), ())), preferred_element_type=jnp.float32
    )
    return join_parts(product, values.shape[0])


CHAINS = 8


def scatter_kernel(cell_ref, rows_ref, out_ref, *accs):
    for acc in accs:
        acc[...] = jnp.zeros_like(acc)
    chains = len(accs)

    def body(i, carry):
        for k in range(chains):
            row = i * chains + k
            cell = cell_ref[row]
            accs[k][pl.ds(cell, 1), :] += rows_ref[pl.ds(row, 1), :]
        return carry

    lax.fori_loop(0, rows_ref.shape[0] // chains, body, 0, unroll=8)
    total = accs[0][...]
    for acc in accs[1:]:
        total = total + acc[...]
    out_ref[...] = total.T


def scatter_rows(surface_cell, rows_major, cells):
    width = rows_major.shape[1]
    return pl.pallas_call(
        scatter_kernel,
        grid_spec=pltpu.PrefetchScalarGridSpec(
            num_scalar_prefetch=1,
            grid=(1,),
            in_specs=[pl.BlockSpec(rows_major.shape, lambda i, c: (0, 0))],
            out_specs=pl.BlockSpec((width, cells), lambda i, c: (0, 0)),
            scratch_shapes=[pltpu.VMEM((cells, width), jnp.float32) for _ in range(CHAINS)],
        ),
        out_shape=jax.ShapeDtypeStruct((width, cells), jnp.float32),
        compiler_params=pltpu.CompilerParams(vmem_limit_bytes=48 * 1024 * 1024),
    )(surface_cell, rows_major)


GATHER_UNROLL = 128


def gather_kernel(cell_ref, state_ref, out_ref, table_ref):
    table_ref[...] = state_ref[...].T

    def body(i, carry):
        for k in range(GATHER_UNROLL):
            row = i * GATHER_UNROLL + k
            out_ref[pl.ds(row, 1), :] = table_ref[pl.ds(cell_ref[row], 1), :]
        return carry

    lax.fori_loop(0, out_ref.shape[0] // GATHER_UNROLL, body, 0)


def gather_rows(surface_cell, state):
    rows = surface_cell.shape[0]
    channels, cells = state.shape
    return pl.pallas_call(
        gather_kernel,
        grid_spec=pltpu.PrefetchScalarGridSpec(
            num_scalar_prefetch=1,
            grid=(1,),
            in_specs=[pl.BlockSpec(state.shape, lambda i, c: (0, 0))],
            out_specs=pl.BlockSpec((rows, channels), lambda i, c: (0, 0)),
            scratch_shapes=[pltpu.VMEM((cells, channels), state.dtype)],
        ),
        out_shape=jax.ShapeDtypeStruct((rows, channels), state.dtype),
        compiler_params=pltpu.CompilerParams(vmem_limit_bytes=48 * 1024 * 1024),
    )(surface_cell, state)


MESH_IDS = pl.DeviceIdType.MESH


def reduce_kernel(nx, ny, x_ref, out_ref, part_a, part_b, got_a, got_b, sems):
    b0 = lax.axis_index("gx")
    a0 = lax.axis_index("gy")
    barrier = pltpu.get_barrier_semaphore()
    for t in range(1, ny):
        pl.semaphore_signal(barrier, inc=1, device_id=(b0, lax.rem(a0 + t, ny)), device_id_type=MESH_IDS)
    for t in range(1, nx):
        pl.semaphore_signal(barrier, inc=1, device_id=(lax.rem(b0 + t, nx), a0), device_id_type=MESH_IDS)
    pl.semaphore_wait(barrier, nx + ny - 2)

    def exchange(phase, src_of, dst_of, peers, along_x):
        copies = []
        for t in range(1, peers):
            if along_x:
                peer = lax.rem(b0 + t, nx)
                me, device = b0, (peer, a0)
            else:
                peer = lax.rem(a0 + t, ny)
                me, device = a0, (b0, peer)
            copy = pltpu.make_async_remote_copy(
                src_ref=src_of(peer),
                dst_ref=dst_of(me),
                send_sem=sems.at[phase, 0, peer],
                recv_sem=sems.at[phase, 1, me],
                device_id=device,
                device_id_type=MESH_IDS,
            )
            copy.start()
            copies.append((peer, device))
        for peer, device in copies:
            pltpu.make_async_remote_copy(
                src_ref=src_of(peer),
                dst_ref=dst_of(peer),
                send_sem=sems.at[phase, 0, peer],
                recv_sem=sems.at[phase, 1, peer],
                device_id=device,
                device_id_type=MESH_IDS,
            ).wait()

    exchange(0, lambda a: x_ref.at[a], lambda a: got_a.at[a], ny, False)
    got_a[a0] = x_ref[a0]
    part_a[...] = jnp.sum(got_a[...], axis=0)
    exchange(1, lambda b: part_a, lambda b: got_b.at[b], nx, True)
    got_b[b0] = part_a[...]
    part_b[...] = jnp.sum(got_b[...], axis=0)
    exchange(2, lambda a: part_b, lambda a: out_ref.at[a], ny, False)
    out_ref[a0] = part_b[...]


def exchange_kernel(nx, ny, x_ref, out_ref, landing, send_sems, recv_sems):
    total = nx * ny
    me = lax.axis_index("gx") * ny + lax.axis_index("gy")
    barrier = pltpu.get_barrier_semaphore()

    def where(peer):
        return (peer // ny, lax.rem(peer, ny))

    def copy_to(peer, slot):
        return pltpu.make_async_remote_copy(
            src_ref=x_ref.at[peer],
            dst_ref=landing.at[slot],
            send_sem=send_sems.at[peer],
            recv_sem=recv_sems.at[slot],
            device_id=where(peer),
            device_id_type=MESH_IDS,
        )

    def greet(t, carry):
        pl.semaphore_signal(barrier, inc=1, device_id=where(lax.rem(me + t, total)), device_id_type=MESH_IDS)
        return carry

    lax.fori_loop(1, total, greet, 0, unroll=8)
    pl.semaphore_wait(barrier, total - 1)

    def send(t, carry):
        copy_to(lax.rem(me + t, total), me).start()
        return carry

    lax.fori_loop(1, total, send, 0, unroll=8)
    landing[me] = x_ref[me]

    def finish(t, carry):
        peer = lax.rem(me + t, total)
        copy_to(peer, peer).wait()
        return carry

    lax.fori_loop(1, total, finish, 0, unroll=8)
    out_ref[...] = landing[...]


def exchange(blocks, exchange_id):
    nx = lax.axis_size("gx")
    ny = lax.axis_size("gy")
    return pl.pallas_call(
        functools.partial(exchange_kernel, nx, ny),
        in_specs=[pl.BlockSpec(memory_space=pltpu.VMEM)],
        out_specs=pl.BlockSpec(memory_space=pltpu.VMEM),
        out_shape=jax.ShapeDtypeStruct(blocks.shape, blocks.dtype),
        scratch_shapes=[
            pltpu.VMEM(blocks.shape, blocks.dtype),
            pltpu.SemaphoreType.DMA((nx * ny,)),
            pltpu.SemaphoreType.DMA((nx * ny,)),
        ],
        compiler_params=pltpu.CompilerParams(collective_id=exchange_id, has_side_effects=True),
    )(blocks)


def sum_over_devices(partial, owners):
    nx = lax.axis_size("gx")
    ny = lax.axis_size("gy")
    lanes = partial.size // (nx * ny)
    shaped = partial.reshape(ny, nx, lanes)
    peers = max(nx, ny)
    total = pl.pallas_call(
        functools.partial(reduce_kernel, nx, ny),
        in_specs=[pl.BlockSpec(memory_space=pltpu.VMEM)],
        out_specs=pl.BlockSpec(memory_space=pltpu.VMEM),
        out_shape=jax.ShapeDtypeStruct(shaped.shape, jnp.float32),
        scratch_shapes=[
            pltpu.VMEM((nx, lanes), jnp.float32),
            pltpu.VMEM((nx, lanes), jnp.float32),
            pltpu.VMEM((ny, nx, lanes), jnp.float32),
            pltpu.VMEM((nx, nx, lanes), jnp.float32),
            pltpu.SemaphoreType.DMA((3, 2, peers)),
        ],
        compiler_params=pltpu.CompilerParams(collective_id=0, has_side_effects=True),
    )(shaped)
    return total.reshape(partial.shape)


def sum_over_devices_a2a(partial, owners):
    chunks = partial.reshape(owners, -1)
    got = lax.all_to_all(chunks, ("gx", "gy"), split_axis=0, concat_axis=0, tiled=True)
    mine = jnp.sum(got, axis=0, keepdims=True)
    spread = jnp.broadcast_to(mine, chunks.shape)
    full = lax.all_to_all(spread, ("gx", "gy"), split_axis=0, concat_axis=0, tiled=True)
    return full.reshape(partial.shape)


def on_device(cell_state, geometry, surface_cell, counts, wavenumbers, target, direction_weight):
    owners = lax.axis_size(("gx", "gy"))
    rows_dev = surface_cell.shape[0]
    capacity = rows_dev // owners
    live_own = rows_dev // 4
    count_dirs = target.shape[2]
    num_freqs = wavenumbers.shape[0]
    living = (jnp.arange(rows_dev) < counts[0]).astype(jnp.float32)
    outgoing = (
        jnp.concatenate(
            [gather_rows(surface_cell, cell_state).T, geometry, jnp.ones((1, rows_dev), jnp.float32)], axis=0
        )
        * living[None, :]
    )
    outgoing = outgoing.reshape(24, capacity, owners).transpose(2, 0, 1).reshape(owners, -1, 128)
    arrived = exchange(outgoing, 1).reshape(owners, 24, capacity).transpose(1, 0, 2)
    marker = arrived[23]
    per_source = jnp.sum(marker, axis=1).astype(jnp.int32)
    offset = jnp.cumsum(per_source) - per_source
    position = offset[:, None] + jnp.arange(capacity, dtype=jnp.int32)[None, :]
    packed_slot = jnp.where(marker > 0.5, position, live_own).reshape(capacity * owners)
    selector = (packed_slot[:, None] == jnp.arange(live_own, dtype=jnp.int32)[None, :]).astype(jnp.bfloat16)
    compact = permute_columns(arrived[:23].reshape(23, capacity * owners), selector)
    east_x, north_y, upward = directions(count_dirs)
    direction_basis = jnp.stack([jnp.ones_like(east_x), east_x, north_y, upward])

    points = compact[16:19].T
    dirs_block = jnp.broadcast_to(jnp.stack([east_x, north_y, upward])[:, None, :], (3, ROW_CHUNK, count_dirs))
    kernel_all, sums = forward_sums(wavenumbers, points, dirs_block, compact)
    sums = sums[:, :8]
    far_field = sum_over_devices(far_field_of(sums, wavenumbers, direction_basis), owners)
    objective, weights = adjoint_weights(
        far_field, target, direction_weight, wavenumbers, direction_basis
    )

    padded = jnp.concatenate([weights, jnp.zeros_like(weights)], axis=1)
    products = adjoint_products(padded, kernel_all)[:, :8]
    backward = adjoint_sources(products, compact[19:22])
    spread = unpermute_columns(backward, selector)
    spread = spread.reshape(16, owners, capacity).transpose(1, 0, 2).reshape(owners, -1, 128)
    returned = exchange(spread, 2).reshape(owners, 16, capacity).transpose(2, 0, 1).reshape(rows_dev, 16)
    rows_major = returned * living[:, None]
    cell_adjoint = scatter_rows(surface_cell, rows_major, cell_state.shape[1])
    return (far_field, objective, cell_adjoint)


def solution(mesh):
    placed = (
        P(None, ("gx", "gy")),
        P(None, ("gx", "gy")),
        P(("gx", "gy")),
        P(("gx", "gy")),
        P(),
        P(),
        P(),
    )
    return jax.shard_map(
        on_device,
        mesh=mesh,
        in_specs=placed,
        out_specs=(P(), P(), P(None, ("gx", "gy"))),
        check_vma=False,
    )
```

```python
import functools
import math

import jax
import jax.numpy as jnp
from jax import lax
from jax.experimental import pallas as pl
from jax.experimental.pallas import tpu as pltpu
from jax.sharding import PartitionSpec as P

GOLDEN = math.pi * (3.0 - math.sqrt(5.0))
PI_A = round(math.pi * 32768.0) / 32768.0
PI_B = math.pi - PI_A
INV_PI = 1.0 / math.pi
SIN_C = [-0.16666657019913644, 0.00833301540393062, -0.00019806478078586938, 2.599750005030262e-06]
COS_C = [-0.4999993175258851, 0.041663973510963626, -0.0013855797199316853, 2.3191254010748703e-05]
SINPI_C = [3.141592578574041, -5.1677067848796066, 2.5500297991194887, -0.5980355679943354, 0.07720094563063706]
COSPI_C = [-4.934795411606951, 4.05844824012755, -1.332068921858188, 0.22002136541700046]


ROOT2 = math.sqrt(2.0)


def sincos_half_turns(v):
    w = v - jnp.floor(v + 0.5)
    z = w * w
    ps = SINPI_C[-1] * ROOT2
    for c in SINPI_C[-2::-1]:
        ps = c * ROOT2 + z * ps
    pc = COSPI_C[-1] * ROOT2
    for c in COSPI_C[-2::-1]:
        pc = c * ROOT2 + z * pc
    sine_half = w * ps
    cosine_half = ROOT2 + z * pc
    return (cosine_half * cosine_half - 1.0, sine_half * cosine_half)


def sincos_turns(u):
    n = jnp.floor(u + 0.5)
    w = u - n
    z = w * w
    ps = SINPI_C[-1]
    for c in SINPI_C[-2::-1]:
        ps = c + z * ps
    pc = COSPI_C[-1]
    for c in COSPI_C[-2::-1]:
        pc = c + z * pc
    half = n * 0.5
    sign = 1.0 - 4.0 * (half - jnp.floor(half))
    return (sign * (1.0 + z * pc), (sign * w) * ps)


def sincos(theta):
    n = jnp.floor(theta * INV_PI + 0.5)
    r = (theta - n * PI_A) - n * PI_B
    z = r * r
    ps = SIN_C[-1]
    for c in SIN_C[-2::-1]:
        ps = c + z * ps
    pc = COS_C[-1]
    for c in COS_C[-2::-1]:
        pc = c + z * pc
    half = n * 0.5
    sign = 1.0 - 4.0 * (half - jnp.floor(half))
    return (sign * (1.0 + z * pc), sign * (r + (r * z) * ps))


def directions(count_dirs):
    lattice = jnp.arange(count_dirs).astype(jnp.float32)
    height = 1.0 - (2.0 * lattice + 1.0) / count_dirs
    radius_xy = jnp.sqrt(1.0 - height * height)
    azimuth = jnp.mod(lattice * GOLDEN, 2.0 * math.pi)
    return (radius_xy * jnp.cos(azimuth), radius_xy * jnp.sin(azimuth), height)


def kernel_block(points, wavenum, east_x, north_y, upward):
    phases = wavenum * (
        points[0][:, None] * east_x[None, :]
        + points[1][:, None] * north_y[None, :]
        + points[2][:, None] * upward[None, :]
    )
    cosine, sine = sincos(phases)
    return jnp.concatenate([cosine, sine], axis=1).astype(jnp.bfloat16)


def source_rows(rows_block, level):
    surface_area = rows_block[22]
    normal = rows_block[19:22]
    pressure_real = rows_block[level] * surface_area
    pressure_imag = rows_block[4 + level] * surface_area
    return jnp.stack(
        [
            rows_block[8 + level] * surface_area,
            normal[0] * pressure_real,
            normal[1] * pressure_real,
            normal[2] * pressure_real,
            rows_block[12 + level] * surface_area,
            normal[0] * pressure_imag,
            normal[1] * pressure_imag,
            normal[2] * pressure_imag,
        ]
    ).astype(jnp.bfloat16)


def far_field_of(sums, wavenumbers, direction_basis):
    half_width = sums.shape[2] // 2
    cosine_part = sums[:, :, :half_width]
    sine_part = sums[:, :, half_width:]
    real_q = cosine_part[:, 0:4] + sine_part[:, 4:8]
    imag_q = cosine_part[:, 4:8] - sine_part[:, 0:4]
    real_z = jnp.sum(direction_basis[None] * real_q, axis=1)
    imag_z = jnp.sum(direction_basis[None] * imag_q, axis=1)
    wavenum = wavenumbers[:, None]
    return jnp.stack([-wavenum * imag_z, wavenum * real_z], axis=1)


def adjoint_weights(far_field, target, direction_weight, wavenumbers, direction_basis):
    count_dirs = far_field.shape[2]
    mismatch = far_field - target
    objective = jnp.sum(direction_weight * mismatch * mismatch) / count_dirs
    gradient = 2.0 * direction_weight * mismatch / count_dirs
    wavenum = wavenumbers[:, None]
    real_gz = wavenum * gradient[:, 1]
    imag_gz = -wavenum * gradient[:, 0]
    real_gq = direction_basis[None] * real_gz[:, None]
    imag_gq = direction_basis[None] * imag_gz[:, None]
    upper_half = jnp.concatenate([real_gq, -imag_gq], axis=2)
    lower_half = jnp.concatenate([imag_gq, real_gq], axis=2)
    return (objective, jnp.concatenate([upper_half, lower_half], axis=1).astype(jnp.bfloat16))


def adjoint_sources(products, normal):
    pressure_real = jnp.sum(normal[None] * products[:, 1:4], axis=1)
    pressure_imag = jnp.sum(normal[None] * products[:, 5:8], axis=1)
    return jnp.concatenate([pressure_real, pressure_imag, products[:, 0], products[:, 4]], axis=0)


ROW_BLOCK = 128
ADJ_BLOCK = 256
ROW_CHUNK = 32
LANE_CHUNK = 256


def forward_kernel(wave_ref, pts_ref, dirs_ref, rows_ref, cs_ref, q_ref, src_scr):
    step = pl.program_id(0)
    num_freqs = cs_ref.shape[0]
    count_dirs = dirs_ref.shape[2]
    turns = [wave_ref[level] * (0.5 * INV_PI) for level in range(num_freqs)]

    @pl.loop(0, ROW_BLOCK // ROW_CHUNK)
    def _(i):
        r0 = pl.multiple_of(i * ROW_CHUNK, ROW_CHUNK)
        coords = [
            jnp.broadcast_to(pts_ref[pl.ds(r0, ROW_CHUNK), c : c + 1], (ROW_CHUNK, LANE_CHUNK))
            for c in range(3)
        ]
        for j0 in range(0, count_dirs, LANE_CHUNK):
            lanes = slice(j0, j0 + LANE_CHUNK)
            along = (
                coords[0] * dirs_ref[0, :, lanes]
                + coords[1] * dirs_ref[1, :, lanes]
                + coords[2] * dirs_ref[2, :, lanes]
            )
            for level in range(num_freqs):
                cosine, sine = sincos_half_turns(turns[level] * along)
                cs_ref[level, pl.ds(r0, ROW_CHUNK), lanes] = cosine.astype(jnp.bfloat16)
                cs_ref[level, pl.ds(r0, ROW_CHUNK), j0 + count_dirs : j0 + count_dirs + LANE_CHUNK] = (
                    sine.astype(jnp.bfloat16)
                )

    @pl.when(step == 0)
    def _():
        q_ref[...] = jnp.zeros_like(q_ref)

    area = rows_ref[22:23, :]
    src_scr[...] = jnp.zeros_like(src_scr)
    for level in range(num_freqs):
        pressure_real = rows_ref[level : level + 1, :] * area
        pressure_imag = rows_ref[4 + level : 5 + level, :] * area
        src_scr[0:1, :] = rows_ref[8 + level : 9 + level, :] * area
        src_scr[4:5, :] = rows_ref[12 + level : 13 + level, :] * area
        for c in range(3):
            normal = rows_ref[19 + c : 20 + c, :]
            src_scr[1 + c : 2 + c, :] = normal * pressure_real
            src_scr[5 + c : 6 + c, :] = normal * pressure_imag
        source = src_scr[...].astype(jnp.bfloat16)
        q_ref[level] += jnp.dot(source, cs_ref[level], preferred_element_type=jnp.float32)


def forward_sums(wavenumbers, points, dirs_block, compact):
    num_freqs = wavenumbers.shape[0]
    rows = points.shape[0]
    count_dirs = dirs_block.shape[2]
    grid = (rows // ROW_BLOCK,)
    return pl.pallas_call(
        forward_kernel,
        grid=grid,
        in_specs=[
            pl.BlockSpec(memory_space=pltpu.SMEM),
            pl.BlockSpec((ROW_BLOCK, 3), lambda b: (b, 0)),
            pl.BlockSpec(dirs_block.shape, lambda b: (0, 0, 0)),
            pl.BlockSpec((compact.shape[0], ROW_BLOCK), lambda b: (0, b)),
        ],
        out_specs=[
            pl.BlockSpec((num_freqs, ROW_BLOCK, 2 * count_dirs), lambda b: (0, b, 0)),
            pl.BlockSpec((num_freqs, 16, 2 * count_dirs), lambda b: (0, 0, 0)),
        ],
        out_shape=[
            jax.ShapeDtypeStruct((num_freqs, rows, 2 * count_dirs), jnp.bfloat16),
            jax.ShapeDtypeStruct((num_freqs, 16, 2 * count_dirs), jnp.float32),
        ],
        scratch_shapes=[pltpu.VMEM((16, ROW_BLOCK), jnp.float32)],
        compiler_params=pltpu.CompilerParams(
            dimension_semantics=("arbitrary",), vmem_limit_bytes=48 * 1024 * 1024
        ),
        cost_estimate=pl.CostEstimate(
            flops=2 * 16 * rows * 2 * count_dirs * num_freqs + 60 * rows * count_dirs * num_freqs,
            transcendentals=0,
            bytes_accessed=2 * rows * 2 * count_dirs * num_freqs,
        ),
    )(wavenumbers, points, dirs_block, compact)


def adjoint_kernel(w_ref, cs_ref, out_ref):
    for level in range(cs_ref.shape[0]):
        out_ref[level] = lax.dot_general(
            w_ref[level], cs_ref[level], (((1,), (1,)), ((), ())), preferred_element_type=jnp.float32
        )


def adjoint_products(weights, kernel_all):
    num_freqs, rows, width = kernel_all.shape
    return pl.pallas_call(
        adjoint_kernel,
        grid=(rows // ADJ_BLOCK,),
        in_specs=[
            pl.BlockSpec(weights.shape, lambda b: (0, 0, 0)),
            pl.BlockSpec((num_freqs, ADJ_BLOCK, width), lambda b: (0, b, 0)),
        ],
        out_specs=pl.BlockSpec((num_freqs, weights.shape[1], ADJ_BLOCK), lambda b: (0, 0, b)),
        out_shape=jax.ShapeDtypeStruct((num_freqs, weights.shape[1], rows), jnp.float32),
        compiler_params=pltpu.CompilerParams(
            dimension_semantics=("arbitrary",), vmem_limit_bytes=48 * 1024 * 1024
        ),
        cost_estimate=pl.CostEstimate(
            flops=2 * weights.shape[1] * rows * width * num_freqs,
            transcendentals=0,
            bytes_accessed=2 * rows * width * num_freqs,
        ),
    )(weights, kernel_all)


def split_bf16(values):
    high = lax.reduce_precision(values, exponent_bits=8, mantissa_bits=7)
    rest = values - high
    middle = lax.reduce_precision(rest, exponent_bits=8, mantissa_bits=7)
    low = rest - middle
    return jnp.concatenate([high, middle, low], axis=0).astype(jnp.bfloat16)


def join_parts(product, channels):
    return (product[:channels] + product[channels : 2 * channels]) + product[2 * channels :]


def permute_columns(values, selector):
    product = jnp.dot(split_bf16(values), selector, preferred_element_type=jnp.float32)
    return join_parts(product, values.shape[0])


def unpermute_columns(values, selector):
    product = lax.dot_general(
        split_bf16(values), selector, (((1,), (1,)), ((), ())), preferred_element_type=jnp.float32
    )
    return join_parts(product, values.shape[0])


CHAINS = 8


def scatter_kernel(cell_ref, rows_ref, out_ref, *accs):
    for acc in accs:
        acc[...] = jnp.zeros_like(acc)
    chains = len(accs)

    def body(i, carry):
        for k in range(chains):
            row = i * chains + k
            cell = cell_ref[row]
            accs[k][pl.ds(cell, 1), :] += rows_ref[pl.ds(row, 1), :]
        return carry

    lax.fori_loop(0, rows_ref.shape[0] // chains, body, 0, unroll=8)
    total = accs[0][...]
    for acc in accs[1:]:
        total = total + acc[...]
    out_ref[...] = total.T


def scatter_rows(surface_cell, rows_major, cells):
    width = rows_major.shape[1]
    return pl.pallas_call(
        scatter_kernel,
        grid_spec=pltpu.PrefetchScalarGridSpec(
            num_scalar_prefetch=1,
            grid=(1,),
            in_specs=[pl.BlockSpec(rows_major.shape, lambda i, c: (0, 0))],
            out_specs=pl.BlockSpec((width, cells), lambda i, c: (0, 0)),
            scratch_shapes=[pltpu.VMEM((cells, width), jnp.float32) for _ in range(CHAINS)],
        ),
        out_shape=jax.ShapeDtypeStruct((width, cells), jnp.float32),
        compiler_params=pltpu.CompilerParams(vmem_limit_bytes=48 * 1024 * 1024),
    )(surface_cell, rows_major)


GATHER_UNROLL = 128


def gather_kernel(cell_ref, state_ref, out_ref, table_ref):
    table_ref[...] = state_ref[...].T

    def body(i, carry):
        for k in range(GATHER_UNROLL):
            row = i * GATHER_UNROLL + k
            out_ref[pl.ds(row, 1), :] = table_ref[pl.ds(cell_ref[row], 1), :]
        return carry

    lax.fori_loop(0, out_ref.shape[0] // GATHER_UNROLL, body, 0)


def gather_rows(surface_cell, state):
    rows = surface_cell.shape[0]
    channels, cells = state.shape
    return pl.pallas_call(
        gather_kernel,
        grid_spec=pltpu.PrefetchScalarGridSpec(
            num_scalar_prefetch=1,
            grid=(1,),
            in_specs=[pl.BlockSpec(state.shape, lambda i, c: (0, 0))],
            out_specs=pl.BlockSpec((rows, channels), lambda i, c: (0, 0)),
            scratch_shapes=[pltpu.VMEM((cells, channels), state.dtype)],
        ),
        out_shape=jax.ShapeDtypeStruct((rows, channels), state.dtype),
        compiler_params=pltpu.CompilerParams(vmem_limit_bytes=48 * 1024 * 1024),
    )(surface_cell, state)


MESH_IDS = pl.DeviceIdType.MESH


def reduce_kernel(nx, ny, x_ref, out_ref, part_a, part_b, got_a, got_b, sems):
    b0 = lax.axis_index("gx")
    a0 = lax.axis_index("gy")
    barrier = pltpu.get_barrier_semaphore()
    for t in range(1, ny):
        pl.semaphore_signal(barrier, inc=1, device_id=(b0, lax.rem(a0 + t, ny)), device_id_type=MESH_IDS)
    for t in range(1, nx):
        pl.semaphore_signal(barrier, inc=1, device_id=(lax.rem(b0 + t, nx), a0), device_id_type=MESH_IDS)
    pl.semaphore_wait(barrier, nx + ny - 2)

    def exchange(phase, src_of, dst_of, peers, along_x):
        copies = []
        for t in range(1, peers):
            if along_x:
                peer = lax.rem(b0 + t, nx)
                me, device = b0, (peer, a0)
            else:
                peer = lax.rem(a0 + t, ny)
                me, device = a0, (b0, peer)
            copy = pltpu.make_async_remote_copy(
                src_ref=src_of(peer),
                dst_ref=dst_of(me),
                send_sem=sems.at[phase, 0, peer],
                recv_sem=sems.at[phase, 1, me],
                device_id=device,
                device_id_type=MESH_IDS,
            )
            copy.start()
            copies.append((peer, device))
        for peer, device in copies:
            pltpu.make_async_remote_copy(
                src_ref=src_of(peer),
                dst_ref=dst_of(peer),
                send_sem=sems.at[phase, 0, peer],
                recv_sem=sems.at[phase, 1, peer],
                device_id=device,
                device_id_type=MESH_IDS,
            ).wait()

    exchange(0, lambda a: x_ref.at[a], lambda a: got_a.at[a], ny, False)
    got_a[a0] = x_ref[a0]
    part_a[...] = jnp.sum(got_a[...], axis=0)
    exchange(1, lambda b: part_a, lambda b: got_b.at[b], nx, True)
    got_b[b0] = part_a[...]
    part_b[...] = jnp.sum(got_b[...], axis=0)
    exchange(2, lambda a: part_b, lambda a: out_ref.at[a], ny, False)
    out_ref[a0] = part_b[...]


def exchange_kernel(nx, ny, x_ref, out_ref, landing, send_sems, recv_sems):
    total = nx * ny
    me = lax.axis_index("gx") * ny + lax.axis_index("gy")
    barrier = pltpu.get_barrier_semaphore()

    def where(peer):
        return (peer // ny, lax.rem(peer, ny))

    def copy_to(peer, slot):
        return pltpu.make_async_remote_copy(
            src_ref=x_ref.at[peer],
            dst_ref=landing.at[slot],
            send_sem=send_sems.at[peer],
            recv_sem=recv_sems.at[slot],
            device_id=where(peer),
            device_id_type=MESH_IDS,
        )

    def greet(t, carry):
        pl.semaphore_signal(barrier, inc=1, device_id=where(lax.rem(me + t, total)), device_id_type=MESH_IDS)
        return carry

    lax.fori_loop(1, total, greet, 0, unroll=8)
    pl.semaphore_wait(barrier, total - 1)

    def send(t, carry):
        copy_to(lax.rem(me + t, total), me).start()
        return carry

    lax.fori_loop(1, total, send, 0, unroll=8)
    landing[me] = x_ref[me]

    def finish(t, carry):
        peer = lax.rem(me + t, total)
        copy_to(peer, peer).wait()
        return carry

    lax.fori_loop(1, total, finish, 0, unroll=8)
    out_ref[...] = landing[...]


def exchange(blocks, exchange_id):
    nx = lax.axis_size("gx")
    ny = lax.axis_size("gy")
    return pl.pallas_call(
        functools.partial(exchange_kernel, nx, ny),
        in_specs=[pl.BlockSpec(memory_space=pltpu.VMEM)],
        out_specs=pl.BlockSpec(memory_space=pltpu.VMEM),
        out_shape=jax.ShapeDtypeStruct(blocks.shape, blocks.dtype),
        scratch_shapes=[
            pltpu.VMEM(blocks.shape, blocks.dtype),
            pltpu.SemaphoreType.DMA((nx * ny,)),
            pltpu.SemaphoreType.DMA((nx * ny,)),
        ],
        compiler_params=pltpu.CompilerParams(collective_id=exchange_id, has_side_effects=True),
    )(blocks)


def sum_over_devices(partial, owners):
    nx = lax.axis_size("gx")
    ny = lax.axis_size("gy")
    lanes = partial.size // (nx * ny)
    shaped = partial.reshape(ny, nx, lanes)
    peers = max(nx, ny)
    total = pl.pallas_call(
        functools.partial(reduce_kernel, nx, ny),
        in_specs=[pl.BlockSpec(memory_space=pltpu.VMEM)],
        out_specs=pl.BlockSpec(memory_space=pltpu.VMEM),
        out_shape=jax.ShapeDtypeStruct(shaped.shape, jnp.float32),
        scratch_shapes=[
            pltpu.VMEM((nx, lanes), jnp.float32),
            pltpu.VMEM((nx, lanes), jnp.float32),
            pltpu.VMEM((ny, nx, lanes), jnp.float32),
            pltpu.VMEM((nx, nx, lanes), jnp.float32),
            pltpu.SemaphoreType.DMA((3, 2, peers)),
        ],
        compiler_params=pltpu.CompilerParams(collective_id=0, has_side_effects=True),
    )(shaped)
    return total.reshape(partial.shape)


def sum_over_devices_a2a(partial, owners):
    chunks = partial.reshape(owners, -1)
    got = lax.all_to_all(chunks, ("gx", "gy"), split_axis=0, concat_axis=0, tiled=True)
    mine = jnp.sum(got, axis=0, keepdims=True)
    spread = jnp.broadcast_to(mine, chunks.shape)
    full = lax.all_to_all(spread, ("gx", "gy"), split_axis=0, concat_axis=0, tiled=True)
    return full.reshape(partial.shape)


def on_device(cell_state, geometry, surface_cell, counts, wavenumbers, target, direction_weight):
    owners = lax.axis_size(("gx", "gy"))
    rows_dev = surface_cell.shape[0]
    capacity = rows_dev // owners
    live_own = rows_dev // 4
    count_dirs = target.shape[2]
    num_freqs = wavenumbers.shape[0]
    living = (jnp.arange(rows_dev) < counts[0]).astype(jnp.float32)
    outgoing = (
        jnp.concatenate(
            [gather_rows(surface_cell, cell_state).T, geometry, jnp.ones((1, rows_dev), jnp.float32)], axis=0
        )
        * living[None, :]
    )
    outgoing = outgoing.reshape(24, capacity, owners).transpose(2, 0, 1).reshape(owners, -1, 128)
    arrived = exchange(outgoing, 1).reshape(owners, 24, capacity).transpose(1, 0, 2)
    marker = arrived[23]
    per_source = jnp.sum(marker, axis=1).astype(jnp.int32)
    offset = jnp.cumsum(per_source) - per_source
    position = offset[:, None] + jnp.arange(capacity, dtype=jnp.int32)[None, :]
    packed_slot = jnp.where(marker > 0.5, position, live_own).reshape(capacity * owners)
    selector = (packed_slot[:, None] == jnp.arange(live_own, dtype=jnp.int32)[None, :]).astype(jnp.bfloat16)
    compact = permute_columns(arrived[:23].reshape(23, capacity * owners), selector)
    east_x, north_y, upward = directions(count_dirs)
    direction_basis = jnp.stack([jnp.ones_like(east_x), east_x, north_y, upward])

    points = compact[16:19].T
    dirs_block = jnp.broadcast_to(jnp.stack([east_x, north_y, upward])[:, None, :], (3, ROW_CHUNK, count_dirs))
    kernel_all, sums = forward_sums(wavenumbers, points, dirs_block, compact)
    sums = sums[:, :8]
    far_field = sum_over_devices(far_field_of(sums, wavenumbers, direction_basis), owners)
    objective, weights = adjoint_weights(
        far_field, target, direction_weight, wavenumbers, direction_basis
    )

    padded = jnp.concatenate([weights, jnp.zeros_like(weights)], axis=1)
    products = adjoint_products(padded, kernel_all)[:, :8]
    backward = adjoint_sources(products, compact[19:22])
    spread = unpermute_columns(backward, selector)
    spread = spread.reshape(16, owners, capacity).transpose(1, 0, 2).reshape(owners, -1, 128)
    returned = exchange(spread, 2).reshape(owners, 16, capacity).transpose(2, 0, 1).reshape(rows_dev, 16)
    rows_major = returned * living[:, None]
    cell_adjoint = scatter_rows(surface_cell, rows_major, cell_state.shape[1])
    return (far_field, objective, cell_adjoint)


def solution(mesh):
    placed = (
        P(None, ("gx", "gy")),
        P(None, ("gx", "gy")),
        P(("gx", "gy")),
        P(("gx", "gy")),
        P(),
        P(),
        P(),
    )
    return jax.shard_map(
        on_device,
        mesh=mesh,
        in_specs=placed,
        out_specs=(P(), P(), P(None, ("gx", "gy"))),
        check_vma=False,
    )
```

```python
import functools
import math

import jax
import jax.numpy as jnp
from jax import lax
from jax.experimental import pallas as pl
from jax.experimental.pallas import tpu as pltpu
from jax.sharding import PartitionSpec as P

GOLDEN = math.pi * (3.0 - math.sqrt(5.0))
PI_A = round(math.pi * 32768.0) / 32768.0
PI_B = math.pi - PI_A
INV_PI = 1.0 / math.pi
SIN_C = [-0.16666657019913644, 0.00833301540393062, -0.00019806478078586938, 2.599750005030262e-06]
COS_C = [-0.4999993175258851, 0.041663973510963626, -0.0013855797199316853, 2.3191254010748703e-05]
SINPI_C = [3.141592578574041, -5.1677067848796066, 2.5500297991194887, -0.5980355679943354, 0.07720094563063706]
COSPI_C = [-4.934795411606951, 4.05844824012755, -1.332068921858188, 0.22002136541700046]


ROOT2 = math.sqrt(2.0)


def sincos_half_turns(v):
    w = v - jnp.floor(v + 0.5)
    z = w * w
    ps = SINPI_C[-1] * ROOT2
    for c in SINPI_C[-2::-1]:
        ps = c * ROOT2 + z * ps
    pc = COSPI_C[-1] * ROOT2
    for c in COSPI_C[-2::-1]:
        pc = c * ROOT2 + z * pc
    sine_half = w * ps
    cosine_half = ROOT2 + z * pc
    return (cosine_half * cosine_half - 1.0, sine_half * cosine_half)


def sincos_turns(u):
    n = jnp.floor(u + 0.5)
    w = u - n
    z = w * w
    ps = SINPI_C[-1]
    for c in SINPI_C[-2::-1]:
        ps = c + z * ps
    pc = COSPI_C[-1]
    for c in COSPI_C[-2::-1]:
        pc = c + z * pc
    half = n * 0.5
    sign = 1.0 - 4.0 * (half - jnp.floor(half))
    return (sign * (1.0 + z * pc), (sign * w) * ps)


def sincos(theta):
    n = jnp.floor(theta * INV_PI + 0.5)
    r = (theta - n * PI_A) - n * PI_B
    z = r * r
    ps = SIN_C[-1]
    for c in SIN_C[-2::-1]:
        ps = c + z * ps
    pc = COS_C[-1]
    for c in COS_C[-2::-1]:
        pc = c + z * pc
    half = n * 0.5
    sign = 1.0 - 4.0 * (half - jnp.floor(half))
    return (sign * (1.0 + z * pc), sign * (r + (r * z) * ps))


def directions(count_dirs):
    lattice = jnp.arange(count_dirs).astype(jnp.float32)
    height = 1.0 - (2.0 * lattice + 1.0) / count_dirs
    radius_xy = jnp.sqrt(1.0 - height * height)
    azimuth = jnp.mod(lattice * GOLDEN, 2.0 * math.pi)
    return (radius_xy * jnp.cos(azimuth), radius_xy * jnp.sin(azimuth), height)


def kernel_block(points, wavenum, east_x, north_y, upward):
    phases = wavenum * (
        points[0][:, None] * east_x[None, :]
        + points[1][:, None] * north_y[None, :]
        + points[2][:, None] * upward[None, :]
    )
    cosine, sine = sincos(phases)
    return jnp.concatenate([cosine, sine], axis=1).astype(jnp.bfloat16)


def source_rows(rows_block, level):
    surface_area = rows_block[22]
    normal = rows_block[19:22]
    pressure_real = rows_block[level] * surface_area
    pressure_imag = rows_block[4 + level] * surface_area
    return jnp.stack(
        [
            rows_block[8 + level] * surface_area,
            normal[0] * pressure_real,
            normal[1] * pressure_real,
            normal[2] * pressure_real,
            rows_block[12 + level] * surface_area,
            normal[0] * pressure_imag,
            normal[1] * pressure_imag,
            normal[2] * pressure_imag,
        ]
    ).astype(jnp.bfloat16)


def far_field_of(sums, wavenumbers, direction_basis):
    half_width = sums.shape[2] // 2
    cosine_part = sums[:, :, :half_width]
    sine_part = sums[:, :, half_width:]
    real_q = cosine_part[:, 0:4] + sine_part[:, 4:8]
    imag_q = cosine_part[:, 4:8] - sine_part[:, 0:4]
    real_z = jnp.sum(direction_basis[None] * real_q, axis=1)
    imag_z = jnp.sum(direction_basis[None] * imag_q, axis=1)
    wavenum = wavenumbers[:, None]
    return jnp.stack([-wavenum * imag_z, wavenum * real_z], axis=1)


def adjoint_weights(far_field, target, direction_weight, wavenumbers, direction_basis):
    count_dirs = far_field.shape[2]
    mismatch = far_field - target
    objective = jnp.sum(direction_weight * mismatch * mismatch) / count_dirs
    gradient = 2.0 * direction_weight * mismatch / count_dirs
    wavenum = wavenumbers[:, None]
    real_gz = wavenum * gradient[:, 1]
    imag_gz = -wavenum * gradient[:, 0]
    real_gq = direction_basis[None] * real_gz[:, None]
    imag_gq = direction_basis[None] * imag_gz[:, None]
    upper_half = jnp.concatenate([real_gq, -imag_gq], axis=2)
    lower_half = jnp.concatenate([imag_gq, real_gq], axis=2)
    return (objective, jnp.concatenate([upper_half, lower_half], axis=1).astype(jnp.bfloat16))


def adjoint_sources(products, normal):
    pressure_real = jnp.sum(normal[None] * products[:, 1:4], axis=1)
    pressure_imag = jnp.sum(normal[None] * products[:, 5:8], axis=1)
    return jnp.concatenate([pressure_real, pressure_imag, products[:, 0], products[:, 4]], axis=0)


ROW_BLOCK = 128
ADJ_BLOCK = 512
ROW_CHUNK = 32
LANE_CHUNK = 256


def forward_kernel(wave_ref, pts_ref, dirs_ref, rows_ref, cs_ref, q_ref, src_scr):
    step = pl.program_id(0)
    num_freqs = cs_ref.shape[0]
    count_dirs = dirs_ref.shape[2]
    turns = [wave_ref[level] * (0.5 * INV_PI) for level in range(num_freqs)]

    @pl.loop(0, ROW_BLOCK // ROW_CHUNK)
    def _(i):
        r0 = pl.multiple_of(i * ROW_CHUNK, ROW_CHUNK)
        coords = [
            jnp.broadcast_to(pts_ref[pl.ds(r0, ROW_CHUNK), c : c + 1], (ROW_CHUNK, LANE_CHUNK))
            for c in range(3)
        ]
        for j0 in range(0, count_dirs, LANE_CHUNK):
            lanes = slice(j0, j0 + LANE_CHUNK)
            along = (
                coords[0] * dirs_ref[0, :, lanes]
                + coords[1] * dirs_ref[1, :, lanes]
                + coords[2] * dirs_ref[2, :, lanes]
            )
            for level in range(num_freqs):
                cosine, sine = sincos_half_turns(turns[level] * along)
                cs_ref[level, pl.ds(r0, ROW_CHUNK), lanes] = cosine.astype(jnp.bfloat16)
                cs_ref[level, pl.ds(r0, ROW_CHUNK), j0 + count_dirs : j0 + count_dirs + LANE_CHUNK] = (
                    sine.astype(jnp.bfloat16)
                )

    @pl.when(step == 0)
    def _():
        q_ref[...] = jnp.zeros_like(q_ref)

    area = rows_ref[22:23, :]
    src_scr[...] = jnp.zeros_like(src_scr)
    for level in range(num_freqs):
        pressure_real = rows_ref[level : level + 1, :] * area
        pressure_imag = rows_ref[4 + level : 5 + level, :] * area
        src_scr[0:1, :] = rows_ref[8 + level : 9 + level, :] * area
        src_scr[4:5, :] = rows_ref[12 + level : 13 + level, :] * area
        for c in range(3):
            normal = rows_ref[19 + c : 20 + c, :]
            src_scr[1 + c : 2 + c, :] = normal * pressure_real
            src_scr[5 + c : 6 + c, :] = normal * pressure_imag
        source = src_scr[...].astype(jnp.bfloat16)
        q_ref[level] += jnp.dot(source, cs_ref[level], preferred_element_type=jnp.float32)


def forward_sums(wavenumbers, points, dirs_block, compact):
    num_freqs = wavenumbers.shape[0]
    rows = points.shape[0]
    count_dirs = dirs_block.shape[2]
    grid = (rows // ROW_BLOCK,)
    return pl.pallas_call(
        forward_kernel,
        grid=grid,
        in_specs=[
            pl.BlockSpec(memory_space=pltpu.SMEM),
            pl.BlockSpec((ROW_BLOCK, 3), lambda b: (b, 0)),
            pl.BlockSpec(dirs_block.shape, lambda b: (0, 0, 0)),
            pl.BlockSpec((compact.shape[0], ROW_BLOCK), lambda b: (0, b)),
        ],
        out_specs=[
            pl.BlockSpec((num_freqs, ROW_BLOCK, 2 * count_dirs), lambda b: (0, b, 0)),
            pl.BlockSpec((num_freqs, 16, 2 * count_dirs), lambda b: (0, 0, 0)),
        ],
        out_shape=[
            jax.ShapeDtypeStruct((num_freqs, rows, 2 * count_dirs), jnp.bfloat16),
            jax.ShapeDtypeStruct((num_freqs, 16, 2 * count_dirs), jnp.float32),
        ],
        scratch_shapes=[pltpu.VMEM((16, ROW_BLOCK), jnp.float32)],
        compiler_params=pltpu.CompilerParams(
            dimension_semantics=("arbitrary",), vmem_limit_bytes=48 * 1024 * 1024
        ),
        cost_estimate=pl.CostEstimate(
            flops=2 * 16 * rows * 2 * count_dirs * num_freqs + 60 * rows * count_dirs * num_freqs,
            transcendentals=0,
            bytes_accessed=2 * rows * 2 * count_dirs * num_freqs,
        ),
    )(wavenumbers, points, dirs_block, compact)


def adjoint_kernel(w_ref, cs_ref, out_ref):
    for level in range(cs_ref.shape[0]):
        out_ref[level] = lax.dot_general(
            w_ref[level], cs_ref[level], (((1,), (1,)), ((), ())), preferred_element_type=jnp.float32
        )


def adjoint_products(weights, kernel_all):
    num_freqs, rows, width = kernel_all.shape
    return pl.pallas_call(
        adjoint_kernel,
        grid=(rows // ADJ_BLOCK,),
        in_specs=[
            pl.BlockSpec(weights.shape, lambda b: (0, 0, 0)),
            pl.BlockSpec((num_freqs, ADJ_BLOCK, width), lambda b: (0, b, 0)),
        ],
        out_specs=pl.BlockSpec((num_freqs, weights.shape[1], ADJ_BLOCK), lambda b: (0, 0, b)),
        out_shape=jax.ShapeDtypeStruct((num_freqs, weights.shape[1], rows), jnp.float32),
        compiler_params=pltpu.CompilerParams(
            dimension_semantics=("arbitrary",), vmem_limit_bytes=48 * 1024 * 1024
        ),
        cost_estimate=pl.CostEstimate(
            flops=2 * weights.shape[1] * rows * width * num_freqs,
            transcendentals=0,
            bytes_accessed=2 * rows * width * num_freqs,
        ),
    )(weights, kernel_all)


def split_bf16(values):
    high = lax.reduce_precision(values, exponent_bits=8, mantissa_bits=7)
    rest = values - high
    middle = lax.reduce_precision(rest, exponent_bits=8, mantissa_bits=7)
    low = rest - middle
    return jnp.concatenate([high, middle, low], axis=0).astype(jnp.bfloat16)


def join_parts(product, channels):
    return (product[:channels] + product[channels : 2 * channels]) + product[2 * channels :]


def permute_columns(values, selector):
    product = jnp.dot(split_bf16(values), selector, preferred_element_type=jnp.float32)
    return join_parts(product, values.shape[0])


def unpermute_columns(values, selector):
    product = lax.dot_general(
        split_bf16(values), selector, (((1,), (1,)), ((), ())), preferred_element_type=jnp.float32
    )
    return join_parts(product, values.shape[0])


CHAINS = 8


def scatter_kernel(cell_ref, rows_ref, out_ref, *accs):
    for acc in accs:
        acc[...] = jnp.zeros_like(acc)
    chains = len(accs)

    def body(i, carry):
        for k in range(chains):
            row = i * chains + k
            cell = cell_ref[row]
            accs[k][pl.ds(cell, 1), :] += rows_ref[pl.ds(row, 1), :]
        return carry

    lax.fori_loop(0, rows_ref.shape[0] // chains, body, 0, unroll=8)
    total = accs[0][...]
    for acc in accs[1:]:
        total = total + acc[...]
    out_ref[...] = total.T


def scatter_rows(surface_cell, rows_major, cells):
    width = rows_major.shape[1]
    return pl.pallas_call(
        scatter_kernel,
        grid_spec=pltpu.PrefetchScalarGridSpec(
            num_scalar_prefetch=1,
            grid=(1,),
            in_specs=[pl.BlockSpec(rows_major.shape, lambda i, c: (0, 0))],
            out_specs=pl.BlockSpec((width, cells), lambda i, c: (0, 0)),
            scratch_shapes=[pltpu.VMEM((cells, width), jnp.float32) for _ in range(CHAINS)],
        ),
        out_shape=jax.ShapeDtypeStruct((width, cells), jnp.float32),
        compiler_params=pltpu.CompilerParams(vmem_limit_bytes=48 * 1024 * 1024),
    )(surface_cell, rows_major)


GATHER_UNROLL = 128


def gather_kernel(cell_ref, state_ref, out_ref, table_ref):
    table_ref[...] = state_ref[...].T

    def body(i, carry):
        for k in range(GATHER_UNROLL):
            row = i * GATHER_UNROLL + k
            out_ref[pl.ds(row, 1), :] = table_ref[pl.ds(cell_ref[row], 1), :]
        return carry

    lax.fori_loop(0, out_ref.shape[0] // GATHER_UNROLL, body, 0)


def gather_rows(surface_cell, state):
    rows = surface_cell.shape[0]
    channels, cells = state.shape
    return pl.pallas_call(
        gather_kernel,
        grid_spec=pltpu.PrefetchScalarGridSpec(
            num_scalar_prefetch=1,
            grid=(1,),
            in_specs=[pl.BlockSpec(state.shape, lambda i, c: (0, 0))],
            out_specs=pl.BlockSpec((rows, channels), lambda i, c: (0, 0)),
            scratch_shapes=[pltpu.VMEM((cells, channels), state.dtype)],
        ),
        out_shape=jax.ShapeDtypeStruct((rows, channels), state.dtype),
        compiler_params=pltpu.CompilerParams(vmem_limit_bytes=48 * 1024 * 1024),
    )(surface_cell, state)


MESH_IDS = pl.DeviceIdType.MESH


def reduce_kernel(nx, ny, x_ref, out_ref, part_a, part_b, got_a, got_b, sems):
    b0 = lax.axis_index("gx")
    a0 = lax.axis_index("gy")
    barrier = pltpu.get_barrier_semaphore()
    for t in range(1, ny):
        pl.semaphore_signal(barrier, inc=1, device_id=(b0, lax.rem(a0 + t, ny)), device_id_type=MESH_IDS)
    for t in range(1, nx):
        pl.semaphore_signal(barrier, inc=1, device_id=(lax.rem(b0 + t, nx), a0), device_id_type=MESH_IDS)
    pl.semaphore_wait(barrier, nx + ny - 2)

    def exchange(phase, src_of, dst_of, peers, along_x):
        copies = []
        for t in range(1, peers):
            if along_x:
                peer = lax.rem(b0 + t, nx)
                me, device = b0, (peer, a0)
            else:
                peer = lax.rem(a0 + t, ny)
                me, device = a0, (b0, peer)
            copy = pltpu.make_async_remote_copy(
                src_ref=src_of(peer),
                dst_ref=dst_of(me),
                send_sem=sems.at[phase, 0, peer],
                recv_sem=sems.at[phase, 1, me],
                device_id=device,
                device_id_type=MESH_IDS,
            )
            copy.start()
            copies.append((peer, device))
        for peer, device in copies:
            pltpu.make_async_remote_copy(
                src_ref=src_of(peer),
                dst_ref=dst_of(peer),
                send_sem=sems.at[phase, 0, peer],
                recv_sem=sems.at[phase, 1, peer],
                device_id=device,
                device_id_type=MESH_IDS,
            ).wait()

    exchange(0, lambda a: x_ref.at[a], lambda a: got_a.at[a], ny, False)
    got_a[a0] = x_ref[a0]
    part_a[...] = jnp.sum(got_a[...], axis=0)
    exchange(1, lambda b: part_a, lambda b: got_b.at[b], nx, True)
    got_b[b0] = part_a[...]
    part_b[...] = jnp.sum(got_b[...], axis=0)
    exchange(2, lambda a: part_b, lambda a: out_ref.at[a], ny, False)
    out_ref[a0] = part_b[...]


def exchange_kernel(nx, ny, x_ref, out_ref, landing, send_sems, recv_sems):
    total = nx * ny
    me = lax.axis_index("gx") * ny + lax.axis_index("gy")
    barrier = pltpu.get_barrier_semaphore()

    def where(peer):
        return (peer // ny, lax.rem(peer, ny))

    def copy_to(peer, slot):
        return pltpu.make_async_remote_copy(
            src_ref=x_ref.at[peer],
            dst_ref=landing.at[slot],
            send_sem=send_sems.at[peer],
            recv_sem=recv_sems.at[slot],
            device_id=where(peer),
            device_id_type=MESH_IDS,
        )

    def greet(t, carry):
        pl.semaphore_signal(barrier, inc=1, device_id=where(lax.rem(me + t, total)), device_id_type=MESH_IDS)
        return carry

    lax.fori_loop(1, total, greet, 0, unroll=8)
    pl.semaphore_wait(barrier, total - 1)

    def send(t, carry):
        copy_to(lax.rem(me + t, total), me).start()
        return carry

    lax.fori_loop(1, total, send, 0, unroll=8)
    landing[me] = x_ref[me]

    def finish(t, carry):
        peer = lax.rem(me + t, total)
        copy_to(peer, peer).wait()
        return carry

    lax.fori_loop(1, total, finish, 0, unroll=8)
    out_ref[...] = landing[...]


def exchange(blocks, exchange_id):
    nx = lax.axis_size("gx")
    ny = lax.axis_size("gy")
    return pl.pallas_call(
        functools.partial(exchange_kernel, nx, ny),
        in_specs=[pl.BlockSpec(memory_space=pltpu.VMEM)],
        out_specs=pl.BlockSpec(memory_space=pltpu.VMEM),
        out_shape=jax.ShapeDtypeStruct(blocks.shape, blocks.dtype),
        scratch_shapes=[
            pltpu.VMEM(blocks.shape, blocks.dtype),
            pltpu.SemaphoreType.DMA((nx * ny,)),
            pltpu.SemaphoreType.DMA((nx * ny,)),
        ],
        compiler_params=pltpu.CompilerParams(collective_id=exchange_id, has_side_effects=True),
    )(blocks)


def sum_over_devices(partial, owners):
    nx = lax.axis_size("gx")
    ny = lax.axis_size("gy")
    lanes = partial.size // (nx * ny)
    shaped = partial.reshape(ny, nx, lanes)
    peers = max(nx, ny)
    total = pl.pallas_call(
        functools.partial(reduce_kernel, nx, ny),
        in_specs=[pl.BlockSpec(memory_space=pltpu.VMEM)],
        out_specs=pl.BlockSpec(memory_space=pltpu.VMEM),
        out_shape=jax.ShapeDtypeStruct(shaped.shape, jnp.float32),
        scratch_shapes=[
            pltpu.VMEM((nx, lanes), jnp.float32),
            pltpu.VMEM((nx, lanes), jnp.float32),
            pltpu.VMEM((ny, nx, lanes), jnp.float32),
            pltpu.VMEM((nx, nx, lanes), jnp.float32),
            pltpu.SemaphoreType.DMA((3, 2, peers)),
        ],
        compiler_params=pltpu.CompilerParams(collective_id=0, has_side_effects=True),
    )(shaped)
    return total.reshape(partial.shape)


def sum_over_devices_a2a(partial, owners):
    chunks = partial.reshape(owners, -1)
    got = lax.all_to_all(chunks, ("gx", "gy"), split_axis=0, concat_axis=0, tiled=True)
    mine = jnp.sum(got, axis=0, keepdims=True)
    spread = jnp.broadcast_to(mine, chunks.shape)
    full = lax.all_to_all(spread, ("gx", "gy"), split_axis=0, concat_axis=0, tiled=True)
    return full.reshape(partial.shape)


def on_device(cell_state, geometry, surface_cell, counts, wavenumbers, target, direction_weight):
    owners = lax.axis_size(("gx", "gy"))
    rows_dev = surface_cell.shape[0]
    capacity = rows_dev // owners
    live_own = rows_dev // 4
    count_dirs = target.shape[2]
    num_freqs = wavenumbers.shape[0]
    living = (jnp.arange(rows_dev) < counts[0]).astype(jnp.float32)
    outgoing = (
        jnp.concatenate(
            [gather_rows(surface_cell, cell_state).T, geometry, jnp.ones((1, rows_dev), jnp.float32)], axis=0
        )
        * living[None, :]
    )
    outgoing = outgoing.reshape(24, capacity, owners).transpose(2, 0, 1).reshape(owners, -1, 128)
    arrived = exchange(outgoing, 1).reshape(owners, 24, capacity).transpose(1, 0, 2)
    marker = arrived[23]
    per_source = jnp.sum(marker, axis=1).astype(jnp.int32)
    offset = jnp.cumsum(per_source) - per_source
    position = offset[:, None] + jnp.arange(capacity, dtype=jnp.int32)[None, :]
    packed_slot = jnp.where(marker > 0.5, position, live_own).reshape(capacity * owners)
    selector = (packed_slot[:, None] == jnp.arange(live_own, dtype=jnp.int32)[None, :]).astype(jnp.bfloat16)
    compact = permute_columns(arrived[:23].reshape(23, capacity * owners), selector)
    east_x, north_y, upward = directions(count_dirs)
    direction_basis = jnp.stack([jnp.ones_like(east_x), east_x, north_y, upward])

    points = compact[16:19].T
    dirs_block = jnp.broadcast_to(jnp.stack([east_x, north_y, upward])[:, None, :], (3, ROW_CHUNK, count_dirs))
    kernel_all, sums = forward_sums(wavenumbers, points, dirs_block, compact)
    sums = sums[:, :8]
    far_field = sum_over_devices(far_field_of(sums, wavenumbers, direction_basis), owners)
    objective, weights = adjoint_weights(
        far_field, target, direction_weight, wavenumbers, direction_basis
    )

    padded = jnp.concatenate([weights, jnp.zeros_like(weights)], axis=1)
    products = adjoint_products(padded, kernel_all)[:, :8]
    backward = adjoint_sources(products, compact[19:22])
    spread = unpermute_columns(backward, selector)
    spread = spread.reshape(16, owners, capacity).transpose(1, 0, 2).reshape(owners, -1, 128)
    returned = exchange(spread, 2).reshape(owners, 16, capacity).transpose(2, 0, 1).reshape(rows_dev, 16)
    rows_major = returned * living[:, None]
    cell_adjoint = scatter_rows(surface_cell, rows_major, cell_state.shape[1])
    return (far_field, objective, cell_adjoint)


def solution(mesh):
    placed = (
        P(None, ("gx", "gy")),
        P(None, ("gx", "gy")),
        P(("gx", "gy")),
        P(("gx", "gy")),
        P(),
        P(),
        P(),
    )
    return jax.shard_map(
        on_device,
        mesh=mesh,
        in_specs=placed,
        out_specs=(P(), P(), P(None, ("gx", "gy"))),
        check_vma=False,
    )
```

```python
import functools
import math

import jax
import jax.numpy as jnp
from jax import lax
from jax.experimental import pallas as pl
from jax.experimental.pallas import tpu as pltpu
from jax.sharding import PartitionSpec as P

GOLDEN = math.pi * (3.0 - math.sqrt(5.0))
PI_A = round(math.pi * 32768.0) / 32768.0
PI_B = math.pi - PI_A
INV_PI = 1.0 / math.pi
SIN_C = [-0.16666657019913644, 0.00833301540393062, -0.00019806478078586938, 2.599750005030262e-06]
COS_C = [-0.4999993175258851, 0.041663973510963626, -0.0013855797199316853, 2.3191254010748703e-05]
SINPI_C = [3.141592578574041, -5.1677067848796066, 2.5500297991194887, -0.5980355679943354, 0.07720094563063706]
COSPI_C = [-4.934795411606951, 4.05844824012755, -1.332068921858188, 0.22002136541700046]


ROOT2 = math.sqrt(2.0)


def sincos_half_turns(v):
    w = v - jnp.floor(v + 0.5)
    z = w * w
    ps = SINPI_C[-1] * ROOT2
    for c in SINPI_C[-2::-1]:
        ps = c * ROOT2 + z * ps
    pc = COSPI_C[-1] * ROOT2
    for c in COSPI_C[-2::-1]:
        pc = c * ROOT2 + z * pc
    sine_half = w * ps
    cosine_half = ROOT2 + z * pc
    return (cosine_half * cosine_half - 1.0, sine_half * cosine_half)


def sincos_turns(u):
    n = jnp.floor(u + 0.5)
    w = u - n
    z = w * w
    ps = SINPI_C[-1]
    for c in SINPI_C[-2::-1]:
        ps = c + z * ps
    pc = COSPI_C[-1]
    for c in COSPI_C[-2::-1]:
        pc = c + z * pc
    half = n * 0.5
    sign = 1.0 - 4.0 * (half - jnp.floor(half))
    return (sign * (1.0 + z * pc), (sign * w) * ps)


def sincos(theta):
    n = jnp.floor(theta * INV_PI + 0.5)
    r = (theta - n * PI_A) - n * PI_B
    z = r * r
    ps = SIN_C[-1]
    for c in SIN_C[-2::-1]:
        ps = c + z * ps
    pc = COS_C[-1]
    for c in COS_C[-2::-1]:
        pc = c + z * pc
    half = n * 0.5
    sign = 1.0 - 4.0 * (half - jnp.floor(half))
    return (sign * (1.0 + z * pc), sign * (r + (r * z) * ps))


def directions(count_dirs):
    lattice = jnp.arange(count_dirs).astype(jnp.float32)
    height = 1.0 - (2.0 * lattice + 1.0) / count_dirs
    radius_xy = jnp.sqrt(1.0 - height * height)
    azimuth = jnp.mod(lattice * GOLDEN, 2.0 * math.pi)
    return (radius_xy * jnp.cos(azimuth), radius_xy * jnp.sin(azimuth), height)


def kernel_block(points, wavenum, east_x, north_y, upward):
    phases = wavenum * (
        points[0][:, None] * east_x[None, :]
        + points[1][:, None] * north_y[None, :]
        + points[2][:, None] * upward[None, :]
    )
    cosine, sine = sincos(phases)
    return jnp.concatenate([cosine, sine], axis=1).astype(jnp.bfloat16)


def source_rows(rows_block, level):
    surface_area = rows_block[22]
    normal = rows_block[19:22]
    pressure_real = rows_block[level] * surface_area
    pressure_imag = rows_block[4 + level] * surface_area
    return jnp.stack(
        [
            rows_block[8 + level] * surface_area,
            normal[0] * pressure_real,
            normal[1] * pressure_real,
            normal[2] * pressure_real,
            rows_block[12 + level] * surface_area,
            normal[0] * pressure_imag,
            normal[1] * pressure_imag,
            normal[2] * pressure_imag,
        ]
    ).astype(jnp.bfloat16)


def far_field_of(sums, wavenumbers, direction_basis):
    half_width = sums.shape[2] // 2
    cosine_part = sums[:, :, :half_width]
    sine_part = sums[:, :, half_width:]
    real_q = cosine_part[:, 0:4] + sine_part[:, 4:8]
    imag_q = cosine_part[:, 4:8] - sine_part[:, 0:4]
    real_z = jnp.sum(direction_basis[None] * real_q, axis=1)
    imag_z = jnp.sum(direction_basis[None] * imag_q, axis=1)
    wavenum = wavenumbers[:, None]
    return jnp.stack([-wavenum * imag_z, wavenum * real_z], axis=1)


def adjoint_weights(far_field, target, direction_weight, wavenumbers, direction_basis):
    count_dirs = far_field.shape[2]
    mismatch = far_field - target
    objective = jnp.sum(direction_weight * mismatch * mismatch) / count_dirs
    gradient = 2.0 * direction_weight * mismatch / count_dirs
    wavenum = wavenumbers[:, None]
    real_gz = wavenum * gradient[:, 1]
    imag_gz = -wavenum * gradient[:, 0]
    real_gq = direction_basis[None] * real_gz[:, None]
    imag_gq = direction_basis[None] * imag_gz[:, None]
    upper_half = jnp.concatenate([real_gq, -imag_gq], axis=2)
    lower_half = jnp.concatenate([imag_gq, real_gq], axis=2)
    return (objective, jnp.concatenate([upper_half, lower_half], axis=1).astype(jnp.bfloat16))


def adjoint_sources(products, normal):
    pressure_real = jnp.sum(normal[None] * products[:, 1:4], axis=1)
    pressure_imag = jnp.sum(normal[None] * products[:, 5:8], axis=1)
    return jnp.concatenate([pressure_real, pressure_imag, products[:, 0], products[:, 4]], axis=0)


ROW_BLOCK = 128
ADJ_BLOCK = 256
ROW_CHUNK = 32
LANE_CHUNK = 256


def forward_kernel(wave_ref, pts_ref, dirs_ref, rows_ref, cs_ref, q_ref, src_scr):
    step = pl.program_id(0)
    num_freqs = cs_ref.shape[0]
    count_dirs = dirs_ref.shape[2]
    turns = [wave_ref[level] * (0.5 * INV_PI) for level in range(num_freqs)]

    @pl.loop(0, ROW_BLOCK // ROW_CHUNK)
    def _(i):
        r0 = pl.multiple_of(i * ROW_CHUNK, ROW_CHUNK)
        coords = [
            jnp.broadcast_to(pts_ref[pl.ds(r0, ROW_CHUNK), c : c + 1], (ROW_CHUNK, LANE_CHUNK))
            for c in range(3)
        ]
        for j0 in range(0, count_dirs, LANE_CHUNK):
            lanes = slice(j0, j0 + LANE_CHUNK)
            along = (
                coords[0] * dirs_ref[0, :, lanes]
                + coords[1] * dirs_ref[1, :, lanes]
                + coords[2] * dirs_ref[2, :, lanes]
            )
            for level in range(num_freqs):
                cosine, sine = sincos_half_turns(turns[level] * along)
                cs_ref[level, pl.ds(r0, ROW_CHUNK), lanes] = cosine.astype(jnp.bfloat16)
                cs_ref[level, pl.ds(r0, ROW_CHUNK), j0 + count_dirs : j0 + count_dirs + LANE_CHUNK] = (
                    sine.astype(jnp.bfloat16)
                )

    @pl.when(step == 0)
    def _():
        q_ref[...] = jnp.zeros_like(q_ref)

    area = rows_ref[22:23, :]
    src_scr[...] = jnp.zeros_like(src_scr)
    for level in range(num_freqs):
        pressure_real = rows_ref[level : level + 1, :] * area
        pressure_imag = rows_ref[4 + level : 5 + level, :] * area
        src_scr[0:1, :] = rows_ref[8 + level : 9 + level, :] * area
        src_scr[4:5, :] = rows_ref[12 + level : 13 + level, :] * area
        for c in range(3):
            normal = rows_ref[19 + c : 20 + c, :]
            src_scr[1 + c : 2 + c, :] = normal * pressure_real
            src_scr[5 + c : 6 + c, :] = normal * pressure_imag
        source = src_scr[...].astype(jnp.bfloat16)
        q_ref[level] += jnp.dot(source, cs_ref[level], preferred_element_type=jnp.float32)


def forward_sums(wavenumbers, points, dirs_block, compact):
    num_freqs = wavenumbers.shape[0]
    rows = points.shape[0]
    count_dirs = dirs_block.shape[2]
    grid = (rows // ROW_BLOCK,)
    return pl.pallas_call(
        forward_kernel,
        grid=grid,
        in_specs=[
            pl.BlockSpec(memory_space=pltpu.SMEM),
            pl.BlockSpec((ROW_BLOCK, 3), lambda b: (b, 0)),
            pl.BlockSpec(dirs_block.shape, lambda b: (0, 0, 0)),
            pl.BlockSpec((compact.shape[0], ROW_BLOCK), lambda b: (0, b)),
        ],
        out_specs=[
            pl.BlockSpec((num_freqs, ROW_BLOCK, 2 * count_dirs), lambda b: (0, b, 0)),
            pl.BlockSpec((num_freqs, 16, 2 * count_dirs), lambda b: (0, 0, 0)),
        ],
        out_shape=[
            jax.ShapeDtypeStruct((num_freqs, rows, 2 * count_dirs), jnp.bfloat16),
            jax.ShapeDtypeStruct((num_freqs, 16, 2 * count_dirs), jnp.float32),
        ],
        scratch_shapes=[pltpu.VMEM((16, ROW_BLOCK), jnp.float32)],
        compiler_params=pltpu.CompilerParams(
            dimension_semantics=("arbitrary",), vmem_limit_bytes=48 * 1024 * 1024
        ),
        cost_estimate=pl.CostEstimate(
            flops=2 * 16 * rows * 2 * count_dirs * num_freqs + 60 * rows * count_dirs * num_freqs,
            transcendentals=0,
            bytes_accessed=2 * rows * 2 * count_dirs * num_freqs,
        ),
    )(wavenumbers, points, dirs_block, compact)


def adjoint_kernel(w_ref, cs_ref, out_ref):
    for level in range(cs_ref.shape[0]):
        out_ref[level] = lax.dot_general(
            w_ref[level], cs_ref[level], (((1,), (1,)), ((), ())), preferred_element_type=jnp.float32
        )


def adjoint_products(weights, kernel_all):
    num_freqs, rows, width = kernel_all.shape
    return pl.pallas_call(
        adjoint_kernel,
        grid=(rows // ADJ_BLOCK,),
        in_specs=[
            pl.BlockSpec(weights.shape, lambda b: (0, 0, 0)),
            pl.BlockSpec((num_freqs, ADJ_BLOCK, width), lambda b: (0, b, 0)),
        ],
        out_specs=pl.BlockSpec((num_freqs, weights.shape[1], ADJ_BLOCK), lambda b: (0, 0, b)),
        out_shape=jax.ShapeDtypeStruct((num_freqs, weights.shape[1], rows), jnp.float32),
        compiler_params=pltpu.CompilerParams(
            dimension_semantics=("arbitrary",), vmem_limit_bytes=48 * 1024 * 1024
        ),
        cost_estimate=pl.CostEstimate(
            flops=2 * weights.shape[1] * rows * width * num_freqs,
            transcendentals=0,
            bytes_accessed=2 * rows * width * num_freqs,
        ),
    )(weights, kernel_all)


def split_bf16(values):
    high = lax.reduce_precision(values, exponent_bits=8, mantissa_bits=7)
    rest = values - high
    middle = lax.reduce_precision(rest, exponent_bits=8, mantissa_bits=7)
    low = rest - middle
    return jnp.concatenate([high, middle, low], axis=0).astype(jnp.bfloat16)


def join_parts(product, channels):
    return (product[:channels] + product[channels : 2 * channels]) + product[2 * channels :]


def permute_columns(values, selector):
    product = jnp.dot(split_bf16(values), selector, preferred_element_type=jnp.float32)
    return join_parts(product, values.shape[0])


def unpermute_columns(values, selector):
    product = lax.dot_general(
        split_bf16(values), selector, (((1,), (1,)), ((), ())), preferred_element_type=jnp.float32
    )
    return join_parts(product, values.shape[0])


CHAINS = 8


def scatter_kernel(cell_ref, rows_ref, out_ref, *accs):
    for acc in accs:
        acc[...] = jnp.zeros_like(acc)
    chains = len(accs)

    def body(i, carry):
        for k in range(chains):
            row = i * chains + k
            cell = cell_ref[row]
            accs[k][pl.ds(cell, 1), :] += rows_ref[pl.ds(row, 1), :]
        return carry

    lax.fori_loop(0, rows_ref.shape[0] // chains, body, 0, unroll=16)
    total = accs[0][...]
    for acc in accs[1:]:
        total = total + acc[...]
    out_ref[...] = total.T


def scatter_rows(surface_cell, rows_major, cells):
    width = rows_major.shape[1]
    return pl.pallas_call(
        scatter_kernel,
        grid_spec=pltpu.PrefetchScalarGridSpec(
            num_scalar_prefetch=1,
            grid=(1,),
            in_specs=[pl.BlockSpec(rows_major.shape, lambda i, c: (0, 0))],
            out_specs=pl.BlockSpec((width, cells), lambda i, c: (0, 0)),
            scratch_shapes=[pltpu.VMEM((cells, width), jnp.float32) for _ in range(CHAINS)],
        ),
        out_shape=jax.ShapeDtypeStruct((width, cells), jnp.float32),
        compiler_params=pltpu.CompilerParams(vmem_limit_bytes=48 * 1024 * 1024),
    )(surface_cell, rows_major)


GATHER_UNROLL = 128


def gather_kernel(cell_ref, state_ref, out_ref, table_ref):
    table_ref[...] = state_ref[...].T

    def body(i, carry):
        for k in range(GATHER_UNROLL):
            row = i * GATHER_UNROLL + k
            out_ref[pl.ds(row, 1), :] = table_ref[pl.ds(cell_ref[row], 1), :]
        return carry

    lax.fori_loop(0, out_ref.shape[0] // GATHER_UNROLL, body, 0)


def gather_rows(surface_cell, state):
    rows = surface_cell.shape[0]
    channels, cells = state.shape
    return pl.pallas_call(
        gather_kernel,
        grid_spec=pltpu.PrefetchScalarGridSpec(
            num_scalar_prefetch=1,
            grid=(1,),
            in_specs=[pl.BlockSpec(state.shape, lambda i, c: (0, 0))],
            out_specs=pl.BlockSpec((rows, channels), lambda i, c: (0, 0)),
            scratch_shapes=[pltpu.VMEM((cells, channels), state.dtype)],
        ),
        out_shape=jax.ShapeDtypeStruct((rows, channels), state.dtype),
        compiler_params=pltpu.CompilerParams(vmem_limit_bytes=48 * 1024 * 1024),
    )(surface_cell, state)


MESH_IDS = pl.DeviceIdType.MESH


def reduce_kernel(nx, ny, x_ref, out_ref, part_a, part_b, got_a, got_b, sems):
    b0 = lax.axis_index("gx")
    a0 = lax.axis_index("gy")
    barrier = pltpu.get_barrier_semaphore()
    for t in range(1, ny):
        pl.semaphore_signal(barrier, inc=1, device_id=(b0, lax.rem(a0 + t, ny)), device_id_type=MESH_IDS)
    for t in range(1, nx):
        pl.semaphore_signal(barrier, inc=1, device_id=(lax.rem(b0 + t, nx), a0), device_id_type=MESH_IDS)
    pl.semaphore_wait(barrier, nx + ny - 2)

    def exchange(phase, src_of, dst_of, peers, along_x):
        copies = []
        for t in range(1, peers):
            if along_x:
                peer = lax.rem(b0 + t, nx)
                me, device = b0, (peer, a0)
            else:
                peer = lax.rem(a0 + t, ny)
                me, device = a0, (b0, peer)
            copy = pltpu.make_async_remote_copy(
                src_ref=src_of(peer),
                dst_ref=dst_of(me),
                send_sem=sems.at[phase, 0, peer],
                recv_sem=sems.at[phase, 1, me],
                device_id=device,
                device_id_type=MESH_IDS,
            )
            copy.start()
            copies.append((peer, device))
        for peer, device in copies:
            pltpu.make_async_remote_copy(
                src_ref=src_of(peer),
                dst_ref=dst_of(peer),
                send_sem=sems.at[phase, 0, peer],
                recv_sem=sems.at[phase, 1, peer],
                device_id=device,
                device_id_type=MESH_IDS,
            ).wait()

    exchange(0, lambda a: x_ref.at[a], lambda a: got_a.at[a], ny, False)
    got_a[a0] = x_ref[a0]
    part_a[...] = jnp.sum(got_a[...], axis=0)
    exchange(1, lambda b: part_a, lambda b: got_b.at[b], nx, True)
    got_b[b0] = part_a[...]
    part_b[...] = jnp.sum(got_b[...], axis=0)
    exchange(2, lambda a: part_b, lambda a: out_ref.at[a], ny, False)
    out_ref[a0] = part_b[...]


def exchange_kernel(nx, ny, x_ref, out_ref, landing, send_sems, recv_sems):
    total = nx * ny
    me = lax.axis_index("gx") * ny + lax.axis_index("gy")
    barrier = pltpu.get_barrier_semaphore()

    def where(peer):
        return (peer // ny, lax.rem(peer, ny))

    def copy_to(peer, slot):
        return pltpu.make_async_remote_copy(
            src_ref=x_ref.at[peer],
            dst_ref=landing.at[slot],
            send_sem=send_sems.at[peer],
            recv_sem=recv_sems.at[slot],
            device_id=where(peer),
            device_id_type=MESH_IDS,
        )

    def greet(t, carry):
        pl.semaphore_signal(barrier, inc=1, device_id=where(lax.rem(me + t, total)), device_id_type=MESH_IDS)
        return carry

    lax.fori_loop(1, total, greet, 0, unroll=16)
    pl.semaphore_wait(barrier, total - 1)

    def send(t, carry):
        copy_to(lax.rem(me + t, total), me).start()
        return carry

    lax.fori_loop(1, total, send, 0, unroll=16)
    landing[me] = x_ref[me]

    def finish(t, carry):
        peer = lax.rem(me + t, total)
        copy_to(peer, peer).wait()
        return carry

    lax.fori_loop(1, total, finish, 0, unroll=16)
    out_ref[...] = landing[...]


def exchange(blocks, exchange_id):
    nx = lax.axis_size("gx")
    ny = lax.axis_size("gy")
    return pl.pallas_call(
        functools.partial(exchange_kernel, nx, ny),
        in_specs=[pl.BlockSpec(memory_space=pltpu.VMEM)],
        out_specs=pl.BlockSpec(memory_space=pltpu.VMEM),
        out_shape=jax.ShapeDtypeStruct(blocks.shape, blocks.dtype),
        scratch_shapes=[
            pltpu.VMEM(blocks.shape, blocks.dtype),
            pltpu.SemaphoreType.DMA((nx * ny,)),
            pltpu.SemaphoreType.DMA((nx * ny,)),
        ],
        compiler_params=pltpu.CompilerParams(collective_id=exchange_id, has_side_effects=True),
    )(blocks)


def sum_over_devices(partial, owners):
    nx = lax.axis_size("gx")
    ny = lax.axis_size("gy")
    lanes = partial.size // (nx * ny)
    shaped = partial.reshape(ny, nx, lanes)
    peers = max(nx, ny)
    total = pl.pallas_call(
        functools.partial(reduce_kernel, nx, ny),
        in_specs=[pl.BlockSpec(memory_space=pltpu.VMEM)],
        out_specs=pl.BlockSpec(memory_space=pltpu.VMEM),
        out_shape=jax.ShapeDtypeStruct(shaped.shape, jnp.float32),
        scratch_shapes=[
            pltpu.VMEM((nx, lanes), jnp.float32),
            pltpu.VMEM((nx, lanes), jnp.float32),
            pltpu.VMEM((ny, nx, lanes), jnp.float32),
            pltpu.VMEM((nx, nx, lanes), jnp.float32),
            pltpu.SemaphoreType.DMA((3, 2, peers)),
        ],
        compiler_params=pltpu.CompilerParams(collective_id=0, has_side_effects=True),
    )(shaped)
    return total.reshape(partial.shape)


def sum_over_devices_a2a(partial, owners):
    chunks = partial.reshape(owners, -1)
    got = lax.all_to_all(chunks, ("gx", "gy"), split_axis=0, concat_axis=0, tiled=True)
    mine = jnp.sum(got, axis=0, keepdims=True)
    spread = jnp.broadcast_to(mine, chunks.shape)
    full = lax.all_to_all(spread, ("gx", "gy"), split_axis=0, concat_axis=0, tiled=True)
    return full.reshape(partial.shape)


def on_device(cell_state, geometry, surface_cell, counts, wavenumbers, target, direction_weight):
    owners = lax.axis_size(("gx", "gy"))
    rows_dev = surface_cell.shape[0]
    capacity = rows_dev // owners
    live_own = rows_dev // 4
    count_dirs = target.shape[2]
    num_freqs = wavenumbers.shape[0]
    living = (jnp.arange(rows_dev) < counts[0]).astype(jnp.float32)
    outgoing = (
        jnp.concatenate(
            [gather_rows(surface_cell, cell_state).T, geometry, jnp.ones((1, rows_dev), jnp.float32)], axis=0
        )
        * living[None, :]
    )
    outgoing = outgoing.reshape(24, capacity, owners).transpose(2, 0, 1).reshape(owners, -1, 128)
    arrived = exchange(outgoing, 1).reshape(owners, 24, capacity).transpose(1, 0, 2)
    marker = arrived[23]
    per_source = jnp.sum(marker, axis=1).astype(jnp.int32)
    offset = jnp.cumsum(per_source) - per_source
    position = offset[:, None] + jnp.arange(capacity, dtype=jnp.int32)[None, :]
    packed_slot = jnp.where(marker > 0.5, position, live_own).reshape(capacity * owners)
    selector = (packed_slot[:, None] == jnp.arange(live_own, dtype=jnp.int32)[None, :]).astype(jnp.bfloat16)
    compact = permute_columns(arrived[:23].reshape(23, capacity * owners), selector)
    east_x, north_y, upward = directions(count_dirs)
    direction_basis = jnp.stack([jnp.ones_like(east_x), east_x, north_y, upward])

    points = compact[16:19].T
    dirs_block = jnp.broadcast_to(jnp.stack([east_x, north_y, upward])[:, None, :], (3, ROW_CHUNK, count_dirs))
    kernel_all, sums = forward_sums(wavenumbers, points, dirs_block, compact)
    sums = sums[:, :8]
    far_field = sum_over_devices(far_field_of(sums, wavenumbers, direction_basis), owners)
    objective, weights = adjoint_weights(
        far_field, target, direction_weight, wavenumbers, direction_basis
    )

    padded = jnp.concatenate([weights, jnp.zeros_like(weights)], axis=1)
    products = adjoint_products(padded, kernel_all)[:, :8]
    backward = adjoint_sources(products, compact[19:22])
    spread = unpermute_columns(backward, selector)
    spread = spread.reshape(16, owners, capacity).transpose(1, 0, 2).reshape(owners, -1, 128)
    returned = exchange(spread, 2).reshape(owners, 16, capacity).transpose(2, 0, 1).reshape(rows_dev, 16)
    rows_major = returned * living[:, None]
    cell_adjoint = scatter_rows(surface_cell, rows_major, cell_state.shape[1])
    return (far_field, objective, cell_adjoint)


def solution(mesh):
    placed = (
        P(None, ("gx", "gy")),
        P(None, ("gx", "gy")),
        P(("gx", "gy")),
        P(("gx", "gy")),
        P(),
        P(),
        P(),
    )
    return jax.shard_map(
        on_device,
        mesh=mesh,
        in_specs=placed,
        out_specs=(P(), P(), P(None, ("gx", "gy"))),
        check_vma=False,
    )
```
